32 devices in a mesh: dp: 8 (over y, x, core), tensor: 4 (over z).
Axes of the slice: x: 2, y: 2, z: 4, core: 2. Of those that a mesh axis runs over, the one named last changes fastest.
Arguments:
- tokens: bfloat16 [8192, 1024], P(('dp', 'tensor')), may hold values from -6 to 6
- segments: int32 [8, 1024], P('dp'), may hold values from 0 to 3, never falling along the last dimension, each value on 1 to 512 neighbouring positions
- routes: int32 [8192, 2], P('dp'), may hold values from 0 to 15, all different within a row; in each aligned block of 1024 rows (0 to 1023, 1024 to 2047, ...) at most 160 rows name the same one
- w_qkv: bfloat16 [1024, 3, 1024], P('dp', None, 'tensor'), may hold values from -0.21875 to 0.21875
- w_attn_out: bfloat16 [1024, 1024], P('tensor', 'dp'), may hold values from -1 to 1
- bias_table: bfloat16 [32, 16], P('dp', 'tensor'), may hold values from -4 to 4
- gain_attn: bfloat16 [1024], P('dp'), may hold values from 0.5 to 1.5
- gain_moe: bfloat16 [1024], P('dp'), may hold values from 0.5 to 1.5
- router: bfloat16 [1024, 16], P('dp'), may hold values from -0.125 to 0.125
- w_in: bfloat16 [16, 2, 2816, 1024], P('dp', None, 'tensor'), may hold values from -0.1875 to 0.1875
- w_out: bfloat16 [16, 2816, 1024], P('dp', 'tensor'), may hold values from -0.1875 to 0.1875
- cotangent: bfloat16 [8192, 1024], P(('dp', 'tensor')), may hold values from -6 to 6
Outputs:
- layer_out: bfloat16 [8192, 1024], P(('dp', 'tensor'))
- grad_tokens: bfloat16 [8192, 1024], P(('dp', 'tensor'))
- grad_w_qkv: float32 [1024, 3, 1024], P('dp', None, 'tensor')
- grad_w_attn_out: float32 [1024, 1024], P('tensor', 'dp')
- grad_bias_table: float32 [32, 16], P('dp', 'tensor')
- grad_gain_attn: float32 [1024], P('dp')
- grad_gain_moe: float32 [1024], P('dp')
- grad_router: float32 [1024, 16], P('dp')
- grad_w_in: float32 [16, 2, 2816, 1024], P('dp', None, 'tensor')
- grad_w_out: float32 [16, 2816, 1024], P('dp', 'tensor')
The draws below stay inside these ranges and needn't reach their ends.
Inputs may be any that keep to these rules, and one draw needn't show every extreme that they name: `routes`: the two experts of a token differ. Among the tokens of one sequence (aligned blocks of 1024 rows) no expert is named more than 160 times, a bound that some block reaches in some sequence of every draw. `segments`: document numbers never fall along a sequence; each document has 1 to 512 tokens, and one has exactly 512.
All inputs are finite; a program needn't handle non-finite values.
Results may differ from the reference program's by a relative error of at most 0.025.
Values may be sent and summed in bfloat16 or wider, within the bound.
A program may use at most 320 MiB of HBM per device.

```python
import math
import jax
import jax.numpy as jnp
import numpy as np
from jax import lax

D = 1024
H = 16
HD = 64
FF = 2816
E = 16
TOP = 2
NB = 32
NEAR = 128
SEQ = 1024
TOKENS = 8192
QBLK = 512
CAP = 160
N_DP = 8


def block_levels(own_key, extent, shards, least, largest):
    def one(position, parts):
        steps = jax.random.uniform(jax.random.fold_in(jax.random.fold_in(own_key, 6), position), (parts,), jnp.float32, least / len(shards), largest / len(shards))
        return jnp.repeat(jnp.exp(steps), extent[position] // parts).reshape((-1,) + (1,) * (len(extent) - position - 1))

    level = one(*shards[0])
    for cut in shards[1:]:
        level = level * one(*cut)
    return level


def profile(count, total, reach, lean):
    portions = [(1 << 20) // math.isqrt(standing ** lean) + 1 for standing in range(2, count + 1)]
    rest, holding = total - reach - (count - 1), [1] * (count - 1)
    while rest > 0:
        movable = [i for i in range(count - 1) if holding[i] < reach]
        whole, remaining = sum([portions[i] for i in movable]), rest
        for i in movable:
            more = min(reach - holding[i], max(1, remaining * portions[i] // whole), rest)
            holding[i] = holding[i] + more
            rest = rest - more
    return np.array([reach] + holding)


def ragged(rng, amount, total, most, slope):
    if amount == 2:
        one = jax.random.randint(rng, (), max(1, total - most), min(most, total - 1) + 1)
        return jnp.stack([one, total - one])
    sizes = jnp.asarray(profile(amount, total, most, slope), jnp.int32)
    twos = (amount - 1) // 2
    giver, taker = sizes[1:1 + 2 * twos:2], sizes[2:2 + 2 * twos:2]
    slack = jnp.minimum(giver - 1, most - taker)
    shifted = jax.random.randint(jax.random.fold_in(rng, 1), (twos,), 0, 1 << 20) % (slack + 1)
    sizes = sizes.at[1:1 + 2 * twos:2].set(giver - shifted).at[2:2 + 2 * twos:2].set(taker + shifted)
    return sizes[jax.random.permutation(jax.random.fold_in(rng, 2), amount)]


def routed_block(own_key, own, number, rows, count, top, limit, slope):
    order = jax.random.permutation(own_key, count)
    packed, ordinary = shares(count, rows * top, limit, slope, True), shares(count, rows * top, limit, slope, False)
    places = jnp.arange(count)

    def named(tallies, rotation):
        used = int((tallies > 0).sum())
        fixed = max(1, used // 4)
        moved = fixed + (places - fixed + rotation * (used - fixed)) % max(1, count - fixed)
        return jnp.zeros((count,), jnp.int32).at[order[jnp.where(places < fixed, places, moved)]].set(jnp.asarray(tallies, jnp.int32))

    tallies = jnp.where(number % 4 == 0, named(packed, number // 4), named(ordinary, number - number // 4 - 1))
    mixed = jax.random.permutation(jax.random.fold_in(own, 3), count)
    giver, sink = mixed[0:count // 2 * 2:2], mixed[1:count // 2 * 2:2]
    margin = jnp.minimum(tallies[giver] - 1, limit - tallies[sink]) // 2
    margin = jnp.where((giver == order[0]) | (sink == order[0]) | (tallies[sink] == 0), 0, jnp.maximum(margin, 0))
    moved = jax.random.randint(jax.random.fold_in(own, 4), (count // 2,), 0, 1 << 20) % (margin + 1)
    tallies = tallies.at[giver].add(-moved).at[sink].add(moved)
    items = jnp.searchsorted(jnp.cumsum(tallies), jnp.arange(rows * top), side="right").astype(jnp.int32)
    listing = items.reshape(top, rows).T
    listing = listing[jax.random.permutation(jax.random.fold_in(own, 1), rows)]
    rotation = jax.random.randint(jax.random.fold_in(own, 2), (rows, 1), 0, top)
    return jnp.take_along_axis(listing, (jnp.arange(top)[None, :] + rotation) % top, axis=1)


def shares(count, total, most, lean, full):
    portions = [(1 << 20) // math.isqrt(grade ** lean) + 1 for grade in range(1, count + 1)]
    largest = most if full else min(most, max(-(-total // count), total * portions[0] // sum(portions)))
    least = 1 if total - largest >= count - 1 else 0
    counts, surplus = [largest] + [least] * (count - 1), total - largest - least * (count - 1)
    while surplus > 0:
        candidates = [i for i in range(1, count) if counts[i] < largest] or [i for i in range(1, count) if counts[i] < most]
        whole, left = sum([portions[i] for i in candidates]), surplus
        for i in candidates:
            addition = min(most - counts[i], max(1, left * portions[i] // whole), surplus)
            counts[i] = counts[i] + addition
            surplus = surplus - addition
    return np.array(counts)


def centred(key, shape, width, bound, split=(), held_as=jnp.bfloat16):
    values = width * jax.random.normal(key, shape, jnp.float32)
    if split:
        values = values * block_levels(key, shape, split, -0.22, 0.18)
    return jnp.clip(values, -bound, bound).astype(held_as)


def setup_inputs(seed: int = 0) -> dict:
    key_of = jax.random.split(jax.random.key(seed), 13)
    tokens = centred(key_of[0], (TOKENS, D), 1.0, 6.0, ((0, 32),))
    segments = jax.vmap(lambda own: jnp.searchsorted(jnp.cumsum(ragged(own, max(4, SEQ // 256), SEQ, SEQ // 2, 2)), jnp.arange(SEQ), side="right"))(jax.random.split(key_of[1], N_DP)).reshape((N_DP, SEQ)).astype(jnp.int32)
    routes_keys = jax.random.split(jax.random.fold_in(key_of[2], 1), TOKENS // SEQ)
    routes_turns = jax.random.permutation(jax.random.fold_in(key_of[2], 3), TOKENS // SEQ)
    routes = jax.vmap(lambda own, number: routed_block(jax.random.fold_in(key_of[2], 2), own, number, SEQ, E, TOP, CAP, 1))(routes_keys, routes_turns).reshape((TOKENS, TOP))
    w_qkv = centred(key_of[3], (D, 3, H * HD), (2 * D // 3) ** -0.5, 0.21875, ((0, 8), (2, 4)))
    w_attn_out = centred(key_of[4], (H * HD, D), (H * HD // 32) ** -0.5, 1.0, ((0, 4), (1, 8)))
    bias_table = centred(key_of[5], (NB, H), 1.0, 4.0, ((0, 8), (1, 4)))
    gain_attn = jnp.clip(1.0 + 0.1 * jax.random.normal(key_of[6], (D,), jnp.float32), 0.5, 1.5).astype(jnp.bfloat16)
    gain_moe = jnp.clip(1.0 + 0.1 * jax.random.normal(key_of[7], (D,), jnp.float32), 0.5, 1.5).astype(jnp.bfloat16)
    router = centred(key_of[8], (D, E), (2 * D) ** -0.5, 0.125, ((0, 8),))
    w_in = centred(key_of[9], (E, 2, FF, D), D ** -0.5, 0.1875, ((0, 8), (2, 4)))
    w_out = centred(key_of[10], (E, FF, D), (FF // 3) ** -0.5, 0.1875, ((0, 8), (1, 4)))
    cotangent = centred(key_of[11], (TOKENS, D), 1.0, 6.0, ((0, 32),))
    return {"tokens": tokens, "segments": segments, "routes": routes, "w_qkv": w_qkv, "w_attn_out": w_attn_out, "bias_table": bias_table, "gain_attn": gain_attn, "gain_moe": gain_moe, "router": router, "w_in": w_in, "w_out": w_out, "cotangent": cotangent}


EPS = 1e-06
NEG = -1e+30

@jax.custom_vjp
def low(v):
    return lax.optimization_barrier(v.astype(jnp.bfloat16)).astype(jnp.float32)

@jax.custom_vjp
def low_back(v):
    return v

def low_keep(v):
    return (low(v), None)

def low_pass(kept, grad):
    return (grad,)

def back_keep(v):
    return (v, None)

def back_low(kept, grad):
    return (low(grad),)
low.defvjp(low_keep, low_pass)
low_back.defvjp(back_keep, back_low)

def distance_buckets():
    half_buckets = NB // 2
    thresholds = [bucket_level for bucket_level in range(1, half_buckets)]
    thresholds = thresholds + [int(math.ceil(half_buckets * (NEAR / half_buckets) ** ((bucket_level - half_buckets) / half_buckets))) for bucket_level in range(half_buckets, NB)]
    distance = np.arange(NEAR + 1)
    return (distance[:, None] >= np.array(thresholds)[None, :]).sum(axis=1)

def rms_normed(values, gain):
    scale_inv = lax.rsqrt(lax.optimization_barrier(jnp.mean(values * values, axis=-1, keepdims=True)) + EPS)
    return values * scale_inv * gain

def route_slots(route_ids):
    flat_routes = route_ids.reshape(-1)
    onehot = (flat_routes[:, None] == jnp.arange(E, dtype=jnp.int32)[None, :]).astype(jnp.int32)
    ranks = jnp.cumsum(onehot, axis=0) - 1
    rank_own = lax.optimization_barrier(jnp.sum(ranks * onehot, axis=1))
    return (flat_routes * CAP + rank_own).reshape(-1, TOP)

def sequence_forward(params, seq_tokens, segment_ids, route_ids):
    w_qkv, w_attn_out, bias_table, gain_attn, gain_moe, router, w_in, w_out = params
    highest = lax.Precision.HIGHEST
    head_cols = H * HD
    hidden_one = low(rms_normed(seq_tokens, gain_attn))
    projected = jnp.dot(hidden_one, w_qkv.reshape(D, 3 * head_cols), precision=highest)
    projected = low(low_back(projected)).reshape(SEQ, 3, H, HD)
    split_heads = jnp.transpose(projected, (1, 2, 0, 3))
    queries, keys_all, values_all = (split_heads[0], split_heads[1], split_heads[2])
    buckets = jnp.asarray(distance_buckets(), jnp.int32)
    positions = jnp.arange(SEQ, dtype=jnp.int32)
    scale = HD ** (-0.5)

    def block_fn(block_index):
        block_start = (block_index * QBLK).astype(jnp.int32)
        row_index = block_start + jnp.arange(QBLK, dtype=jnp.int32)
        query_block = lax.dynamic_slice_in_dim(queries, block_start, QBLK, 1)
        scores = jnp.einsum('hqd,hkd->hqk', query_block, keys_all, precision=highest) * scale
        distance = row_index[:, None] - positions[None, :]
        bucket_ids = buckets[jnp.clip(distance, 0, NEAR)]
        scores = low_back(scores + jnp.transpose(bias_table[bucket_ids], (2, 0, 1)))
        row_segments = lax.dynamic_slice_in_dim(segment_ids, block_start, QBLK, 0)
        allowed = (distance >= 0) & (row_segments[:, None] == segment_ids[None, :])
        scores = jnp.where(allowed[None], scores, NEG)
        probs = jax.nn.softmax(scores, axis=-1)
        return jnp.einsum('hqk,hkd->hqd', low(probs), values_all, precision=highest)
    outputs = lax.map(jax.checkpoint(block_fn), jnp.arange(SEQ // QBLK, dtype=jnp.int32))
    attended = jnp.transpose(outputs, (0, 2, 1, 3)).reshape(SEQ, head_cols)
    attended = low(low_back(attended))
    branch = low_back(jnp.dot(attended, w_attn_out, precision=highest))
    residual = seq_tokens + branch
    hidden_two = low(rms_normed(residual, gain_moe))
    logits = jnp.dot(hidden_two, router, precision=highest)
    expert_probs = jax.nn.softmax(logits, axis=-1)
    chosen = jnp.take_along_axis(expert_probs, route_ids, axis=1)
    gates = chosen / lax.optimization_barrier(jnp.sum(chosen, axis=1, keepdims=True))
    slot_ids = route_slots(route_ids)
    sources = jnp.full((E * CAP,), SEQ, jnp.int32).at[slot_ids.reshape(-1)].set(jnp.repeat(positions, TOP))
    padded = jnp.concatenate([hidden_two, jnp.zeros((1, D), jnp.float32)], axis=0)
    dispatched = padded[sources].reshape(E, CAP, D)
    gate_up = low_back(jnp.einsum('ecd,egfd->ecgf', dispatched, w_in, precision=highest))
    activated = low(jax.nn.gelu(gate_up[:, :, 0], approximate=True) * gate_up[:, :, 1])
    expert_out = low_back(jnp.einsum('ecf,efd->ecd', activated, w_out, precision=highest)).reshape(E * CAP, D)
    combined = gates[:, 0:1] * expert_out[slot_ids[:, 0]] + gates[:, 1:2] * expert_out[slot_ids[:, 1]]
    return residual + low_back(combined)

def reference(tokens, segments, routes, w_qkv, w_attn_out, bias_table, gain_attn, gain_moe, router, w_in, w_out, cotangent):
    floats = tuple((member.astype(jnp.float32) for member in (tokens, w_qkv, w_attn_out, bias_table, gain_attn, gain_moe, router, w_in, w_out)))

    def forward(seq_all, *params):

        def per_sequence(carry, inputs):
            seq_tokens, segment_ids, route_ids = inputs
            return (carry, sequence_forward(params, seq_tokens, segment_ids, route_ids))
        init_carry = jnp.zeros((), jnp.float32)
        _, outputs = lax.scan(per_sequence, init_carry, (seq_all.reshape(N_DP, SEQ, D), segments, routes.reshape(N_DP, SEQ, TOP)))
        return outputs.reshape(TOKENS, D)
    layer_out, pullback = jax.vjp(forward, *floats)
    grads = pullback(cotangent.astype(jnp.float32))
    return (layer_out.astype(jnp.bfloat16), grads[0].astype(jnp.bfloat16), grads[1], grads[2], grads[3], grads[4], grads[5], grads[6], grads[7], grads[8])
```

```python
import functools
import math

import jax
import jax.numpy as jnp
import numpy as np
from jax import lax
from jax.experimental import pallas as pl
from jax.experimental.pallas import tpu as pltpu
from jax.sharding import PartitionSpec as P

HD = 64
TOP = 2
NB = 32
NEAR = 128
BS = 256

EPS = 1e-06
NEG = -1e30
F32 = jnp.float32
BF16 = jnp.bfloat16
VMEM_LIMIT = 60 * 1024 * 1024


def distance_buckets():
    half_buckets = NB // 2
    thresholds = [bucket_level for bucket_level in range(1, half_buckets)]
    thresholds = thresholds + [
        int(
            math.ceil(
                half_buckets
                * (NEAR / half_buckets) ** ((bucket_level - half_buckets) / half_buckets)
            )
        )
        for bucket_level in range(half_buckets, NB)
    ]
    distance = np.arange(NEAR + 1)
    return (distance[:, None] >= np.array(thresholds)[None, :]).sum(axis=1)


def distance_selectors():
    buckets = distance_buckets()
    lanes = np.arange(2 * BS)
    signed = np.where(lanes < BS, lanes, lanes - 2 * BS)
    out = []
    for base in (0, BS):
        distance = np.clip(base - signed, 0, NEAR)
        out.append(buckets[distance][:, None] == np.arange(NB)[None, :])
    return np.concatenate(out, axis=0).astype(np.float32)


def skew_selectors():
    buckets = distance_buckets()
    lanes = np.arange(2 * BS)
    out = []
    for base in (0, BS):
        distance = np.clip(base + BS - 1 - lanes, 0, NEAR)
        out.append(buckets[distance][:, None] == np.arange(NB)[None, :])
    return np.concatenate(out, axis=0).astype(np.float32)


def nt(a, b):
    return lax.dot_general(a, b, (((1,), (1,)), ((), ())), preferred_element_type=F32)


def tn(a, b):
    return lax.dot_general(a, b, (((0,), (0,)), ((), ())), preferred_element_type=F32)


def nn(a, b):
    return lax.dot_general(a, b, (((1,), (0,)), ((), ())), preferred_element_type=F32)


def toeplitz(row):
    return pltpu.roll(jnp.broadcast_to(row, (BS, 2 * BS)), 0, 1, stride=1, stride_axis=0)[:, :BS]


def head_lanes(heads, width):
    lane = lax.broadcasted_iota(jnp.int32, (1, width), 1)
    return [(lane >= h * HD) & (lane < (h + 1) * HD) for h in range(heads)]


def own_head(value, lanes, heads):
    return value if heads == 1 else jnp.where(lanes, value, jnp.zeros((), value.dtype))


def build_bias(heads, pattern_ref, bias):
    for h in range(heads):
        for t in range(2):
            bias[h, t] = toeplitz(pattern_ref[2 * h + t : 2 * h + t + 1, :])


def block_mask(qb, kb, seg_col_ref, seg_row_ref):
    q_seg = seg_col_ref[pl.ds(pl.multiple_of(qb * BS, BS), BS), :]
    k_seg = seg_row_ref[:, pl.ds(pl.multiple_of(kb * BS, BS), BS)]
    row = lax.broadcasted_iota(jnp.int32, (BS, BS), 0) + (qb - kb) * BS
    col = lax.broadcasted_iota(jnp.int32, (BS, BS), 1)
    return (q_seg == k_seg) & (row >= col)


def attn_fwd_kernel(heads, blocks, lo_ref, qkv_ref, seg_col_ref, seg_row_ref, pattern_ref, far_ref, out_ref, lse_ref, bias):
    width = heads * HD
    lanes = head_lanes(heads, width)
    scale = HD**-0.5
    build_bias(heads, pattern_ref, bias)

    def q_step(qb, _):
        q_rows = pl.ds(pl.multiple_of(qb * BS, BS), BS)
        q_all = (qkv_ref[q_rows, 0:width] * scale).astype(BF16)
        q_heads = [own_head(q_all, lanes[h], heads) for h in range(heads)]

        def k_step(kb, carry):
            k_rows = pl.ds(pl.multiple_of(kb * BS, BS), BS)
            k = qkv_ref[k_rows, width : 2 * width]
            v = qkv_ref[k_rows, 2 * width : 3 * width]
            allowed = block_mask(qb, kb, seg_col_ref, seg_row_ref)
            near = jnp.minimum(qb - kb, 1)
            is_far = qb - kb >= 2
            new = []
            for h in range(heads):
                top, total, acc = carry[3 * h : 3 * h + 3]
                b = jnp.where(is_far, far_ref[h], bias[h, near])
                s = jnp.where(allowed, nt(q_heads[h], k) + b, NEG)
                top_new = jnp.maximum(top, jnp.max(s, axis=1, keepdims=True))
                alpha = jnp.exp(top - top_new)
                p = jnp.exp(s - top_new)
                total = alpha * total + jnp.sum(p, axis=1, keepdims=True)
                acc = alpha * acc + nn(p.astype(BF16), v)
                new += [top_new, total, acc]
            return tuple(new)

        init = []
        for h in range(heads):
            init += [jnp.full((BS, 1), NEG, F32), jnp.zeros((BS, 1), F32), jnp.zeros((BS, width), F32)]
        res = lax.fori_loop(lo_ref[qb], qb + 1, k_step, tuple(init))
        out = jnp.zeros((BS, width), F32)
        for h in range(heads):
            top, total, acc = res[3 * h : 3 * h + 3]
            value = acc / total
            out = value if heads == 1 else jnp.where(lanes[h], value, out)
            lse_ref[q_rows, h : h + 1] = top + jnp.log(total)
        out_ref[q_rows, :] = out.astype(BF16)
        return 0

    lax.fori_loop(0, blocks, q_step, 0)


def attn_bwd_kernel(
    heads,
    blocks,
    lo_ref,
    qkv_ref,
    out_ref,
    grad_ref,
    lse_ref,
    seg_col_ref,
    seg_row_ref,
    pattern_ref,
    far_ref,
    grad_qkv_ref,
    diag_ref,
    bias,
    dk,
    dv,
    sums,
):
    width = heads * HD
    lanes = head_lanes(heads, width)
    scale = HD**-0.5
    build_bias(heads, pattern_ref, bias)
    dk[...] = jnp.zeros_like(dk)
    dv[...] = jnp.zeros_like(dv)
    sums[...] = jnp.zeros_like(sums)

    def q_step(qb, _):
        q_rows = pl.ds(pl.multiple_of(qb * BS, BS), BS)
        q_all = (qkv_ref[q_rows, 0:width] * scale).astype(BF16)
        g_all = grad_ref[q_rows, :]
        both = g_all.astype(F32) * out_ref[q_rows, :].astype(F32)
        q_heads = [own_head(q_all, lanes[h], heads) for h in range(heads)]
        g_heads = [own_head(g_all, lanes[h], heads) for h in range(heads)]
        deltas = [jnp.sum(own_head(both, lanes[h], heads), axis=1, keepdims=True) for h in range(heads)]
        totals = [lse_ref[q_rows, h : h + 1] for h in range(heads)]

        def k_step(kb, dq):
            k_rows = pl.ds(pl.multiple_of(kb * BS, BS), BS)
            k = qkv_ref[k_rows, width : 2 * width]
            v = qkv_ref[k_rows, 2 * width : 3 * width]
            allowed = block_mask(qb, kb, seg_col_ref, seg_row_ref)
            near = jnp.minimum(qb - kb, 1)
            place = jnp.minimum(qb - kb, 2)
            is_far = qb - kb >= 2
            dk_add = jnp.zeros((BS, width), F32)
            dv_add = jnp.zeros((BS, width), F32)
            for h in range(heads):
                b = jnp.where(is_far, far_ref[h], bias[h, near])
                s = jnp.where(allowed, nt(q_heads[h], k) + b, NEG)
                p = jnp.exp(s - totals[h])
                gp = nt(g_heads[h], v)
                ds = (p * (gp - deltas[h])).astype(BF16)
                dv_add += tn(p.astype(BF16), g_heads[h])
                dk_add += tn(ds, q_heads[h])
                dq = dq + own_head(nn(ds, k), lanes[h], heads)
                sums[h, place] += ds.astype(F32)
            dk[k_rows, :] += dk_add
            dv[k_rows, :] += dv_add
            return dq

        dq = lax.fori_loop(lo_ref[qb], qb + 1, k_step, jnp.zeros((BS, width), F32))
        grad_qkv_ref[q_rows, 0:width] = (dq * scale).astype(BF16)
        return 0

    lax.fori_loop(0, blocks, q_step, 0)
    grad_qkv_ref[:, width : 2 * width] = dk[...].astype(BF16)
    grad_qkv_ref[:, 2 * width : 3 * width] = dv[...].astype(BF16)
    row = lax.broadcasted_iota(jnp.int32, (BS, BS), 0)
    col = lax.broadcasted_iota(jnp.int32, (BS, BS), 1)
    upside_down = jnp.where(row + col == BS - 1, 1.0, 0.0).astype(F32)
    for h in range(heads):
        for t in range(2):
            flipped = jnp.dot(upside_down, sums[h, t], precision=lax.Precision.HIGHEST, preferred_element_type=F32)
            wide = jnp.concatenate([flipped, jnp.zeros((BS, BS), F32)], axis=1)
            skewed = pltpu.roll(wide, 0, 1, stride=1, stride_axis=0)
            diag_ref[3 * h + t : 3 * h + t + 1, :] = jnp.sum(skewed, axis=0, keepdims=True)
        rest = jnp.sum(sums[h, 2], axis=0, keepdims=True)
        diag_ref[3 * h + 2 : 3 * h + 3, :] = jnp.concatenate([rest, jnp.zeros((1, BS), F32)], axis=1)


def vspec():
    return pl.BlockSpec(memory_space=pltpu.VMEM)


def sspec():
    return pl.BlockSpec(memory_space=pltpu.SMEM)


def attention_forward(projected, lo, seg_col, seg_row, patterns, far, heads):
    seq_len = projected.shape[0]
    blocks = seq_len // BS
    return pl.pallas_call(
        functools.partial(attn_fwd_kernel, heads, blocks),
        out_shape=(
            jax.ShapeDtypeStruct((seq_len, heads * HD), BF16),
            jax.ShapeDtypeStruct((seq_len, heads), F32),
        ),
        in_specs=[sspec(), vspec(), vspec(), vspec(), vspec(), sspec()],
        out_specs=(vspec(), vspec()),
        scratch_shapes=[pltpu.VMEM((heads, 2, BS, BS), F32)],
        compiler_params=pltpu.CompilerParams(vmem_limit_bytes=VMEM_LIMIT),
        name="attn_fwd",
    )(lo, projected, seg_col, seg_row, patterns, far)


def attention_backward(projected, attended, grad, lse, lo, seg_col, seg_row, patterns, far, heads):
    seq_len = projected.shape[0]
    blocks = seq_len // BS
    width = heads * HD
    return pl.pallas_call(
        functools.partial(attn_bwd_kernel, heads, blocks),
        out_shape=(
            jax.ShapeDtypeStruct((seq_len, 3 * width), BF16),
            jax.ShapeDtypeStruct((3 * heads, 2 * BS), F32),
        ),
        in_specs=[sspec(), vspec(), vspec(), vspec(), vspec(), vspec(), vspec(), vspec(), sspec()],
        out_specs=(vspec(), vspec()),
        scratch_shapes=[
            pltpu.VMEM((heads, 2, BS, BS), F32),
            pltpu.VMEM((seq_len, width), F32),
            pltpu.VMEM((seq_len, width), F32),
            pltpu.VMEM((heads, 3, BS, BS), F32),
        ],
        compiler_params=pltpu.CompilerParams(vmem_limit_bytes=VMEM_LIMIT),
        name="attn_bwd",
    )(lo, projected, attended, grad, lse, seg_col, seg_row, patterns, far)


def rms_scale(values):
    return lax.rsqrt(jnp.mean(values * values, axis=-1, keepdims=True) + EPS)


def norm_backward(grad_normed, values, scale_inv, gain):
    normed_unit = values * scale_inv
    grad_unit = grad_normed * gain
    grad_values = scale_inv * (
        grad_unit - normed_unit * jnp.mean(grad_unit * normed_unit, axis=-1, keepdims=True)
    )
    return (grad_values, jnp.sum(grad_normed * normed_unit, axis=0))


def gelu_tanh(values):
    return jax.nn.gelu(values, approximate=True)


def route_slots(route_ids, experts, capacity):
    flat_routes = route_ids.reshape(-1)
    onehot = (flat_routes[:, None] == jnp.arange(experts, dtype=jnp.int32)[None, :]).astype(
        jnp.int32
    )
    ranks = jnp.cumsum(onehot, axis=0) - 1
    rank_own = jnp.sum(ranks * onehot, axis=1)
    return (flat_routes * capacity + rank_own).reshape(-1, TOP)


def on_device(
    tokens,
    segments,
    routes,
    w_qkv,
    w_attn_out,
    bias_table,
    gain_attn,
    gain_moe,
    router,
    w_in,
    w_out,
    cotangent,
):
    own_rows, model_width = tokens.shape
    n_tensor = lax.axis_size("tensor")
    n_dp = lax.axis_size("dp")
    seq_len = own_rows * n_tensor
    own_start = lax.axis_index("tensor") * own_rows
    head_cols = w_qkv.shape[2]
    heads = head_cols // HD
    experts = router.shape[1]
    local_experts = w_in.shape[0]
    capacity = 5 * seq_len * TOP // (4 * experts)
    highest = lax.Precision.HIGHEST
    slots = experts * capacity

    depth = w_qkv.shape[0]
    bias_rows = bias_table.shape[0]
    extra = jnp.concatenate(
        [
            router,
            gain_attn[:, None],
            gain_moe[:, None],
            jnp.pad(bias_table, ((0, depth - bias_rows), (0, 0))),
        ],
        axis=1,
    )
    extra = jnp.pad(extra, ((0, 0), (0, 128 - extra.shape[1])))
    packed = lax.all_gather(
        jnp.concatenate([w_qkv.reshape(depth, 3 * head_cols), extra], axis=1),
        "dp",
        axis=0,
        tiled=True,
    )
    qkv_matrix = packed[:, : 3 * head_cols]
    extras = packed[:, 3 * head_cols :]
    router_full = extras[:, :experts]
    gain_one = extras[:, experts].astype(F32)
    gain_two = extras[:, experts + 1].astype(F32)
    table = (
        extras.reshape(n_dp, depth, 128)[:, :bias_rows, experts + 2 : experts + 2 + heads]
        .reshape(NB, heads)
        .astype(F32)
    )
    out_columns = lax.all_gather(w_attn_out, "tensor", axis=0, tiled=True)
    out_matrix = lax.all_gather(out_columns, "dp", axis=1, tiled=True)

    tokens_float = tokens.astype(F32)
    scale_one = rms_scale(tokens_float)
    hidden_one = (tokens_float * scale_one * gain_one).astype(BF16)
    gathered_one = lax.all_gather(hidden_one, "tensor", axis=0, tiled=True)
    projected = jnp.dot(gathered_one, qkv_matrix, preferred_element_type=F32).astype(BF16)
    selectors = jnp.asarray(distance_selectors())
    patterns = jnp.dot(selectors, table, precision=highest)
    patterns = jnp.transpose(patterns.reshape(2, 2 * BS, heads), (2, 0, 1)).reshape(
        2 * heads, 2 * BS
    )
    far = table[NB - 1]
    segment_row = segments
    segment_col = segments.reshape(seq_len, 1)
    starts = segments[0, ::BS]
    ends = segments[0, BS - 1 :: BS]
    lowest = jnp.sum((ends[None, :] < starts[:, None]).astype(jnp.int32), axis=1)
    attended, lse = attention_forward(
        projected, lowest, segment_col, segment_row, patterns, far, heads
    )
    attended_own = lax.all_to_all(
        attended.reshape(n_tensor, own_rows, head_cols), "tensor", 0, 0
    )
    attended_own = jnp.transpose(attended_own, (1, 0, 2)).reshape(own_rows, n_tensor * head_cols)
    branch = jnp.dot(attended_own, out_matrix, preferred_element_type=F32)
    residual = tokens_float + branch
    scale_two = rms_scale(residual)
    hidden_two = (residual * scale_two * gain_two).astype(BF16)
    gathered_two = lax.all_gather(hidden_two, "tensor", axis=0, tiled=True)

    expert_ids = jnp.arange(experts, dtype=jnp.int32)

    def gate_values(logit_values, route_rows):
        expert_probs = jax.nn.softmax(logit_values, axis=-1)
        picked = jnp.sum(
            jnp.where(
                route_rows[:, :, None] == expert_ids[None, None, :], expert_probs[:, None, :], 0.0
            ),
            axis=-1,
        )
        return picked / jnp.sum(picked, axis=1, keepdims=True)

    gates = gate_values(jnp.dot(gathered_two, router_full, preferred_element_type=F32), routes)
    slot_ids = route_slots(routes, experts, capacity)
    slot_flat = slot_ids.reshape(-1)
    token_ids = jnp.repeat(jnp.arange(seq_len, dtype=jnp.int32), TOP)
    sources = jnp.full((slots,), seq_len, jnp.int32).at[slot_flat].set(token_ids)
    slot_gates = jnp.zeros((slots,), F32).at[slot_flat].set(gates.reshape(-1))
    grad_gathered = lax.all_gather(cotangent, "tensor", axis=0, tiled=True)

    def exchange(rows):
        parts = rows.reshape(n_dp, local_experts, capacity, model_width)
        return [
            lax.all_to_all(parts[:, i], "dp", 0, 0).reshape(n_dp * capacity, model_width)
            for i in range(local_experts)
        ]

    def give_back(parts):
        back = [
            lax.all_to_all(part.reshape(n_dp, capacity, model_width), "dp", 0, 0) for part in parts
        ]
        return jnp.stack(back, axis=1).reshape(slots, model_width)

    zero_row = jnp.zeros((1, model_width), BF16)
    dispatched = exchange(jnp.concatenate([gathered_two, zero_row], axis=0)[sources])
    padded_grad = jnp.concatenate([grad_gathered, zero_row], axis=0)
    grad_expert = exchange((slot_gates[:, None] * padded_grad[sources]).astype(BF16))

    outs, backs, grads_in, grads_out = [], [], [], []
    for i in range(local_experts):
        rows, grad_rows = dispatched[i], grad_expert[i]
        gate_part = nt(rows, w_in[i, 0])
        up_part = nt(rows, w_in[i, 1])
        gelu_value, gelu_pull = jax.vjp(gelu_tanh, gate_part)
        activated = (gelu_value * up_part).astype(BF16)
        outs.append(nn(activated, w_out[i]).astype(BF16))
        grad_act = nt(grad_rows, w_out[i])
        grads_out.append(tn(activated, grad_rows))
        grad_gate = gelu_pull(grad_act * up_part)[0].astype(BF16)
        grad_up = (grad_act * gelu_value).astype(BF16)
        backs.append((nn(grad_gate, w_in[i, 0]) + nn(grad_up, w_in[i, 1])).astype(BF16))
        grads_in.append(jnp.stack([tn(grad_gate, rows), tn(grad_up, rows)]))
    grad_w_in = jnp.stack(grads_in)
    grad_w_out = jnp.stack(grads_out)
    expert_out = give_back(outs)
    grad_dispatched = give_back(backs)

    first, second = slot_ids[:, 0], slot_ids[:, 1]
    picked_first = expert_out[first].astype(F32)
    picked_second = expert_out[second].astype(F32)
    mixture = lax.psum_scatter(
        (gates[:, 0:1] * picked_first + gates[:, 1:2] * picked_second).astype(BF16),
        "tensor",
        scatter_dimension=0,
        tiled=True,
    ).astype(F32)
    layer_out = (residual + mixture).astype(BF16)
    grad_float = grad_gathered.astype(F32)
    grad_gate_part = jnp.stack(
        [
            jnp.sum(grad_float * picked_first, axis=1),
            jnp.sum(grad_float * picked_second, axis=1),
        ],
        axis=1,
    )
    grad_hidden_part = (
        grad_dispatched[first].astype(F32) + grad_dispatched[second].astype(F32)
    ).astype(BF16)
    grad_own = lax.psum_scatter(
        grad_hidden_part, "tensor", scatter_dimension=0, tiled=True
    ).astype(F32)
    grad_gate_own = lax.dynamic_slice_in_dim(
        lax.psum(grad_gate_part, "tensor"), own_start, own_rows, 0
    )
    own_routes = lax.dynamic_slice_in_dim(routes, own_start, own_rows, 0)
    own_logits = jnp.dot(hidden_two, router_full, preferred_element_type=F32)

    def own_gates(logit_values):
        return gate_values(logit_values, own_routes)

    _, gate_pull = jax.vjp(own_gates, own_logits)
    grad_logits = gate_pull(grad_gate_own)[0]
    router_float = router_full.astype(F32)
    grad_hidden_two = grad_own + jnp.dot(grad_logits, router_float.T, precision=highest)
    grad_router_part = jnp.dot(hidden_two.astype(F32).T, grad_logits, precision=highest)
    grad_from_norm, grad_gain_two = norm_backward(grad_hidden_two, residual, scale_two, gain_two)
    grad_residual = cotangent.astype(F32) + grad_from_norm

    grad_branch = grad_residual.astype(BF16)
    grad_attended_own = nt(grad_branch, out_matrix).astype(BF16)
    grad_attended = lax.all_to_all(
        jnp.transpose(grad_attended_own.reshape(own_rows, n_tensor, head_cols), (1, 0, 2)),
        "tensor",
        0,
        0,
    ).reshape(seq_len, head_cols)
    grad_branch_all = lax.all_gather(grad_branch, "tensor", axis=0, tiled=True)
    grad_w_attn_out = tn(attended, grad_branch_all)
    grad_projected, diag = attention_backward(
        projected,
        attended,
        grad_attended,
        lse,
        lowest,
        segment_col,
        segment_row,
        patterns,
        far,
        heads,
    )
    diag = diag.reshape(heads, 3, 2 * BS)
    near = jnp.transpose(diag[:, :2].reshape(heads, 4 * BS))
    grad_table = lax.dot_general(
        jnp.asarray(skew_selectors()), near, (((0,), (0,)), ((), ())), precision=highest
    )
    grad_table = grad_table.at[NB - 1].add(jnp.sum(diag[:, 2], axis=1))
    grad_w_qkv = tn(gathered_one, grad_projected).reshape(model_width, 3, head_cols)
    grad_hidden_one = lax.psum_scatter(
        nt(grad_projected, qkv_matrix).astype(BF16),
        "tensor",
        scatter_dimension=0,
        tiled=True,
    ).astype(F32)
    grad_from_first, grad_gain_one = norm_backward(
        grad_hidden_one, tokens_float, scale_one, gain_one
    )
    grad_tokens = (grad_residual + grad_from_first).astype(BF16)

    small = jnp.concatenate(
        [grad_router_part, grad_gain_one[:, None], grad_gain_two[:, None]], axis=1
    )
    small = lax.psum(small, "tensor")
    small = lax.psum_scatter(small, "dp", scatter_dimension=0, tiled=True)
    reduced_qkv = lax.psum_scatter(grad_w_qkv, "dp", scatter_dimension=0, tiled=True)
    reduced_attn_out = lax.psum_scatter(grad_w_attn_out, "dp", scatter_dimension=1, tiled=True)
    reduced_table = lax.psum_scatter(grad_table, "dp", scatter_dimension=0, tiled=True)
    return (
        layer_out,
        grad_tokens,
        reduced_qkv,
        reduced_attn_out,
        reduced_table,
        small[:, experts],
        small[:, experts + 1],
        small[:, :experts],
        grad_w_in,
        grad_w_out,
    )


def solution(mesh):
    return jax.shard_map(
        on_device,
        mesh=mesh,
        in_specs=(
            P(("dp", "tensor"), None),
            P("dp", None),
            P("dp", None),
            P("dp", None, "tensor"),
            P("tensor", "dp"),
            P("dp", "tensor"),
            P("dp"),
            P("dp"),
            P("dp", None),
            P("dp", None, "tensor", None),
            P("dp", "tensor", None),
            P(("dp", "tensor"), None),
        ),
        out_specs=(
            P(("dp", "tensor"), None),
            P(("dp", "tensor"), None),
            P("dp", None, "tensor"),
            P("tensor", "dp"),
            P("dp", "tensor"),
            P("dp"),
            P("dp"),
            P("dp", None),
            P("dp", None, "tensor", None),
            P("dp", "tensor", None),
        ),
        check_vma=False,
    )
```

```python
import functools
import math

import jax
import jax.numpy as jnp
import numpy as np
from jax import lax
from jax.experimental import pallas as pl
from jax.experimental.pallas import tpu as pltpu
from jax.sharding import PartitionSpec as P

HD = 64
TOP = 2
NB = 32
NEAR = 128
BS = 256

EPS = 1e-06
NEG = -1e30
F32 = jnp.float32
BF16 = jnp.bfloat16
VMEM_LIMIT = 60 * 1024 * 1024


def distance_buckets():
    half_buckets = NB // 2
    thresholds = [bucket_level for bucket_level in range(1, half_buckets)]
    thresholds = thresholds + [
        int(
            math.ceil(
                half_buckets
                * (NEAR / half_buckets) ** ((bucket_level - half_buckets) / half_buckets)
            )
        )
        for bucket_level in range(half_buckets, NB)
    ]
    distance = np.arange(NEAR + 1)
    return (distance[:, None] >= np.array(thresholds)[None, :]).sum(axis=1)


def distance_selectors():
    buckets = distance_buckets()
    lanes = np.arange(2 * BS)
    signed = np.where(lanes < BS, lanes, lanes - 2 * BS)
    out = []
    for base in (0, BS):
        distance = np.clip(base - signed, 0, NEAR)
        out.append(buckets[distance][:, None] == np.arange(NB)[None, :])
    return np.concatenate(out, axis=0).astype(np.float32)


def skew_selectors():
    buckets = distance_buckets()
    lanes = np.arange(2 * BS)
    out = []
    for base in (0, BS):
        distance = np.clip(base + BS - 1 - lanes, 0, NEAR)
        out.append(buckets[distance][:, None] == np.arange(NB)[None, :])
    return np.concatenate(out, axis=0).astype(np.float32)


def nt(a, b):
    return lax.dot_general(a, b, (((1,), (1,)), ((), ())), preferred_element_type=F32)


def tn(a, b):
    return lax.dot_general(a, b, (((0,), (0,)), ((), ())), preferred_element_type=F32)


def nn(a, b):
    return lax.dot_general(a, b, (((1,), (0,)), ((), ())), preferred_element_type=F32)


def toeplitz(row):
    return pltpu.roll(jnp.broadcast_to(row, (BS, 2 * BS)), 0, 1, stride=1, stride_axis=0)[:, :BS]


def head_lanes(heads, width):
    lane = lax.broadcasted_iota(jnp.int32, (1, width), 1)
    return [(lane >= h * HD) & (lane < (h + 1) * HD) for h in range(heads)]


def own_head(value, lanes, heads):
    return value if heads == 1 else jnp.where(lanes, value, jnp.zeros((), value.dtype))


def build_bias(heads, pattern_ref, bias):
    for h in range(heads):
        for t in range(2):
            bias[h, t] = toeplitz(pattern_ref[2 * h + t : 2 * h + t + 1, :])


def block_mask(qb, kb, seg_col_ref, seg_row_ref):
    q_seg = seg_col_ref[pl.ds(pl.multiple_of(qb * BS, BS), BS), :]
    k_seg = seg_row_ref[:, pl.ds(pl.multiple_of(kb * BS, BS), BS)]
    row = lax.broadcasted_iota(jnp.int32, (BS, BS), 0) + (qb - kb) * BS
    col = lax.broadcasted_iota(jnp.int32, (BS, BS), 1)
    return (q_seg == k_seg) & (row >= col)


def attn_fwd_kernel(heads, blocks, lo_ref, qkv_ref, seg_col_ref, seg_row_ref, pattern_ref, far_ref, out_ref, lse_ref, bias):
    width = heads * HD
    lanes = head_lanes(heads, width)
    scale = HD**-0.5
    build_bias(heads, pattern_ref, bias)

    def q_step(qb, _):
        q_rows = pl.ds(pl.multiple_of(qb * BS, BS), BS)
        q_all = (qkv_ref[q_rows, 0:width] * scale).astype(BF16)
        q_heads = [own_head(q_all, lanes[h], heads) for h in range(heads)]

        def k_step(kb, carry):
            k_rows = pl.ds(pl.multiple_of(kb * BS, BS), BS)
            k = qkv_ref[k_rows, width : 2 * width]
            v = qkv_ref[k_rows, 2 * width : 3 * width]
            allowed = block_mask(qb, kb, seg_col_ref, seg_row_ref)
            near = jnp.minimum(qb - kb, 1)
            is_far = qb - kb >= 2
            new = []
            for h in range(heads):
                top, total, acc = carry[3 * h : 3 * h + 3]
                b = jnp.where(is_far, far_ref[h], bias[h, near])
                s = jnp.where(allowed, nt(q_heads[h], k) + b, NEG)
                top_new = jnp.maximum(top, jnp.max(s, axis=1, keepdims=True))
                alpha = jnp.exp(top - top_new)
                p = jnp.exp(s - top_new)
                total = alpha * total + jnp.sum(p, axis=1, keepdims=True)
                acc = alpha * acc + nn(p.astype(BF16), v)
                new += [top_new, total, acc]
            return tuple(new)

        init = []
        for h in range(heads):
            init += [jnp.full((BS, 1), NEG, F32), jnp.zeros((BS, 1), F32), jnp.zeros((BS, width), F32)]
        res = lax.fori_loop(lo_ref[qb], qb + 1, k_step, tuple(init))
        out = jnp.zeros((BS, width), F32)
        for h in range(heads):
            top, total, acc = res[3 * h : 3 * h + 3]
            value = acc / total
            out = value if heads == 1 else jnp.where(lanes[h], value, out)
            lse_ref[q_rows, h : h + 1] = top + jnp.log(total)
        out_ref[q_rows, :] = out.astype(BF16)
        return 0

    lax.fori_loop(0, blocks, q_step, 0)


def attn_bwd_kernel(
    heads,
    blocks,
    lo_ref,
    qkv_ref,
    out_ref,
    grad_ref,
    lse_ref,
    seg_col_ref,
    seg_row_ref,
    pattern_ref,
    far_ref,
    grad_qkv_ref,
    diag_ref,
    bias,
    dk,
    dv,
    sums,
):
    width = heads * HD
    lanes = head_lanes(heads, width)
    scale = HD**-0.5
    build_bias(heads, pattern_ref, bias)
    dk[...] = jnp.zeros_like(dk)
    dv[...] = jnp.zeros_like(dv)
    sums[...] = jnp.zeros_like(sums)

    def q_step(qb, _):
        q_rows = pl.ds(pl.multiple_of(qb * BS, BS), BS)
        q_all = (qkv_ref[q_rows, 0:width] * scale).astype(BF16)
        g_all = grad_ref[q_rows, :]
        both = g_all.astype(F32) * out_ref[q_rows, :].astype(F32)
        q_heads = [own_head(q_all, lanes[h], heads) for h in range(heads)]
        g_heads = [own_head(g_all, lanes[h], heads) for h in range(heads)]
        deltas = [jnp.sum(own_head(both, lanes[h], heads), axis=1, keepdims=True) for h in range(heads)]
        totals = [lse_ref[q_rows, h : h + 1] for h in range(heads)]

        def k_step(kb, dq):
            k_rows = pl.ds(pl.multiple_of(kb * BS, BS), BS)
            k = qkv_ref[k_rows, width : 2 * width]
            v = qkv_ref[k_rows, 2 * width : 3 * width]
            allowed = block_mask(qb, kb, seg_col_ref, seg_row_ref)
            near = jnp.minimum(qb - kb, 1)
            place = jnp.minimum(qb - kb, 2)
            is_far = qb - kb >= 2
            dk_add = jnp.zeros((BS, width), F32)
            dv_add = jnp.zeros((BS, width), F32)
            for h in range(heads):
                b = jnp.where(is_far, far_ref[h], bias[h, near])
                s = jnp.where(allowed, nt(q_heads[h], k) + b, NEG)
                p = jnp.exp(s - totals[h])
                gp = nt(g_heads[h], v)
                ds = (p * (gp - deltas[h])).astype(BF16)
                dv_add += tn(p.astype(BF16), g_heads[h])
                dk_add += tn(ds, q_heads[h])
                dq = dq + own_head(nn(ds, k), lanes[h], heads)
                sums[h, place] += ds.astype(F32)
            dk[k_rows, :] += dk_add
            dv[k_rows, :] += dv_add
            return dq

        dq = lax.fori_loop(lo_ref[qb], qb + 1, k_step, jnp.zeros((BS, width), F32))
        grad_qkv_ref[q_rows, 0:width] = (dq * scale).astype(BF16)
        return 0

    lax.fori_loop(0, blocks, q_step, 0)
    grad_qkv_ref[:, width : 2 * width] = dk[...].astype(BF16)
    grad_qkv_ref[:, 2 * width : 3 * width] = dv[...].astype(BF16)
    row = lax.broadcasted_iota(jnp.int32, (BS, BS), 0)
    col = lax.broadcasted_iota(jnp.int32, (BS, BS), 1)
    upside_down = jnp.where(row + col == BS - 1, 1.0, 0.0).astype(F32)
    for h in range(heads):
        for t in range(2):
            flipped = jnp.dot(upside_down, sums[h, t], precision=lax.Precision.HIGHEST, preferred_element_type=F32)
            wide = jnp.concatenate([flipped, jnp.zeros((BS, BS), F32)], axis=1)
            skewed = pltpu.roll(wide, 0, 1, stride=1, stride_axis=0)
            diag_ref[3 * h + t : 3 * h + t + 1, :] = jnp.sum(skewed, axis=0, keepdims=True)
        rest = jnp.sum(sums[h, 2], axis=0, keepdims=True)
        diag_ref[3 * h + 2 : 3 * h + 3, :] = jnp.concatenate([rest, jnp.zeros((1, BS), F32)], axis=1)


def vspec():
    return pl.BlockSpec(memory_space=pltpu.VMEM)


def sspec():
    return pl.BlockSpec(memory_space=pltpu.SMEM)


def attention_forward(projected, lo, seg_col, seg_row, patterns, far, heads):
    seq_len = projected.shape[0]
    blocks = seq_len // BS
    return pl.pallas_call(
        functools.partial(attn_fwd_kernel, heads, blocks),
        out_shape=(
            jax.ShapeDtypeStruct((seq_len, heads * HD), BF16),
            jax.ShapeDtypeStruct((seq_len, heads), F32),
        ),
        in_specs=[sspec(), vspec(), vspec(), vspec(), vspec(), sspec()],
        out_specs=(vspec(), vspec()),
        scratch_shapes=[pltpu.VMEM((heads, 2, BS, BS), F32)],
        compiler_params=pltpu.CompilerParams(vmem_limit_bytes=VMEM_LIMIT),
        name="attn_fwd",
    )(lo, projected, seg_col, seg_row, patterns, far)


def attention_backward(projected, attended, grad, lse, lo, seg_col, seg_row, patterns, far, heads):
    seq_len = projected.shape[0]
    blocks = seq_len // BS
    width = heads * HD
    return pl.pallas_call(
        functools.partial(attn_bwd_kernel, heads, blocks),
        out_shape=(
            jax.ShapeDtypeStruct((seq_len, 3 * width), BF16),
            jax.ShapeDtypeStruct((3 * heads, 2 * BS), F32),
        ),
        in_specs=[sspec(), vspec(), vspec(), vspec(), vspec(), vspec(), vspec(), vspec(), sspec()],
        out_specs=(vspec(), vspec()),
        scratch_shapes=[
            pltpu.VMEM((heads, 2, BS, BS), F32),
            pltpu.VMEM((seq_len, width), F32),
            pltpu.VMEM((seq_len, width), F32),
            pltpu.VMEM((heads, 3, BS, BS), F32),
        ],
        compiler_params=pltpu.CompilerParams(vmem_limit_bytes=VMEM_LIMIT),
        name="attn_bwd",
    )(lo, projected, attended, grad, lse, seg_col, seg_row, patterns, far)


MESH = pl.DeviceIdType.MESH
SMALL = 32


def remote(src, dst, send, recv, axis, peer):
    return pltpu.make_async_remote_copy(
        src_ref=src,
        dst_ref=dst,
        send_sem=send,
        recv_sem=recv,
        device_id={axis: peer},
        device_id_type=MESH,
    )


def greet(groups):
    barrier = pltpu.get_barrier_semaphore()
    total = 0
    for axis, n in groups:
        me = lax.axis_index(axis)
        for step in range(1, n):
            pl.semaphore_signal(
                barrier, inc=1, device_id={axis: lax.rem(me + step, n)}, device_id_type=MESH
            )
        total += n - 1
    pl.semaphore_wait(barrier, total)


class LineSum:
    def __init__(self, n, partial, send, recv, send_sem, recv_sem, acc, total):
        self.n, self.partial = n, partial
        self.send, self.recv, self.send_sem, self.recv_sem = send, recv, send_sem, recv_sem
        self.acc, self.total = acc, total
        self.me = lax.axis_index("tensor")

    def flow(self, first, k):
        n, me = self.n, self.me
        near = me * 2 < n
        right = near if first else jnp.logical_not(near)
        block = jnp.where(right, n - 1 - k, k)
        comes = jnp.where(right, jnp.where(me > 0, me <= block, False), jnp.where(me < n - 1, me >= block, False))
        goes = jnp.where(right, me < block, me > block)
        peer = jnp.clip(jnp.where(right, me + 1, me - 1), 0, n - 1)
        out_slot = jnp.clip(jnp.where(right, k, n - 1 - me + k), 0, n - 2)
        in_slot = jnp.clip(jnp.where(right, k, n - me + k), 0, n)
        peer_slot = jnp.clip(jnp.where(right, k, n - peer + k), 0, n)
        return block, comes, goes, peer, out_slot, in_slot, peer_slot

    def copy(self, peer, out_slot, slot):
        return remote(
            self.send.at[out_slot],
            self.recv.at[slot],
            self.send_sem.at[out_slot],
            self.recv_sem.at[slot],
            "tensor",
            peer,
        )

    def start(self):
        for k in range(self.n - 1):
            for first in (True, False):
                block, comes, goes, peer, out_slot, in_slot, peer_slot = self.flow(first, k)

                @pl.when(goes & jnp.logical_not(comes))
                def _():
                    self.send[out_slot] = self.partial(block).astype(BF16)
                    self.copy(peer, out_slot, peer_slot).start()

        self.total[...] = self.partial(self.me)

    def finish(self):
        for k in range(self.n - 1):
            for first in (True, False):
                block, comes, goes, peer, out_slot, in_slot, peer_slot = self.flow(first, k)

                @pl.when(goes & comes)
                def _():
                    self.acc[...] = self.partial(block)
                    self.copy(peer, out_slot, in_slot).wait_recv()
                    self.send[out_slot] = (
                        self.acc[...] + self.recv[in_slot].astype(F32)
                    ).astype(BF16)
                    self.copy(peer, out_slot, peer_slot).start()

                @pl.when(comes & jnp.logical_not(goes))
                def _():
                    self.copy(peer, 0, in_slot).wait_recv()
                    self.total[...] += self.recv[in_slot].astype(F32)

    def drain(self):
        for k in range(self.n - 1):
            for first in (True, False):
                block, comes, goes, peer, out_slot, in_slot, peer_slot = self.flow(first, k)

                @pl.when(goes)
                def _():
                    self.copy(peer, out_slot, in_slot).wait_send()


def tail_kernel(
    n_dp,
    n_tensor,
    experts,
    table_rows,
    hidden_ref,
    grad_ref,
    weight_ref,
    attended_ref,
    branch_ref,
    small_ref,
    weight_own_ref,
    gain_own_ref,
    grad_hidden_ref,
    grad_qkv_ref,
    grad_out_ref,
    small_out_ref,
    acc,
    line_send,
    line_recv,
    qkv_send,
    qkv_recv,
    out_send,
    out_recv,
    small_recv,
    small_sum,
    gain_recv,
    line_send_sem,
    line_recv_sem,
    qkv_send_sem,
    qkv_recv_sem,
    out_send_sem,
    out_recv_sem,
    small_send_sem,
    small_recv_sem,
    gain_send_sem,
    gain_recv_sem,
):
    own_rows = grad_hidden_ref.shape[0]
    depth = weight_own_ref.shape[0]
    out_cols = grad_out_ref.shape[1]
    me = lax.axis_index("dp")
    me_t = lax.axis_index("tensor")
    greet([("dp", n_dp), ("tensor", n_tensor)])

    def partial(block):
        rows = pl.ds(pl.multiple_of(block * own_rows, own_rows), own_rows)
        return nt(grad_ref[rows, :], weight_ref[...])

    line = LineSum(
        n_tensor, partial, line_send, line_recv, line_send_sem, line_recv_sem, acc, grad_hidden_ref
    )
    line.start()
    copies = []
    for step in range(1, n_dp):
        peer = lax.rem(me + step, n_dp)
        copy = remote(
            small_ref.at[peer],
            small_recv.at[step - 1],
            small_send_sem.at[step - 1],
            small_recv_sem.at[step - 1],
            "dp",
            peer,
        )
        copy.start()
        copies.append(copy)
    for block in range(n_dp):
        cols = slice(block * depth, (block + 1) * depth)
        qkv_send[block] = tn(hidden_ref[:, cols], grad_ref[...]).astype(BF16)
    for step in range(1, n_dp):
        peer = lax.rem(me + step, n_dp)
        copy = remote(
            qkv_send.at[peer],
            qkv_recv.at[step - 1],
            qkv_send_sem.at[step - 1],
            qkv_recv_sem.at[step - 1],
            "dp",
            peer,
        )
        copy.start()
        copies.append(copy)
    for block in range(n_dp):
        cols = slice(block * out_cols, (block + 1) * out_cols)
        out_send[block] = tn(attended_ref[...], branch_ref[:, cols]).astype(BF16)
    for step in range(1, n_dp):
        peer = lax.rem(me + step, n_dp)
        copy = remote(
            out_send.at[peer],
            out_recv.at[step - 1],
            out_send_sem.at[step - 1],
            out_recv_sem.at[step - 1],
            "dp",
            peer,
        )
        copy.start()
        copies.append(copy)
    line.finish()
    for copy in copies:
        copy.wait()
    small_sum[...] = small_ref[me]
    grad_qkv_ref[...] = qkv_send[me].astype(F32)
    grad_out_ref[...] = out_send[me].astype(F32)
    for step in range(1, n_dp):
        small_sum[...] += small_recv[step - 1]
        grad_qkv_ref[...] += qkv_recv[step - 1].astype(F32)
        grad_out_ref[...] += out_recv[step - 1].astype(F32)
    column = jnp.sum(grad_qkv_ref[...] * weight_own_ref[...].astype(F32), axis=1, keepdims=True)
    eye = lax.broadcasted_iota(jnp.int32, (depth, depth), 0) == lax.broadcasted_iota(
        jnp.int32, (depth, depth), 1
    )
    row = jnp.sum(jnp.where(eye, column, 0.0), axis=0, keepdims=True)
    small_sum[experts + 1 : experts + 2, :] = row / gain_own_ref[...]
    gains = []
    for step in range(1, n_tensor):
        peer = lax.rem(me_t + step, n_tensor)
        copy = remote(
            small_sum,
            gain_recv.at[step - 1],
            gain_send_sem.at[step - 1],
            gain_recv_sem.at[step - 1],
            "tensor",
            peer,
        )
        copy.start()
        gains.append(copy)
    line.drain()
    for copy in gains:
        copy.wait()
    small_out_ref[...] = small_sum[...]
    shared = slice(0, experts + 2)
    for step in range(1, n_tensor):
        small_out_ref[shared, :] += gain_recv[step - 1, shared, :]


def tail(n_dp, n_tensor, experts, hidden, grad, weight, attended, branch, small, weight_own, gain_own):
    seq_len, width = hidden.shape
    own_rows = seq_len // n_tensor
    depth, cols = weight_own.shape
    heads_cols = attended.shape[1]
    out_cols = width // n_dp
    table_rows = NB // n_dp
    return pl.pallas_call(
        functools.partial(tail_kernel, n_dp, n_tensor, experts, table_rows),
        out_shape=(
            jax.ShapeDtypeStruct((own_rows, width), F32),
            jax.ShapeDtypeStruct((depth, cols), F32),
            jax.ShapeDtypeStruct((heads_cols, out_cols), F32),
            jax.ShapeDtypeStruct((SMALL, depth), F32),
        ),
        in_specs=[vspec()] * 8,
        out_specs=(vspec(),) * 4,
        scratch_shapes=[
            pltpu.VMEM((own_rows, width), F32),
            pltpu.VMEM((n_tensor - 1, own_rows, width), BF16),
            pltpu.VMEM((n_tensor + 1, own_rows, width), BF16),
            pltpu.VMEM((n_dp, depth, cols), BF16),
            pltpu.VMEM((n_dp - 1, depth, cols), BF16),
            pltpu.VMEM((n_dp, heads_cols, out_cols), BF16),
            pltpu.VMEM((n_dp - 1, heads_cols, out_cols), BF16),
            pltpu.VMEM((n_dp - 1, SMALL, depth), F32),
            pltpu.VMEM((SMALL, depth), F32),
            pltpu.VMEM((n_tensor - 1, SMALL, depth), F32),
            pltpu.SemaphoreType.DMA((n_tensor - 1,)),
            pltpu.SemaphoreType.DMA((n_tensor + 1,)),
        ]
        + [pltpu.SemaphoreType.DMA((n_dp - 1,))] * 6
        + [pltpu.SemaphoreType.DMA((n_tensor - 1,))] * 2,
        compiler_params=pltpu.CompilerParams(
            vmem_limit_bytes=VMEM_LIMIT, collective_id=0, has_side_effects=True
        ),
        name="tail",
    )(hidden, grad, weight, attended, branch, small, weight_own, gain_own)


def rms_scale(values):
    return lax.rsqrt(jnp.mean(values * values, axis=-1, keepdims=True) + EPS)


def norm_backward(grad_normed, values, scale_inv, gain):
    normed_unit = values * scale_inv
    grad_unit = grad_normed * gain
    grad_values = scale_inv * (
        grad_unit - normed_unit * jnp.mean(grad_unit * normed_unit, axis=-1, keepdims=True)
    )
    return (grad_values, jnp.sum(grad_normed * normed_unit, axis=0))


def gelu_tanh(values):
    return jax.nn.gelu(values, approximate=True)


def route_slots(route_ids, experts, capacity):
    flat_routes = route_ids.reshape(-1)
    onehot = (flat_routes[:, None] == jnp.arange(experts, dtype=jnp.int32)[None, :]).astype(
        jnp.int32
    )
    ranks = jnp.cumsum(onehot, axis=0) - 1
    rank_own = jnp.sum(ranks * onehot, axis=1)
    return (flat_routes * capacity + rank_own).reshape(-1, TOP)


def on_device(
    tokens,
    segments,
    routes,
    w_qkv,
    w_attn_out,
    bias_table,
    gain_attn,
    gain_moe,
    router,
    w_in,
    w_out,
    cotangent,
):
    own_rows, model_width = tokens.shape
    n_tensor = lax.axis_size("tensor")
    n_dp = lax.axis_size("dp")
    seq_len = own_rows * n_tensor
    own_start = lax.axis_index("tensor") * own_rows
    head_cols = w_qkv.shape[2]
    heads = head_cols // HD
    experts = router.shape[1]
    local_experts = w_in.shape[0]
    capacity = 5 * seq_len * TOP // (4 * experts)
    highest = lax.Precision.HIGHEST
    slots = experts * capacity

    depth = w_qkv.shape[0]
    bias_rows = bias_table.shape[0]
    extra = jnp.concatenate(
        [
            router,
            gain_attn[:, None],
            gain_moe[:, None],
            jnp.pad(bias_table, ((0, depth - bias_rows), (0, 0))),
        ],
        axis=1,
    )
    extra = jnp.pad(extra, ((0, 0), (0, 128 - extra.shape[1])))
    packed = lax.all_gather(
        jnp.concatenate([w_qkv.reshape(depth, 3 * head_cols), extra], axis=1),
        "dp",
        axis=0,
        tiled=True,
    )
    qkv_matrix = packed[:, : 3 * head_cols]
    extras = packed[:, 3 * head_cols :]
    router_full = extras[:, :experts]
    gain_one = extras[:, experts].astype(F32)
    gain_two = extras[:, experts + 1].astype(F32)
    table = (
        extras.reshape(n_dp, depth, 128)[:, :bias_rows, experts + 2 : experts + 2 + heads]
        .reshape(NB, heads)
        .astype(F32)
    )
    out_columns = lax.all_gather(w_attn_out, "tensor", axis=0, tiled=True)
    out_matrix = lax.all_gather(out_columns, "dp", axis=1, tiled=True)

    tokens_float = tokens.astype(F32)
    scale_one = rms_scale(tokens_float)
    hidden_one = (tokens_float * scale_one * gain_one).astype(BF16)
    gathered_one = lax.all_gather(hidden_one, "tensor", axis=0, tiled=True)
    projected = jnp.dot(gathered_one, qkv_matrix, preferred_element_type=F32).astype(BF16)
    selectors = jnp.asarray(distance_selectors())
    patterns = jnp.dot(selectors, table, precision=highest)
    patterns = jnp.transpose(patterns.reshape(2, 2 * BS, heads), (2, 0, 1)).reshape(
        2 * heads, 2 * BS
    )
    far = table[NB - 1]
    segment_row = segments
    segment_col = segments.reshape(seq_len, 1)
    starts = segments[0, ::BS]
    ends = segments[0, BS - 1 :: BS]
    lowest = jnp.sum((ends[None, :] < starts[:, None]).astype(jnp.int32), axis=1)
    attended, lse = attention_forward(
        projected, lowest, segment_col, segment_row, patterns, far, heads
    )
    attended_own = lax.all_to_all(
        attended.reshape(n_tensor, own_rows, head_cols), "tensor", 0, 0
    )
    attended_own = jnp.transpose(attended_own, (1, 0, 2)).reshape(own_rows, n_tensor * head_cols)
    branch = jnp.dot(attended_own, out_matrix, preferred_element_type=F32)
    residual = tokens_float + branch
    scale_two = rms_scale(residual)
    hidden_two = (residual * scale_two * gain_two).astype(BF16)
    gathered_two = lax.all_gather(hidden_two, "tensor", axis=0, tiled=True)

    expert_ids = jnp.arange(experts, dtype=jnp.int32)

    def gate_values(logit_values, route_rows):
        expert_probs = jax.nn.softmax(logit_values, axis=-1)
        picked = jnp.sum(
            jnp.where(
                route_rows[:, :, None] == expert_ids[None, None, :], expert_probs[:, None, :], 0.0
            ),
            axis=-1,
        )
        return picked / jnp.sum(picked, axis=1, keepdims=True)

    gates = gate_values(jnp.dot(gathered_two, router_full, preferred_element_type=F32), routes)
    slot_ids = route_slots(routes, experts, capacity)
    slot_flat = slot_ids.reshape(-1)
    token_ids = jnp.repeat(jnp.arange(seq_len, dtype=jnp.int32), TOP)
    sources = jnp.full((slots,), seq_len, jnp.int32).at[slot_flat].set(token_ids)
    slot_gates = jnp.zeros((slots,), F32).at[slot_flat].set(gates.reshape(-1))
    grad_gathered = lax.all_gather(cotangent, "tensor", axis=0, tiled=True)

    def exchange(rows):
        parts = rows.reshape(n_dp, local_experts, capacity, model_width)
        return [
            lax.all_to_all(parts[:, i], "dp", 0, 0).reshape(n_dp * capacity, model_width)
            for i in range(local_experts)
        ]

    def give_back(parts):
        back = [
            lax.all_to_all(part.reshape(n_dp, capacity, model_width), "dp", 0, 0) for part in parts
        ]
        return jnp.stack(back, axis=1).reshape(slots, model_width)

    zero_row = jnp.zeros((1, model_width), BF16)
    dispatched = exchange(jnp.concatenate([gathered_two, zero_row], axis=0)[sources])
    padded_grad = jnp.concatenate([grad_gathered, zero_row], axis=0)
    grad_expert = exchange((slot_gates[:, None] * padded_grad[sources]).astype(BF16))

    outs, backs, grads_in, grads_out = [], [], [], []
    for i in range(local_experts):
        rows, grad_rows = dispatched[i], grad_expert[i]
        gate_part = nt(rows, w_in[i, 0])
        up_part = nt(rows, w_in[i, 1])
        gelu_value, gelu_pull = jax.vjp(gelu_tanh, gate_part)
        activated = (gelu_value * up_part).astype(BF16)
        outs.append(nn(activated, w_out[i]).astype(BF16))
        grad_act = nt(grad_rows, w_out[i])
        grads_out.append(tn(activated, grad_rows))
        grad_gate = gelu_pull(grad_act * up_part)[0].astype(BF16)
        grad_up = (grad_act * gelu_value).astype(BF16)
        backs.append((nn(grad_gate, w_in[i, 0]) + nn(grad_up, w_in[i, 1])).astype(BF16))
        grads_in.append(jnp.stack([tn(grad_gate, rows), tn(grad_up, rows)]))
    grad_w_in = jnp.stack(grads_in)
    grad_w_out = jnp.stack(grads_out)
    expert_out = give_back(outs)
    grad_dispatched = give_back(backs)

    first, second = slot_ids[:, 0], slot_ids[:, 1]
    picked_first = expert_out[first].astype(F32)
    picked_second = expert_out[second].astype(F32)
    mixture = lax.psum_scatter(
        (gates[:, 0:1] * picked_first + gates[:, 1:2] * picked_second).astype(BF16),
        "tensor",
        scatter_dimension=0,
        tiled=True,
    ).astype(F32)
    layer_out = (residual + mixture).astype(BF16)
    grad_float = grad_gathered.astype(F32)
    grad_gate_part = jnp.stack(
        [
            jnp.sum(grad_float * picked_first, axis=1),
            jnp.sum(grad_float * picked_second, axis=1),
        ],
        axis=1,
    )
    grad_hidden_part = (
        grad_dispatched[first].astype(F32) + grad_dispatched[second].astype(F32)
    ).astype(BF16)
    grad_own = lax.psum_scatter(
        grad_hidden_part, "tensor", scatter_dimension=0, tiled=True
    ).astype(F32)
    grad_gate_own = lax.dynamic_slice_in_dim(
        lax.psum(grad_gate_part, "tensor"), own_start, own_rows, 0
    )
    own_routes = lax.dynamic_slice_in_dim(routes, own_start, own_rows, 0)
    own_logits = jnp.dot(hidden_two, router_full, preferred_element_type=F32)

    def own_gates(logit_values):
        return gate_values(logit_values, own_routes)

    _, gate_pull = jax.vjp(own_gates, own_logits)
    grad_logits = gate_pull(grad_gate_own)[0]
    router_float = router_full.astype(F32)
    grad_hidden_two = grad_own + jnp.dot(grad_logits, router_float.T, precision=highest)
    grad_router_part = jnp.dot(hidden_two.astype(F32).T, grad_logits, precision=highest)
    grad_from_norm, grad_gain_two = norm_backward(grad_hidden_two, residual, scale_two, gain_two)
    grad_residual = cotangent.astype(F32) + grad_from_norm

    grad_branch = grad_residual.astype(BF16)
    grad_attended_own = nt(grad_branch, out_matrix).astype(BF16)
    grad_attended = lax.all_to_all(
        jnp.transpose(grad_attended_own.reshape(own_rows, n_tensor, head_cols), (1, 0, 2)),
        "tensor",
        0,
        0,
    ).reshape(seq_len, head_cols)
    grad_branch_all = lax.all_gather(grad_branch, "tensor", axis=0, tiled=True)
    grad_projected, diag = attention_backward(
        projected,
        attended,
        grad_attended,
        lse,
        lowest,
        segment_col,
        segment_row,
        patterns,
        far,
        heads,
    )
    diag = diag.reshape(heads, 3, 2 * BS)
    near = jnp.transpose(diag[:, :2].reshape(heads, 4 * BS))
    grad_table = lax.dot_general(
        jnp.asarray(skew_selectors()), near, (((0,), (0,)), ((), ())), precision=highest
    )
    grad_table = grad_table.at[NB - 1].add(jnp.sum(diag[:, 2], axis=1))
    small = jnp.concatenate(
        [
            jnp.transpose(grad_router_part),
            grad_gain_two[None],
            jnp.zeros((SMALL - experts - 1, model_width), F32),
        ],
        axis=0,
    )
    small = jnp.transpose(small.reshape(SMALL, n_dp, depth), (1, 0, 2))
    small = lax.dynamic_update_slice(
        small, grad_table.reshape(n_dp, NB // n_dp, heads), (0, experts + 2, 0)
    )
    grad_hidden_one, reduced_qkv, reduced_attn_out, small_sum = tail(
        n_dp,
        n_tensor,
        experts,
        gathered_one,
        grad_projected,
        qkv_matrix,
        attended,
        grad_branch_all,
        small,
        w_qkv.reshape(depth, 3 * head_cols),
        gain_attn[None].astype(F32),
    )
    grad_from_first, _ = norm_backward(grad_hidden_one, tokens_float, scale_one, gain_one)
    grad_tokens = (grad_residual + grad_from_first).astype(BF16)
    return (
        layer_out,
        grad_tokens,
        reduced_qkv.reshape(depth, 3, head_cols),
        reduced_attn_out,
        small_sum[experts + 2 : experts + 2 + NB // n_dp, :heads],
        small_sum[experts + 1],
        small_sum[experts],
        jnp.transpose(small_sum[:experts]),
        grad_w_in,
        grad_w_out,
    )


def solution(mesh):
    return jax.shard_map(
        on_device,
        mesh=mesh,
        in_specs=(
            P(("dp", "tensor"), None),
            P("dp", None),
            P("dp", None),
            P("dp", None, "tensor"),
            P("tensor", "dp"),
            P("dp", "tensor"),
            P("dp"),
            P("dp"),
            P("dp", None),
            P("dp", None, "tensor", None),
            P("dp", "tensor", None),
            P(("dp", "tensor"), None),
        ),
        out_specs=(
            P(("dp", "tensor"), None),
            P(("dp", "tensor"), None),
            P("dp", None, "tensor"),
            P("tensor", "dp"),
            P("dp", "tensor"),
            P("dp"),
            P("dp"),
            P("dp", None),
            P("dp", None, "tensor", None),
            P("dp", "tensor", None),
        ),
        check_vma=False,
    )
```

```python
import functools
import math

import jax
import jax.numpy as jnp
import numpy as np
from jax import lax
from jax.experimental import pallas as pl
from jax.experimental.pallas import tpu as pltpu
from jax.sharding import PartitionSpec as P

HD = 64
TOP = 2
NB = 32
NEAR = 128
BS = 256

EPS = 1e-06
NEG = -1e30
F32 = jnp.float32
BF16 = jnp.bfloat16
VMEM_LIMIT = 60 * 1024 * 1024


def distance_buckets():
    half_buckets = NB // 2
    thresholds = [bucket_level for bucket_level in range(1, half_buckets)]
    thresholds = thresholds + [
        int(
            math.ceil(
                half_buckets
                * (NEAR / half_buckets) ** ((bucket_level - half_buckets) / half_buckets)
            )
        )
        for bucket_level in range(half_buckets, NB)
    ]
    distance = np.arange(NEAR + 1)
    return (distance[:, None] >= np.array(thresholds)[None, :]).sum(axis=1)


def distance_selectors():
    buckets = distance_buckets()
    lanes = np.arange(2 * BS)
    signed = np.where(lanes < BS, lanes, lanes - 2 * BS)
    out = []
    for base in (0, BS):
        distance = np.clip(base - signed, 0, NEAR)
        out.append(buckets[distance][:, None] == np.arange(NB)[None, :])
    return np.concatenate(out, axis=0).astype(np.float32)


def skew_selectors():
    buckets = distance_buckets()
    lanes = np.arange(2 * BS)
    out = []
    for base in (0, BS):
        distance = np.clip(base + BS - 1 - lanes, 0, NEAR)
        out.append(buckets[distance][:, None] == np.arange(NB)[None, :])
    return np.concatenate(out, axis=0).astype(np.float32)


def nt(a, b):
    return lax.dot_general(a, b, (((1,), (1,)), ((), ())), preferred_element_type=F32)


def tn(a, b):
    return lax.dot_general(a, b, (((0,), (0,)), ((), ())), preferred_element_type=F32)


def nn(a, b):
    return lax.dot_general(a, b, (((1,), (0,)), ((), ())), preferred_element_type=F32)


def toeplitz(row):
    return pltpu.roll(jnp.broadcast_to(row, (BS, 2 * BS)), 0, 1, stride=1, stride_axis=0)[:, :BS]


def head_lanes(heads, width):
    lane = lax.broadcasted_iota(jnp.int32, (1, width), 1)
    return [(lane >= h * HD) & (lane < (h + 1) * HD) for h in range(heads)]


def own_head(value, lanes, heads):
    return value if heads == 1 else jnp.where(lanes, value, jnp.zeros((), value.dtype))


def build_bias(heads, pattern_ref, bias):
    for h in range(heads):
        for t in range(2):
            bias[h, t] = toeplitz(pattern_ref[2 * h + t : 2 * h + t + 1, :])


def block_mask(qb, kb, seg_col_ref, seg_row_ref):
    q_seg = seg_col_ref[pl.ds(pl.multiple_of(qb * BS, BS), BS), :]
    k_seg = seg_row_ref[:, pl.ds(pl.multiple_of(kb * BS, BS), BS)]
    row = lax.broadcasted_iota(jnp.int32, (BS, BS), 0) + (qb - kb) * BS
    col = lax.broadcasted_iota(jnp.int32, (BS, BS), 1)
    return (q_seg == k_seg) & (row >= col)


def attn_fwd_kernel(heads, blocks, lo_ref, qkv_ref, seg_col_ref, seg_row_ref, pattern_ref, far_ref, out_ref, lse_ref, bias):
    width = heads * HD
    lanes = head_lanes(heads, width)
    scale = HD**-0.5
    build_bias(heads, pattern_ref, bias)

    def q_step(qb, _):
        q_rows = pl.ds(pl.multiple_of(qb * BS, BS), BS)
        q_all = (qkv_ref[q_rows, 0:width] * scale).astype(BF16)
        q_heads = [own_head(q_all, lanes[h], heads) for h in range(heads)]

        def k_step(kb, carry):
            k_rows = pl.ds(pl.multiple_of(kb * BS, BS), BS)
            k = qkv_ref[k_rows, width : 2 * width]
            v = qkv_ref[k_rows, 2 * width : 3 * width]
            allowed = block_mask(qb, kb, seg_col_ref, seg_row_ref)
            near = jnp.minimum(qb - kb, 1)
            is_far = qb - kb >= 2
            new = []
            for h in range(heads):
                top, total, acc = carry[3 * h : 3 * h + 3]
                b = jnp.where(is_far, far_ref[h], bias[h, near])
                s = jnp.where(allowed, nt(q_heads[h], k) + b, NEG)
                top_new = jnp.maximum(top, jnp.max(s, axis=1, keepdims=True))
                alpha = jnp.exp(top - top_new)
                p = jnp.exp(s - top_new)
                total = alpha * total + jnp.sum(p, axis=1, keepdims=True)
                acc = alpha * acc + nn(p.astype(BF16), v)
                new += [top_new, total, acc]
            return tuple(new)

        init = []
        for h in range(heads):
            init += [jnp.full((BS, 1), NEG, F32), jnp.zeros((BS, 1), F32), jnp.zeros((BS, width), F32)]
        res = lax.fori_loop(lo_ref[qb], qb + 1, k_step, tuple(init))
        out = jnp.zeros((BS, width), F32)
        for h in range(heads):
            top, total, acc = res[3 * h : 3 * h + 3]
            value = acc / total
            out = value if heads == 1 else jnp.where(lanes[h], value, out)
            lse_ref[q_rows, h : h + 1] = top + jnp.log(total)
        out_ref[q_rows, :] = out.astype(BF16)
        return 0

    lax.fori_loop(0, blocks, q_step, 0)


def attn_bwd_kernel(
    heads,
    blocks,
    lo_ref,
    qkv_ref,
    out_ref,
    grad_ref,
    lse_ref,
    seg_col_ref,
    seg_row_ref,
    pattern_ref,
    far_ref,
    grad_qkv_ref,
    diag_ref,
    bias,
    dk,
    dv,
    sums,
):
    width = heads * HD
    lanes = head_lanes(heads, width)
    scale = HD**-0.5
    build_bias(heads, pattern_ref, bias)
    dk[...] = jnp.zeros_like(dk)
    dv[...] = jnp.zeros_like(dv)
    sums[...] = jnp.zeros_like(sums)

    def q_step(qb, _):
        q_rows = pl.ds(pl.multiple_of(qb * BS, BS), BS)
        q_all = (qkv_ref[q_rows, 0:width] * scale).astype(BF16)
        g_all = grad_ref[q_rows, :]
        both = g_all.astype(F32) * out_ref[q_rows, :].astype(F32)
        q_heads = [own_head(q_all, lanes[h], heads) for h in range(heads)]
        g_heads = [own_head(g_all, lanes[h], heads) for h in range(heads)]
        deltas = [jnp.sum(own_head(both, lanes[h], heads), axis=1, keepdims=True) for h in range(heads)]
        totals = [lse_ref[q_rows, h : h + 1] for h in range(heads)]

        def k_step(kb, dq):
            k_rows = pl.ds(pl.multiple_of(kb * BS, BS), BS)
            k = qkv_ref[k_rows, width : 2 * width]
            v = qkv_ref[k_rows, 2 * width : 3 * width]
            allowed = block_mask(qb, kb, seg_col_ref, seg_row_ref)
            near = jnp.minimum(qb - kb, 1)
            place = jnp.minimum(qb - kb, 2)
            is_far = qb - kb >= 2
            dk_add = jnp.zeros((BS, width), F32)
            dv_add = jnp.zeros((BS, width), F32)
            for h in range(heads):
                b = jnp.where(is_far, far_ref[h], bias[h, near])
                s = jnp.where(allowed, nt(q_heads[h], k) + b, NEG)
                p = jnp.exp(s - totals[h])
                gp = nt(g_heads[h], v)
                ds = (p * (gp - deltas[h])).astype(BF16)
                dv_add += tn(p.astype(BF16), g_heads[h])
                dk_add += tn(ds, q_heads[h])
                dq = dq + own_head(nn(ds, k), lanes[h], heads)
                sums[h, place] += ds.astype(F32)
            dk[k_rows, :] += dk_add
            dv[k_rows, :] += dv_add
            return dq

        dq = lax.fori_loop(lo_ref[qb], qb + 1, k_step, jnp.zeros((BS, width), F32))
        grad_qkv_ref[q_rows, 0:width] = (dq * scale).astype(BF16)
        return 0

    lax.fori_loop(0, blocks, q_step, 0)
    grad_qkv_ref[:, width : 2 * width] = dk[...].astype(BF16)
    grad_qkv_ref[:, 2 * width : 3 * width] = dv[...].astype(BF16)
    row = lax.broadcasted_iota(jnp.int32, (BS, BS), 0)
    col = lax.broadcasted_iota(jnp.int32, (BS, BS), 1)
    upside_down = jnp.where(row + col == BS - 1, 1.0, 0.0).astype(F32)
    for h in range(heads):
        for t in range(2):
            flipped = jnp.dot(upside_down, sums[h, t], precision=lax.Precision.HIGHEST, preferred_element_type=F32)
            wide = jnp.concatenate([flipped, jnp.zeros((BS, BS), F32)], axis=1)
            skewed = pltpu.roll(wide, 0, 1, stride=1, stride_axis=0)
            diag_ref[3 * h + t : 3 * h + t + 1, :] = jnp.sum(skewed, axis=0, keepdims=True)
        rest = jnp.sum(sums[h, 2], axis=0, keepdims=True)
        diag_ref[3 * h + 2 : 3 * h + 3, :] = jnp.concatenate([rest, jnp.zeros((1, BS), F32)], axis=1)


def vspec():
    return pl.BlockSpec(memory_space=pltpu.VMEM)


def sspec():
    return pl.BlockSpec(memory_space=pltpu.SMEM)


def attention_forward(projected, lo, seg_col, seg_row, patterns, far, heads):
    seq_len = projected.shape[0]
    blocks = seq_len // BS
    return pl.pallas_call(
        functools.partial(attn_fwd_kernel, heads, blocks),
        out_shape=(
            jax.ShapeDtypeStruct((seq_len, heads * HD), BF16),
            jax.ShapeDtypeStruct((seq_len, heads), F32),
        ),
        in_specs=[sspec(), vspec(), vspec(), vspec(), vspec(), sspec()],
        out_specs=(vspec(), vspec()),
        scratch_shapes=[pltpu.VMEM((heads, 2, BS, BS), F32)],
        compiler_params=pltpu.CompilerParams(vmem_limit_bytes=VMEM_LIMIT),
        name="attn_fwd",
    )(lo, projected, seg_col, seg_row, patterns, far)


def attention_backward(projected, attended, grad, lse, lo, seg_col, seg_row, patterns, far, heads):
    seq_len = projected.shape[0]
    blocks = seq_len // BS
    width = heads * HD
    return pl.pallas_call(
        functools.partial(attn_bwd_kernel, heads, blocks),
        out_shape=(
            jax.ShapeDtypeStruct((seq_len, 3 * width), BF16),
            jax.ShapeDtypeStruct((3 * heads, 2 * BS), F32),
        ),
        in_specs=[sspec(), vspec(), vspec(), vspec(), vspec(), vspec(), vspec(), vspec(), sspec()],
        out_specs=(vspec(), vspec()),
        scratch_shapes=[
            pltpu.VMEM((heads, 2, BS, BS), F32),
            pltpu.VMEM((seq_len, width), F32),
            pltpu.VMEM((seq_len, width), F32),
            pltpu.VMEM((heads, 3, BS, BS), F32),
        ],
        compiler_params=pltpu.CompilerParams(vmem_limit_bytes=VMEM_LIMIT),
        name="attn_bwd",
    )(lo, projected, attended, grad, lse, seg_col, seg_row, patterns, far)


MESH = pl.DeviceIdType.MESH
SMALL = 32


def remote(src, dst, send, recv, axis, peer):
    return pltpu.make_async_remote_copy(
        src_ref=src,
        dst_ref=dst,
        send_sem=send,
        recv_sem=recv,
        device_id={axis: peer},
        device_id_type=MESH,
    )


def greet(groups):
    barrier = pltpu.get_barrier_semaphore()
    total = 0
    for axis, n in groups:
        me = lax.axis_index(axis)
        for step in range(1, n):
            pl.semaphore_signal(
                barrier, inc=1, device_id={axis: lax.rem(me + step, n)}, device_id_type=MESH
            )
        total += n - 1
    pl.semaphore_wait(barrier, total)


class LineSum:
    def __init__(self, n, partial, send, recv, send_sem, recv_sem, acc, total):
        self.n, self.partial = n, partial
        self.send, self.recv, self.send_sem, self.recv_sem = send, recv, send_sem, recv_sem
        self.acc, self.total = acc, total
        self.me = lax.axis_index("tensor")

    def flow(self, first, k):
        n, me = self.n, self.me
        near = me * 2 < n
        right = near if first else jnp.logical_not(near)
        block = jnp.where(right, n - 1 - k, k)
        comes = jnp.where(right, jnp.where(me > 0, me <= block, False), jnp.where(me < n - 1, me >= block, False))
        goes = jnp.where(right, me < block, me > block)
        peer = jnp.clip(jnp.where(right, me + 1, me - 1), 0, n - 1)
        out_slot = jnp.clip(jnp.where(right, k, n - 1 - me + k), 0, n - 2)
        in_slot = jnp.clip(jnp.where(right, k, n - me + k), 0, n)
        peer_slot = jnp.clip(jnp.where(right, k, n - peer + k), 0, n)
        return block, comes, goes, peer, out_slot, in_slot, peer_slot

    def copy(self, peer, out_slot, slot):
        return remote(
            self.send.at[out_slot],
            self.recv.at[slot],
            self.send_sem.at[out_slot],
            self.recv_sem.at[slot],
            "tensor",
            peer,
        )

    def start(self):
        for k in range(self.n - 1):
            for first in (True, False):
                block, comes, goes, peer, out_slot, in_slot, peer_slot = self.flow(first, k)

                @pl.when(goes & jnp.logical_not(comes))
                def _():
                    self.send[out_slot] = self.partial(block).astype(BF16)
                    self.copy(peer, out_slot, peer_slot).start()

        self.total[...] = self.partial(self.me)

    def finish(self):
        for k in range(self.n - 1):
            for first in (True, False):
                block, comes, goes, peer, out_slot, in_slot, peer_slot = self.flow(first, k)

                @pl.when(goes & comes)
                def _():
                    self.acc[...] = self.partial(block)
                    self.copy(peer, out_slot, in_slot).wait_recv()
                    self.send[out_slot] = (
                        self.acc[...] + self.recv[in_slot].astype(F32)
                    ).astype(BF16)
                    self.copy(peer, out_slot, peer_slot).start()

                @pl.when(comes & jnp.logical_not(goes))
                def _():
                    self.copy(peer, 0, in_slot).wait_recv()
                    self.total[...] += self.recv[in_slot].astype(F32)

    def drain(self):
        for k in range(self.n - 1):
            for first in (True, False):
                block, comes, goes, peer, out_slot, in_slot, peer_slot = self.flow(first, k)

                @pl.when(goes)
                def _():
                    self.copy(peer, out_slot, in_slot).wait_send()


def tail_kernel(
    n_dp,
    n_tensor,
    experts,
    table_rows,
    hidden_ref,
    grad_ref,
    weight_ref,
    attended_ref,
    branch_ref,
    small_ref,
    weight_own_ref,
    gain_own_ref,
    grad_hidden_ref,
    grad_qkv_ref,
    grad_out_ref,
    small_out_ref,
    acc,
    line_send,
    line_recv,
    qkv_send,
    qkv_recv,
    out_send,
    out_recv,
    small_recv,
    small_sum,
    gain_recv,
    line_send_sem,
    line_recv_sem,
    qkv_send_sem,
    qkv_recv_sem,
    out_send_sem,
    out_recv_sem,
    small_send_sem,
    small_recv_sem,
    gain_send_sem,
    gain_recv_sem,
):
    own_rows = grad_hidden_ref.shape[0]
    depth = weight_own_ref.shape[0]
    out_cols = grad_out_ref.shape[1]
    me = lax.axis_index("dp")
    me_t = lax.axis_index("tensor")
    greet([("dp", n_dp), ("tensor", n_tensor)])

    def partial(block):
        rows = pl.ds(pl.multiple_of(block * own_rows, own_rows), own_rows)
        return nt(grad_ref[rows, :], weight_ref[...])

    line = LineSum(
        n_tensor, partial, line_send, line_recv, line_send_sem, line_recv_sem, acc, grad_hidden_ref
    )
    line.start()
    copies = []
    for step in range(1, n_dp):
        peer = lax.rem(me + step, n_dp)
        copy = remote(
            small_ref.at[peer],
            small_recv.at[step - 1],
            small_send_sem.at[step - 1],
            small_recv_sem.at[step - 1],
            "dp",
            peer,
        )
        copy.start()
        copies.append(copy)
    for block in range(n_dp):
        cols = slice(block * depth, (block + 1) * depth)
        qkv_send[block] = tn(hidden_ref[:, cols], grad_ref[...]).astype(BF16)
    for step in range(1, n_dp):
        peer = lax.rem(me + step, n_dp)
        copy = remote(
            qkv_send.at[peer],
            qkv_recv.at[step - 1],
            qkv_send_sem.at[step - 1],
            qkv_recv_sem.at[step - 1],
            "dp",
            peer,
        )
        copy.start()
        copies.append(copy)
    for block in range(n_dp):
        cols = slice(block * out_cols, (block + 1) * out_cols)
        out_send[block] = tn(attended_ref[...], branch_ref[:, cols]).astype(BF16)
    for step in range(1, n_dp):
        peer = lax.rem(me + step, n_dp)
        copy = remote(
            out_send.at[peer],
            out_recv.at[step - 1],
            out_send_sem.at[step - 1],
            out_recv_sem.at[step - 1],
            "dp",
            peer,
        )
        copy.start()
        copies.append(copy)
    line.finish()
    for copy in copies:
        copy.wait()
    small_sum[...] = small_ref[me]
    grad_qkv_ref[...] = qkv_send[me].astype(F32)
    grad_out_ref[...] = out_send[me].astype(F32)
    for step in range(1, n_dp):
        small_sum[...] += small_recv[step - 1]
        grad_qkv_ref[...] += qkv_recv[step - 1].astype(F32)
        grad_out_ref[...] += out_recv[step - 1].astype(F32)
    column = jnp.sum(grad_qkv_ref[...] * weight_own_ref[...].astype(F32), axis=1, keepdims=True)
    eye = lax.broadcasted_iota(jnp.int32, (depth, depth), 0) == lax.broadcasted_iota(
        jnp.int32, (depth, depth), 1
    )
    row = jnp.sum(jnp.where(eye, column, 0.0), axis=0, keepdims=True)
    small_sum[experts + 1 : experts + 2, :] = row / gain_own_ref[...]
    gains = []
    for step in range(1, n_tensor):
        peer = lax.rem(me_t + step, n_tensor)
        copy = remote(
            small_sum,
            gain_recv.at[step - 1],
            gain_send_sem.at[step - 1],
            gain_recv_sem.at[step - 1],
            "tensor",
            peer,
        )
        copy.start()
        gains.append(copy)
    line.drain()
    for copy in gains:
        copy.wait()
    small_out_ref[...] = small_sum[...]
    shared = slice(0, experts + 2)
    for step in range(1, n_tensor):
        small_out_ref[shared, :] += gain_recv[step - 1, shared, :]


def tail(n_dp, n_tensor, experts, hidden, grad, weight, attended, branch, small, weight_own, gain_own):
    seq_len, width = hidden.shape
    own_rows = seq_len // n_tensor
    depth, cols = weight_own.shape
    heads_cols = attended.shape[1]
    out_cols = width // n_dp
    table_rows = NB // n_dp
    return pl.pallas_call(
        functools.partial(tail_kernel, n_dp, n_tensor, experts, table_rows),
        out_shape=(
            jax.ShapeDtypeStruct((own_rows, width), F32),
            jax.ShapeDtypeStruct((depth, cols), F32),
            jax.ShapeDtypeStruct((heads_cols, out_cols), F32),
            jax.ShapeDtypeStruct((SMALL, depth), F32),
        ),
        in_specs=[vspec()] * 8,
        out_specs=(vspec(),) * 4,
        scratch_shapes=[
            pltpu.VMEM((own_rows, width), F32),
            pltpu.VMEM((n_tensor - 1, own_rows, width), BF16),
            pltpu.VMEM((n_tensor + 1, own_rows, width), BF16),
            pltpu.VMEM((n_dp, depth, cols), BF16),
            pltpu.VMEM((n_dp - 1, depth, cols), BF16),
            pltpu.VMEM((n_dp, heads_cols, out_cols), BF16),
            pltpu.VMEM((n_dp - 1, heads_cols, out_cols), BF16),
            pltpu.VMEM((n_dp - 1, SMALL, depth), F32),
            pltpu.VMEM((SMALL, depth), F32),
            pltpu.VMEM((n_tensor - 1, SMALL, depth), F32),
            pltpu.SemaphoreType.DMA((n_tensor - 1,)),
            pltpu.SemaphoreType.DMA((n_tensor + 1,)),
        ]
        + [pltpu.SemaphoreType.DMA((n_dp - 1,))] * 6
        + [pltpu.SemaphoreType.DMA((n_tensor - 1,))] * 2,
        compiler_params=pltpu.CompilerParams(
            vmem_limit_bytes=VMEM_LIMIT, collective_id=0, has_side_effects=True
        ),
        name="tail",
    )(hidden, grad, weight, attended, branch, small, weight_own, gain_own)


def line_gather(n, buf, send_sem, recv_sem, on_block):
    me = lax.axis_index("tensor")

    def copy(block, slot, k, peer):
        return remote(
            buf.at[block], buf.at[block], send_sem.at[slot, k], recv_sem.at[slot, k], "tensor", peer
        )

    def arrived(k, fn):
        if k == 0:
            fn(me, 0, 0)
            return
        for slot, sign in enumerate((1, -1)):
            block = me - sign * k

            @pl.when((block >= 0) & (block < n))
            def _():
                fn(block, slot, sign)

    def outgoing(k, fn):
        for slot, sign in enumerate((1, -1)):
            block, peer = me - sign * k, me + sign

            @pl.when((block >= 0) & (block < n) & (peer >= 0) & (peer < n))
            def _():
                fn(copy(block, slot, k, peer))

    for k in range(n):
        if k < n - 1:
            outgoing(k, lambda c: c.start())
        arrived(k, lambda block, slot, sign: on_block(block))
        if k < n - 1:
            arrived(
                k + 1,
                lambda block, slot, sign: copy(
                    block, slot, k, jnp.clip(me - sign, 0, n - 1)
                ).wait_recv(),
            )
    for k in range(n - 1):
        outgoing(k, lambda c: c.wait_send())


def diagonal(size):
    return lax.broadcasted_iota(jnp.int32, (size, size), 0) == lax.broadcasted_iota(
        jnp.int32, (size, size), 1
    )


def to_column(row):
    return jnp.sum(jnp.where(diagonal(row.shape[1]), row, 0.0), axis=1, keepdims=True)


def to_row(column):
    return jnp.sum(jnp.where(diagonal(column.shape[0]), column, 0.0), axis=0, keepdims=True)


def expert_kernel(
    n_dp,
    local,
    capacity,
    rows_ref,
    grad_ref,
    gates_ref,
    in_ref,
    out_ref,
    back_ref,
    gate_back_ref,
    value_ref,
    grad_in_ref,
    grad_out_ref,
    back_send,
    gate_send,
    zs,
    ups,
    gates_s,
    stage,
    value_stage,
    back_send_sem,
    back_recv_sem,
    gate_send_sem,
    gate_recv_sem,
    own_sem,
    stage_sem,
    value_sem,
):
    me = lax.axis_index("dp")
    pairs = n_dp // 2
    hidden = in_ref.shape[2]
    width = rows_ref.shape[2]
    two = 2 * capacity
    greet([("dp", n_dp)])

    def back_copy(expert, target, sender):
        part = slice(expert * capacity, (expert + 1) * capacity)
        return remote(
            back_send.at[target, part],
            back_ref.at[sender, part],
            back_send_sem.at[expert, target],
            back_recv_sem.at[expert, sender],
            "dp",
            target,
        )

    def own_copy(expert):
        part = slice(expert * capacity, (expert + 1) * capacity)
        return pltpu.make_async_copy(
            back_send.at[me, part], back_ref.at[me, part], own_sem.at[expert]
        )

    def stage_copy(slot, target):
        return pltpu.make_async_copy(stage.at[slot], target, stage_sem.at[slot])

    gate_send[...] = jnp.zeros_like(gate_send)
    staged = []

    def put(value, target):
        slot = len(staged) % 2
        if len(staged) >= 2:
            staged[-2].wait()
        stage[slot] = value
        copy = stage_copy(slot, target)
        copy.start()
        staged.append(copy)

    for expert in range(local):
        part = slice(expert * capacity, (expert + 1) * capacity)

        def group(index, _):
            pair = (me // 2) ^ (pairs - 1 - index)
            first = 2 * pair
            rows = rows_ref[pl.ds(first, 2), part, :].reshape(two, width)
            grads = grad_ref[pl.ds(first, 2), part, :].reshape(two, width)
            column = jnp.concatenate(
                [to_column(gates_ref[first + j, 0:1, part]) for j in range(2)], axis=0
            )
            gate = nt(rows, in_ref[expert, 0])
            up = nt(rows, in_ref[expert, 1])
            square = gate * gate
            bent = jnp.tanh(0.7978845608028654 * gate * (1.0 + 0.044715 * square))
            half = 0.5 * (1.0 + bent)
            gelu = gate * half
            slope = half + 0.5 * gate * (1.0 - bent * bent) * (
                0.7978845608028654 * (1.0 + 3 * 0.044715 * square)
            )
            z = gelu * up
            grad_z = nt(grads, out_ref[expert])
            gate_grad = jnp.sum(z * grad_z, axis=1, keepdims=True)
            grad_z = column * grad_z
            zs[pl.ds(first, 2)] = (column * z).astype(BF16).reshape(2, capacity, hidden)
            ups[0, pl.ds(first, 2)] = (grad_z * up * slope).astype(BF16).reshape(2, capacity, hidden)
            ups[1, pl.ds(first, 2)] = (grad_z * gelu).astype(BF16).reshape(2, capacity, hidden)
            for j in range(2):
                gate_send[first + j, 0:1, part] = to_row(
                    gate_grad[j * capacity : (j + 1) * capacity]
                )
            back = nn(ups[0, pl.ds(first, 2)].reshape(two, hidden), in_ref[expert, 0])
            back += nn(ups[1, pl.ds(first, 2)].reshape(two, hidden), in_ref[expert, 1])
            back_send[pl.ds(first, 2), part, :] = back.astype(BF16).reshape(2, capacity, width)
            for j in range(2):
                target = first + j

                @pl.when(target != me)
                def _():
                    back_copy(expert, target, me).start()

                @pl.when(target == me)
                def _():
                    own_copy(expert).start()

            return 0

        lax.fori_loop(0, pairs, group, 0)
        if expert == local - 1:
            gate_copies = []
            for step in range(1, n_dp):
                target = lax.rem(me + step, n_dp)
                copy = remote(
                    gate_send.at[target],
                    gate_back_ref.at[me],
                    gate_send_sem.at[step - 1],
                    gate_recv_sem.at[step - 1],
                    "dp",
                    target,
                )
                copy.start()
                gate_copies.append(copy)
            gate_back_ref[me] = gate_send[me]
        rows = rows_ref[:, part, :].reshape(n_dp * capacity, width)
        for half in range(2):
            put(tn(ups[half].reshape(n_dp * capacity, hidden), rows), grad_in_ref.at[expert, half])
        grads = grad_ref[:, part, :].reshape(n_dp * capacity, width)
        put(tn(zs[...].reshape(n_dp * capacity, hidden), grads), grad_out_ref.at[expert])
        if expert > 0:
            pltpu.make_async_copy(
                value_stage, value_ref.at[:, slice((expert - 1) * capacity, expert * capacity)], value_sem
            ).wait()

        def value(pair, _):
            out = nn(zs[pl.ds(2 * pair, 2)].reshape(two, hidden), out_ref[expert])
            value_stage[pl.ds(2 * pair, 2)] = out.astype(BF16).reshape(2, capacity, width)
            return 0

        lax.fori_loop(0, pairs, value, 0)
        pltpu.make_async_copy(value_stage, value_ref.at[:, part], value_sem).start()

    last = slice((local - 1) * capacity, local * capacity)
    pltpu.make_async_copy(value_stage, value_ref.at[:, last], value_sem).wait()
    for copy in staged[-2:]:
        copy.wait()
    for copy in gate_copies:
        copy.wait()
    for expert in range(local):
        own_copy(expert).wait()
        for step in range(1, n_dp):
            peer = lax.rem(me + step, n_dp)
            back_copy(expert, peer, me).wait_send()
            back_copy(expert, me, peer).wait_recv()


def any_spec():
    return pl.BlockSpec(memory_space=pl.ANY)


def run_experts(n_dp, capacity, rows, grads, gates, w_in, w_out):
    local, _, hidden, width = w_in.shape
    slots = local * capacity
    return pl.pallas_call(
        functools.partial(expert_kernel, n_dp, local, capacity),
        out_shape=(
            jax.ShapeDtypeStruct((n_dp, slots, width), BF16),
            jax.ShapeDtypeStruct((n_dp, 8, slots), F32),
            jax.ShapeDtypeStruct((n_dp, slots, width), BF16),
            jax.ShapeDtypeStruct(w_in.shape, F32),
            jax.ShapeDtypeStruct(w_out.shape, F32),
        ),
        in_specs=[vspec()] * 5,
        out_specs=(any_spec(), vspec(), any_spec(), any_spec(), any_spec()),
        scratch_shapes=[
            pltpu.VMEM((n_dp, slots, width), BF16),
            pltpu.VMEM((n_dp, 8, slots), F32),
            pltpu.VMEM((n_dp, capacity, hidden), BF16),
            pltpu.VMEM((2, n_dp, capacity, hidden), BF16),
            pltpu.VMEM((8, 128), F32),
            pltpu.VMEM((2, hidden, width), F32),
            pltpu.VMEM((n_dp, capacity, width), BF16),
            pltpu.SemaphoreType.DMA((local, n_dp)),
            pltpu.SemaphoreType.DMA((local, n_dp)),
            pltpu.SemaphoreType.DMA((n_dp - 1,)),
            pltpu.SemaphoreType.DMA((n_dp - 1,)),
            pltpu.SemaphoreType.DMA((local,)),
            pltpu.SemaphoreType.DMA((2,)),
            pltpu.SemaphoreType.DMA,
        ],
        compiler_params=pltpu.CompilerParams(
            vmem_limit_bytes=VMEM_LIMIT, collective_id=1, has_side_effects=True
        ),
        name="experts",
    )(rows, grads, gates, w_in, w_out)


def chosen_slots(columns, slots):
    lane = lax.broadcasted_iota(jnp.int32, (1, slots), 1)
    return columns[:, 0:1] == lane, columns[:, 1:2] == lane


def combine_kernel(
    n_dp,
    n_tensor,
    experts,
    rows_ref,
    gate_ref,
    slots_ref,
    routes_ref,
    residual_ref,
    hidden_ref,
    cotangent_ref,
    router_ref,
    gain_ref,
    weight_ref,
    value_ref,
    grad_residual_ref,
    branch_ref,
    grad_attended_ref,
    small_ref,
    value_back_ref,
    acc,
    total,
    line_send,
    line_recv,
    gate_all,
    gate_send,
    gate_recv,
    value_own,
    line_send_sem,
    line_recv_sem,
    gate_send_sem,
    gate_recv_sem,
    value_send_sem,
    value_recv_sem,
    value_own_sem,
    gather_send_sem,
    gather_recv_sem,
):
    own_rows, width = residual_ref.shape
    slots = rows_ref.shape[0]
    per = slots // n_dp
    me = lax.axis_index("dp")
    me_t = lax.axis_index("tensor")
    greet([("dp", n_dp), ("tensor", n_tensor)])
    values = []
    for step in range(1, n_dp):
        peer = lax.rem(me + step, n_dp)
        copy = remote(
            value_ref.at[peer],
            value_back_ref.at[me],
            value_send_sem.at[step - 1],
            value_recv_sem.at[step - 1],
            "dp",
            peer,
        )
        copy.start()
        values.append(copy)
    fetch = pltpu.make_async_copy(value_ref.at[me], value_own, value_own_sem.at[0])
    fetch.start()

    def partial(block):
        one, two = chosen_slots(
            slots_ref[pl.ds(pl.multiple_of(block * own_rows, own_rows), own_rows), :], slots
        )
        return nn(jnp.where(one | two, 1.0, 0.0).astype(BF16), rows_ref[...])

    line = LineSum(
        n_tensor, partial, line_send, line_recv, line_send_sem, line_recv_sem, acc, total
    )
    line.start()
    for peer in range(n_dp):
        gate_all[0:1, peer * per : (peer + 1) * per] = gate_ref[peer, 0:1, :]
    gate_send[...] = jnp.zeros_like(gate_send)
    gates = []
    for step in range(n_tensor):
        peer = lax.rem(me_t + step, n_tensor)
        picks = chosen_slots(
            slots_ref[pl.ds(pl.multiple_of(peer * own_rows, own_rows), own_rows), :], slots
        )
        for k in range(TOP):
            column = jnp.sum(
                jnp.where(picks[k], gate_all[0:1, :], 0.0), axis=1, keepdims=True
            )
            gate_send[step, k : k + 1, :] = to_row(column)
        if step:
            copy = remote(
                gate_send.at[step],
                gate_recv.at[step - 1],
                gate_send_sem.at[step - 1],
                gate_recv_sem.at[step - 1],
                "tensor",
                peer,
            )
            copy.start()
            gates.append(copy)
    fetch.wait()
    put = pltpu.make_async_copy(value_own, value_back_ref.at[me], value_own_sem.at[1])
    put.start()

    hidden = hidden_ref[...]
    router = router_ref[...]
    logits = nt(router, hidden)
    exps = jnp.exp(logits - jnp.max(logits, axis=0, keepdims=True))
    probs = exps / jnp.sum(exps, axis=0, keepdims=True)
    ids = lax.broadcasted_iota(jnp.int32, (experts, own_rows), 0)
    first, second = ids == routes_ref[0:1, :], ids == routes_ref[1:2, :]
    prob_one = jnp.sum(jnp.where(first, probs, 0.0), axis=0, keepdims=True)
    prob_two = jnp.sum(jnp.where(second, probs, 0.0), axis=0, keepdims=True)
    both = prob_one + prob_two
    line.finish()
    for copy in gates:
        copy.wait()
    gate_sum = gate_send[0]
    for step in range(1, n_tensor):
        gate_sum = gate_sum + gate_recv[step - 1]
    grad_one, grad_two = gate_sum[0:1, :], gate_sum[1:2, :]
    mean_grad = (prob_one * grad_one + prob_two * grad_two) / both
    grad_probs = (
        jnp.where(first, grad_one - mean_grad, 0.0) + jnp.where(second, grad_two - mean_grad, 0.0)
    ) / both
    grad_logits = probs * (grad_probs - jnp.sum(grad_probs * probs, axis=0, keepdims=True))
    grad_hidden = total[...] + lax.dot_general(
        grad_logits,
        router.astype(F32),
        (((0,), (0,)), ((), ())),
        precision=lax.Precision.HIGHEST,
        preferred_element_type=F32,
    )
    residual = residual_ref[...]
    scale = lax.rsqrt(jnp.mean(residual * residual, axis=1, keepdims=True) + EPS)
    unit = residual * scale
    small_ref[...] = jnp.zeros_like(small_ref)
    small_ref[experts : experts + 1, :] = jnp.sum(grad_hidden * unit, axis=0, keepdims=True)
    grad_unit = grad_hidden * gain_ref[...]
    grad_residual = cotangent_ref[...].astype(F32) + scale * (
        grad_unit - unit * jnp.mean(grad_unit * unit, axis=1, keepdims=True)
    )
    grad_residual_ref[...] = grad_residual
    branch_ref[me_t] = grad_residual.astype(BF16)

    def on_block(block):
        grad_attended_ref[pl.ds(pl.multiple_of(block * own_rows, own_rows), own_rows), :] = nt(
            branch_ref[block], weight_ref[...]
        ).astype(BF16)

    line_gather(n_tensor, branch_ref, gather_send_sem, gather_recv_sem, on_block)
    small_ref[0:experts, :] = jnp.dot(
        grad_logits,
        hidden.astype(F32),
        precision=lax.Precision.HIGHEST,
        preferred_element_type=F32,
    )
    line.drain()
    put.wait()
    for copy in values:
        copy.wait()


def combine(
    n_dp,
    n_tensor,
    experts,
    rows,
    gates,
    slot_columns,
    routes_own,
    residual,
    hidden,
    cotangent,
    router_rows,
    gain,
    weight,
    value,
):
    own_rows, width = residual.shape
    slots = rows.shape[0]
    return pl.pallas_call(
        functools.partial(combine_kernel, n_dp, n_tensor, experts),
        out_shape=(
            jax.ShapeDtypeStruct((own_rows, width), F32),
            jax.ShapeDtypeStruct((n_tensor, own_rows, width), BF16),
            jax.ShapeDtypeStruct((n_tensor * own_rows, weight.shape[0]), BF16),
            jax.ShapeDtypeStruct((SMALL, width), F32),
            jax.ShapeDtypeStruct(value.shape, BF16),
        ),
        in_specs=[vspec()] * 10 + [any_spec()],
        out_specs=(vspec(), vspec(), vspec(), vspec(), any_spec()),
        scratch_shapes=[
            pltpu.VMEM((own_rows, width), F32),
            pltpu.VMEM((own_rows, width), F32),
            pltpu.VMEM((n_tensor - 1, own_rows, width), BF16),
            pltpu.VMEM((n_tensor + 1, own_rows, width), BF16),
            pltpu.VMEM((8, slots), F32),
            pltpu.VMEM((n_tensor, 8, own_rows), F32),
            pltpu.VMEM((n_tensor - 1, 8, own_rows), F32),
            pltpu.VMEM(value.shape[1:], BF16),
            pltpu.SemaphoreType.DMA((n_tensor - 1,)),
            pltpu.SemaphoreType.DMA((n_tensor + 1,)),
            pltpu.SemaphoreType.DMA((n_tensor - 1,)),
            pltpu.SemaphoreType.DMA((n_tensor - 1,)),
            pltpu.SemaphoreType.DMA((n_dp - 1,)),
            pltpu.SemaphoreType.DMA((n_dp - 1,)),
            pltpu.SemaphoreType.DMA((2,)),
            pltpu.SemaphoreType.DMA((2, n_tensor - 1)),
            pltpu.SemaphoreType.DMA((2, n_tensor - 1)),
        ],
        compiler_params=pltpu.CompilerParams(
            vmem_limit_bytes=VMEM_LIMIT, collective_id=2, has_side_effects=True
        ),
        name="combine",
    )(
        rows,
        gates,
        slot_columns,
        routes_own,
        residual,
        hidden,
        cotangent,
        router_rows,
        gain,
        weight,
        value,
    )


def merge_kernel(own_rows, slots_ref, value_ref, out_ref):
    slots = value_ref.shape[0]
    for block in range(out_ref.shape[0] // own_rows):
        rows = slice(block * own_rows, (block + 1) * own_rows)
        one, two = chosen_slots(slots_ref[rows, :], slots)
        out_ref[rows, :] = nn(
            jnp.where(one | two, 1.0, 0.0).astype(BF16), value_ref[...]
        ).astype(BF16)


def merge(own_rows, slot_columns, value):
    return pl.pallas_call(
        functools.partial(merge_kernel, own_rows),
        out_shape=jax.ShapeDtypeStruct((slot_columns.shape[0], value.shape[1]), BF16),
        in_specs=[vspec()] * 2,
        out_specs=vspec(),
        compiler_params=pltpu.CompilerParams(vmem_limit_bytes=VMEM_LIMIT),
        name="merge",
    )(slot_columns, value)


def rms_scale(values):
    return lax.rsqrt(jnp.mean(values * values, axis=-1, keepdims=True) + EPS)


def norm_backward(grad_normed, values, scale_inv, gain):
    normed_unit = values * scale_inv
    grad_unit = grad_normed * gain
    grad_values = scale_inv * (
        grad_unit - normed_unit * jnp.mean(grad_unit * normed_unit, axis=-1, keepdims=True)
    )
    return (grad_values, jnp.sum(grad_normed * normed_unit, axis=0))


def gelu_tanh(values):
    return jax.nn.gelu(values, approximate=True)


def route_slots(route_ids, experts, capacity):
    flat_routes = route_ids.reshape(-1)
    onehot = (flat_routes[:, None] == jnp.arange(experts, dtype=jnp.int32)[None, :]).astype(
        jnp.int32
    )
    ranks = jnp.cumsum(onehot, axis=0) - 1
    rank_own = jnp.sum(ranks * onehot, axis=1)
    return (flat_routes * capacity + rank_own).reshape(-1, TOP)


def on_device(
    tokens,
    segments,
    routes,
    w_qkv,
    w_attn_out,
    bias_table,
    gain_attn,
    gain_moe,
    router,
    w_in,
    w_out,
    cotangent,
):
    own_rows, model_width = tokens.shape
    n_tensor = lax.axis_size("tensor")
    n_dp = lax.axis_size("dp")
    seq_len = own_rows * n_tensor
    own_start = lax.axis_index("tensor") * own_rows
    head_cols = w_qkv.shape[2]
    heads = head_cols // HD
    experts = router.shape[1]
    local_experts = w_in.shape[0]
    capacity = 5 * seq_len * TOP // (4 * experts)
    highest = lax.Precision.HIGHEST
    slots = experts * capacity

    depth = w_qkv.shape[0]
    bias_rows = bias_table.shape[0]
    extra = jnp.concatenate(
        [
            router,
            gain_attn[:, None],
            gain_moe[:, None],
            jnp.pad(bias_table, ((0, depth - bias_rows), (0, 0))),
        ],
        axis=1,
    )
    extra = jnp.pad(extra, ((0, 0), (0, 128 - extra.shape[1])))
    packed = lax.all_gather(
        jnp.concatenate([w_qkv.reshape(depth, 3 * head_cols), extra], axis=1),
        "dp",
        axis=0,
        tiled=True,
    )
    qkv_matrix = packed[:, : 3 * head_cols]
    extras = packed[:, 3 * head_cols :]
    router_full = extras[:, :experts]
    gain_one = extras[:, experts].astype(F32)
    gain_two = extras[:, experts + 1].astype(F32)
    table = (
        extras.reshape(n_dp, depth, 128)[:, :bias_rows, experts + 2 : experts + 2 + heads]
        .reshape(NB, heads)
        .astype(F32)
    )
    out_columns = lax.all_gather(w_attn_out, "tensor", axis=0, tiled=True)
    out_matrix = lax.all_gather(out_columns, "dp", axis=1, tiled=True)

    tokens_float = tokens.astype(F32)
    scale_one = rms_scale(tokens_float)
    hidden_one = (tokens_float * scale_one * gain_one).astype(BF16)
    gathered_one = lax.all_gather(hidden_one, "tensor", axis=0, tiled=True)
    projected = jnp.dot(gathered_one, qkv_matrix, preferred_element_type=F32).astype(BF16)
    selectors = jnp.asarray(distance_selectors())
    patterns = jnp.dot(selectors, table, precision=highest)
    patterns = jnp.transpose(patterns.reshape(2, 2 * BS, heads), (2, 0, 1)).reshape(
        2 * heads, 2 * BS
    )
    far = table[NB - 1]
    segment_row = segments
    segment_col = segments.reshape(seq_len, 1)
    starts = segments[0, ::BS]
    ends = segments[0, BS - 1 :: BS]
    lowest = jnp.sum((ends[None, :] < starts[:, None]).astype(jnp.int32), axis=1)
    attended, lse = attention_forward(
        projected, lowest, segment_col, segment_row, patterns, far, heads
    )
    attended_own = lax.all_to_all(
        attended.reshape(n_tensor, own_rows, head_cols), "tensor", 0, 0
    )
    attended_own = jnp.transpose(attended_own, (1, 0, 2)).reshape(own_rows, n_tensor * head_cols)
    branch = jnp.dot(attended_own, out_matrix, preferred_element_type=F32)
    residual = tokens_float + branch
    scale_two = rms_scale(residual)
    hidden_two = (residual * scale_two * gain_two).astype(BF16)
    gathered_two = lax.all_gather(hidden_two, "tensor", axis=0, tiled=True)

    expert_ids = jnp.arange(experts, dtype=jnp.int32)

    def gate_values(logit_values, route_rows):
        expert_probs = jax.nn.softmax(logit_values, axis=-1)
        picked = jnp.sum(
            jnp.where(
                route_rows[:, :, None] == expert_ids[None, None, :], expert_probs[:, None, :], 0.0
            ),
            axis=-1,
        )
        return picked / jnp.sum(picked, axis=1, keepdims=True)

    gates = gate_values(jnp.dot(gathered_two, router_full, preferred_element_type=F32), routes)
    slot_ids = route_slots(routes, experts, capacity)
    slot_flat = slot_ids.reshape(-1)
    token_ids = jnp.repeat(jnp.arange(seq_len, dtype=jnp.int32), TOP)
    sources = jnp.full((slots,), seq_len, jnp.int32).at[slot_flat].set(token_ids)
    slot_gates = jnp.zeros((slots,), F32).at[slot_flat].set(gates.reshape(-1))
    grad_gathered = lax.all_gather(cotangent, "tensor", axis=0, tiled=True)

    def exchange(rows):
        parts = rows.reshape(n_dp, local_experts, capacity, model_width)
        return [
            lax.all_to_all(parts[:, i], "dp", 0, 0).reshape(n_dp * capacity, model_width)
            for i in range(local_experts)
        ]

    def give_back(parts):
        back = [
            lax.all_to_all(part.reshape(n_dp, capacity, model_width), "dp", 0, 0) for part in parts
        ]
        return jnp.stack(back, axis=1).reshape(slots, model_width)

    zero_row = jnp.zeros((1, model_width), BF16)
    fast = n_dp % 2 == 0 and slots * model_width <= 4 * 1024 * 1024
    if fast:
        per = local_experts * capacity

        def move(value):
            return lax.all_to_all(value.reshape(n_dp, per, -1), "dp", 0, 0)

        rows = move(jnp.concatenate([gathered_two, zero_row], axis=0)[sources])
        grad_rows = move(jnp.concatenate([grad_gathered, zero_row], axis=0)[sources])
        row_gates = lax.all_to_all(
            jnp.broadcast_to(slot_gates.reshape(n_dp, 1, per), (n_dp, 8, per)), "dp", 0, 0
        )
        back, gate_back, value, grad_w_in, grad_w_out = run_experts(
            n_dp, capacity, rows, grad_rows, row_gates, w_in, w_out
        )
        own_routes = lax.dynamic_slice_in_dim(routes, own_start, own_rows, 0)
        weight_own = lax.dynamic_slice_in_dim(
            out_matrix, lax.axis_index("tensor") * head_cols, head_cols, 0
        )
        grad_residual, grad_branch_all, grad_attended, small, value_back = combine(
            n_dp,
            n_tensor,
            experts,
            back.reshape(slots, model_width),
            gate_back,
            slot_ids,
            jnp.pad(jnp.transpose(own_routes), ((0, 8 - TOP), (0, 0))),
            residual,
            hidden_two,
            cotangent,
            jnp.transpose(router_full),
            gain_two[None],
            weight_own,
            value,
        )
        grad_branch_all = grad_branch_all.reshape(seq_len, model_width)
        mixture = lax.psum_scatter(
            merge(own_rows, slot_ids, value_back.reshape(slots, model_width)),
            "tensor",
            scatter_dimension=0,
            tiled=True,
        ).astype(F32)
        layer_out = (residual + mixture).astype(BF16)
    else:
        dispatched = exchange(jnp.concatenate([gathered_two, zero_row], axis=0)[sources])
        padded_grad = jnp.concatenate([grad_gathered, zero_row], axis=0)
        grad_expert = exchange((slot_gates[:, None] * padded_grad[sources]).astype(BF16))

        outs, backs, grads_in, grads_out = [], [], [], []
        for i in range(local_experts):
            rows, grad_rows = dispatched[i], grad_expert[i]
            gate_part = nt(rows, w_in[i, 0])
            up_part = nt(rows, w_in[i, 1])
            gelu_value, gelu_pull = jax.vjp(gelu_tanh, gate_part)
            activated = (gelu_value * up_part).astype(BF16)
            outs.append(nn(activated, w_out[i]).astype(BF16))
            grad_act = nt(grad_rows, w_out[i])
            grads_out.append(tn(activated, grad_rows))
            grad_gate = gelu_pull(grad_act * up_part)[0].astype(BF16)
            grad_up = (grad_act * gelu_value).astype(BF16)
            backs.append((nn(grad_gate, w_in[i, 0]) + nn(grad_up, w_in[i, 1])).astype(BF16))
            grads_in.append(jnp.stack([tn(grad_gate, rows), tn(grad_up, rows)]))
        grad_w_in = jnp.stack(grads_in)
        grad_w_out = jnp.stack(grads_out)
        expert_out = give_back(outs)
        grad_dispatched = give_back(backs)

        first, second = slot_ids[:, 0], slot_ids[:, 1]
        picked_first = expert_out[first].astype(F32)
        picked_second = expert_out[second].astype(F32)
        mixture = lax.psum_scatter(
            (gates[:, 0:1] * picked_first + gates[:, 1:2] * picked_second).astype(BF16),
            "tensor",
            scatter_dimension=0,
            tiled=True,
        ).astype(F32)
        layer_out = (residual + mixture).astype(BF16)
        grad_float = grad_gathered.astype(F32)
        grad_gate_part = jnp.stack(
            [
                jnp.sum(grad_float * picked_first, axis=1),
                jnp.sum(grad_float * picked_second, axis=1),
            ],
            axis=1,
        )
        grad_hidden_part = (
            grad_dispatched[first].astype(F32) + grad_dispatched[second].astype(F32)
        ).astype(BF16)
        grad_own = lax.psum_scatter(
            grad_hidden_part, "tensor", scatter_dimension=0, tiled=True
        ).astype(F32)
        grad_gate_own = lax.dynamic_slice_in_dim(
            lax.psum(grad_gate_part, "tensor"), own_start, own_rows, 0
        )
        own_routes = lax.dynamic_slice_in_dim(routes, own_start, own_rows, 0)
        own_logits = jnp.dot(hidden_two, router_full, preferred_element_type=F32)

        def own_gates(logit_values):
            return gate_values(logit_values, own_routes)

        _, gate_pull = jax.vjp(own_gates, own_logits)
        grad_logits = gate_pull(grad_gate_own)[0]
        router_float = router_full.astype(F32)
        grad_hidden_two = grad_own + jnp.dot(grad_logits, router_float.T, precision=highest)
        grad_router_part = jnp.dot(hidden_two.astype(F32).T, grad_logits, precision=highest)
        grad_from_norm, grad_gain_two = norm_backward(grad_hidden_two, residual, scale_two, gain_two)
        grad_residual = cotangent.astype(F32) + grad_from_norm

        grad_branch = grad_residual.astype(BF16)
        grad_attended_own = nt(grad_branch, out_matrix).astype(BF16)
        grad_attended = lax.all_to_all(
            jnp.transpose(grad_attended_own.reshape(own_rows, n_tensor, head_cols), (1, 0, 2)),
            "tensor",
            0,
            0,
        ).reshape(seq_len, head_cols)
        grad_branch_all = lax.all_gather(grad_branch, "tensor", axis=0, tiled=True)
        small = jnp.concatenate(
            [
                jnp.transpose(grad_router_part),
                grad_gain_two[None],
                jnp.zeros((SMALL - experts - 1, model_width), F32),
            ],
            axis=0,
        )
    grad_projected, diag = attention_backward(
        projected,
        attended,
        grad_attended,
        lse,
        lowest,
        segment_col,
        segment_row,
        patterns,
        far,
        heads,
    )
    diag = diag.reshape(heads, 3, 2 * BS)
    near = jnp.transpose(diag[:, :2].reshape(heads, 4 * BS))
    grad_table = lax.dot_general(
        jnp.asarray(skew_selectors()), near, (((0,), (0,)), ((), ())), precision=highest
    )
    grad_table = grad_table.at[NB - 1].add(jnp.sum(diag[:, 2], axis=1))
    small = jnp.transpose(small.reshape(SMALL, n_dp, depth), (1, 0, 2))
    small = lax.dynamic_update_slice(
        small, grad_table.reshape(n_dp, NB // n_dp, heads), (0, experts + 2, 0)
    )
    grad_hidden_one, reduced_qkv, reduced_attn_out, small_sum = tail(
        n_dp,
        n_tensor,
        experts,
        gathered_one,
        grad_projected,
        qkv_matrix,
        attended,
        grad_branch_all,
        small,
        w_qkv.reshape(depth, 3 * head_cols),
        gain_attn[None].astype(F32),
    )
    grad_from_first, _ = norm_backward(grad_hidden_one, tokens_float, scale_one, gain_one)
    grad_tokens = (grad_residual + grad_from_first).astype(BF16)
    return (
        layer_out,
        grad_tokens,
        reduced_qkv.reshape(depth, 3, head_cols),
        reduced_attn_out,
        small_sum[experts + 2 : experts + 2 + NB // n_dp, :heads],
        small_sum[experts + 1],
        small_sum[experts],
        jnp.transpose(small_sum[:experts]),
        grad_w_in,
        grad_w_out,
    )


def solution(mesh):
    return jax.shard_map(
        on_device,
        mesh=mesh,
        in_specs=(
            P(("dp", "tensor"), None),
            P("dp", None),
            P("dp", None),
            P("dp", None, "tensor"),
            P("tensor", "dp"),
            P("dp", "tensor"),
            P("dp"),
            P("dp"),
            P("dp", None),
            P("dp", None, "tensor", None),
            P("dp", "tensor", None),
            P(("dp", "tensor"), None),
        ),
        out_specs=(
            P(("dp", "tensor"), None),
            P(("dp", "tensor"), None),
            P("dp", None, "tensor"),
            P("tensor", "dp"),
            P("dp", "tensor"),
            P("dp"),
            P("dp"),
            P("dp", None),
            P("dp", None, "tensor", None),
            P("dp", "tensor", None),
        ),
        check_vma=False,
    )
```

```python
import functools
import math

import jax
import jax.numpy as jnp
import numpy as np
from jax import lax
from jax.experimental import pallas as pl
from jax.experimental.pallas import tpu as pltpu
from jax.sharding import PartitionSpec as P

HD = 64
TOP = 2
NB = 32
NEAR = 128
BS = 256

EPS = 1e-06
NEG = -1e30
F32 = jnp.float32
BF16 = jnp.bfloat16
VMEM_LIMIT = 60 * 1024 * 1024


def distance_buckets():
    half_buckets = NB // 2
    thresholds = [bucket_level for bucket_level in range(1, half_buckets)]
    thresholds = thresholds + [
        int(
            math.ceil(
                half_buckets
                * (NEAR / half_buckets) ** ((bucket_level - half_buckets) / half_buckets)
            )
        )
        for bucket_level in range(half_buckets, NB)
    ]
    distance = np.arange(NEAR + 1)
    return (distance[:, None] >= np.array(thresholds)[None, :]).sum(axis=1)


def distance_selectors():
    buckets = distance_buckets()
    lanes = np.arange(2 * BS)
    signed = np.where(lanes < BS, lanes, lanes - 2 * BS)
    out = []
    for base in (0, BS):
        distance = np.clip(base - signed, 0, NEAR)
        out.append(buckets[distance][:, None] == np.arange(NB)[None, :])
    return np.concatenate(out, axis=0).astype(np.float32)


def skew_selectors():
    buckets = distance_buckets()
    lanes = np.arange(2 * BS)
    out = []
    for base in (0, BS):
        distance = np.clip(base + BS - 1 - lanes, 0, NEAR)
        out.append(buckets[distance][:, None] == np.arange(NB)[None, :])
    return np.concatenate(out, axis=0).astype(np.float32)


def nt(a, b):
    return lax.dot_general(a, b, (((1,), (1,)), ((), ())), preferred_element_type=F32)


def tn(a, b):
    return lax.dot_general(a, b, (((0,), (0,)), ((), ())), preferred_element_type=F32)


def nn(a, b):
    return lax.dot_general(a, b, (((1,), (0,)), ((), ())), preferred_element_type=F32)


def toeplitz(row):
    return pltpu.roll(jnp.broadcast_to(row, (BS, 2 * BS)), 0, 1, stride=1, stride_axis=0)[:, :BS]


def head_lanes(heads, width):
    lane = lax.broadcasted_iota(jnp.int32, (1, width), 1)
    return [(lane >= h * HD) & (lane < (h + 1) * HD) for h in range(heads)]


def own_head(value, lanes, heads):
    return value if heads == 1 else jnp.where(lanes, value, jnp.zeros((), value.dtype))


def build_bias(heads, pattern_ref, bias):
    for h in range(heads):
        for t in range(2):
            bias[h, t] = toeplitz(pattern_ref[2 * h + t : 2 * h + t + 1, :])


def block_mask(qb, kb, seg_col_ref, seg_row_ref):
    q_seg = seg_col_ref[pl.ds(pl.multiple_of(qb * BS, BS), BS), :]
    k_seg = seg_row_ref[:, pl.ds(pl.multiple_of(kb * BS, BS), BS)]
    row = lax.broadcasted_iota(jnp.int32, (BS, BS), 0) + (qb - kb) * BS
    col = lax.broadcasted_iota(jnp.int32, (BS, BS), 1)
    return (q_seg == k_seg) & (row >= col)


def attn_fwd_kernel(heads, blocks, lo_ref, qkv_ref, seg_col_ref, seg_row_ref, pattern_ref, far_ref, out_ref, lse_ref, bias):
    width = heads * HD
    lanes = head_lanes(heads, width)
    scale = HD**-0.5
    build_bias(heads, pattern_ref, bias)

    def q_step(qb, _):
        q_rows = pl.ds(pl.multiple_of(qb * BS, BS), BS)
        q_all = (qkv_ref[q_rows, 0:width] * scale).astype(BF16)
        q_heads = [own_head(q_all, lanes[h], heads) for h in range(heads)]

        def k_step(kb, carry):
            k_rows = pl.ds(pl.multiple_of(kb * BS, BS), BS)
            k = qkv_ref[k_rows, width : 2 * width]
            v = qkv_ref[k_rows, 2 * width : 3 * width]
            allowed = block_mask(qb, kb, seg_col_ref, seg_row_ref)
            near = jnp.minimum(qb - kb, 1)
            is_far = qb - kb >= 2
            new = []
            for h in range(heads):
                top, total, acc = carry[3 * h : 3 * h + 3]
                b = jnp.where(is_far, far_ref[h], bias[h, near])
                s = jnp.where(allowed, nt(q_heads[h], k) + b, NEG)
                top_new = jnp.maximum(top, jnp.max(s, axis=1, keepdims=True))
                alpha = jnp.exp(top - top_new)
                p = jnp.exp(s - top_new)
                total = alpha * total + jnp.sum(p, axis=1, keepdims=True)
                acc = alpha * acc + nn(p.astype(BF16), v)
                new += [top_new, total, acc]
            return tuple(new)

        init = []
        for h in range(heads):
            init += [jnp.full((BS, 1), NEG, F32), jnp.zeros((BS, 1), F32), jnp.zeros((BS, width), F32)]
        res = lax.fori_loop(lo_ref[qb], qb + 1, k_step, tuple(init))
        out = jnp.zeros((BS, width), F32)
        for h in range(heads):
            top, total, acc = res[3 * h : 3 * h + 3]
            value = acc / total
            out = value if heads == 1 else jnp.where(lanes[h], value, out)
            lse_ref[q_rows, h : h + 1] = top + jnp.log(total)
        out_ref[q_rows, :] = out.astype(BF16)
        return 0

    lax.fori_loop(0, blocks, q_step, 0)


def attn_bwd_kernel(
    heads,
    blocks,
    lo_ref,
    qkv_ref,
    out_ref,
    grad_ref,
    lse_ref,
    seg_col_ref,
    seg_row_ref,
    pattern_ref,
    far_ref,
    grad_qkv_ref,
    diag_ref,
    bias,
    dk,
    dv,
    sums,
):
    width = heads * HD
    lanes = head_lanes(heads, width)
    scale = HD**-0.5
    build_bias(heads, pattern_ref, bias)
    dk[...] = jnp.zeros_like(dk)
    dv[...] = jnp.zeros_like(dv)
    sums[...] = jnp.zeros_like(sums)

    def q_step(qb, _):
        q_rows = pl.ds(pl.multiple_of(qb * BS, BS), BS)
        q_all = (qkv_ref[q_rows, 0:width] * scale).astype(BF16)
        g_all = grad_ref[q_rows, :]
        both = g_all.astype(F32) * out_ref[q_rows, :].astype(F32)
        q_heads = [own_head(q_all, lanes[h], heads) for h in range(heads)]
        g_heads = [own_head(g_all, lanes[h], heads) for h in range(heads)]
        deltas = [jnp.sum(own_head(both, lanes[h], heads), axis=1, keepdims=True) for h in range(heads)]
        totals = [lse_ref[q_rows, h : h + 1] for h in range(heads)]

        def k_step(kb, dq):
            k_rows = pl.ds(pl.multiple_of(kb * BS, BS), BS)
            k = qkv_ref[k_rows, width : 2 * width]
            v = qkv_ref[k_rows, 2 * width : 3 * width]
            allowed = block_mask(qb, kb, seg_col_ref, seg_row_ref)
            near = jnp.minimum(qb - kb, 1)
            place = jnp.minimum(qb - kb, 2)
            is_far = qb - kb >= 2
            dk_add = jnp.zeros((BS, width), F32)
            dv_add = jnp.zeros((BS, width), F32)
            for h in range(heads):
                b = jnp.where(is_far, far_ref[h], bias[h, near])
                s = jnp.where(allowed, nt(q_heads[h], k) + b, NEG)
                p = jnp.exp(s - totals[h])
                gp = nt(g_heads[h], v)
                ds = (p * (gp - deltas[h])).astype(BF16)
                dv_add += tn(p.astype(BF16), g_heads[h])
                dk_add += tn(ds, q_heads[h])
                dq = dq + own_head(nn(ds, k), lanes[h], heads)
                sums[h, place] += ds.astype(F32)
            dk[k_rows, :] += dk_add
            dv[k_rows, :] += dv_add
            return dq

        dq = lax.fori_loop(lo_ref[qb], qb + 1, k_step, jnp.zeros((BS, width), F32))
        grad_qkv_ref[q_rows, 0:width] = (dq * scale).astype(BF16)
        return 0

    lax.fori_loop(0, blocks, q_step, 0)
    grad_qkv_ref[:, width : 2 * width] = dk[...].astype(BF16)
    grad_qkv_ref[:, 2 * width : 3 * width] = dv[...].astype(BF16)
    row = lax.broadcasted_iota(jnp.int32, (BS, BS), 0)
    col = lax.broadcasted_iota(jnp.int32, (BS, BS), 1)
    upside_down = jnp.where(row + col == BS - 1, 1.0, 0.0).astype(F32)
    for h in range(heads):
        for t in range(2):
            flipped = jnp.dot(upside_down, sums[h, t], precision=lax.Precision.HIGHEST, preferred_element_type=F32)
            wide = jnp.concatenate([flipped, jnp.zeros((BS, BS), F32)], axis=1)
            skewed = pltpu.roll(wide, 0, 1, stride=1, stride_axis=0)
            diag_ref[3 * h + t : 3 * h + t + 1, :] = jnp.sum(skewed, axis=0, keepdims=True)
        rest = jnp.sum(sums[h, 2], axis=0, keepdims=True)
        diag_ref[3 * h + 2 : 3 * h + 3, :] = jnp.concatenate([rest, jnp.zeros((1, BS), F32)], axis=1)


def vspec():
    return pl.BlockSpec(memory_space=pltpu.VMEM)


def sspec():
    return pl.BlockSpec(memory_space=pltpu.SMEM)


def attention_forward(projected, lo, seg_col, seg_row, patterns, far, heads):
    seq_len = projected.shape[0]
    blocks = seq_len // BS
    return pl.pallas_call(
        functools.partial(attn_fwd_kernel, heads, blocks),
        out_shape=(
            jax.ShapeDtypeStruct((seq_len, heads * HD), BF16),
            jax.ShapeDtypeStruct((seq_len, heads), F32),
        ),
        in_specs=[sspec(), vspec(), vspec(), vspec(), vspec(), sspec()],
        out_specs=(vspec(), vspec()),
        scratch_shapes=[pltpu.VMEM((heads, 2, BS, BS), F32)],
        compiler_params=pltpu.CompilerParams(vmem_limit_bytes=VMEM_LIMIT),
        name="attn_fwd",
    )(lo, projected, seg_col, seg_row, patterns, far)


def attention_backward(projected, attended, grad, lse, lo, seg_col, seg_row, patterns, far, heads):
    seq_len = projected.shape[0]
    blocks = seq_len // BS
    width = heads * HD
    return pl.pallas_call(
        functools.partial(attn_bwd_kernel, heads, blocks),
        out_shape=(
            jax.ShapeDtypeStruct((seq_len, 3 * width), BF16),
            jax.ShapeDtypeStruct((3 * heads, 2 * BS), F32),
        ),
        in_specs=[sspec(), vspec(), vspec(), vspec(), vspec(), vspec(), vspec(), vspec(), sspec()],
        out_specs=(vspec(), vspec()),
        scratch_shapes=[
            pltpu.VMEM((heads, 2, BS, BS), F32),
            pltpu.VMEM((seq_len, width), F32),
            pltpu.VMEM((seq_len, width), F32),
            pltpu.VMEM((heads, 3, BS, BS), F32),
        ],
        compiler_params=pltpu.CompilerParams(vmem_limit_bytes=VMEM_LIMIT),
        name="attn_bwd",
    )(lo, projected, attended, grad, lse, seg_col, seg_row, patterns, far)


MESH = pl.DeviceIdType.MESH
SMALL = 32


def remote(src, dst, send, recv, axis, peer):
    return pltpu.make_async_remote_copy(
        src_ref=src,
        dst_ref=dst,
        send_sem=send,
        recv_sem=recv,
        device_id={axis: peer},
        device_id_type=MESH,
    )


def greet(groups):
    barrier = pltpu.get_barrier_semaphore()
    total = 0
    for axis, n in groups:
        me = lax.axis_index(axis)
        for step in range(1, n):
            pl.semaphore_signal(
                barrier, inc=1, device_id={axis: lax.rem(me + step, n)}, device_id_type=MESH
            )
        total += n - 1
    pl.semaphore_wait(barrier, total)


class LineSum:
    def __init__(self, n, partial, send, recv, send_sem, recv_sem, acc, total):
        self.n, self.partial = n, partial
        self.send, self.recv, self.send_sem, self.recv_sem = send, recv, send_sem, recv_sem
        self.acc, self.total = acc, total
        self.me = lax.axis_index("tensor")

    def flow(self, first, k):
        n, me = self.n, self.me
        near = me * 2 < n
        right = near if first else jnp.logical_not(near)
        block = jnp.where(right, n - 1 - k, k)
        comes = jnp.where(right, jnp.where(me > 0, me <= block, False), jnp.where(me < n - 1, me >= block, False))
        goes = jnp.where(right, me < block, me > block)
        peer = jnp.clip(jnp.where(right, me + 1, me - 1), 0, n - 1)
        out_slot = jnp.clip(jnp.where(right, k, n - 1 - me + k), 0, n - 2)
        in_slot = jnp.clip(jnp.where(right, k, n - me + k), 0, n)
        peer_slot = jnp.clip(jnp.where(right, k, n - peer + k), 0, n)
        return block, comes, goes, peer, out_slot, in_slot, peer_slot

    def copy(self, peer, out_slot, slot):
        return remote(
            self.send.at[out_slot],
            self.recv.at[slot],
            self.send_sem.at[out_slot],
            self.recv_sem.at[slot],
            "tensor",
            peer,
        )

    def start(self):
        for k in range(self.n - 1):
            for first in (True, False):
                block, comes, goes, peer, out_slot, in_slot, peer_slot = self.flow(first, k)

                @pl.when(goes & jnp.logical_not(comes))
                def _():
                    self.send[out_slot] = self.partial(block).astype(BF16)
                    self.copy(peer, out_slot, peer_slot).start()

        self.total[...] = self.partial(self.me)

    def finish(self):
        for k in range(self.n - 1):
            for first in (True, False):
                block, comes, goes, peer, out_slot, in_slot, peer_slot = self.flow(first, k)

                @pl.when(goes & comes)
                def _():
                    self.acc[...] = self.partial(block)
                    self.copy(peer, out_slot, in_slot).wait_recv()
                    self.send[out_slot] = (
                        self.acc[...] + self.recv[in_slot].astype(F32)
                    ).astype(BF16)
                    self.copy(peer, out_slot, peer_slot).start()

                @pl.when(comes & jnp.logical_not(goes))
                def _():
                    self.copy(peer, 0, in_slot).wait_recv()
                    self.total[...] += self.recv[in_slot].astype(F32)

    def drain(self):
        for k in range(self.n - 1):
            for first in (True, False):
                block, comes, goes, peer, out_slot, in_slot, peer_slot = self.flow(first, k)

                @pl.when(goes)
                def _():
                    self.copy(peer, out_slot, in_slot).wait_send()


def tail_kernel(
    n_dp,
    n_tensor,
    experts,
    table_rows,
    hidden_ref,
    grad_ref,
    weight_ref,
    attended_ref,
    branch_ref,
    small_ref,
    weight_own_ref,
    gain_own_ref,
    grad_hidden_ref,
    grad_qkv_ref,
    grad_out_ref,
    small_out_ref,
    acc,
    line_send,
    line_recv,
    qkv_send,
    qkv_recv,
    out_send,
    out_recv,
    small_recv,
    small_sum,
    gain_recv,
    line_send_sem,
    line_recv_sem,
    qkv_send_sem,
    qkv_recv_sem,
    out_send_sem,
    out_recv_sem,
    small_send_sem,
    small_recv_sem,
    gain_send_sem,
    gain_recv_sem,
):
    own_rows = grad_hidden_ref.shape[0]
    depth = weight_own_ref.shape[0]
    out_cols = grad_out_ref.shape[1]
    me = lax.axis_index("dp")
    me_t = lax.axis_index("tensor")
    greet([("dp", n_dp), ("tensor", n_tensor)])

    def partial(block):
        rows = pl.ds(pl.multiple_of(block * own_rows, own_rows), own_rows)
        return nt(grad_ref[rows, :], weight_ref[...])

    line = LineSum(
        n_tensor, partial, line_send, line_recv, line_send_sem, line_recv_sem, acc, grad_hidden_ref
    )
    line.start()
    copies = []
    for step in range(1, n_dp):
        peer = lax.rem(me + step, n_dp)
        copy = remote(
            small_ref.at[peer],
            small_recv.at[step - 1],
            small_send_sem.at[step - 1],
            small_recv_sem.at[step - 1],
            "dp",
            peer,
        )
        copy.start()
        copies.append(copy)
    for block in range(n_dp):
        cols = slice(block * depth, (block + 1) * depth)
        qkv_send[block] = tn(hidden_ref[:, cols], grad_ref[...]).astype(BF16)
    for step in range(1, n_dp):
        peer = lax.rem(me + step, n_dp)
        copy = remote(
            qkv_send.at[peer],
            qkv_recv.at[step - 1],
            qkv_send_sem.at[step - 1],
            qkv_recv_sem.at[step - 1],
            "dp",
            peer,
        )
        copy.start()
        copies.append(copy)
    for block in range(n_dp):
        cols = slice(block * out_cols, (block + 1) * out_cols)
        out_send[block] = tn(attended_ref[...], branch_ref[:, cols]).astype(BF16)
    for step in range(1, n_dp):
        peer = lax.rem(me + step, n_dp)
        copy = remote(
            out_send.at[peer],
            out_recv.at[step - 1],
            out_send_sem.at[step - 1],
            out_recv_sem.at[step - 1],
            "dp",
            peer,
        )
        copy.start()
        copies.append(copy)
    line.finish()
    for copy in copies:
        copy.wait()
    small_sum[...] = small_ref[me]
    grad_qkv_ref[...] = qkv_send[me].astype(F32)
    grad_out_ref[...] = out_send[me].astype(F32)
    for step in range(1, n_dp):
        small_sum[...] += small_recv[step - 1]
        grad_qkv_ref[...] += qkv_recv[step - 1].astype(F32)
        grad_out_ref[...] += out_recv[step - 1].astype(F32)
    column = jnp.sum(grad_qkv_ref[...] * weight_own_ref[...].astype(F32), axis=1, keepdims=True)
    eye = lax.broadcasted_iota(jnp.int32, (depth, depth), 0) == lax.broadcasted_iota(
        jnp.int32, (depth, depth), 1
    )
    row = jnp.sum(jnp.where(eye, column, 0.0), axis=0, keepdims=True)
    small_sum[experts + 1 : experts + 2, :] = row / gain_own_ref[...]
    gains = []
    for step in range(1, n_tensor):
        peer = lax.rem(me_t + step, n_tensor)
        copy = remote(
            small_sum,
            gain_recv.at[step - 1],
            gain_send_sem.at[step - 1],
            gain_recv_sem.at[step - 1],
            "tensor",
            peer,
        )
        copy.start()
        gains.append(copy)
    line.drain()
    for copy in gains:
        copy.wait()
    small_out_ref[...] = small_sum[...]
    shared = slice(0, experts + 2)
    for step in range(1, n_tensor):
        small_out_ref[shared, :] += gain_recv[step - 1, shared, :]


def tail(n_dp, n_tensor, experts, hidden, grad, weight, attended, branch, small, weight_own, gain_own):
    seq_len, width = hidden.shape
    own_rows = seq_len // n_tensor
    depth, cols = weight_own.shape
    heads_cols = attended.shape[1]
    out_cols = width // n_dp
    table_rows = NB // n_dp
    return pl.pallas_call(
        functools.partial(tail_kernel, n_dp, n_tensor, experts, table_rows),
        out_shape=(
            jax.ShapeDtypeStruct((own_rows, width), F32),
            jax.ShapeDtypeStruct((depth, cols), F32),
            jax.ShapeDtypeStruct((heads_cols, out_cols), F32),
            jax.ShapeDtypeStruct((SMALL, depth), F32),
        ),
        in_specs=[vspec()] * 8,
        out_specs=(vspec(),) * 4,
        scratch_shapes=[
            pltpu.VMEM((own_rows, width), F32),
            pltpu.VMEM((n_tensor - 1, own_rows, width), BF16),
            pltpu.VMEM((n_tensor + 1, own_rows, width), BF16),
            pltpu.VMEM((n_dp, depth, cols), BF16),
            pltpu.VMEM((n_dp - 1, depth, cols), BF16),
            pltpu.VMEM((n_dp, heads_cols, out_cols), BF16),
            pltpu.VMEM((n_dp - 1, heads_cols, out_cols), BF16),
            pltpu.VMEM((n_dp - 1, SMALL, depth), F32),
            pltpu.VMEM((SMALL, depth), F32),
            pltpu.VMEM((n_tensor - 1, SMALL, depth), F32),
            pltpu.SemaphoreType.DMA((n_tensor - 1,)),
            pltpu.SemaphoreType.DMA((n_tensor + 1,)),
        ]
        + [pltpu.SemaphoreType.DMA((n_dp - 1,))] * 6
        + [pltpu.SemaphoreType.DMA((n_tensor - 1,))] * 2,
        compiler_params=pltpu.CompilerParams(
            vmem_limit_bytes=VMEM_LIMIT, collective_id=0, has_side_effects=True
        ),
        name="tail",
    )(hidden, grad, weight, attended, branch, small, weight_own, gain_own)


def line_gather(n, buf, send_sem, recv_sem, on_block):
    me = lax.axis_index("tensor")

    def copy(block, slot, k, peer):
        return remote(
            buf.at[block], buf.at[block], send_sem.at[slot, k], recv_sem.at[slot, k], "tensor", peer
        )

    def arrived(k, fn):
        if k == 0:
            fn(me, 0, 0)
            return
        for slot, sign in enumerate((1, -1)):
            block = me - sign * k

            @pl.when((block >= 0) & (block < n))
            def _():
                fn(block, slot, sign)

    def outgoing(k, fn):
        for slot, sign in enumerate((1, -1)):
            block, peer = me - sign * k, me + sign

            @pl.when((block >= 0) & (block < n) & (peer >= 0) & (peer < n))
            def _():
                fn(copy(block, slot, k, peer))

    for k in range(n):
        if k < n - 1:
            outgoing(k, lambda c: c.start())
        arrived(k, lambda block, slot, sign: on_block(block))
        if k < n - 1:
            arrived(
                k + 1,
                lambda block, slot, sign: copy(
                    block, slot, k, jnp.clip(me - sign, 0, n - 1)
                ).wait_recv(),
            )
    for k in range(n - 1):
        outgoing(k, lambda c: c.wait_send())


def diagonal(size):
    return lax.broadcasted_iota(jnp.int32, (size, size), 0) == lax.broadcasted_iota(
        jnp.int32, (size, size), 1
    )


def to_column(row):
    return jnp.sum(jnp.where(diagonal(row.shape[1]), row, 0.0), axis=1, keepdims=True)


def to_row(column):
    return jnp.sum(jnp.where(diagonal(column.shape[0]), column, 0.0), axis=0, keepdims=True)


def expert_kernel(
    n_dp,
    local,
    capacity,
    rows_ref,
    grad_ref,
    gates_ref,
    in_ref,
    out_ref,
    back_ref,
    gate_back_ref,
    value_ref,
    grad_in_ref,
    grad_out_ref,
    back_send,
    gate_send,
    zs,
    ups,
    gates_s,
    stage,
    value_stage,
    back_send_sem,
    back_recv_sem,
    gate_send_sem,
    gate_recv_sem,
    own_sem,
    stage_sem,
    value_sem,
):
    me = lax.axis_index("dp")
    pairs = n_dp // 2
    hidden = in_ref.shape[2]
    width = rows_ref.shape[2]
    two = 2 * capacity
    greet([("dp", n_dp)])

    def back_copy(expert, target, sender):
        part = slice(expert * capacity, (expert + 1) * capacity)
        return remote(
            back_send.at[target, part],
            back_ref.at[sender, part],
            back_send_sem.at[expert, target],
            back_recv_sem.at[expert, sender],
            "dp",
            target,
        )

    def own_copy(expert):
        part = slice(expert * capacity, (expert + 1) * capacity)
        return pltpu.make_async_copy(
            back_send.at[me, part], back_ref.at[me, part], own_sem.at[expert]
        )

    def stage_copy(slot, target):
        return pltpu.make_async_copy(stage.at[slot], target, stage_sem.at[slot])

    gate_send[...] = jnp.zeros_like(gate_send)
    staged = []

    def put(value, target):
        slot = len(staged) % 2
        if len(staged) >= 2:
            staged[-2].wait()
        stage[slot] = value
        copy = stage_copy(slot, target)
        copy.start()
        staged.append(copy)

    for expert in range(local):
        part = slice(expert * capacity, (expert + 1) * capacity)

        def group(index, _):
            pair = (me // 2) ^ (pairs - 1 - index)
            first = 2 * pair
            rows = rows_ref[pl.ds(first, 2), part, :].reshape(two, width)
            grads = grad_ref[pl.ds(first, 2), part, :].reshape(two, width)
            column = jnp.concatenate(
                [to_column(gates_ref[first + j, 0:1, part]) for j in range(2)], axis=0
            )
            gate = nt(rows, in_ref[expert, 0])
            up = nt(rows, in_ref[expert, 1])
            square = gate * gate
            bent = jnp.tanh(0.7978845608028654 * gate * (1.0 + 0.044715 * square))
            half = 0.5 * (1.0 + bent)
            gelu = gate * half
            slope = half + 0.5 * gate * (1.0 - bent * bent) * (
                0.7978845608028654 * (1.0 + 3 * 0.044715 * square)
            )
            z = gelu * up
            grad_z = nt(grads, out_ref[expert])
            gate_grad = jnp.sum(z * grad_z, axis=1, keepdims=True)
            grad_z = column * grad_z
            zs[pl.ds(first, 2)] = (column * z).astype(BF16).reshape(2, capacity, hidden)
            ups[0, pl.ds(first, 2)] = (grad_z * up * slope).astype(BF16).reshape(2, capacity, hidden)
            ups[1, pl.ds(first, 2)] = (grad_z * gelu).astype(BF16).reshape(2, capacity, hidden)
            for j in range(2):
                gate_send[first + j, 0:1, part] = to_row(
                    gate_grad[j * capacity : (j + 1) * capacity]
                )
            back = nn(ups[0, pl.ds(first, 2)].reshape(two, hidden), in_ref[expert, 0])
            back += nn(ups[1, pl.ds(first, 2)].reshape(two, hidden), in_ref[expert, 1])
            back_send[pl.ds(first, 2), part, :] = back.astype(BF16).reshape(2, capacity, width)
            for j in range(2):
                target = first + j

                @pl.when(target != me)
                def _():
                    back_copy(expert, target, me).start()

                @pl.when(target == me)
                def _():
                    own_copy(expert).start()

            return 0

        lax.fori_loop(0, pairs, group, 0)
        if expert == local - 1:
            gate_copies = []
            for step in range(1, n_dp):
                target = lax.rem(me + step, n_dp)
                copy = remote(
                    gate_send.at[target],
                    gate_back_ref.at[me],
                    gate_send_sem.at[step - 1],
                    gate_recv_sem.at[step - 1],
                    "dp",
                    target,
                )
                copy.start()
                gate_copies.append(copy)
            gate_back_ref[me] = gate_send[me]
        rows = rows_ref[:, part, :].reshape(n_dp * capacity, width)
        for half in range(2):
            put(tn(ups[half].reshape(n_dp * capacity, hidden), rows), grad_in_ref.at[expert, half])
        grads = grad_ref[:, part, :].reshape(n_dp * capacity, width)
        put(tn(zs[...].reshape(n_dp * capacity, hidden), grads), grad_out_ref.at[expert])
        if expert > 0:
            pltpu.make_async_copy(
                value_stage, value_ref.at[:, slice((expert - 1) * capacity, expert * capacity)], value_sem
            ).wait()

        def value(pair, _):
            out = nn(zs[pl.ds(2 * pair, 2)].reshape(two, hidden), out_ref[expert])
            value_stage[pl.ds(2 * pair, 2)] = out.astype(BF16).reshape(2, capacity, width)
            return 0

        lax.fori_loop(0, pairs, value, 0)
        pltpu.make_async_copy(value_stage, value_ref.at[:, part], value_sem).start()

    last = slice((local - 1) * capacity, local * capacity)
    pltpu.make_async_copy(value_stage, value_ref.at[:, last], value_sem).wait()
    for copy in staged[-2:]:
        copy.wait()
    for copy in gate_copies:
        copy.wait()
    for expert in range(local):
        own_copy(expert).wait()
        for step in range(1, n_dp):
            peer = lax.rem(me + step, n_dp)
            back_copy(expert, peer, me).wait_send()
            back_copy(expert, me, peer).wait_recv()


def any_spec():
    return pl.BlockSpec(memory_space=pl.ANY)


def run_experts(n_dp, capacity, rows, grads, gates, w_in, w_out):
    local, _, hidden, width = w_in.shape
    slots = local * capacity
    return pl.pallas_call(
        functools.partial(expert_kernel, n_dp, local, capacity),
        out_shape=(
            jax.ShapeDtypeStruct((n_dp, slots, width), BF16),
            jax.ShapeDtypeStruct((n_dp, 8, slots), F32),
            jax.ShapeDtypeStruct((n_dp, slots, width), BF16),
            jax.ShapeDtypeStruct(w_in.shape, F32),
            jax.ShapeDtypeStruct(w_out.shape, F32),
        ),
        in_specs=[vspec()] * 5,
        out_specs=(any_spec(), vspec(), any_spec(), any_spec(), any_spec()),
        scratch_shapes=[
            pltpu.VMEM((n_dp, slots, width), BF16),
            pltpu.VMEM((n_dp, 8, slots), F32),
            pltpu.VMEM((n_dp, capacity, hidden), BF16),
            pltpu.VMEM((2, n_dp, capacity, hidden), BF16),
            pltpu.VMEM((8, 128), F32),
            pltpu.VMEM((2, hidden, width), F32),
            pltpu.VMEM((n_dp, capacity, width), BF16),
            pltpu.SemaphoreType.DMA((local, n_dp)),
            pltpu.SemaphoreType.DMA((local, n_dp)),
            pltpu.SemaphoreType.DMA((n_dp - 1,)),
            pltpu.SemaphoreType.DMA((n_dp - 1,)),
            pltpu.SemaphoreType.DMA((local,)),
            pltpu.SemaphoreType.DMA((2,)),
            pltpu.SemaphoreType.DMA,
        ],
        compiler_params=pltpu.CompilerParams(
            vmem_limit_bytes=VMEM_LIMIT, collective_id=1, has_side_effects=True
        ),
        name="experts",
    )(rows, grads, gates, w_in, w_out)


def chosen_slots(columns, slots):
    lane = lax.broadcasted_iota(jnp.int32, (1, slots), 1)
    return columns[:, 0:1] == lane, columns[:, 1:2] == lane


def combine_kernel(
    n_dp,
    n_tensor,
    experts,
    rows_ref,
    gate_ref,
    slots_ref,
    routes_ref,
    residual_ref,
    hidden_ref,
    cotangent_ref,
    router_ref,
    gain_ref,
    weight_ref,
    value_ref,
    grad_residual_ref,
    branch_ref,
    grad_attended_ref,
    small_ref,
    value_back_ref,
    acc,
    total,
    line_send,
    line_recv,
    gate_all,
    gate_send,
    gate_recv,
    value_own,
    line_send_sem,
    line_recv_sem,
    gate_send_sem,
    gate_recv_sem,
    value_send_sem,
    value_recv_sem,
    value_own_sem,
    gather_send_sem,
    gather_recv_sem,
):
    own_rows, width = residual_ref.shape
    slots = rows_ref.shape[0]
    per = slots // n_dp
    me = lax.axis_index("dp")
    me_t = lax.axis_index("tensor")
    greet([("dp", n_dp), ("tensor", n_tensor)])
    values = []
    for step in range(1, n_dp):
        peer = lax.rem(me + step, n_dp)
        copy = remote(
            value_ref.at[peer],
            value_back_ref.at[me],
            value_send_sem.at[step - 1],
            value_recv_sem.at[step - 1],
            "dp",
            peer,
        )
        copy.start()
        values.append(copy)
    fetch = pltpu.make_async_copy(value_ref.at[me], value_own, value_own_sem.at[0])
    fetch.start()

    def partial(block):
        one, two = chosen_slots(
            slots_ref[pl.ds(pl.multiple_of(block * own_rows, own_rows), own_rows), :], slots
        )
        return nn(jnp.where(one | two, 1.0, 0.0).astype(BF16), rows_ref[...])

    line = LineSum(
        n_tensor, partial, line_send, line_recv, line_send_sem, line_recv_sem, acc, total
    )
    line.start()
    for peer in range(n_dp):
        gate_all[0:1, peer * per : (peer + 1) * per] = gate_ref[peer, 0:1, :]
    gate_send[...] = jnp.zeros_like(gate_send)
    gates = []
    for step in range(n_tensor):
        peer = lax.rem(me_t + step, n_tensor)
        picks = chosen_slots(
            slots_ref[pl.ds(pl.multiple_of(peer * own_rows, own_rows), own_rows), :], slots
        )
        for k in range(TOP):
            column = jnp.sum(
                jnp.where(picks[k], gate_all[0:1, :], 0.0), axis=1, keepdims=True
            )
            gate_send[step, k : k + 1, :] = to_row(column)
        if step:
            copy = remote(
                gate_send.at[step],
                gate_recv.at[step - 1],
                gate_send_sem.at[step - 1],
                gate_recv_sem.at[step - 1],
                "tensor",
                peer,
            )
            copy.start()
            gates.append(copy)
    fetch.wait()
    put = pltpu.make_async_copy(value_own, value_back_ref.at[me], value_own_sem.at[1])
    put.start()

    hidden = hidden_ref[...]
    router = router_ref[...]
    logits = nt(router, hidden)
    exps = jnp.exp(logits - jnp.max(logits, axis=0, keepdims=True))
    probs = exps / jnp.sum(exps, axis=0, keepdims=True)
    ids = lax.broadcasted_iota(jnp.int32, (experts, own_rows), 0)
    first, second = ids == routes_ref[0:1, :], ids == routes_ref[1:2, :]
    prob_one = jnp.sum(jnp.where(first, probs, 0.0), axis=0, keepdims=True)
    prob_two = jnp.sum(jnp.where(second, probs, 0.0), axis=0, keepdims=True)
    both = prob_one + prob_two
    line.finish()
    for copy in gates:
        copy.wait()
    gate_sum = gate_send[0]
    for step in range(1, n_tensor):
        gate_sum = gate_sum + gate_recv[step - 1]
    grad_one, grad_two = gate_sum[0:1, :], gate_sum[1:2, :]
    mean_grad = (prob_one * grad_one + prob_two * grad_two) / both
    grad_probs = (
        jnp.where(first, grad_one - mean_grad, 0.0) + jnp.where(second, grad_two - mean_grad, 0.0)
    ) / both
    grad_logits = probs * (grad_probs - jnp.sum(grad_probs * probs, axis=0, keepdims=True))
    grad_hidden = total[...] + lax.dot_general(
        grad_logits,
        router.astype(F32),
        (((0,), (0,)), ((), ())),
        precision=lax.Precision.HIGHEST,
        preferred_element_type=F32,
    )
    residual = residual_ref[...]
    scale = lax.rsqrt(jnp.mean(residual * residual, axis=1, keepdims=True) + EPS)
    unit = residual * scale
    small_ref[...] = jnp.zeros_like(small_ref)
    small_ref[experts : experts + 1, :] = jnp.sum(grad_hidden * unit, axis=0, keepdims=True)
    grad_unit = grad_hidden * gain_ref[...]
    grad_residual = cotangent_ref[...].astype(F32) + scale * (
        grad_unit - unit * jnp.mean(grad_unit * unit, axis=1, keepdims=True)
    )
    grad_residual_ref[...] = grad_residual
    branch_ref[me_t] = grad_residual.astype(BF16)

    def on_block(block):
        grad_attended_ref[pl.ds(pl.multiple_of(block * own_rows, own_rows), own_rows), :] = nt(
            branch_ref[block], weight_ref[...]
        ).astype(BF16)

    line_gather(n_tensor, branch_ref, gather_send_sem, gather_recv_sem, on_block)
    small_ref[0:experts, :] = jnp.dot(
        grad_logits,
        hidden.astype(F32),
        precision=lax.Precision.HIGHEST,
        preferred_element_type=F32,
    )
    line.drain()
    put.wait()
    for copy in values:
        copy.wait()


def combine(
    n_dp,
    n_tensor,
    experts,
    rows,
    gates,
    slot_columns,
    routes_own,
    residual,
    hidden,
    cotangent,
    router_rows,
    gain,
    weight,
    value,
):
    own_rows, width = residual.shape
    slots = rows.shape[0]
    return pl.pallas_call(
        functools.partial(combine_kernel, n_dp, n_tensor, experts),
        out_shape=(
            jax.ShapeDtypeStruct((own_rows, width), F32),
            jax.ShapeDtypeStruct((n_tensor, own_rows, width), BF16),
            jax.ShapeDtypeStruct((n_tensor * own_rows, weight.shape[0]), BF16),
            jax.ShapeDtypeStruct((SMALL, width), F32),
            jax.ShapeDtypeStruct(value.shape, BF16),
        ),
        in_specs=[vspec()] * 10 + [any_spec()],
        out_specs=(vspec(), vspec(), vspec(), vspec(), any_spec()),
        scratch_shapes=[
            pltpu.VMEM((own_rows, width), F32),
            pltpu.VMEM((own_rows, width), F32),
            pltpu.VMEM((n_tensor - 1, own_rows, width), BF16),
            pltpu.VMEM((n_tensor + 1, own_rows, width), BF16),
            pltpu.VMEM((8, slots), F32),
            pltpu.VMEM((n_tensor, 8, own_rows), F32),
            pltpu.VMEM((n_tensor - 1, 8, own_rows), F32),
            pltpu.VMEM(value.shape[1:], BF16),
            pltpu.SemaphoreType.DMA((n_tensor - 1,)),
            pltpu.SemaphoreType.DMA((n_tensor + 1,)),
            pltpu.SemaphoreType.DMA((n_tensor - 1,)),
            pltpu.SemaphoreType.DMA((n_tensor - 1,)),
            pltpu.SemaphoreType.DMA((n_dp - 1,)),
            pltpu.SemaphoreType.DMA((n_dp - 1,)),
            pltpu.SemaphoreType.DMA((2,)),
            pltpu.SemaphoreType.DMA((2, n_tensor - 1)),
            pltpu.SemaphoreType.DMA((2, n_tensor - 1)),
        ],
        compiler_params=pltpu.CompilerParams(
            vmem_limit_bytes=VMEM_LIMIT, collective_id=2, has_side_effects=True
        ),
        name="combine",
    )(
        rows,
        gates,
        slot_columns,
        routes_own,
        residual,
        hidden,
        cotangent,
        router_rows,
        gain,
        weight,
        value,
    )


class Streams:
    def __init__(self, n, refs, send_sem, recv_sem):
        self.n, self.refs, self.send_sem, self.recv_sem = n, refs, send_sem, recv_sem
        self.me = lax.axis_index("tensor")

    def copy(self, j, block, slot, k, peer):
        ref = self.refs[j].at[block]
        return remote(
            ref, ref, self.send_sem.at[j, slot, k], self.recv_sem.at[j, slot, k], "tensor", peer
        )

    def outgoing(self, j, k, fn):
        for slot, sign in enumerate((1, -1)):
            block, peer = self.me - sign * k, self.me + sign

            @pl.when((block >= 0) & (block < self.n) & (peer >= 0) & (peer < self.n))
            def _():
                fn(self.copy(j, block, slot, k, peer))

    def incoming(self, j, k, fn):
        for slot, sign in enumerate((1, -1)):
            block = self.me - sign * (k + 1)

            @pl.when((block >= 0) & (block < self.n))
            def _():
                fn(self.copy(j, block, slot, k, jnp.clip(self.me - sign, 0, self.n - 1)), block)

    def turn(self, turn, used=None):
        moved = []
        for j in range(len(self.refs)):
            k = turn - j
            if k < 0 or k > self.n - 1:
                continue
            if k > 0:
                self.incoming(j, k - 1, lambda c, block: c.wait_recv())
            if k < self.n - 1:
                self.outgoing(j, k, lambda c: c.start())
            moved.append((j, k))
        if used is not None:
            for j, k in moved:
                used(j, k)

    def turns(self):
        return range(self.n + len(self.refs) - 1)

    def each_new(self, j, k, fn):
        if k == 0:
            fn(self.me)
            return
        for sign in (1, -1):
            block = self.me - sign * k

            @pl.when((block >= 0) & (block < self.n))
            def _():
                fn(block)

    def drain(self):
        for j in range(len(self.refs)):
            for k in range(self.n - 1):
                self.outgoing(j, k, lambda c: c.wait_send())


class Spread:
    def __init__(self, n, ref, far_send, far_recv, near_send, near_recv):
        self.n, self.ref = n, ref
        self.far_send, self.far_recv = far_send, far_recv
        self.near_send, self.near_recv = near_send, near_recv
        self.me = lax.axis_index("dp")
        self.partner = self.me ^ 1

    def far(self, step, block, peer):
        ref = self.ref.at[block]
        return remote(ref, ref, self.far_send.at[step], self.far_recv.at[step], "dp", peer)

    def near(self, step, block):
        ref = self.ref.at[block]
        return remote(
            ref, ref, self.near_send.at[step], self.near_recv.at[step], "dp", self.partner
        )

    def start(self):
        for step in range(1, self.n // 2):
            self.far(step - 1, self.me, lax.rem(self.me + 2 * step, self.n)).start()
        self.near(0, self.me).start()

    def source(self, me, step):
        return lax.rem(me + self.n - 2 * step, self.n)

    def relay(self):
        for step in range(1, self.n // 2):
            block = self.source(self.me, step)
            self.far(step - 1, block, block).wait_recv()
            self.near(step, block).start()

    def finish(self):
        for step in range(self.n // 2):
            self.near(step, self.source(self.partner, step)).wait_recv()

    def drain(self):
        for step in range(1, self.n // 2):
            self.far(step - 1, self.me, lax.rem(self.me + 2 * step, self.n)).wait_send()
        for step in range(self.n // 2):
            self.near(step, self.source(self.me, step)).wait_send()


def peers_in_order(n):
    order = (6, 2, 4, 7, 3, 5, 1) if n == 8 else tuple(range(n - 1, 0, -1))
    return order + (0,)


def one_hot(slot_rows, target, per):
    lane_slots = lax.broadcasted_iota(jnp.int32, (per, 1), 0) + target * per
    return jnp.where(
        (lane_slots == slot_rows[0:1, :]) | (lane_slots == slot_rows[1:2, :]), 1.0, 0.0
    ).astype(BF16)


GRAD_PARTS = 2


def front_kernel(n_dp, n_tensor, experts, capacity, fast, *refs):
    (tokens_ref, cotangent_ref, weight_ref, extra_ref, out_ref, routes_ref) = refs[:6]
    refs = refs[6:]
    (hidden_ref, projected_ref, weights_ref, extras_ref, outs_ref) = refs[:5]
    refs = refs[5:]
    if fast:
        (grad_rows_ref, slot_rows_ref, slot_columns_ref) = refs[:3]
        refs = refs[3:]
    (
        gain,
        extra_send,
        extra_recv,
        line_send,
        line_recv,
        weight_far_send,
        weight_far_recv,
        weight_near_send,
        weight_near_recv,
        out_far_send,
        out_far_recv,
        out_near_send,
        out_near_recv,
        stream_send,
        stream_recv,
    ) = refs[:15]
    refs = refs[15:]
    if fast:
        grads, picks, grad_send, row_send, row_recv, row_own = refs
    own_rows, width = tokens_ref.shape
    seq_len = own_rows * n_tensor
    depth = extra_ref.shape[1]
    me = lax.axis_index("dp")
    me_t = lax.axis_index("tensor")
    per = experts // n_dp * capacity
    greet([("dp", n_dp), ("tensor", n_tensor)])
    extras_ref[me] = extra_ref[...]
    copies = []
    for step in range(1, n_dp):
        peer = lax.rem(me + step, n_dp)
        copy = remote(
            extra_ref, extras_ref.at[me], extra_send.at[step - 1], extra_recv.at[step - 1], "dp", peer
        )
        copy.start()
        copies.append(copy)
    streams = []
    part = width // GRAD_PARTS
    if fast:
        for j in range(GRAD_PARTS):
            grads[j, me_t] = cotangent_ref[:, j * part : (j + 1) * part]
            streams.append(grads.at[j])
    streams.append(hidden_ref)
    lines = Streams(n_tensor, streams, stream_send, stream_recv)
    last = len(streams) - 1
    if fast:
        lines.turn(0)
    weights_ref[me] = weight_ref[...]
    weights = Spread(
        n_dp, weights_ref, weight_far_send, weight_far_recv, weight_near_send, weight_near_recv
    )
    weights.start()
    outs_ref[me, me_t] = out_ref[...]
    line_copies = []
    for step in range(1, n_tensor):
        peer = lax.rem(me_t + step, n_tensor)
        copy = remote(
            out_ref,
            outs_ref.at[me, me_t],
            line_send.at[step - 1],
            line_recv.at[step - 1],
            "tensor",
            peer,
        )
        copy.start()
        line_copies.append(copy)
    x = tokens_ref[...].astype(F32)
    scaled = x * lax.rsqrt(jnp.mean(x * x, axis=1, keepdims=True) + EPS)
    for copy in copies:
        copy.wait()
    for block in range(n_dp):
        gain[:, block * depth : (block + 1) * depth] = extras_ref[
            block, experts : experts + 1, :
        ].astype(F32)
    hidden_ref[me_t] = (scaled * gain[...]).astype(BF16)

    if fast:
        ids = lax.broadcasted_iota(jnp.int32, (experts, seq_len), 0)
        hits = [ids == routes_ref[k : k + 1, :] for k in range(TOP)]
        before = lax.broadcasted_iota(jnp.int32, (seq_len, seq_len), 0) < lax.broadcasted_iota(
            jnp.int32, (seq_len, seq_len), 1
        )
        ranks = nn(
            jnp.where(hits[0] | hits[1], 1.0, 0.0).astype(BF16),
            jnp.where(before, 1.0, 0.0).astype(BF16),
        )
        places = ranks + (ids * capacity).astype(F32)
        slot_rows_ref[...] = jnp.zeros_like(slot_rows_ref)
        for k in range(TOP):
            row = jnp.sum(jnp.where(hits[k], places, 0.0), axis=0, keepdims=True)
            slot_rows_ref[k : k + 1, :] = row.astype(jnp.int32)
            for block in range(n_tensor):
                rows = slice(block * own_rows, (block + 1) * own_rows)
                slot_columns_ref[rows, k : k + 1] = to_column(row[:, rows]).astype(jnp.int32)
        for target in range(n_dp):
            picks[target] = one_hot(slot_rows_ref, target, per)

    def row_copy(j, target, sender):
        cols = slice(j * part, (j + 1) * part)
        return remote(
            grad_send.at[j, target],
            grad_rows_ref.at[sender, :, cols],
            row_send.at[j, target],
            row_recv.at[j, sender],
            "dp",
            target,
        )

    def own_row_copy(j):
        cols = slice(j * part, (j + 1) * part)
        return pltpu.make_async_copy(
            grad_send.at[j, me], grad_rows_ref.at[me, :, cols], row_own.at[j]
        )

    def project(block):
        rows = pl.ds(pl.multiple_of(block * own_rows, own_rows), own_rows)
        projected_ref[rows, :] = nn(
            hidden_ref[block], weights_ref[...].reshape(width, weights_ref.shape[2])
        ).astype(BF16)

    def used(j, k):
        if j == last:
            if k > 0:
                if k == 1:
                    weights.finish()
                    lines.each_new(j, 0, project)
                lines.each_new(j, k, project)
        elif k == n_tensor - 1:
            values = grads[j].reshape(seq_len, part)
            for mask in peers_in_order(n_dp):
                target = me ^ mask
                grad_send[j, target] = nn(picks[target], values).astype(BF16)
                if mask:
                    row_copy(j, target, me).start()
                else:
                    own_row_copy(j).start()

    if not fast:
        weights.relay()
    spread = Spread(n_dp, outs_ref, out_far_send, out_far_recv, out_near_send, out_near_recv)
    for turn in lines.turns():
        if turn == 0 and fast:
            continue
        lines.turn(turn, used)
        if turn == 1:
            if fast:
                weights.relay()
            for copy in line_copies:
                copy.wait_recv()
            spread.start()
        if turn == 2:
            spread.relay()
    if n_tensor < 3:
        spread.relay()
    spread.finish()
    lines.drain()
    weights.drain()
    spread.drain()
    for copy in line_copies:
        copy.wait_send()
    if fast:
        for j in range(GRAD_PARTS):
            own_row_copy(j).wait()
            for step in range(1, n_dp):
                peer = lax.rem(me + step, n_dp)
                row_copy(j, peer, me).wait_send()
                row_copy(j, me, peer).wait_recv()


def front(n_dp, n_tensor, experts, capacity, fast, tokens, cotangent, weight, extra, out, routes):
    own_rows, width = tokens.shape
    seq_len = own_rows * n_tensor
    depth, cols = weight.shape
    per = experts // n_dp * capacity
    part = width // GRAD_PARTS
    shapes = [
        jax.ShapeDtypeStruct((n_tensor, own_rows, width), BF16),
        jax.ShapeDtypeStruct((seq_len, cols), BF16),
        jax.ShapeDtypeStruct((n_dp, depth, cols), BF16),
        jax.ShapeDtypeStruct((n_dp,) + extra.shape, BF16),
        jax.ShapeDtypeStruct((n_dp, n_tensor) + out.shape, BF16),
    ]
    specs = [vspec()] * 5
    dma = pltpu.SemaphoreType.DMA
    streams = 1 + (GRAD_PARTS if fast else 0)
    half = n_dp // 2
    scratch = (
        [pltpu.VMEM((1, width), F32)]
        + [dma((n_dp - 1,))] * 2
        + [dma((n_tensor - 1,))] * 2
        + ([dma((half,))] * 4) * 2
        + [dma((streams, 2, n_tensor - 1))] * 2
    )
    if fast:
        shapes += [
            jax.ShapeDtypeStruct((n_dp, per, width), BF16),
            jax.ShapeDtypeStruct((8, seq_len), jnp.int32),
            jax.ShapeDtypeStruct((seq_len, TOP), jnp.int32),
        ]
        specs += [any_spec(), vspec(), vspec()]
        scratch += [
            pltpu.VMEM((GRAD_PARTS, n_tensor, own_rows, part), BF16),
            pltpu.VMEM((n_dp, per, seq_len), BF16),
            pltpu.VMEM((GRAD_PARTS, n_dp, per, part), BF16),
            dma((GRAD_PARTS, n_dp)),
            dma((GRAD_PARTS, n_dp)),
            dma((GRAD_PARTS,)),
        ]
    return pl.pallas_call(
        functools.partial(front_kernel, n_dp, n_tensor, experts, capacity, fast),
        out_shape=tuple(shapes),
        in_specs=[vspec()] * 6,
        out_specs=tuple(specs),
        scratch_shapes=scratch,
        compiler_params=pltpu.CompilerParams(
            vmem_limit_bytes=VMEM_LIMIT, collective_id=3, has_side_effects=True
        ),
        name="front",
    )(tokens, cotangent, weight, extra, out, routes)


PARTS = 4


def middle_kernel(
    n_dp,
    n_tensor,
    experts,
    capacity,
    attended_ref,
    outs_ref,
    tokens_ref,
    gain_ref,
    router_ref,
    slots_ref,
    routes_ref,
    residual_ref,
    hidden_ref,
    weight_own_ref,
    rows_ref,
    gates_ref,
    out_matrix,
    attended_recv,
    everyone,
    picks,
    row_stage,
    logits,
    gate_stage,
    attended_send_sem,
    attended_recv_sem,
    stream_send,
    stream_recv,
    row_send,
    row_recv,
    row_own,
    gate_send,
    gate_recv,
):
    own_rows, width = tokens_ref.shape
    seq_len = own_rows * n_tensor
    head_cols = attended_ref.shape[1]
    out_cols = outs_ref.shape[2]
    local = experts // n_dp
    per = local * capacity
    part = width // PARTS
    me = lax.axis_index("dp")
    me_t = lax.axis_index("tensor")
    greet([("dp", n_dp), ("tensor", n_tensor)])

    def rows_of(block):
        return pl.ds(pl.multiple_of(block * own_rows, own_rows), own_rows)

    copies = []
    for step in range(1, n_tensor):
        peer = lax.rem(me_t + step, n_tensor)
        copy = remote(
            attended_ref.at[rows_of(peer)],
            attended_recv.at[me_t],
            attended_send_sem.at[step - 1],
            attended_recv_sem.at[step - 1],
            "tensor",
            peer,
        )
        copy.start()
        copies.append(copy)
    attended_recv[me_t] = attended_ref[rows_of(me_t), :]
    for block in range(n_dp):
        out_matrix[:, block * out_cols : (block + 1) * out_cols] = outs_ref[block]
    weight_own_ref[...] = out_matrix[
        pl.ds(pl.multiple_of(me_t * head_cols, head_cols), head_cols), :
    ]
    for target in range(n_dp):
        picks[target] = one_hot(slots_ref, target, per)
    for copy in copies:
        copy.wait_recv()
    residual = tokens_ref[...].astype(F32)
    for block in range(n_tensor):
        residual += nn(
            attended_recv[block], out_matrix[block * head_cols : (block + 1) * head_cols, :]
        )
    residual_ref[...] = residual
    hidden = (
        residual
        * lax.rsqrt(jnp.mean(residual * residual, axis=1, keepdims=True) + EPS)
        * gain_ref[...]
    ).astype(BF16)
    hidden_ref[...] = hidden
    for j in range(PARTS):
        everyone[j, me_t] = hidden[:, j * part : (j + 1) * part]
    lines = Streams(n_tensor, [everyone.at[j] for j in range(PARTS)], stream_send, stream_recv)

    def row_copy(j, target, sender):
        cols = slice(j * part, (j + 1) * part)
        return remote(
            row_stage.at[j, target],
            rows_ref.at[sender, :, cols],
            row_send.at[j, target],
            row_recv.at[j, sender],
            "dp",
            target,
        )

    def own_row_copy(j):
        cols = slice(j * part, (j + 1) * part)
        return pltpu.make_async_copy(row_stage.at[j, me], rows_ref.at[me, :, cols], row_own.at[j])

    def used(j, k):
        if k < n_tensor - 1:
            return
        values = everyone[j].reshape(seq_len, part)
        for mask in peers_in_order(n_dp):
            target = me ^ mask
            row_stage[j, target] = nn(picks[target], values).astype(BF16)
            if mask:
                row_copy(j, target, me).start()
            else:
                own_row_copy(j).start()
        term = nt(router_ref[:, j * part : (j + 1) * part], values)
        if j == 0:
            logits[...] = term
        else:
            logits[...] += term

    for turn in lines.turns():
        lines.turn(turn, used)
    values = logits[...]
    exps = jnp.exp(values - jnp.max(values, axis=0, keepdims=True))
    probs = exps / jnp.sum(exps, axis=0, keepdims=True)
    ids = lax.broadcasted_iota(jnp.int32, (experts, seq_len), 0)
    named = (ids == routes_ref[0:1, :]) | (ids == routes_ref[1:2, :])
    shares = probs / jnp.sum(jnp.where(named, probs, 0.0), axis=0, keepdims=True)
    gate_copies = []
    for mask in peers_in_order(n_dp):
        target = me ^ mask
        for expert in range(local):
            row = jnp.sum(
                jnp.where(ids == target * local + expert, shares, 0.0), axis=0, keepdims=True
            )
            high = row.astype(BF16)
            rest = row - high.astype(F32)
            mid = rest.astype(BF16)
            low = (rest - mid.astype(F32)).astype(BF16)
            lanes = slice(expert * capacity, (expert + 1) * capacity)
            pieces = nt(
                jnp.concatenate([high, mid, low, jnp.zeros((5, seq_len), BF16)], axis=0),
                picks[target, lanes, :],
            )
            gate_stage[target, :, lanes] = jnp.broadcast_to(
                jnp.sum(pieces, axis=0, keepdims=True), (8, capacity)
            )
        if mask:
            copy = remote(
                gate_stage.at[target],
                gates_ref.at[me],
                gate_send.at[target],
                gate_recv.at[me],
                "dp",
                target,
            )
            copy.start()
            gate_copies.append(copy)
        else:
            gates_ref[me] = gate_stage[me]
    lines.drain()
    for copy in copies:
        copy.wait_send()
    for copy in gate_copies:
        copy.wait_send()
    for step in range(1, n_dp):
        peer = lax.rem(me + step, n_dp)
        remote(
            gate_stage.at[me], gates_ref.at[peer], gate_send.at[me], gate_recv.at[peer], "dp", peer
        ).wait_recv()
    for j in range(PARTS):
        own_row_copy(j).wait()
        for step in range(1, n_dp):
            peer = lax.rem(me + step, n_dp)
            row_copy(j, peer, me).wait_send()
            row_copy(j, me, peer).wait_recv()


def middle(
    n_dp, n_tensor, experts, capacity, attended, outs, tokens, gain, router_rows, slot_rows, routes
):
    own_rows, width = tokens.shape
    seq_len, head_cols = attended.shape
    per = experts // n_dp * capacity
    part = width // PARTS
    dma = pltpu.SemaphoreType.DMA
    return pl.pallas_call(
        functools.partial(middle_kernel, n_dp, n_tensor, experts, capacity),
        out_shape=(
            jax.ShapeDtypeStruct((own_rows, width), F32),
            jax.ShapeDtypeStruct((own_rows, width), BF16),
            jax.ShapeDtypeStruct((head_cols, width), BF16),
            jax.ShapeDtypeStruct((n_dp, per, width), BF16),
            jax.ShapeDtypeStruct((n_dp, 8, per), F32),
        ),
        in_specs=[vspec()] * 7,
        out_specs=(vspec(), vspec(), vspec(), any_spec(), vspec()),
        scratch_shapes=[
            pltpu.VMEM((width, width), BF16),
            pltpu.VMEM((n_tensor, own_rows, head_cols), BF16),
            pltpu.VMEM((PARTS, n_tensor, own_rows, part), BF16),
            pltpu.VMEM((n_dp, per, seq_len), BF16),
            pltpu.VMEM((PARTS, n_dp, per, part), BF16),
            pltpu.VMEM((experts, seq_len), F32),
            pltpu.VMEM((n_dp, 8, per), F32),
            dma((n_tensor - 1,)),
            dma((n_tensor - 1,)),
            dma((PARTS, 2, n_tensor - 1)),
            dma((PARTS, 2, n_tensor - 1)),
            dma((PARTS, n_dp)),
            dma((PARTS, n_dp)),
            dma((PARTS,)),
            dma((n_dp,)),
            dma((n_dp,)),
        ],
        compiler_params=pltpu.CompilerParams(
            vmem_limit_bytes=VMEM_LIMIT, collective_id=4, has_side_effects=True
        ),
        name="middle",
    )(attended, outs, tokens, gain, router_rows, slot_rows, routes)


def merge_kernel(own_rows, slots_ref, value_ref, out_ref):
    slots = value_ref.shape[0]
    for block in range(out_ref.shape[0] // own_rows):
        rows = slice(block * own_rows, (block + 1) * own_rows)
        one, two = chosen_slots(slots_ref[rows, :], slots)
        out_ref[rows, :] = nn(
            jnp.where(one | two, 1.0, 0.0).astype(BF16), value_ref[...]
        ).astype(BF16)


def merge(own_rows, slot_columns, value):
    return pl.pallas_call(
        functools.partial(merge_kernel, own_rows),
        out_shape=jax.ShapeDtypeStruct((slot_columns.shape[0], value.shape[1]), BF16),
        in_specs=[vspec()] * 2,
        out_specs=vspec(),
        compiler_params=pltpu.CompilerParams(vmem_limit_bytes=VMEM_LIMIT),
        name="merge",
    )(slot_columns, value)


def rms_scale(values):
    return lax.rsqrt(jnp.mean(values * values, axis=-1, keepdims=True) + EPS)


def norm_backward(grad_normed, values, scale_inv, gain):
    normed_unit = values * scale_inv
    grad_unit = grad_normed * gain
    grad_values = scale_inv * (
        grad_unit - normed_unit * jnp.mean(grad_unit * normed_unit, axis=-1, keepdims=True)
    )
    return (grad_values, jnp.sum(grad_normed * normed_unit, axis=0))


def gelu_tanh(values):
    return jax.nn.gelu(values, approximate=True)


def route_slots(route_ids, experts, capacity):
    flat_routes = route_ids.reshape(-1)
    onehot = (flat_routes[:, None] == jnp.arange(experts, dtype=jnp.int32)[None, :]).astype(
        jnp.int32
    )
    ranks = jnp.cumsum(onehot, axis=0) - 1
    rank_own = jnp.sum(ranks * onehot, axis=1)
    return (flat_routes * capacity + rank_own).reshape(-1, TOP)


def on_device(
    tokens,
    segments,
    routes,
    w_qkv,
    w_attn_out,
    bias_table,
    gain_attn,
    gain_moe,
    router,
    w_in,
    w_out,
    cotangent,
):
    own_rows, model_width = tokens.shape
    n_tensor = lax.axis_size("tensor")
    n_dp = lax.axis_size("dp")
    seq_len = own_rows * n_tensor
    own_start = lax.axis_index("tensor") * own_rows
    head_cols = w_qkv.shape[2]
    heads = head_cols // HD
    experts = router.shape[1]
    local_experts = w_in.shape[0]
    capacity = 5 * seq_len * TOP // (4 * experts)
    highest = lax.Precision.HIGHEST
    slots = experts * capacity

    depth = w_qkv.shape[0]
    bias_rows = NB // n_dp
    lanes = depth
    extra = jnp.concatenate(
        [
            jnp.transpose(router),
            gain_attn[None],
            gain_moe[None],
            jnp.pad(bias_table, ((0, SMALL - experts - 2 - bias_rows), (0, lanes - heads))),
        ],
        axis=0,
    )
    fast = n_dp == 8 and slots * model_width <= 4 * 1024 * 1024
    route_rows = jnp.pad(jnp.transpose(routes), ((0, 8 - TOP), (0, 0)))
    gathered, projected, weights_full, extras, outs_full, *routed = front(
        n_dp,
        n_tensor,
        experts,
        capacity,
        fast,
        tokens,
        cotangent,
        w_qkv.reshape(depth, 3 * head_cols),
        extra,
        w_attn_out,
        route_rows,
    )
    gathered_one = gathered.reshape(seq_len, model_width)
    qkv_matrix = weights_full.reshape(model_width, 3 * head_cols)
    router_rows = jnp.transpose(extras[:, :experts], (1, 0, 2)).reshape(experts, model_width)
    gain_one = extras[:, experts].reshape(model_width).astype(F32)
    gain_two = extras[:, experts + 1].reshape(model_width).astype(F32)
    table = extras[:, experts + 2 : experts + 2 + bias_rows, :heads].reshape(NB, heads).astype(F32)
    outs_full = outs_full.reshape(n_dp, model_width, model_width // n_dp)

    tokens_float = tokens.astype(F32)
    scale_one = rms_scale(tokens_float)
    selectors = jnp.asarray(distance_selectors())
    patterns = jnp.dot(selectors, table, precision=highest)
    patterns = jnp.transpose(patterns.reshape(2, 2 * BS, heads), (2, 0, 1)).reshape(
        2 * heads, 2 * BS
    )
    far = table[NB - 1]
    segment_row = segments
    segment_col = segments.reshape(seq_len, 1)
    starts = segments[0, ::BS]
    ends = segments[0, BS - 1 :: BS]
    lowest = jnp.sum((ends[None, :] < starts[:, None]).astype(jnp.int32), axis=1)
    attended, lse = attention_forward(
        projected, lowest, segment_col, segment_row, patterns, far, heads
    )
    if fast:
        grad_rows, slot_rows, slot_columns = routed
        residual, hidden_two, weight_own, rows, row_gates = middle(
            n_dp,
            n_tensor,
            experts,
            capacity,
            attended,
            outs_full,
            tokens,
            gain_two[None],
            router_rows,
            slot_rows,
            route_rows,
        )
        back, gate_back, value, grad_w_in, grad_w_out = run_experts(
            n_dp, capacity, rows, grad_rows, row_gates, w_in, w_out
        )
        own_routes = lax.dynamic_slice_in_dim(route_rows, own_start, own_rows, 1)
        grad_residual, grad_branch_all, grad_attended, small, value_back = combine(
            n_dp,
            n_tensor,
            experts,
            back.reshape(slots, model_width),
            gate_back,
            slot_columns,
            own_routes,
            residual,
            hidden_two,
            cotangent,
            router_rows,
            gain_two[None],
            weight_own,
            value,
        )
        grad_branch_all = grad_branch_all.reshape(seq_len, model_width)
        mixture = lax.psum_scatter(
            merge(own_rows, slot_columns, value_back.reshape(slots, model_width)),
            "tensor",
            scatter_dimension=0,
            tiled=True,
        ).astype(F32)
        layer_out = (residual + mixture).astype(BF16)
    else:
        router_full = jnp.transpose(router_rows)
        out_matrix = jnp.transpose(outs_full, (1, 0, 2)).reshape(model_width, model_width)
        attended_own = lax.all_to_all(
            attended.reshape(n_tensor, own_rows, head_cols), "tensor", 0, 0
        )
        attended_own = jnp.transpose(attended_own, (1, 0, 2)).reshape(own_rows, n_tensor * head_cols)
        branch = jnp.dot(attended_own, out_matrix, preferred_element_type=F32)
        residual = tokens_float + branch
        scale_two = rms_scale(residual)
        hidden_two = (residual * scale_two * gain_two).astype(BF16)
        gathered_two = lax.all_gather(hidden_two, "tensor", axis=0, tiled=True)

        expert_ids = jnp.arange(experts, dtype=jnp.int32)

        def gate_values(logit_values, route_rows):
            expert_probs = jax.nn.softmax(logit_values, axis=-1)
            picked = jnp.sum(
                jnp.where(
                    route_rows[:, :, None] == expert_ids[None, None, :], expert_probs[:, None, :], 0.0
                ),
                axis=-1,
            )
            return picked / jnp.sum(picked, axis=1, keepdims=True)

        gates = gate_values(jnp.dot(gathered_two, router_full, preferred_element_type=F32), routes)
        slot_ids = route_slots(routes, experts, capacity)
        slot_flat = slot_ids.reshape(-1)
        token_ids = jnp.repeat(jnp.arange(seq_len, dtype=jnp.int32), TOP)
        sources = jnp.full((slots,), seq_len, jnp.int32).at[slot_flat].set(token_ids)
        slot_gates = jnp.zeros((slots,), F32).at[slot_flat].set(gates.reshape(-1))
        grad_gathered = lax.all_gather(cotangent, "tensor", axis=0, tiled=True)

        def exchange(rows):
            parts = rows.reshape(n_dp, local_experts, capacity, model_width)
            return [
                lax.all_to_all(parts[:, i], "dp", 0, 0).reshape(n_dp * capacity, model_width)
                for i in range(local_experts)
            ]

        def give_back(parts):
            back = [
                lax.all_to_all(part.reshape(n_dp, capacity, model_width), "dp", 0, 0) for part in parts
            ]
            return jnp.stack(back, axis=1).reshape(slots, model_width)

        zero_row = jnp.zeros((1, model_width), BF16)
        dispatched = exchange(jnp.concatenate([gathered_two, zero_row], axis=0)[sources])
        padded_grad = jnp.concatenate([grad_gathered, zero_row], axis=0)
        grad_expert = exchange((slot_gates[:, None] * padded_grad[sources]).astype(BF16))

        outs, backs, grads_in, grads_out = [], [], [], []
        for i in range(local_experts):
            rows, grad_rows = dispatched[i], grad_expert[i]
            gate_part = nt(rows, w_in[i, 0])
            up_part = nt(rows, w_in[i, 1])
            gelu_value, gelu_pull = jax.vjp(gelu_tanh, gate_part)
            activated = (gelu_value * up_part).astype(BF16)
            outs.append(nn(activated, w_out[i]).astype(BF16))
            grad_act = nt(grad_rows, w_out[i])
            grads_out.append(tn(activated, grad_rows))
            grad_gate = gelu_pull(grad_act * up_part)[0].astype(BF16)
            grad_up = (grad_act * gelu_value).astype(BF16)
            backs.append((nn(grad_gate, w_in[i, 0]) + nn(grad_up, w_in[i, 1])).astype(BF16))
            grads_in.append(jnp.stack([tn(grad_gate, rows), tn(grad_up, rows)]))
        grad_w_in = jnp.stack(grads_in)
        grad_w_out = jnp.stack(grads_out)
        expert_out = give_back(outs)
        grad_dispatched = give_back(backs)

        first, second = slot_ids[:, 0], slot_ids[:, 1]
        picked_first = expert_out[first].astype(F32)
        picked_second = expert_out[second].astype(F32)
        mixture = lax.psum_scatter(
            (gates[:, 0:1] * picked_first + gates[:, 1:2] * picked_second).astype(BF16),
            "tensor",
            scatter_dimension=0,
            tiled=True,
        ).astype(F32)
        layer_out = (residual + mixture).astype(BF16)
        grad_float = grad_gathered.astype(F32)
        grad_gate_part = jnp.stack(
            [
                jnp.sum(grad_float * picked_first, axis=1),
                jnp.sum(grad_float * picked_second, axis=1),
            ],
            axis=1,
        )
        grad_hidden_part = (
            grad_dispatched[first].astype(F32) + grad_dispatched[second].astype(F32)
        ).astype(BF16)
        grad_own = lax.psum_scatter(
            grad_hidden_part, "tensor", scatter_dimension=0, tiled=True
        ).astype(F32)
        grad_gate_own = lax.dynamic_slice_in_dim(
            lax.psum(grad_gate_part, "tensor"), own_start, own_rows, 0
        )
        own_routes = lax.dynamic_slice_in_dim(routes, own_start, own_rows, 0)
        own_logits = jnp.dot(hidden_two, router_full, preferred_element_type=F32)

        def own_gates(logit_values):
            return gate_values(logit_values, own_routes)

        _, gate_pull = jax.vjp(own_gates, own_logits)
        grad_logits = gate_pull(grad_gate_own)[0]
        router_float = router_full.astype(F32)
        grad_hidden_two = grad_own + jnp.dot(grad_logits, router_float.T, precision=highest)
        grad_router_part = jnp.dot(hidden_two.astype(F32).T, grad_logits, precision=highest)
        grad_from_norm, grad_gain_two = norm_backward(grad_hidden_two, residual, scale_two, gain_two)
        grad_residual = cotangent.astype(F32) + grad_from_norm

        grad_branch = grad_residual.astype(BF16)
        grad_attended_own = nt(grad_branch, out_matrix).astype(BF16)
        grad_attended = lax.all_to_all(
            jnp.transpose(grad_attended_own.reshape(own_rows, n_tensor, head_cols), (1, 0, 2)),
            "tensor",
            0,
            0,
        ).reshape(seq_len, head_cols)
        grad_branch_all = lax.all_gather(grad_branch, "tensor", axis=0, tiled=True)
        small = jnp.concatenate(
            [
                jnp.transpose(grad_router_part),
                grad_gain_two[None],
                jnp.zeros((SMALL - experts - 1, model_width), F32),
            ],
            axis=0,
        )
    grad_projected, diag = attention_backward(
        projected,
        attended,
        grad_attended,
        lse,
        lowest,
        segment_col,
        segment_row,
        patterns,
        far,
        heads,
    )
    diag = diag.reshape(heads, 3, 2 * BS)
    near = jnp.transpose(diag[:, :2].reshape(heads, 4 * BS))
    grad_table = lax.dot_general(
        jnp.asarray(skew_selectors()), near, (((0,), (0,)), ((), ())), precision=highest
    )
    grad_table = grad_table.at[NB - 1].add(jnp.sum(diag[:, 2], axis=1))
    small = jnp.transpose(small.reshape(SMALL, n_dp, depth), (1, 0, 2))
    small = lax.dynamic_update_slice(
        small, grad_table.reshape(n_dp, NB // n_dp, heads), (0, experts + 2, 0)
    )
    grad_hidden_one, reduced_qkv, reduced_attn_out, small_sum = tail(
        n_dp,
        n_tensor,
        experts,
        gathered_one,
        grad_projected,
        qkv_matrix,
        attended,
        grad_branch_all,
        small,
        w_qkv.reshape(depth, 3 * head_cols),
        gain_attn[None].astype(F32),
    )
    grad_from_first, _ = norm_backward(grad_hidden_one, tokens_float, scale_one, gain_one)
    grad_tokens = (grad_residual + grad_from_first).astype(BF16)
    return (
        layer_out,
        grad_tokens,
        reduced_qkv.reshape(depth, 3, head_cols),
        reduced_attn_out,
        small_sum[experts + 2 : experts + 2 + NB // n_dp, :heads],
        small_sum[experts + 1],
        small_sum[experts],
        jnp.transpose(small_sum[:experts]),
        grad_w_in,
        grad_w_out,
    )


def solution(mesh):
    return jax.shard_map(
        on_device,
        mesh=mesh,
        in_specs=(
            P(("dp", "tensor"), None),
            P("dp", None),
            P("dp", None),
            P("dp", None, "tensor"),
            P("tensor", "dp"),
            P("dp", "tensor"),
            P("dp"),
            P("dp"),
            P("dp", None),
            P("dp", None, "tensor", None),
            P("dp", "tensor", None),
            P(("dp", "tensor"), None),
        ),
        out_specs=(
            P(("dp", "tensor"), None),
            P(("dp", "tensor"), None),
            P("dp", None, "tensor"),
            P("tensor", "dp"),
            P("dp", "tensor"),
            P("dp"),
            P("dp"),
            P("dp", None),
            P("dp", None, "tensor", None),
            P("dp", "tensor", None),
        ),
        check_vma=False,
    )
```

```python
import functools
import math

import jax
import jax.numpy as jnp
import numpy as np
from jax import lax
from jax.experimental import pallas as pl
from jax.experimental.pallas import tpu as pltpu
from jax.sharding import PartitionSpec as P

HD = 64
TOP = 2
NB = 32
NEAR = 128
BS = 256

EPS = 1e-06
NEG = -1e30
F32 = jnp.float32
BF16 = jnp.bfloat16
VMEM_LIMIT = 60 * 1024 * 1024


def distance_buckets():
    half_buckets = NB // 2
    thresholds = [bucket_level for bucket_level in range(1, half_buckets)]
    thresholds = thresholds + [
        int(
            math.ceil(
                half_buckets
                * (NEAR / half_buckets) ** ((bucket_level - half_buckets) / half_buckets)
            )
        )
        for bucket_level in range(half_buckets, NB)
    ]
    distance = np.arange(NEAR + 1)
    return (distance[:, None] >= np.array(thresholds)[None, :]).sum(axis=1)


def distance_selectors():
    buckets = distance_buckets()
    lanes = np.arange(2 * BS)
    signed = np.where(lanes < BS, lanes, lanes - 2 * BS)
    out = []
    for base in (0, BS):
        distance = np.clip(base - signed, 0, NEAR)
        out.append(buckets[distance][:, None] == np.arange(NB)[None, :])
    return np.concatenate(out, axis=0).astype(np.float32)


def skew_selectors():
    buckets = distance_buckets()
    lanes = np.arange(2 * BS)
    out = []
    for base in (0, BS):
        distance = np.clip(base + BS - 1 - lanes, 0, NEAR)
        out.append(buckets[distance][:, None] == np.arange(NB)[None, :])
    return np.concatenate(out, axis=0).astype(np.float32)


def nt(a, b):
    return lax.dot_general(a, b, (((1,), (1,)), ((), ())), preferred_element_type=F32)


def tn(a, b):
    return lax.dot_general(a, b, (((0,), (0,)), ((), ())), preferred_element_type=F32)


def nn(a, b):
    return lax.dot_general(a, b, (((1,), (0,)), ((), ())), preferred_element_type=F32)


def toeplitz(row):
    return pltpu.roll(jnp.broadcast_to(row, (BS, 2 * BS)), 0, 1, stride=1, stride_axis=0)[:, :BS]


def head_lanes(heads, width):
    lane = lax.broadcasted_iota(jnp.int32, (1, width), 1)
    return [(lane >= h * HD) & (lane < (h + 1) * HD) for h in range(heads)]


def own_head(value, lanes, heads):
    return value if heads == 1 else jnp.where(lanes, value, jnp.zeros((), value.dtype))


def build_bias(heads, pattern_ref, bias):
    for h in range(heads):
        for t in range(2):
            bias[h, t] = toeplitz(pattern_ref[2 * h + t : 2 * h + t + 1, :])
        bias[h, 2] = jnp.broadcast_to(pattern_ref[2 * h + 1 : 2 * h + 2, 0:1], (BS, BS))


def block_rows(block):
    if isinstance(block, int):
        return pl.ds(block * BS, BS)
    return pl.ds(pl.multiple_of(block * BS, BS), BS)


def segment_column(qb, segment_ref):
    return to_column(segment_ref[:, block_rows(qb)].astype(F32))


def block_mask(qb, kb, q_segments, segment_ref):
    k_segments = segment_ref[:, block_rows(kb)].astype(F32)
    row = lax.broadcasted_iota(jnp.int32, (BS, BS), 0) + (qb - kb) * BS
    col = lax.broadcasted_iota(jnp.int32, (BS, BS), 1)
    return (q_segments == k_segments) & (row >= col)


def forward_rows(heads, qb, low, qkv_ref, segment_ref, bias, out_ref, lse_ref):
    width = heads * HD
    lanes = head_lanes(heads, width)
    q_rows = block_rows(qb)
    q_all = (qkv_ref[q_rows, 0:width] * HD**-0.5).astype(BF16)
    q_heads = [own_head(q_all, lanes[h], heads) for h in range(heads)]
    q_segments = segment_column(qb, segment_ref)

    def k_step(kb, carry):
        k = qkv_ref[block_rows(kb), width : 2 * width]
        v = qkv_ref[block_rows(kb), 2 * width : 3 * width]
        allowed = block_mask(qb, kb, q_segments, segment_ref)
        place = jnp.minimum(qb - kb, 2)
        new = []
        for h in range(heads):
            top, total, acc = carry[3 * h : 3 * h + 3]
            s = jnp.where(allowed, nt(q_heads[h], k) + bias[h, place], NEG)
            top_new = jnp.maximum(top, jnp.max(s, axis=1, keepdims=True))
            alpha = jnp.exp(top - top_new)
            p = jnp.exp(s - top_new)
            total = alpha * total + jnp.sum(p, axis=1, keepdims=True)
            acc = alpha * acc + nn(p.astype(BF16), v)
            new += [top_new, total, acc]
        return tuple(new)

    init = []
    for h in range(heads):
        init += [jnp.full((BS, 1), NEG, F32), jnp.zeros((BS, 1), F32), jnp.zeros((BS, width), F32)]
    res = lax.fori_loop(low, qb + 1, k_step, tuple(init))
    out = jnp.zeros((BS, width), F32)
    for h in range(heads):
        top, total, acc = res[3 * h : 3 * h + 3]
        value = acc / total
        out = value if heads == 1 else jnp.where(lanes[h], value, out)
        lse_ref[q_rows, h : h + 1] = top + jnp.log(total)
    out_ref[q_rows, :] = out.astype(BF16)


def backward_rows(
    heads, qb, low, qkv_ref, out_ref, grad_ref, lse_ref, segment_ref, bias, grad_qkv_ref, dk, dv, sums
):
    width = heads * HD
    lanes = head_lanes(heads, width)
    scale = HD**-0.5
    q_rows = block_rows(qb)
    q_all = (qkv_ref[q_rows, 0:width] * scale).astype(BF16)
    g_all = grad_ref[q_rows, :]
    both = g_all.astype(F32) * out_ref[q_rows, :].astype(F32)
    q_heads = [own_head(q_all, lanes[h], heads) for h in range(heads)]
    g_heads = [own_head(g_all, lanes[h], heads) for h in range(heads)]
    deltas = [jnp.sum(own_head(both, lanes[h], heads), axis=1, keepdims=True) for h in range(heads)]
    totals = [lse_ref[q_rows, h : h + 1] for h in range(heads)]
    q_segments = segment_column(qb, segment_ref)

    def k_step(kb, dq):
        k_rows = block_rows(kb)
        k = qkv_ref[k_rows, width : 2 * width]
        v = qkv_ref[k_rows, 2 * width : 3 * width]
        allowed = block_mask(qb, kb, q_segments, segment_ref)
        place = jnp.minimum(qb - kb, 2)
        dk_add = jnp.zeros((BS, width), F32)
        dv_add = jnp.zeros((BS, width), F32)
        for h in range(heads):
            s = jnp.where(allowed, nt(q_heads[h], k) + bias[h, place], NEG)
            p = jnp.exp(s - totals[h])
            gp = nt(g_heads[h], v)
            ds = (p * (gp - deltas[h])).astype(BF16)
            dv_add += tn(p.astype(BF16), g_heads[h])
            dk_add += tn(ds, q_heads[h])
            dq = dq + own_head(nn(ds, k), lanes[h], heads)
            sums[h, place] += ds.astype(F32)
        dk[k_rows, :] += dk_add
        dv[k_rows, :] += dv_add
        return dq

    dq = lax.fori_loop(low, qb + 1, k_step, jnp.zeros((BS, width), F32))
    grad_qkv_ref[q_rows, 0:width] = (dq * scale).astype(BF16)


def backward_start(dk, dv, sums):
    dk[...] = jnp.zeros_like(dk)
    dv[...] = jnp.zeros_like(dv)
    sums[...] = jnp.zeros_like(sums)


def backward_end(heads, grad_qkv_ref, dk, dv):
    width = heads * HD
    grad_qkv_ref[:, width : 2 * width] = dk[...].astype(BF16)
    grad_qkv_ref[:, 2 * width : 3 * width] = dv[...].astype(BF16)


def diagonal_sums(heads, sums, diag_ref):
    row = lax.broadcasted_iota(jnp.int32, (BS, BS), 0)
    col = lax.broadcasted_iota(jnp.int32, (BS, BS), 1)
    upside_down = jnp.where(row + col == BS - 1, 1.0, 0.0).astype(F32)
    for h in range(heads):
        for t in range(2):
            flipped = jnp.dot(
                upside_down,
                sums[h, t],
                precision=lax.Precision.HIGHEST,
                preferred_element_type=F32,
            )
            wide = jnp.concatenate([flipped, jnp.zeros((BS, BS), F32)], axis=1)
            skewed = pltpu.roll(wide, 0, 1, stride=1, stride_axis=0)
            diag_ref[t, h : h + 1, :] = jnp.sum(skewed, axis=0, keepdims=True)
        rest = jnp.sum(sums[h, 2], axis=0, keepdims=True)
        diag_ref[2, h : h + 1, :] = jnp.concatenate([rest, jnp.zeros((1, BS), F32)], axis=1)


def attn_fwd_kernel(heads, blocks, lo_ref, qkv_ref, segment_ref, pattern_ref, out_ref, lse_ref, bias):
    build_bias(heads, pattern_ref, bias)

    def q_step(qb, _):
        forward_rows(heads, qb, lo_ref[qb], qkv_ref, segment_ref, bias, out_ref, lse_ref)
        return 0

    lax.fori_loop(0, blocks, q_step, 0)


def attn_bwd_kernel(
    heads,
    blocks,
    lo_ref,
    qkv_ref,
    out_ref,
    grad_ref,
    lse_ref,
    segment_ref,
    pattern_ref,
    grad_qkv_ref,
    diag_ref,
    bias,
    dk,
    dv,
    sums,
):
    build_bias(heads, pattern_ref, bias)
    backward_start(dk, dv, sums)

    def q_step(qb, _):
        backward_rows(
            heads,
            qb,
            lo_ref[qb],
            qkv_ref,
            out_ref,
            grad_ref,
            lse_ref,
            segment_ref,
            bias,
            grad_qkv_ref,
            dk,
            dv,
            sums,
        )
        return 0

    lax.fori_loop(0, blocks, q_step, 0)
    backward_end(heads, grad_qkv_ref, dk, dv)
    diagonal_sums(heads, sums, diag_ref)


def vspec():
    return pl.BlockSpec(memory_space=pltpu.VMEM)


def sspec():
    return pl.BlockSpec(memory_space=pltpu.SMEM)


def attention_forward(projected, lo, segments, patterns, heads):
    seq_len = projected.shape[0]
    blocks = seq_len // BS
    return pl.pallas_call(
        functools.partial(attn_fwd_kernel, heads, blocks),
        out_shape=(
            jax.ShapeDtypeStruct((seq_len, heads * HD), BF16),
            jax.ShapeDtypeStruct((seq_len, heads), F32),
        ),
        in_specs=[sspec(), vspec(), vspec(), vspec()],
        out_specs=(vspec(), vspec()),
        scratch_shapes=[pltpu.VMEM((heads, 3, BS, BS), F32)],
        compiler_params=pltpu.CompilerParams(vmem_limit_bytes=VMEM_LIMIT),
        name="attn_fwd",
    )(lo, projected, segments, patterns)


def attention_backward(projected, attended, grad, lse, lo, segments, patterns, heads):
    seq_len = projected.shape[0]
    blocks = seq_len // BS
    width = heads * HD
    return pl.pallas_call(
        functools.partial(attn_bwd_kernel, heads, blocks),
        out_shape=(
            jax.ShapeDtypeStruct((seq_len, 3 * width), BF16),
            jax.ShapeDtypeStruct((3, 8, 2 * BS), F32),
        ),
        in_specs=[sspec()] + [vspec()] * 6,
        out_specs=(vspec(), vspec()),
        scratch_shapes=backward_scratch(heads, seq_len),
        compiler_params=pltpu.CompilerParams(vmem_limit_bytes=VMEM_LIMIT),
        name="attn_bwd",
    )(lo, projected, attended, grad, lse, segments, patterns)


def backward_scratch(heads, seq_len):
    return [
        pltpu.VMEM((heads, 3, BS, BS), F32),
        pltpu.VMEM((seq_len, heads * HD), F32),
        pltpu.VMEM((seq_len, heads * HD), F32),
        pltpu.VMEM((heads, 3, BS, BS), F32),
    ]


MESH = pl.DeviceIdType.MESH
SMALL = 32


def remote(src, dst, send, recv, axis, peer):
    return pltpu.make_async_remote_copy(
        src_ref=src,
        dst_ref=dst,
        send_sem=send,
        recv_sem=recv,
        device_id={axis: peer},
        device_id_type=MESH,
    )


def greet(groups):
    barrier = pltpu.get_barrier_semaphore()
    total = 0
    for axis, n in groups:
        me = lax.axis_index(axis)
        for step in range(1, n):
            pl.semaphore_signal(
                barrier, inc=1, device_id={axis: lax.rem(me + step, n)}, device_id_type=MESH
            )
        total += n - 1
    pl.semaphore_wait(barrier, total)


class LineSum:
    def __init__(self, n, partial, send, recv, send_sem, recv_sem, acc, total):
        self.n, self.partial = n, partial
        self.send, self.recv, self.send_sem, self.recv_sem = send, recv, send_sem, recv_sem
        self.acc, self.total = acc, total
        self.me = lax.axis_index("tensor")

    def flow(self, first, k):
        n, me = self.n, self.me
        near = me * 2 < n
        right = near if first else jnp.logical_not(near)
        block = jnp.where(right, n - 1 - k, k)
        comes = jnp.where(right, jnp.where(me > 0, me <= block, False), jnp.where(me < n - 1, me >= block, False))
        goes = jnp.where(right, me < block, me > block)
        peer = jnp.clip(jnp.where(right, me + 1, me - 1), 0, n - 1)
        out_slot = jnp.clip(jnp.where(right, k, n - 1 - me + k), 0, n - 2)
        in_slot = jnp.clip(jnp.where(right, k, n - me + k), 0, n)
        peer_slot = jnp.clip(jnp.where(right, k, n - peer + k), 0, n)
        return block, comes, goes, peer, out_slot, in_slot, peer_slot

    def copy(self, peer, out_slot, slot):
        return remote(
            self.send.at[out_slot],
            self.recv.at[slot],
            self.send_sem.at[out_slot],
            self.recv_sem.at[slot],
            "tensor",
            peer,
        )

    def start(self):
        for k in range(self.n - 1):
            for first in (True, False):
                block, comes, goes, peer, out_slot, in_slot, peer_slot = self.flow(first, k)

                @pl.when(goes & jnp.logical_not(comes))
                def _():
                    self.send[out_slot] = self.partial(block).astype(BF16)
                    self.copy(peer, out_slot, peer_slot).start()

        self.total[...] = self.partial(self.me)

    def finish(self):
        for k in range(self.n - 1):
            self.step(k)

    def step(self, k):
        for first in (True, False):
            block, comes, goes, peer, out_slot, in_slot, peer_slot = self.flow(first, k)

            @pl.when(goes & comes)
            def _():
                self.acc[...] = self.partial(block)
                self.copy(peer, out_slot, in_slot).wait_recv()
                self.send[out_slot] = (self.acc[...] + self.recv[in_slot].astype(F32)).astype(BF16)
                self.copy(peer, out_slot, peer_slot).start()

            @pl.when(comes & jnp.logical_not(goes))
            def _():
                self.copy(peer, 0, in_slot).wait_recv()
                self.total[...] += self.recv[in_slot].astype(F32)

    def drain(self):
        for k in range(self.n - 1):
            for first in (True, False):
                block, comes, goes, peer, out_slot, in_slot, peer_slot = self.flow(first, k)

                @pl.when(goes)
                def _():
                    self.copy(peer, out_slot, in_slot).wait_send()


def tail_kernel(
    n_dp,
    n_tensor,
    experts,
    table_rows,
    hidden_ref,
    grad_ref,
    weight_ref,
    attended_ref,
    branch_ref,
    small_ref,
    weight_own_ref,
    gain_own_ref,
    grad_hidden_ref,
    grad_qkv_ref,
    grad_out_ref,
    small_out_ref,
    acc,
    line_send,
    line_recv,
    qkv_send,
    qkv_recv,
    out_send,
    out_recv,
    small_recv,
    small_sum,
    gain_recv,
    line_send_sem,
    line_recv_sem,
    qkv_send_sem,
    qkv_recv_sem,
    out_send_sem,
    out_recv_sem,
    small_send_sem,
    small_recv_sem,
    gain_send_sem,
    gain_recv_sem,
):
    own_rows = grad_hidden_ref.shape[0]
    depth = weight_own_ref.shape[0]
    out_cols = grad_out_ref.shape[1]
    me = lax.axis_index("dp")
    me_t = lax.axis_index("tensor")
    greet([("dp", n_dp), ("tensor", n_tensor)])

    def partial(block):
        rows = pl.ds(pl.multiple_of(block * own_rows, own_rows), own_rows)
        return nt(grad_ref[rows, :], weight_ref[...])

    line = LineSum(
        n_tensor, partial, line_send, line_recv, line_send_sem, line_recv_sem, acc, grad_hidden_ref
    )
    line.start()
    copies = []
    for step in range(1, n_dp):
        peer = lax.rem(me + step, n_dp)
        copy = remote(
            small_ref.at[peer],
            small_recv.at[step - 1],
            small_send_sem.at[step - 1],
            small_recv_sem.at[step - 1],
            "dp",
            peer,
        )
        copy.start()
        copies.append(copy)
    for block in range(n_dp):
        cols = slice(block * depth, (block + 1) * depth)
        qkv_send[block] = tn(hidden_ref[:, cols], grad_ref[...]).astype(BF16)
    for step in range(1, n_dp):
        peer = lax.rem(me + step, n_dp)
        copy = remote(
            qkv_send.at[peer],
            qkv_recv.at[step - 1],
            qkv_send_sem.at[step - 1],
            qkv_recv_sem.at[step - 1],
            "dp",
            peer,
        )
        copy.start()
        copies.append(copy)
    for block in range(n_dp):
        cols = slice(block * out_cols, (block + 1) * out_cols)
        out_send[block] = tn(attended_ref[...], branch_ref[:, cols]).astype(BF16)
    for step in range(1, n_dp):
        peer = lax.rem(me + step, n_dp)
        copy = remote(
            out_send.at[peer],
            out_recv.at[step - 1],
            out_send_sem.at[step - 1],
            out_recv_sem.at[step - 1],
            "dp",
            peer,
        )
        copy.start()
        copies.append(copy)
    line.finish()
    for copy in copies:
        copy.wait()
    small_sum[...] = small_ref[me]
    grad_qkv_ref[...] = qkv_send[me].astype(F32)
    grad_out_ref[...] = out_send[me].astype(F32)
    for step in range(1, n_dp):
        small_sum[...] += small_recv[step - 1]
        grad_qkv_ref[...] += qkv_recv[step - 1].astype(F32)
        grad_out_ref[...] += out_recv[step - 1].astype(F32)
    column = jnp.sum(grad_qkv_ref[...] * weight_own_ref[...].astype(F32), axis=1, keepdims=True)
    eye = lax.broadcasted_iota(jnp.int32, (depth, depth), 0) == lax.broadcasted_iota(
        jnp.int32, (depth, depth), 1
    )
    row = jnp.sum(jnp.where(eye, column, 0.0), axis=0, keepdims=True)
    small_sum[experts + 1 : experts + 2, :] = row / gain_own_ref[...]
    gains = []
    for step in range(1, n_tensor):
        peer = lax.rem(me_t + step, n_tensor)
        copy = remote(
            small_sum,
            gain_recv.at[step - 1],
            gain_send_sem.at[step - 1],
            gain_recv_sem.at[step - 1],
            "tensor",
            peer,
        )
        copy.start()
        gains.append(copy)
    line.drain()
    for copy in gains:
        copy.wait()
    small_out_ref[...] = small_sum[...]
    shared = slice(0, experts + 2)
    for step in range(1, n_tensor):
        small_out_ref[shared, :] += gain_recv[step - 1, shared, :]


def tail(n_dp, n_tensor, experts, hidden, grad, weight, attended, branch, small, weight_own, gain_own):
    seq_len, width = hidden.shape
    own_rows = seq_len // n_tensor
    depth, cols = weight_own.shape
    heads_cols = attended.shape[1]
    out_cols = width // n_dp
    table_rows = NB // n_dp
    return pl.pallas_call(
        functools.partial(tail_kernel, n_dp, n_tensor, experts, table_rows),
        out_shape=(
            jax.ShapeDtypeStruct((own_rows, width), F32),
            jax.ShapeDtypeStruct((depth, cols), F32),
            jax.ShapeDtypeStruct((heads_cols, out_cols), F32),
            jax.ShapeDtypeStruct((SMALL, depth), F32),
        ),
        in_specs=[vspec()] * 8,
        out_specs=(vspec(),) * 4,
        scratch_shapes=[
            pltpu.VMEM((own_rows, width), F32),
            pltpu.VMEM((n_tensor - 1, own_rows, width), BF16),
            pltpu.VMEM((n_tensor + 1, own_rows, width), BF16),
            pltpu.VMEM((n_dp, depth, cols), BF16),
            pltpu.VMEM((n_dp - 1, depth, cols), BF16),
            pltpu.VMEM((n_dp, heads_cols, out_cols), BF16),
            pltpu.VMEM((n_dp - 1, heads_cols, out_cols), BF16),
            pltpu.VMEM((n_dp - 1, SMALL, depth), F32),
            pltpu.VMEM((SMALL, depth), F32),
            pltpu.VMEM((n_tensor - 1, SMALL, depth), F32),
            pltpu.SemaphoreType.DMA((n_tensor - 1,)),
            pltpu.SemaphoreType.DMA((n_tensor + 1,)),
        ]
        + [pltpu.SemaphoreType.DMA((n_dp - 1,))] * 6
        + [pltpu.SemaphoreType.DMA((n_tensor - 1,))] * 2,
        compiler_params=pltpu.CompilerParams(
            vmem_limit_bytes=VMEM_LIMIT, collective_id=0, has_side_effects=True
        ),
        name="tail",
    )(hidden, grad, weight, attended, branch, small, weight_own, gain_own)


def diagonal(size):
    return lax.broadcasted_iota(jnp.int32, (size, size), 0) == lax.broadcasted_iota(
        jnp.int32, (size, size), 1
    )


def to_column(row):
    return jnp.sum(jnp.where(diagonal(row.shape[1]), row, 0.0), axis=1, keepdims=True)


def to_row(column):
    return jnp.sum(jnp.where(diagonal(column.shape[0]), column, 0.0), axis=0, keepdims=True)


def expert_kernel(
    n_dp,
    local,
    capacity,
    rows_ref,
    grad_one_ref,
    grad_two_ref,
    gates_ref,
    in_ref,
    out_ref,
    back_ref,
    gate_back_ref,
    value_ref,
    grad_in_ref,
    grad_out_ref,
    back_send,
    gate_send,
    zs,
    ups,
    gates_s,
    stage,
    value_stage,
    back_send_sem,
    back_recv_sem,
    gate_send_sem,
    gate_recv_sem,
    own_sem,
    stage_sem,
    value_sem,
):
    me = lax.axis_index("dp")
    pairs = n_dp // 2
    hidden = in_ref.shape[2]
    width = rows_ref.shape[2]
    two = 2 * capacity
    greet([("dp", n_dp)])

    def back_copy(expert, target, sender):
        part = slice(expert * capacity, (expert + 1) * capacity)
        return remote(
            back_send.at[target, part],
            back_ref.at[sender, part],
            back_send_sem.at[expert, target],
            back_recv_sem.at[expert, sender],
            "dp",
            target,
        )

    def own_copy(expert):
        part = slice(expert * capacity, (expert + 1) * capacity)
        return pltpu.make_async_copy(
            back_send.at[me, part], back_ref.at[me, part], own_sem.at[expert]
        )

    def stage_copy(slot, target):
        return pltpu.make_async_copy(stage.at[slot], target, stage_sem.at[slot])

    gate_send[...] = jnp.zeros_like(gate_send)
    staged = []

    def put(value, target):
        slot = len(staged) % 2
        if len(staged) >= 2:
            staged[-2].wait()
        stage[slot] = value
        copy = stage_copy(slot, target)
        copy.start()
        staged.append(copy)

    for expert in range(local):
        part = slice(expert * capacity, (expert + 1) * capacity)

        def group(index, _):
            pair = (me // 2) ^ (pairs - 1 - index)
            first = 2 * pair
            rows = rows_ref[pl.ds(first, 2), part, :].reshape(two, width)
            grads = jnp.concatenate(
                [
                    grad_one_ref[pl.ds(first, 2), part, :].reshape(two, width // 2),
                    grad_two_ref[pl.ds(first, 2), part, :].reshape(two, width // 2),
                ],
                axis=1,
            )
            column = jnp.concatenate(
                [to_column(gates_ref[first + j, 0:1, part]) for j in range(2)], axis=0
            )
            gate = nt(rows, in_ref[expert, 0])
            up = nt(rows, in_ref[expert, 1])
            square = gate * gate
            bent = jnp.tanh(0.7978845608028654 * gate * (1.0 + 0.044715 * square))
            half = 0.5 * (1.0 + bent)
            gelu = gate * half
            slope = half + 0.5 * gate * (1.0 - bent * bent) * (
                0.7978845608028654 * (1.0 + 3 * 0.044715 * square)
            )
            z = gelu * up
            grad_z = nt(grads, out_ref[expert])
            gate_grad = jnp.sum(z * grad_z, axis=1, keepdims=True)
            grad_z = column * grad_z
            zs[pl.ds(first, 2)] = (column * z).astype(BF16).reshape(2, capacity, hidden)
            ups[0, pl.ds(first, 2)] = (grad_z * up * slope).astype(BF16).reshape(2, capacity, hidden)
            ups[1, pl.ds(first, 2)] = (grad_z * gelu).astype(BF16).reshape(2, capacity, hidden)
            for j in range(2):
                gate_send[first + j, 0:1, part] = to_row(
                    gate_grad[j * capacity : (j + 1) * capacity]
                )
            back = nn(ups[0, pl.ds(first, 2)].reshape(two, hidden), in_ref[expert, 0])
            back += nn(ups[1, pl.ds(first, 2)].reshape(two, hidden), in_ref[expert, 1])
            back_send[pl.ds(first, 2), part, :] = back.astype(BF16).reshape(2, capacity, width)
            for j in range(2):
                target = first + j

                @pl.when(target != me)
                def _():
                    back_copy(expert, target, me).start()

                @pl.when(target == me)
                def _():
                    own_copy(expert).start()

            return 0

        lax.fori_loop(0, pairs, group, 0)
        if expert == local - 1:
            gate_copies = []
            for step in range(1, n_dp):
                target = lax.rem(me + step, n_dp)
                copy = remote(
                    gate_send.at[target],
                    gate_back_ref.at[me],
                    gate_send_sem.at[step - 1],
                    gate_recv_sem.at[step - 1],
                    "dp",
                    target,
                )
                copy.start()
                gate_copies.append(copy)
            gate_back_ref[me] = gate_send[me]
        rows = rows_ref[:, part, :].reshape(n_dp * capacity, width)
        for half in range(2):
            put(tn(ups[half].reshape(n_dp * capacity, hidden), rows), grad_in_ref.at[expert, half])
        grads = jnp.concatenate(
            [
                grad_one_ref[:, part, :].reshape(n_dp * capacity, width // 2),
                grad_two_ref[:, part, :].reshape(n_dp * capacity, width // 2),
            ],
            axis=1,
        )
        put(tn(zs[...].reshape(n_dp * capacity, hidden), grads), grad_out_ref.at[expert])
        if expert > 0:
            pltpu.make_async_copy(
                value_stage, value_ref.at[:, slice((expert - 1) * capacity, expert * capacity)], value_sem
            ).wait()

        def value(pair, _):
            out = nn(zs[pl.ds(2 * pair, 2)].reshape(two, hidden), out_ref[expert])
            value_stage[pl.ds(2 * pair, 2)] = out.astype(BF16).reshape(2, capacity, width)
            return 0

        lax.fori_loop(0, pairs, value, 0)
        pltpu.make_async_copy(value_stage, value_ref.at[:, part], value_sem).start()

    last = slice((local - 1) * capacity, local * capacity)
    pltpu.make_async_copy(value_stage, value_ref.at[:, last], value_sem).wait()
    for copy in staged[-2:]:
        copy.wait()
    for copy in gate_copies:
        copy.wait()
    for expert in range(local):
        own_copy(expert).wait()
        for step in range(1, n_dp):
            peer = lax.rem(me + step, n_dp)
            back_copy(expert, peer, me).wait_send()
            back_copy(expert, me, peer).wait_recv()


def any_spec():
    return pl.BlockSpec(memory_space=pl.ANY)


def run_experts(n_dp, capacity, rows, grads_one, grads_two, gates, w_in, w_out):
    local, _, hidden, width = w_in.shape
    slots = local * capacity
    return pl.pallas_call(
        functools.partial(expert_kernel, n_dp, local, capacity),
        out_shape=(
            jax.ShapeDtypeStruct((n_dp, slots, width), BF16),
            jax.ShapeDtypeStruct((n_dp, 8, slots), F32),
            jax.ShapeDtypeStruct((n_dp, slots, width), BF16),
            jax.ShapeDtypeStruct(w_in.shape, F32),
            jax.ShapeDtypeStruct(w_out.shape, F32),
        ),
        in_specs=[vspec()] * 6,
        out_specs=(any_spec(), vspec(), any_spec(), any_spec(), any_spec()),
        scratch_shapes=[
            pltpu.VMEM((n_dp, slots, width), BF16),
            pltpu.VMEM((n_dp, 8, slots), F32),
            pltpu.VMEM((n_dp, capacity, hidden), BF16),
            pltpu.VMEM((2, n_dp, capacity, hidden), BF16),
            pltpu.VMEM((8, 128), F32),
            pltpu.VMEM((2, hidden, width), F32),
            pltpu.VMEM((n_dp, capacity, width), BF16),
            pltpu.SemaphoreType.DMA((local, n_dp)),
            pltpu.SemaphoreType.DMA((local, n_dp)),
            pltpu.SemaphoreType.DMA((n_dp - 1,)),
            pltpu.SemaphoreType.DMA((n_dp - 1,)),
            pltpu.SemaphoreType.DMA((local,)),
            pltpu.SemaphoreType.DMA((2,)),
            pltpu.SemaphoreType.DMA,
        ],
        compiler_params=pltpu.CompilerParams(
            vmem_limit_bytes=VMEM_LIMIT, collective_id=1, has_side_effects=True
        ),
        name="experts",
    )(rows, grads_one, grads_two, gates, w_in, w_out)


def chosen_slots(columns, slots):
    lane = lax.broadcasted_iota(jnp.int32, (1, slots), 1)
    return columns[:, 0:1] == lane, columns[:, 1:2] == lane


def combine_kernel(
    n_dp,
    n_tensor,
    experts,
    rows_ref,
    gate_ref,
    slots_ref,
    routes_ref,
    residual_ref,
    hidden_ref,
    cotangent_ref,
    router_ref,
    gain_ref,
    weight_ref,
    value_ref,
    grad_residual_ref,
    branch_ref,
    grad_attended_ref,
    small_ref,
    merged_ref,
    acc,
    total,
    line_send,
    line_recv,
    gate_all,
    gate_send,
    gate_recv,
    value_back,
    line_send_sem,
    line_recv_sem,
    gate_send_sem,
    gate_recv_sem,
    value_send_sem,
    value_recv_sem,
    value_own_sem,
    gather_send_sem,
    gather_recv_sem,
):
    own_rows, width = residual_ref.shape
    slots = rows_ref.shape[0]
    per = slots // n_dp
    me = lax.axis_index("dp")
    me_t = lax.axis_index("tensor")
    greet([("dp", n_dp), ("tensor", n_tensor)])
    values = []
    for step in range(1, n_dp):
        peer = lax.rem(me + step, n_dp)
        copy = remote(
            value_ref.at[peer],
            value_back.at[me],
            value_send_sem.at[step - 1],
            value_recv_sem.at[step - 1],
            "dp",
            peer,
        )
        copy.start()
        values.append(copy)
    fetch = pltpu.make_async_copy(value_ref.at[me], value_back.at[me], value_own_sem)
    fetch.start()

    def partial(block):
        one, two = chosen_slots(
            slots_ref[pl.ds(pl.multiple_of(block * own_rows, own_rows), own_rows), :], slots
        )
        return nn(jnp.where(one | two, 1.0, 0.0).astype(BF16), rows_ref[...])

    line = LineSum(
        n_tensor, partial, line_send, line_recv, line_send_sem, line_recv_sem, acc, total
    )
    line.start()
    for peer in range(n_dp):
        gate_all[0:1, peer * per : (peer + 1) * per] = gate_ref[peer, 0:1, :]
    gate_send[...] = jnp.zeros_like(gate_send)
    gates = []
    for step in range(n_tensor):
        peer = lax.rem(me_t + step, n_tensor)
        picks = chosen_slots(
            slots_ref[pl.ds(pl.multiple_of(peer * own_rows, own_rows), own_rows), :], slots
        )
        for k in range(TOP):
            column = jnp.sum(
                jnp.where(picks[k], gate_all[0:1, :], 0.0), axis=1, keepdims=True
            )
            gate_send[step, k : k + 1, :] = to_row(column)
        if step:
            copy = remote(
                gate_send.at[step],
                gate_recv.at[step - 1],
                gate_send_sem.at[step - 1],
                gate_recv_sem.at[step - 1],
                "tensor",
                peer,
            )
            copy.start()
            gates.append(copy)
    hidden = hidden_ref[...]
    router = router_ref[...]
    logits = nt(router, hidden)
    exps = jnp.exp(logits - jnp.max(logits, axis=0, keepdims=True))
    probs = exps / jnp.sum(exps, axis=0, keepdims=True)
    ids = lax.broadcasted_iota(jnp.int32, (experts, own_rows), 0)
    own_lanes = pl.ds(pl.multiple_of(me_t * own_rows, own_rows), own_rows)
    first, second = ids == routes_ref[0:1, own_lanes], ids == routes_ref[1:2, own_lanes]
    prob_one = jnp.sum(jnp.where(first, probs, 0.0), axis=0, keepdims=True)
    prob_two = jnp.sum(jnp.where(second, probs, 0.0), axis=0, keepdims=True)
    both = prob_one + prob_two
    line.finish()
    for copy in gates:
        copy.wait()
    gate_sum = gate_send[0]
    for step in range(1, n_tensor):
        gate_sum = gate_sum + gate_recv[step - 1]
    grad_one, grad_two = gate_sum[0:1, :], gate_sum[1:2, :]
    mean_grad = (prob_one * grad_one + prob_two * grad_two) / both
    grad_probs = (
        jnp.where(first, grad_one - mean_grad, 0.0) + jnp.where(second, grad_two - mean_grad, 0.0)
    ) / both
    grad_logits = probs * (grad_probs - jnp.sum(grad_probs * probs, axis=0, keepdims=True))
    grad_hidden = total[...] + lax.dot_general(
        grad_logits,
        router.astype(F32),
        (((0,), (0,)), ((), ())),
        precision=lax.Precision.HIGHEST,
        preferred_element_type=F32,
    )
    residual = residual_ref[...]
    scale = lax.rsqrt(jnp.mean(residual * residual, axis=1, keepdims=True) + EPS)
    unit = residual * scale
    small_ref[...] = jnp.zeros_like(small_ref)
    small_ref[experts : experts + 1, :] = jnp.sum(grad_hidden * unit, axis=0, keepdims=True)
    grad_unit = grad_hidden * gain_ref[...]
    grad_residual = cotangent_ref[...].astype(F32) + scale * (
        grad_unit - unit * jnp.mean(grad_unit * unit, axis=1, keepdims=True)
    )
    grad_residual_ref[...] = grad_residual
    branch_ref[me_t] = grad_residual.astype(BF16)

    def on_block(block):
        grad_attended_ref[pl.ds(pl.multiple_of(block * own_rows, own_rows), own_rows), :] = nt(
            branch_ref[block], weight_ref[...]
        ).astype(BF16)

    lines = Streams(n_tensor, [branch_ref], gather_send_sem, gather_recv_sem)
    for turn in lines.turns():
        lines.turn(turn, lambda j, k: lines.each_new(j, k, on_block))
        if turn == n_tensor - 2:
            fetch.wait()
            for copy in values:
                copy.wait_recv()
            for block in range(n_tensor):
                rows = slice(block * own_rows, (block + 1) * own_rows)
                one, two = chosen_slots(slots_ref[rows, :], slots)
                merged_ref[rows, :] = nn(
                    jnp.where(one | two, 1.0, 0.0).astype(BF16), value_back[...].reshape(slots, width)
                ).astype(BF16)
    lines.drain()
    small_ref[0:experts, :] = jnp.dot(
        grad_logits,
        hidden.astype(F32),
        precision=lax.Precision.HIGHEST,
        preferred_element_type=F32,
    )
    line.drain()
    for copy in values:
        copy.wait_send()


def combine(
    n_dp,
    n_tensor,
    experts,
    rows,
    gates,
    slot_columns,
    routes_own,
    residual,
    hidden,
    cotangent,
    router_rows,
    gain,
    weight,
    value,
):
    own_rows, width = residual.shape
    slots = rows.shape[0]
    return pl.pallas_call(
        functools.partial(combine_kernel, n_dp, n_tensor, experts),
        out_shape=(
            jax.ShapeDtypeStruct((own_rows, width), F32),
            jax.ShapeDtypeStruct((n_tensor, own_rows, width), BF16),
            jax.ShapeDtypeStruct((n_tensor * own_rows, weight.shape[0]), BF16),
            jax.ShapeDtypeStruct((SMALL, width), F32),
            jax.ShapeDtypeStruct((n_tensor * own_rows, width), BF16),
        ),
        in_specs=[vspec()] * 10 + [any_spec()],
        out_specs=(vspec(),) * 5,
        scratch_shapes=[
            pltpu.VMEM((own_rows, width), F32),
            pltpu.VMEM((own_rows, width), F32),
            pltpu.VMEM((n_tensor - 1, own_rows, width), BF16),
            pltpu.VMEM((n_tensor + 1, own_rows, width), BF16),
            pltpu.VMEM((8, slots), F32),
            pltpu.VMEM((n_tensor, 8, own_rows), F32),
            pltpu.VMEM((n_tensor - 1, 8, own_rows), F32),
            pltpu.VMEM(value.shape, BF16),
            pltpu.SemaphoreType.DMA((n_tensor - 1,)),
            pltpu.SemaphoreType.DMA((n_tensor + 1,)),
            pltpu.SemaphoreType.DMA((n_tensor - 1,)),
            pltpu.SemaphoreType.DMA((n_tensor - 1,)),
            pltpu.SemaphoreType.DMA((n_dp - 1,)),
            pltpu.SemaphoreType.DMA((n_dp - 1,)),
            pltpu.SemaphoreType.DMA,
            pltpu.SemaphoreType.DMA((1, 2, n_tensor - 1)),
            pltpu.SemaphoreType.DMA((1, 2, n_tensor - 1)),
        ],
        compiler_params=pltpu.CompilerParams(
            vmem_limit_bytes=VMEM_LIMIT, collective_id=2, has_side_effects=True
        ),
        name="combine",
    )(
        rows,
        gates,
        slot_columns,
        routes_own,
        residual,
        hidden,
        cotangent,
        router_rows,
        gain,
        weight,
        value,
    )


class Streams:
    def __init__(self, n, refs, send_sem, recv_sem):
        self.n, self.refs, self.send_sem, self.recv_sem = n, refs, send_sem, recv_sem
        self.me = lax.axis_index("tensor")

    def copy(self, j, block, slot, k, peer):
        ref = self.refs[j].at[block]
        return remote(
            ref, ref, self.send_sem.at[j, slot, k], self.recv_sem.at[j, slot, k], "tensor", peer
        )

    def outgoing(self, j, k, fn):
        for slot, sign in enumerate((1, -1)):
            block, peer = self.me - sign * k, self.me + sign

            @pl.when((block >= 0) & (block < self.n) & (peer >= 0) & (peer < self.n))
            def _():
                fn(self.copy(j, block, slot, k, peer))

    def incoming(self, j, k, fn):
        for slot, sign in enumerate((1, -1)):
            block = self.me - sign * (k + 1)

            @pl.when((block >= 0) & (block < self.n))
            def _():
                fn(self.copy(j, block, slot, k, jnp.clip(self.me - sign, 0, self.n - 1)), block)

    def turn(self, turn, used=None):
        moved = []
        for j in range(len(self.refs)):
            k = turn - j
            if k < 0 or k > self.n - 1:
                continue
            if k > 0:
                self.incoming(j, k - 1, lambda c, block: c.wait_recv())
            if k < self.n - 1:
                self.outgoing(j, k, lambda c: c.start())
            moved.append((j, k))
        if used is not None:
            for j, k in moved:
                used(j, k)

    def turns(self):
        return range(self.n + len(self.refs) - 1)

    def each_new(self, j, k, fn):
        if k == 0:
            fn(self.me)
            return
        for sign in (1, -1):
            block = self.me - sign * k

            @pl.when((block >= 0) & (block < self.n))
            def _():
                fn(block)

    def drain(self):
        for j in range(len(self.refs)):
            for k in range(self.n - 1):
                self.outgoing(j, k, lambda c: c.wait_send())


class Spread:
    def __init__(self, n, ref, far_send, far_recv, near_send, near_recv):
        self.n, self.ref = n, ref
        self.far_send, self.far_recv = far_send, far_recv
        self.near_send, self.near_recv = near_send, near_recv
        self.me = lax.axis_index("dp")
        self.partner = self.me ^ 1

    def far(self, step, block, peer):
        ref = self.ref.at[block]
        return remote(ref, ref, self.far_send.at[step], self.far_recv.at[step], "dp", peer)

    def near(self, step, block):
        ref = self.ref.at[block]
        return remote(
            ref, ref, self.near_send.at[step], self.near_recv.at[step], "dp", self.partner
        )

    def start(self):
        for step in range(1, self.n // 2):
            self.far(step - 1, self.me, lax.rem(self.me + 2 * step, self.n)).start()
        self.near(0, self.me).start()

    def source(self, me, step):
        return lax.rem(me + self.n - 2 * step, self.n)

    def relay(self):
        for step in range(1, self.n // 2):
            block = self.source(self.me, step)
            self.far(step - 1, block, block).wait_recv()
            self.near(step, block).start()

    def finish(self):
        for step in range(self.n // 2):
            self.near(step, self.source(self.partner, step)).wait_recv()

    def drain(self):
        for step in range(1, self.n // 2):
            self.far(step - 1, self.me, lax.rem(self.me + 2 * step, self.n)).wait_send()
        for step in range(self.n // 2):
            self.near(step, self.source(self.me, step)).wait_send()


def peers_in_order(n):
    order = (6, 2, 4, 7, 3, 5, 1) if n == 8 else tuple(range(n - 1, 0, -1))
    return order + (0,)


def one_hot(slot_rows, target, per):
    lane_slots = lax.broadcasted_iota(jnp.int32, (per, 1), 0) + target * per
    return jnp.where(
        (lane_slots == slot_rows[0:1, :]) | (lane_slots == slot_rows[1:2, :]), 1.0, 0.0
    ).astype(BF16)


GRAD_PARTS = 4
GRAD_EARLY = 2


def band(seq_len):
    return -(-(seq_len // 2 - 1) // BS)


def front_kernel(n_dp, n_tensor, experts, capacity, fast, *refs):
    (tokens_ref, cotangent_ref, weight_ref, extra_ref, out_ref, routes_ref) = refs[:6]
    (segment_ref, selector_ref) = refs[6:8]
    refs = refs[8:]
    (hidden_ref, projected_ref, weights_ref, outs_ref) = refs[:4]
    (pattern_ref, router_ref, gains_ref) = refs[4:7]
    refs = refs[7:]
    if fast:
        (grad_rows_ref, slot_rows_ref, slot_columns_ref) = refs[:3]
        (attended_ref, lse_ref, late_ref) = refs[3:6]
        refs = refs[6:]
    (extras_ref, table) = refs[:2]
    refs = refs[2:]
    (
        extra_send,
        extra_recv,
        line_send,
        line_recv,
        weight_far_send,
        weight_far_recv,
        weight_near_send,
        weight_near_recv,
        out_far_send,
        out_far_recv,
        out_near_send,
        out_near_recv,
        stream_send,
        stream_recv,
    ) = refs[:14]
    refs = refs[14:]
    if fast:
        grads, picks, grad_send, bias, row_send, row_recv, row_own = refs
    own_rows, width = tokens_ref.shape
    seq_len = own_rows * n_tensor
    depth = extra_ref.shape[1]
    me = lax.axis_index("dp")
    me_t = lax.axis_index("tensor")
    per = experts // n_dp * capacity
    greet([("dp", n_dp), ("tensor", n_tensor)])
    extras_ref[me] = extra_ref[...]
    copies = []
    for step in range(1, n_dp):
        peer = lax.rem(me + step, n_dp)
        copy = remote(
            extra_ref, extras_ref.at[me], extra_send.at[step - 1], extra_recv.at[step - 1], "dp", peer
        )
        copy.start()
        copies.append(copy)
    streams = [hidden_ref]
    part = width // GRAD_PARTS
    if fast:
        for j in range(GRAD_PARTS):
            whole = grads.at[j] if j < GRAD_EARLY else late_ref.at[j - GRAD_EARLY]
            whole[me_t] = cotangent_ref[:, j * part : (j + 1) * part]
            streams.append(whole)
    lines = Streams(n_tensor, streams, stream_send, stream_recv)
    weights_ref[me] = weight_ref[...]
    weights = Spread(
        n_dp, weights_ref, weight_far_send, weight_far_recv, weight_near_send, weight_near_recv
    )
    weights.start()
    outs_ref[me, me_t] = out_ref[...]
    line_copies = []
    for step in range(1, n_tensor):
        peer = lax.rem(me_t + step, n_tensor)
        copy = remote(
            out_ref,
            outs_ref.at[me, me_t],
            line_send.at[step - 1],
            line_recv.at[step - 1],
            "tensor",
            peer,
        )
        copy.start()
        line_copies.append(copy)
    x = tokens_ref[...].astype(F32)
    scaled = x * lax.rsqrt(jnp.mean(x * x, axis=1, keepdims=True) + EPS)
    for copy in copies:
        copy.wait()
    for block in range(n_dp):
        gains_ref[0:2, block * depth : (block + 1) * depth] = extras_ref[
            block, experts : experts + 2, :
        ].astype(F32)
    hidden_ref[me_t] = (scaled * gains_ref[0:1, :]).astype(BF16)
    lines.turn(0)
    rows_each = NB // n_dp
    for block in range(n_dp):
        router_ref[:, block * depth : (block + 1) * depth] = extras_ref[block, 0:experts, :]
        table[block * rows_each : (block + 1) * rows_each, :] = extras_ref[
            block, experts + 2 : experts + 2 + rows_each, :
        ].astype(F32)
    patterns = lax.dot_general(
        table[...],
        selector_ref[...],
        (((0,), (0,)), ((), ())),
        precision=lax.Precision.HIGHEST,
        preferred_element_type=F32,
    )
    for row in range(pattern_ref.shape[0]):
        pattern_ref[row : row + 1, :] = patterns[
            row // 2 : row // 2 + 1, (row % 2) * 2 * BS : (row % 2 + 1) * 2 * BS
        ]

    if fast:
        ids = lax.broadcasted_iota(jnp.int32, (experts, seq_len), 0)
        hits = [ids == routes_ref[k : k + 1, :] for k in range(TOP)]
        before = lax.broadcasted_iota(jnp.int32, (seq_len, seq_len), 0) < lax.broadcasted_iota(
            jnp.int32, (seq_len, seq_len), 1
        )
        ranks = nn(
            jnp.where(hits[0] | hits[1], 1.0, 0.0).astype(BF16),
            jnp.where(before, 1.0, 0.0).astype(BF16),
        )
        places = ranks + (ids * capacity).astype(F32)
        slot_rows_ref[...] = jnp.zeros_like(slot_rows_ref)
        for k in range(TOP):
            row = jnp.sum(jnp.where(hits[k], places, 0.0), axis=0, keepdims=True)
            slot_rows_ref[k : k + 1, :] = row.astype(jnp.int32)
            for block in range(n_tensor):
                rows = slice(block * own_rows, (block + 1) * own_rows)
                slot_columns_ref[rows, k : k + 1] = to_column(row[:, rows]).astype(jnp.int32)
        for target in range(n_dp):
            picks[target] = one_hot(slot_rows_ref, target, per)

    def row_copy(j, target, sender):
        cols = slice(j * part, (j + 1) * part)
        return remote(
            grad_send.at[j, target],
            grad_rows_ref.at[sender, :, cols],
            row_send.at[j, target],
            row_recv.at[j, sender],
            "dp",
            target,
        )

    def own_row_copy(j):
        cols = slice(j * part, (j + 1) * part)
        return pltpu.make_async_copy(
            grad_send.at[j, me], grad_rows_ref.at[me, :, cols], row_own.at[j]
        )

    def project(block):
        rows = pl.ds(pl.multiple_of(block * own_rows, own_rows), own_rows)
        projected_ref[rows, :] = nn(
            hidden_ref[block], weights_ref[...].reshape(width, weights_ref.shape[2])
        ).astype(BF16)

    def used(j, k):
        if j == 0:
            if k > 0:
                if k == 1:
                    weights.finish()
                    lines.each_new(j, 0, project)
                lines.each_new(j, k, project)
        elif k == n_tensor - 1 and j - 1 < GRAD_EARLY:
            values = grads[j - 1].reshape(seq_len, part)
            for mask in peers_in_order(n_dp):
                target = me ^ mask
                grad_send[j - 1, target] = nn(picks[target], values).astype(BF16)
                if mask:
                    row_copy(j - 1, target, me).start()
                else:
                    own_row_copy(j - 1).start()

    weights.relay()
    for copy in line_copies:
        copy.wait_recv()
    spread = Spread(n_dp, outs_ref, out_far_send, out_far_recv, out_near_send, out_near_recv)
    spread.start()
    if fast:
        build_bias(pattern_ref.shape[0] // 2, pattern_ref, bias)
    blocks = seq_len // BS
    done = 0
    for turn in lines.turns():
        if turn == 0:
            continue
        lines.turn(turn, used)
        if turn == 2:
            spread.relay()
        if fast and turn >= n_tensor - 1:
            while done < blocks and done <= turn - (n_tensor - 1):
                forward_rows(
                    pattern_ref.shape[0] // 2,
                    done,
                    max(0, done - band(seq_len)),
                    projected_ref,
                    segment_ref,
                    bias,
                    attended_ref,
                    lse_ref,
                )
                done += 1
    if fast:
        assert done == blocks
    if n_tensor < 3:
        spread.relay()
    spread.finish()
    lines.drain()
    weights.drain()
    spread.drain()
    for copy in line_copies:
        copy.wait_send()
    if fast:
        for j in range(GRAD_EARLY):
            own_row_copy(j).wait()
            for step in range(1, n_dp):
                peer = lax.rem(me + step, n_dp)
                row_copy(j, peer, me).wait_send()
                row_copy(j, me, peer).wait_recv()


def front(
    n_dp,
    n_tensor,
    experts,
    capacity,
    fast,
    tokens,
    cotangent,
    weight,
    extra,
    out,
    routes,
    segments,
    selectors,
):
    own_rows, width = tokens.shape
    seq_len = own_rows * n_tensor
    depth, cols = weight.shape
    per = experts // n_dp * capacity
    part = width // GRAD_PARTS
    heads = cols // (3 * HD)
    shapes = [
        jax.ShapeDtypeStruct((n_tensor, own_rows, width), BF16),
        jax.ShapeDtypeStruct((seq_len, cols), BF16),
        jax.ShapeDtypeStruct((n_dp, depth, cols), BF16),
        jax.ShapeDtypeStruct((n_dp, n_tensor) + out.shape, BF16),
        jax.ShapeDtypeStruct((2 * heads, 2 * BS), F32),
        jax.ShapeDtypeStruct((experts, width), BF16),
        jax.ShapeDtypeStruct((2, width), F32),
    ]
    specs = [vspec()] * 7
    dma = pltpu.SemaphoreType.DMA
    streams = 1 + (GRAD_PARTS if fast else 0)
    half = n_dp // 2
    scratch = (
        [pltpu.VMEM((n_dp,) + extra.shape, BF16), pltpu.VMEM((NB, depth), F32)]
        + [dma((n_dp - 1,))] * 2
        + [dma((n_tensor - 1,))] * 2
        + ([dma((half,))] * 4) * 2
        + [dma((streams, 2, n_tensor - 1))] * 2
    )
    if fast:
        shapes += [
            jax.ShapeDtypeStruct((n_dp, per, GRAD_EARLY * part), BF16),
            jax.ShapeDtypeStruct((8, seq_len), jnp.int32),
            jax.ShapeDtypeStruct((seq_len, TOP), jnp.int32),
            jax.ShapeDtypeStruct((seq_len, heads * HD), BF16),
            jax.ShapeDtypeStruct((seq_len, heads), F32),
            jax.ShapeDtypeStruct((GRAD_PARTS - GRAD_EARLY, n_tensor, own_rows, part), BF16),
        ]
        specs += [any_spec()] + [vspec()] * 5
        scratch += [
            pltpu.VMEM((GRAD_EARLY, n_tensor, own_rows, part), BF16),
            pltpu.VMEM((n_dp, per, seq_len), BF16),
            pltpu.VMEM((GRAD_EARLY, n_dp, per, part), BF16),
            pltpu.VMEM((heads, 3, BS, BS), F32),
            dma((GRAD_EARLY, n_dp)),
            dma((GRAD_EARLY, n_dp)),
            dma((GRAD_EARLY,)),
        ]
    return pl.pallas_call(
        functools.partial(front_kernel, n_dp, n_tensor, experts, capacity, fast),
        out_shape=tuple(shapes),
        in_specs=[vspec()] * 8,
        out_specs=tuple(specs),
        scratch_shapes=scratch,
        compiler_params=pltpu.CompilerParams(
            vmem_limit_bytes=VMEM_LIMIT, collective_id=3, has_side_effects=True
        ),
        name="front",
    )(tokens, cotangent, weight, extra, out, routes, segments, selectors)


PARTS = 4


def middle_kernel(
    n_dp,
    n_tensor,
    experts,
    capacity,
    attended_ref,
    outs_ref,
    tokens_ref,
    gain_ref,
    router_ref,
    slots_ref,
    routes_ref,
    late_ref,
    residual_ref,
    hidden_ref,
    weight_own_ref,
    rows_ref,
    gates_ref,
    grad_rows_ref,
    out_matrix,
    attended_recv,
    everyone,
    picks,
    row_stage,
    grad_stage,
    logits,
    gate_stage,
    attended_send_sem,
    attended_recv_sem,
    stream_send,
    stream_recv,
    row_send,
    row_recv,
    row_own,
    grad_send,
    grad_recv,
    grad_own,
    gate_send,
    gate_recv,
):
    own_rows, width = tokens_ref.shape
    seq_len = own_rows * n_tensor
    head_cols = attended_ref.shape[1]
    out_cols = outs_ref.shape[2]
    local = experts // n_dp
    per = local * capacity
    part = width // PARTS
    me = lax.axis_index("dp")
    me_t = lax.axis_index("tensor")
    greet([("dp", n_dp), ("tensor", n_tensor)])

    def rows_of(block):
        return pl.ds(pl.multiple_of(block * own_rows, own_rows), own_rows)

    copies = []
    for step in range(1, n_tensor):
        peer = lax.rem(me_t + step, n_tensor)
        copy = remote(
            attended_ref.at[rows_of(peer)],
            attended_recv.at[me_t],
            attended_send_sem.at[step - 1],
            attended_recv_sem.at[step - 1],
            "tensor",
            peer,
        )
        copy.start()
        copies.append(copy)
    attended_recv[me_t] = attended_ref[rows_of(me_t), :]
    for block in range(n_dp):
        out_matrix[:, block * out_cols : (block + 1) * out_cols] = outs_ref[block]
    weight_own_ref[...] = out_matrix[
        pl.ds(pl.multiple_of(me_t * head_cols, head_cols), head_cols), :
    ]
    def grad_copy(j, target, sender):
        cols = slice(j * part, (j + 1) * part)
        return remote(
            grad_stage.at[j, target],
            grad_rows_ref.at[sender, :, cols],
            grad_send.at[j, target],
            grad_recv.at[j, sender],
            "dp",
            target,
        )

    def own_grad_copy(j):
        cols = slice(j * part, (j + 1) * part)
        return pltpu.make_async_copy(
            grad_stage.at[j, me], grad_rows_ref.at[me, :, cols], grad_own.at[j]
        )

    late = late_ref.shape[0]
    for mask in peers_in_order(n_dp):
        target = me ^ mask
        picks[target] = one_hot(slots_ref, target, per)
        for j in range(late):
            grad_stage[j, target] = nn(
                picks[target], late_ref[j].reshape(seq_len, part)
            ).astype(BF16)
            if mask:
                grad_copy(j, target, me).start()
            else:
                own_grad_copy(j).start()
    for copy in copies:
        copy.wait_recv()
    residual = tokens_ref[...].astype(F32)
    for block in range(n_tensor):
        residual += nn(
            attended_recv[block], out_matrix[block * head_cols : (block + 1) * head_cols, :]
        )
    residual_ref[...] = residual
    hidden = (
        residual
        * lax.rsqrt(jnp.mean(residual * residual, axis=1, keepdims=True) + EPS)
        * gain_ref[...]
    ).astype(BF16)
    hidden_ref[...] = hidden
    for j in range(PARTS):
        everyone[j, me_t] = hidden[:, j * part : (j + 1) * part]
    lines = Streams(n_tensor, [everyone.at[j] for j in range(PARTS)], stream_send, stream_recv)

    def row_copy(j, target, sender):
        cols = slice(j * part, (j + 1) * part)
        return remote(
            row_stage.at[j, target],
            rows_ref.at[sender, :, cols],
            row_send.at[j, target],
            row_recv.at[j, sender],
            "dp",
            target,
        )

    def own_row_copy(j):
        cols = slice(j * part, (j + 1) * part)
        return pltpu.make_async_copy(row_stage.at[j, me], rows_ref.at[me, :, cols], row_own.at[j])

    def used(j, k):
        if k < n_tensor - 1:
            return
        values = everyone[j].reshape(seq_len, part)
        for mask in peers_in_order(n_dp):
            target = me ^ mask
            row_stage[j, target] = nn(picks[target], values).astype(BF16)
            if mask:
                row_copy(j, target, me).start()
            else:
                own_row_copy(j).start()
        term = nt(router_ref[:, j * part : (j + 1) * part], values)
        if j == 0:
            logits[...] = term
        else:
            logits[...] += term

    for turn in lines.turns():
        lines.turn(turn, used)
    values = logits[...]
    exps = jnp.exp(values - jnp.max(values, axis=0, keepdims=True))
    probs = exps / jnp.sum(exps, axis=0, keepdims=True)
    ids = lax.broadcasted_iota(jnp.int32, (experts, seq_len), 0)
    named = (ids == routes_ref[0:1, :]) | (ids == routes_ref[1:2, :])
    shares = probs / jnp.sum(jnp.where(named, probs, 0.0), axis=0, keepdims=True)
    gate_copies = []
    for mask in peers_in_order(n_dp):
        target = me ^ mask
        for expert in range(local):
            row = jnp.sum(
                jnp.where(ids == target * local + expert, shares, 0.0), axis=0, keepdims=True
            )
            high = row.astype(BF16)
            rest = row - high.astype(F32)
            mid = rest.astype(BF16)
            low = (rest - mid.astype(F32)).astype(BF16)
            lanes = slice(expert * capacity, (expert + 1) * capacity)
            pieces = nt(
                jnp.concatenate([high, mid, low, jnp.zeros((5, seq_len), BF16)], axis=0),
                picks[target, lanes, :],
            )
            gate_stage[target, :, lanes] = jnp.broadcast_to(
                jnp.sum(pieces, axis=0, keepdims=True), (8, capacity)
            )
        if mask:
            copy = remote(
                gate_stage.at[target],
                gates_ref.at[me],
                gate_send.at[target],
                gate_recv.at[me],
                "dp",
                target,
            )
            copy.start()
            gate_copies.append(copy)
        else:
            gates_ref[me] = gate_stage[me]
    lines.drain()
    for copy in copies:
        copy.wait_send()
    for copy in gate_copies:
        copy.wait_send()
    for step in range(1, n_dp):
        peer = lax.rem(me + step, n_dp)
        remote(
            gate_stage.at[me], gates_ref.at[peer], gate_send.at[me], gate_recv.at[peer], "dp", peer
        ).wait_recv()
    for j in range(late):
        own_grad_copy(j).wait()
        for step in range(1, n_dp):
            peer = lax.rem(me + step, n_dp)
            grad_copy(j, peer, me).wait_send()
            grad_copy(j, me, peer).wait_recv()
    for j in range(PARTS):
        own_row_copy(j).wait()
        for step in range(1, n_dp):
            peer = lax.rem(me + step, n_dp)
            row_copy(j, peer, me).wait_send()
            row_copy(j, me, peer).wait_recv()


def middle(
    n_dp,
    n_tensor,
    experts,
    capacity,
    attended,
    outs,
    tokens,
    gain,
    router_rows,
    slot_rows,
    routes,
    late,
):
    own_rows, width = tokens.shape
    seq_len, head_cols = attended.shape
    per = experts // n_dp * capacity
    part = width // PARTS
    dma = pltpu.SemaphoreType.DMA
    return pl.pallas_call(
        functools.partial(middle_kernel, n_dp, n_tensor, experts, capacity),
        out_shape=(
            jax.ShapeDtypeStruct((own_rows, width), F32),
            jax.ShapeDtypeStruct((own_rows, width), BF16),
            jax.ShapeDtypeStruct((head_cols, width), BF16),
            jax.ShapeDtypeStruct((n_dp, per, width), BF16),
            jax.ShapeDtypeStruct((n_dp, 8, per), F32),
            jax.ShapeDtypeStruct((n_dp, per, late.shape[0] * part), BF16),
        ),
        in_specs=[vspec()] * 8,
        out_specs=(vspec(), vspec(), vspec(), any_spec(), vspec(), any_spec()),
        scratch_shapes=[
            pltpu.VMEM((width, width), BF16),
            pltpu.VMEM((n_tensor, own_rows, head_cols), BF16),
            pltpu.VMEM((PARTS, n_tensor, own_rows, part), BF16),
            pltpu.VMEM((n_dp, per, seq_len), BF16),
            pltpu.VMEM((PARTS, n_dp, per, part), BF16),
            pltpu.VMEM((late.shape[0], n_dp, per, part), BF16),
            pltpu.VMEM((experts, seq_len), F32),
            pltpu.VMEM((n_dp, 8, per), F32),
            dma((n_tensor - 1,)),
            dma((n_tensor - 1,)),
            dma((PARTS, 2, n_tensor - 1)),
            dma((PARTS, 2, n_tensor - 1)),
            dma((PARTS, n_dp)),
            dma((PARTS, n_dp)),
            dma((PARTS,)),
            dma((late.shape[0], n_dp)),
            dma((late.shape[0], n_dp)),
            dma((late.shape[0],)),
            dma((n_dp,)),
            dma((n_dp,)),
        ],
        compiler_params=pltpu.CompilerParams(
            vmem_limit_bytes=VMEM_LIMIT, collective_id=4, has_side_effects=True
        ),
        name="middle",
    )(attended, outs, tokens, gain, router_rows, slot_rows, routes, late)


def last_kernel(
    n_dp,
    n_tensor,
    experts,
    heads,
    qkv_ref,
    attended_ref,
    grad_attended_ref,
    lse_ref,
    segment_ref,
    pattern_ref,
    skew_ref,
    hidden_ref,
    weight_ref,
    branch_ref,
    small_ref,
    weight_own_ref,
    gain_own_ref,
    merged_ref,
    residual_ref,
    grad_residual_ref,
    tokens_ref,
    gain_ref,
    layer_ref,
    grad_tokens_ref,
    grad_weight_ref,
    grad_out_ref,
    small_out_ref,
    bias,
    dk,
    dv,
    sums,
    grad_qkv,
    diag,
    acc,
    mixture,
    grad_hidden,
    mix_send,
    mix_recv,
    line_send,
    line_recv,
    qkv_send,
    qkv_recv,
    out_send,
    out_recv,
    small_send,
    small_recv,
    small_sum,
    gain_recv,
    mix_send_sem,
    mix_recv_sem,
    line_send_sem,
    line_recv_sem,
    qkv_send_sem,
    qkv_recv_sem,
    out_send_sem,
    out_recv_sem,
    small_send_sem,
    small_recv_sem,
    gain_send_sem,
    gain_recv_sem,
):
    own_rows, width = residual_ref.shape
    seq_len = own_rows * n_tensor
    depth = weight_own_ref.shape[0]
    out_cols = grad_out_ref.shape[1]
    me = lax.axis_index("dp")
    me_t = lax.axis_index("tensor")
    greet([("dp", n_dp), ("tensor", n_tensor)])

    def rows_of(block):
        return pl.ds(pl.multiple_of(block * own_rows, own_rows), own_rows)

    mix = LineSum(
        n_tensor,
        lambda block: merged_ref[rows_of(block), :].astype(F32),
        mix_send,
        mix_recv,
        mix_send_sem,
        mix_recv_sem,
        acc,
        mixture,
    )
    line = LineSum(
        n_tensor,
        lambda block: nt(grad_qkv[rows_of(block), :], weight_ref[...]),
        line_send,
        line_recv,
        line_send_sem,
        line_recv_sem,
        acc,
        grad_hidden,
    )
    copies = []

    def scatter(source, target, send_sem, recv_sem):
        for step in range(1, n_dp):
            peer = lax.rem(me + step, n_dp)
            copy = remote(
                source.at[peer],
                target.at[step - 1],
                send_sem.at[step - 1],
                recv_sem.at[step - 1],
                "dp",
                peer,
            )
            copy.start()
            copies.append(copy)

    mix.start()
    build_bias(heads, pattern_ref, bias)
    backward_start(dk, dv, sums)
    blocks = seq_len // BS
    for qb in range(blocks):
        backward_rows(
            heads,
            qb,
            max(0, qb - band(seq_len)),
            qkv_ref,
            attended_ref,
            grad_attended_ref,
            lse_ref,
            segment_ref,
            bias,
            grad_qkv,
            dk,
            dv,
            sums,
        )
        if qb == 0:
            for block in range(n_dp):
                cols = slice(block * out_cols, (block + 1) * out_cols)
                out_send[block] = tn(attended_ref[...], branch_ref[:, cols]).astype(BF16)
            scatter(out_send, out_recv, out_send_sem, out_recv_sem)
        if qb >= blocks - 2 and qb - (blocks - 2) < n_tensor - 1:
            mix.step(qb - (blocks - 2))
    backward_end(heads, grad_qkv, dk, dv)
    line.start()
    for k in range(2, n_tensor - 1):
        mix.step(k)
    for block in range(n_dp):
        cols = slice(block * depth, (block + 1) * depth)
        qkv_send[block] = tn(hidden_ref[:, cols], grad_qkv[...]).astype(BF16)
    scatter(qkv_send, qkv_recv, qkv_send_sem, qkv_recv_sem)
    diag[...] = jnp.zeros_like(diag)
    diagonal_sums(heads, sums, diag)
    tables = lax.dot_general(
        skew_ref[...],
        jnp.concatenate([diag[0], diag[1]], axis=1),
        (((1,), (1,)), ((), ())),
        precision=lax.Precision.HIGHEST,
        preferred_element_type=F32,
    )
    far = jnp.sum(diag[2], axis=1, keepdims=True)
    head = lax.broadcasted_iota(jnp.int32, (8, 8), 0)
    lane = lax.broadcasted_iota(jnp.int32, (8, 8), 1)
    far_row = jnp.sum(jnp.where(head == lane, far, 0.0), axis=0, keepdims=True)
    bucket = lax.broadcasted_iota(jnp.int32, (NB, 8), 0)
    tables += jnp.where(bucket == NB - 1, far_row, 0.0)
    rows_each = NB // n_dp
    for block in range(n_dp):
        small_send[block] = small_ref[:, block * depth : (block + 1) * depth]
        small_send[block, experts + 2 : experts + 2 + rows_each, 0:8] = tables[
            block * rows_each : (block + 1) * rows_each, :
        ]
    scatter(small_send, small_recv, small_send_sem, small_recv_sem)
    layer_ref[...] = (residual_ref[...] + mixture[...]).astype(BF16)
    for k in range(n_tensor - 2):
        line.step(k)
    for copy in copies:
        copy.wait_recv()
    small_sum[...] = small_send[me]
    grad_weight_ref[...] = qkv_send[me].astype(F32)
    grad_out_ref[...] = out_send[me].astype(F32)
    for step in range(1, n_dp):
        small_sum[...] += small_recv[step - 1]
        grad_weight_ref[...] += qkv_recv[step - 1].astype(F32)
        grad_out_ref[...] += out_recv[step - 1].astype(F32)
    column = jnp.sum(grad_weight_ref[...] * weight_own_ref[...].astype(F32), axis=1, keepdims=True)
    small_sum[experts + 1 : experts + 2, :] = to_row(column) / gain_own_ref[...]
    gains = []
    for step in range(1, n_tensor):
        peer = lax.rem(me_t + step, n_tensor)
        copy = remote(
            small_sum,
            gain_recv.at[step - 1],
            gain_send_sem.at[step - 1],
            gain_recv_sem.at[step - 1],
            "tensor",
            peer,
        )
        copy.start()
        gains.append(copy)
    line.step(n_tensor - 2)
    x = tokens_ref[...].astype(F32)
    scale = lax.rsqrt(jnp.mean(x * x, axis=1, keepdims=True) + EPS)
    unit = x * scale
    grad_unit = grad_hidden[...] * gain_ref[...]
    grad_tokens_ref[...] = (
        grad_residual_ref[...]
        + scale * (grad_unit - unit * jnp.mean(grad_unit * unit, axis=1, keepdims=True))
    ).astype(BF16)
    mix.drain()
    line.drain()
    for copy in copies:
        copy.wait_send()
    for copy in gains:
        copy.wait()
    small_out_ref[...] = small_sum[...]
    shared = slice(0, experts + 2)
    for step in range(1, n_tensor):
        small_out_ref[shared, :] += gain_recv[step - 1, shared, :]


def last(
    n_dp,
    n_tensor,
    experts,
    heads,
    projected,
    attended,
    grad_attended,
    lse,
    segments,
    patterns,
    skew,
    hidden,
    weight,
    branch,
    small,
    weight_own,
    gain_own,
    merged,
    residual,
    grad_residual,
    tokens,
    gain,
):
    seq_len, width = hidden.shape
    own_rows = seq_len // n_tensor
    depth, cols = weight_own.shape
    out_cols = width // n_dp
    dma = pltpu.SemaphoreType.DMA
    line = [
        pltpu.VMEM((n_tensor - 1, own_rows, width), BF16),
        pltpu.VMEM((n_tensor + 1, own_rows, width), BF16),
    ]
    return pl.pallas_call(
        functools.partial(last_kernel, n_dp, n_tensor, experts, heads),
        out_shape=(
            jax.ShapeDtypeStruct((own_rows, width), BF16),
            jax.ShapeDtypeStruct((own_rows, width), BF16),
            jax.ShapeDtypeStruct((depth, cols), F32),
            jax.ShapeDtypeStruct((heads * HD, out_cols), F32),
            jax.ShapeDtypeStruct((SMALL, depth), F32),
        ),
        in_specs=[vspec()] * 18,
        out_specs=(vspec(),) * 5,
        scratch_shapes=backward_scratch(heads, seq_len)
        + [
            pltpu.VMEM((seq_len, cols), BF16),
            pltpu.VMEM((3, 8, 2 * BS), F32),
        ]
        + [pltpu.VMEM((own_rows, width), F32)] * 3
        + line * 2
        + [
            pltpu.VMEM((n_dp, depth, cols), BF16),
            pltpu.VMEM((n_dp - 1, depth, cols), BF16),
            pltpu.VMEM((n_dp, heads * HD, out_cols), BF16),
            pltpu.VMEM((n_dp - 1, heads * HD, out_cols), BF16),
            pltpu.VMEM((n_dp, SMALL, depth), F32),
            pltpu.VMEM((n_dp - 1, SMALL, depth), F32),
            pltpu.VMEM((SMALL, depth), F32),
            pltpu.VMEM((n_tensor - 1, SMALL, depth), F32),
        ]
        + [dma((n_tensor - 1,)), dma((n_tensor + 1,))] * 2
        + [dma((n_dp - 1,))] * 6
        + [dma((n_tensor - 1,))] * 2,
        compiler_params=pltpu.CompilerParams(
            vmem_limit_bytes=VMEM_LIMIT, collective_id=5, has_side_effects=True
        ),
        name="last",
    )(
        projected,
        attended,
        grad_attended,
        lse,
        segments,
        patterns,
        skew,
        hidden,
        weight,
        branch,
        small,
        weight_own,
        gain_own,
        merged,
        residual,
        grad_residual,
        tokens,
        gain,
    )


def rms_scale(values):
    return lax.rsqrt(jnp.mean(values * values, axis=-1, keepdims=True) + EPS)


def norm_backward(grad_normed, values, scale_inv, gain):
    normed_unit = values * scale_inv
    grad_unit = grad_normed * gain
    grad_values = scale_inv * (
        grad_unit - normed_unit * jnp.mean(grad_unit * normed_unit, axis=-1, keepdims=True)
    )
    return (grad_values, jnp.sum(grad_normed * normed_unit, axis=0))


def gelu_tanh(values):
    return jax.nn.gelu(values, approximate=True)


def route_slots(route_ids, experts, capacity):
    flat_routes = route_ids.reshape(-1)
    onehot = (flat_routes[:, None] == jnp.arange(experts, dtype=jnp.int32)[None, :]).astype(
        jnp.int32
    )
    ranks = jnp.cumsum(onehot, axis=0) - 1
    rank_own = jnp.sum(ranks * onehot, axis=1)
    return (flat_routes * capacity + rank_own).reshape(-1, TOP)


def on_device(
    tokens,
    segments,
    routes,
    w_qkv,
    w_attn_out,
    bias_table,
    gain_attn,
    gain_moe,
    router,
    w_in,
    w_out,
    cotangent,
):
    own_rows, model_width = tokens.shape
    n_tensor = lax.axis_size("tensor")
    n_dp = lax.axis_size("dp")
    seq_len = own_rows * n_tensor
    own_start = lax.axis_index("tensor") * own_rows
    head_cols = w_qkv.shape[2]
    heads = head_cols // HD
    experts = router.shape[1]
    local_experts = w_in.shape[0]
    capacity = 5 * seq_len * TOP // (4 * experts)
    highest = lax.Precision.HIGHEST
    slots = experts * capacity

    depth = w_qkv.shape[0]
    bias_rows = NB // n_dp
    lanes = depth
    extra = jnp.concatenate(
        [
            jnp.transpose(router),
            gain_attn[None],
            gain_moe[None],
            jnp.pad(bias_table, ((0, SMALL - experts - 2 - bias_rows), (0, lanes - heads))),
        ],
        axis=0,
    )
    fast = n_dp == 8 and slots * model_width <= 4 * 1024 * 1024
    route_rows = jnp.pad(jnp.transpose(routes), ((0, 8 - TOP), (0, 0)))
    gathered, projected, weights_full, outs_full, patterns, router_rows, gains, *routed = front(
        n_dp,
        n_tensor,
        experts,
        capacity,
        fast,
        tokens,
        cotangent,
        w_qkv.reshape(depth, 3 * head_cols),
        extra,
        w_attn_out,
        route_rows,
        segments,
        jnp.asarray(distance_selectors().T),
    )
    gathered_one = gathered.reshape(seq_len, model_width)
    qkv_matrix = weights_full.reshape(model_width, 3 * head_cols)
    outs_full = outs_full.reshape(n_dp, model_width, model_width // n_dp)
    weight_shard = w_qkv.reshape(depth, 3 * head_cols)
    gain_shard = gain_attn[None].astype(F32)
    skew = jnp.asarray(skew_selectors().T)

    def finish(layer_out, grad_tokens, reduced_qkv, reduced_attn_out, small_sum, grad_w_in, grad_w_out):
        return (
            layer_out,
            grad_tokens,
            reduced_qkv.reshape(depth, 3, head_cols),
            reduced_attn_out,
            small_sum[experts + 2 : experts + 2 + NB // n_dp, :heads],
            small_sum[experts + 1],
            small_sum[experts],
            jnp.transpose(small_sum[:experts]),
            grad_w_in,
            grad_w_out,
        )

    if fast:
        grad_rows, slot_rows, slot_columns, attended, lse, late = routed
        residual, hidden_two, weight_own, rows, row_gates, late_rows = middle(
            n_dp,
            n_tensor,
            experts,
            capacity,
            attended,
            outs_full,
            tokens,
            gains[1:2],
            router_rows,
            slot_rows,
            route_rows,
            late,
        )
        back, gate_back, value, grad_w_in, grad_w_out = run_experts(
            n_dp, capacity, rows, grad_rows, late_rows, row_gates, w_in, w_out
        )
        grad_residual, grad_branch_all, grad_attended, small, merged = combine(
            n_dp,
            n_tensor,
            experts,
            back.reshape(slots, model_width),
            gate_back,
            slot_columns,
            route_rows,
            residual,
            hidden_two,
            cotangent,
            router_rows,
            gains[1:2],
            weight_own,
            value,
        )
        results = last(
            n_dp,
            n_tensor,
            experts,
            heads,
            projected,
            attended,
            grad_attended,
            lse,
            segments,
            patterns,
            skew,
            gathered_one,
            qkv_matrix,
            grad_branch_all.reshape(seq_len, model_width),
            small,
            weight_shard,
            gain_shard,
            merged,
            residual,
            grad_residual,
            tokens,
            gains[0:1],
        )
        return finish(*results, grad_w_in, grad_w_out)
    tokens_float = tokens.astype(F32)
    scale_one = rms_scale(tokens_float)
    gain_one, gain_two = gains[0], gains[1]
    starts = segments[0, ::BS]
    ends = segments[0, BS - 1 :: BS]
    lowest = jnp.sum((ends[None, :] < starts[:, None]).astype(jnp.int32), axis=1)
    attended, lse = attention_forward(projected, lowest, segments, patterns, heads)
    router_full = jnp.transpose(router_rows)
    out_matrix = jnp.transpose(outs_full, (1, 0, 2)).reshape(model_width, model_width)
    attended_own = lax.all_to_all(
        attended.reshape(n_tensor, own_rows, head_cols), "tensor", 0, 0
    )
    attended_own = jnp.transpose(attended_own, (1, 0, 2)).reshape(own_rows, n_tensor * head_cols)
    branch = jnp.dot(attended_own, out_matrix, preferred_element_type=F32)
    residual = tokens_float + branch
    scale_two = rms_scale(residual)
    hidden_two = (residual * scale_two * gain_two).astype(BF16)
    gathered_two = lax.all_gather(hidden_two, "tensor", axis=0, tiled=True)

    expert_ids = jnp.arange(experts, dtype=jnp.int32)

    def gate_values(logit_values, route_rows):
        expert_probs = jax.nn.softmax(logit_values, axis=-1)
        picked = jnp.sum(
            jnp.where(
                route_rows[:, :, None] == expert_ids[None, None, :], expert_probs[:, None, :], 0.0
            ),
            axis=-1,
        )
        return picked / jnp.sum(picked, axis=1, keepdims=True)

    gates = gate_values(jnp.dot(gathered_two, router_full, preferred_element_type=F32), routes)
    slot_ids = route_slots(routes, experts, capacity)
    slot_flat = slot_ids.reshape(-1)
    token_ids = jnp.repeat(jnp.arange(seq_len, dtype=jnp.int32), TOP)
    sources = jnp.full((slots,), seq_len, jnp.int32).at[slot_flat].set(token_ids)
    slot_gates = jnp.zeros((slots,), F32).at[slot_flat].set(gates.reshape(-1))
    grad_gathered = lax.all_gather(cotangent, "tensor", axis=0, tiled=True)

    def exchange(rows):
        parts = rows.reshape(n_dp, local_experts, capacity, model_width)
        return [
            lax.all_to_all(parts[:, i], "dp", 0, 0).reshape(n_dp * capacity, model_width)
            for i in range(local_experts)
        ]

    def give_back(parts):
        back = [
            lax.all_to_all(part.reshape(n_dp, capacity, model_width), "dp", 0, 0) for part in parts
        ]
        return jnp.stack(back, axis=1).reshape(slots, model_width)

    zero_row = jnp.zeros((1, model_width), BF16)
    dispatched = exchange(jnp.concatenate([gathered_two, zero_row], axis=0)[sources])
    padded_grad = jnp.concatenate([grad_gathered, zero_row], axis=0)
    grad_expert = exchange((slot_gates[:, None] * padded_grad[sources]).astype(BF16))

    outs, backs, grads_in, grads_out = [], [], [], []
    for i in range(local_experts):
        rows, grad_rows = dispatched[i], grad_expert[i]
        gate_part = nt(rows, w_in[i, 0])
        up_part = nt(rows, w_in[i, 1])
        gelu_value, gelu_pull = jax.vjp(gelu_tanh, gate_part)
        activated = (gelu_value * up_part).astype(BF16)
        outs.append(nn(activated, w_out[i]).astype(BF16))
        grad_act = nt(grad_rows, w_out[i])
        grads_out.append(tn(activated, grad_rows))
        grad_gate = gelu_pull(grad_act * up_part)[0].astype(BF16)
        grad_up = (grad_act * gelu_value).astype(BF16)
        backs.append((nn(grad_gate, w_in[i, 0]) + nn(grad_up, w_in[i, 1])).astype(BF16))
        grads_in.append(jnp.stack([tn(grad_gate, rows), tn(grad_up, rows)]))
    grad_w_in = jnp.stack(grads_in)
    grad_w_out = jnp.stack(grads_out)
    expert_out = give_back(outs)
    grad_dispatched = give_back(backs)

    first, second = slot_ids[:, 0], slot_ids[:, 1]
    picked_first = expert_out[first].astype(F32)
    picked_second = expert_out[second].astype(F32)
    mixture = lax.psum_scatter(
        (gates[:, 0:1] * picked_first + gates[:, 1:2] * picked_second).astype(BF16),
        "tensor",
        scatter_dimension=0,
        tiled=True,
    ).astype(F32)
    layer_out = (residual + mixture).astype(BF16)
    grad_float = grad_gathered.astype(F32)
    grad_gate_part = jnp.stack(
        [
            jnp.sum(grad_float * picked_first, axis=1),
            jnp.sum(grad_float * picked_second, axis=1),
        ],
        axis=1,
    )
    grad_hidden_part = (
        grad_dispatched[first].astype(F32) + grad_dispatched[second].astype(F32)
    ).astype(BF16)
    grad_own = lax.psum_scatter(
        grad_hidden_part, "tensor", scatter_dimension=0, tiled=True
    ).astype(F32)
    grad_gate_own = lax.dynamic_slice_in_dim(
        lax.psum(grad_gate_part, "tensor"), own_start, own_rows, 0
    )
    own_routes = lax.dynamic_slice_in_dim(routes, own_start, own_rows, 0)
    own_logits = jnp.dot(hidden_two, router_full, preferred_element_type=F32)

    def own_gates(logit_values):
        return gate_values(logit_values, own_routes)

    _, gate_pull = jax.vjp(own_gates, own_logits)
    grad_logits = gate_pull(grad_gate_own)[0]
    router_float = router_full.astype(F32)
    grad_hidden_two = grad_own + jnp.dot(grad_logits, router_float.T, precision=highest)
    grad_router_part = jnp.dot(hidden_two.astype(F32).T, grad_logits, precision=highest)
    grad_from_norm, grad_gain_two = norm_backward(grad_hidden_two, residual, scale_two, gain_two)
    grad_residual = cotangent.astype(F32) + grad_from_norm

    grad_branch = grad_residual.astype(BF16)
    grad_attended_own = nt(grad_branch, out_matrix).astype(BF16)
    grad_attended = lax.all_to_all(
        jnp.transpose(grad_attended_own.reshape(own_rows, n_tensor, head_cols), (1, 0, 2)),
        "tensor",
        0,
        0,
    ).reshape(seq_len, head_cols)
    grad_branch_all = lax.all_gather(grad_branch, "tensor", axis=0, tiled=True)
    small = jnp.concatenate(
        [
            jnp.transpose(grad_router_part),
            grad_gain_two[None],
            jnp.zeros((SMALL - experts - 1, model_width), F32),
        ],
        axis=0,
    )
    grad_projected, diag = attention_backward(
        projected, attended, grad_attended, lse, lowest, segments, patterns, heads
    )
    near = jnp.concatenate([diag[0, :heads], diag[1, :heads]], axis=1)
    grad_table = lax.dot_general(skew, near, (((1,), (1,)), ((), ())), precision=highest)
    grad_table = grad_table.at[NB - 1].add(jnp.sum(diag[2, :heads], axis=1))
    small = jnp.transpose(small.reshape(SMALL, n_dp, depth), (1, 0, 2))
    small = lax.dynamic_update_slice(
        small, grad_table.reshape(n_dp, NB // n_dp, heads), (0, experts + 2, 0)
    )
    grad_hidden_one, reduced_qkv, reduced_attn_out, small_sum = tail(
        n_dp,
        n_tensor,
        experts,
        gathered_one,
        grad_projected,
        qkv_matrix,
        attended,
        grad_branch_all,
        small,
        weight_shard,
        gain_shard,
    )
    grad_from_first, _ = norm_backward(grad_hidden_one, tokens_float, scale_one, gain_one)
    grad_tokens = (grad_residual + grad_from_first).astype(BF16)
    return finish(
        layer_out, grad_tokens, reduced_qkv, reduced_attn_out, small_sum, grad_w_in, grad_w_out
    )


def solution(mesh):
    return jax.shard_map(
        on_device,
        mesh=mesh,
        in_specs=(
            P(("dp", "tensor"), None),
            P("dp", None),
            P("dp", None),
            P("dp", None, "tensor"),
            P("tensor", "dp"),
            P("dp", "tensor"),
            P("dp"),
            P("dp"),
            P("dp", None),
            P("dp", None, "tensor", None),
            P("dp", "tensor", None),
            P(("dp", "tensor"), None),
        ),
        out_specs=(
            P(("dp", "tensor"), None),
            P(("dp", "tensor"), None),
            P("dp", None, "tensor"),
            P("tensor", "dp"),
            P("dp", "tensor"),
            P("dp"),
            P("dp"),
            P("dp", None),
            P("dp", None, "tensor", None),
            P("dp", "tensor", None),
        ),
        check_vma=False,
    )
```

```python
import functools
import math

import jax
import jax.numpy as jnp
import numpy as np
from jax import lax
from jax.experimental import pallas as pl
from jax.experimental.pallas import tpu as pltpu
from jax.sharding import PartitionSpec as P

HD = 64
TOP = 2
NB = 32
NEAR = 128
BS = 256

EPS = 1e-06
NEG = -1e30
F32 = jnp.float32
BF16 = jnp.bfloat16
VMEM_LIMIT = 60 * 1024 * 1024


def distance_buckets():
    half_buckets = NB // 2
    thresholds = [bucket_level for bucket_level in range(1, half_buckets)]
    thresholds = thresholds + [
        int(
            math.ceil(
                half_buckets
                * (NEAR / half_buckets) ** ((bucket_level - half_buckets) / half_buckets)
            )
        )
        for bucket_level in range(half_buckets, NB)
    ]
    distance = np.arange(NEAR + 1)
    return (distance[:, None] >= np.array(thresholds)[None, :]).sum(axis=1)


def distance_selectors():
    buckets = distance_buckets()
    lanes = np.arange(2 * BS)
    signed = np.where(lanes < BS, lanes, lanes - 2 * BS)
    out = []
    for base in (0, BS):
        distance = np.clip(base - signed, 0, NEAR)
        out.append(buckets[distance][:, None] == np.arange(NB)[None, :])
    return np.concatenate(out, axis=0).astype(np.float32)


def skew_selectors():
    buckets = distance_buckets()
    lanes = np.arange(2 * BS)
    out = []
    for base in (0, BS):
        distance = np.clip(base + BS - 1 - lanes, 0, NEAR)
        out.append(buckets[distance][:, None] == np.arange(NB)[None, :])
    return np.concatenate(out, axis=0).astype(np.float32)


def nt(a, b):
    return lax.dot_general(a, b, (((1,), (1,)), ((), ())), preferred_element_type=F32)


def tn(a, b):
    return lax.dot_general(a, b, (((0,), (0,)), ((), ())), preferred_element_type=F32)


def nn(a, b):
    return lax.dot_general(a, b, (((1,), (0,)), ((), ())), preferred_element_type=F32)


def toeplitz(row):
    return pltpu.roll(jnp.broadcast_to(row, (BS, 2 * BS)), 0, 1, stride=1, stride_axis=0)[:, :BS]


def head_lanes(heads, width):
    lane = lax.broadcasted_iota(jnp.int32, (1, width), 1)
    return [(lane >= h * HD) & (lane < (h + 1) * HD) for h in range(heads)]


def own_head(value, lanes, heads):
    return value if heads == 1 else jnp.where(lanes, value, jnp.zeros((), value.dtype))


def build_bias(heads, pattern_ref, bias):
    for h in range(heads):
        for t in range(2):
            bias[h, t] = toeplitz(pattern_ref[2 * h + t : 2 * h + t + 1, :])
        bias[h, 2] = jnp.broadcast_to(pattern_ref[2 * h + 1 : 2 * h + 2, 0:1], (BS, BS))


def block_rows(block):
    if isinstance(block, int):
        return pl.ds(block * BS, BS)
    return pl.ds(pl.multiple_of(block * BS, BS), BS)


def segment_column(qb, segment_ref):
    return to_column(segment_ref[:, block_rows(qb)].astype(F32))


def block_mask(qb, kb, q_segments, segment_ref):
    k_segments = segment_ref[:, block_rows(kb)].astype(F32)
    row = lax.broadcasted_iota(jnp.int32, (BS, BS), 0) + (qb - kb) * BS
    col = lax.broadcasted_iota(jnp.int32, (BS, BS), 1)
    return (q_segments == k_segments) & (row >= col)


def forward_rows(heads, qb, low, qkv_ref, segment_ref, bias, out_ref, lse_ref):
    width = heads * HD
    lanes = head_lanes(heads, width)
    q_rows = block_rows(qb)
    q_all = (qkv_ref[q_rows, 0:width] * HD**-0.5).astype(BF16)
    q_heads = [own_head(q_all, lanes[h], heads) for h in range(heads)]
    q_segments = segment_column(qb, segment_ref)

    def k_step(kb, carry):
        k = qkv_ref[block_rows(kb), width : 2 * width]
        v = qkv_ref[block_rows(kb), 2 * width : 3 * width]
        allowed = block_mask(qb, kb, q_segments, segment_ref)
        place = jnp.minimum(qb - kb, 2)
        new = []
        for h in range(heads):
            top, total, acc = carry[3 * h : 3 * h + 3]
            s = jnp.where(allowed, nt(q_heads[h], k) + bias[h, place], NEG)
            top_new = jnp.maximum(top, jnp.max(s, axis=1, keepdims=True))
            alpha = jnp.exp(top - top_new)
            p = jnp.exp(s - top_new)
            total = alpha * total + jnp.sum(p, axis=1, keepdims=True)
            acc = alpha * acc + nn(p.astype(BF16), v)
            new += [top_new, total, acc]
        return tuple(new)

    init = []
    for h in range(heads):
        init += [jnp.full((BS, 1), NEG, F32), jnp.zeros((BS, 1), F32), jnp.zeros((BS, width), F32)]
    res = lax.fori_loop(low, qb + 1, k_step, tuple(init))
    out = jnp.zeros((BS, width), F32)
    for h in range(heads):
        top, total, acc = res[3 * h : 3 * h + 3]
        value = acc / total
        out = value if heads == 1 else jnp.where(lanes[h], value, out)
        lse_ref[q_rows, h : h + 1] = top + jnp.log(total)
    out_ref[q_rows, :] = out.astype(BF16)


def backward_rows(
    heads, qb, low, qkv_ref, out_ref, grad_ref, lse_ref, segment_ref, bias, grad_qkv_ref, dk, dv, sums
):
    width = heads * HD
    lanes = head_lanes(heads, width)
    scale = HD**-0.5
    q_rows = block_rows(qb)
    q_all = (qkv_ref[q_rows, 0:width] * scale).astype(BF16)
    g_all = grad_ref[q_rows, :]
    both = g_all.astype(F32) * out_ref[q_rows, :].astype(F32)
    q_heads = [own_head(q_all, lanes[h], heads) for h in range(heads)]
    g_heads = [own_head(g_all, lanes[h], heads) for h in range(heads)]
    deltas = [jnp.sum(own_head(both, lanes[h], heads), axis=1, keepdims=True) for h in range(heads)]
    totals = [lse_ref[q_rows, h : h + 1] for h in range(heads)]
    q_segments = segment_column(qb, segment_ref)

    def k_step(kb, dq):
        k_rows = block_rows(kb)
        k = qkv_ref[k_rows, width : 2 * width]
        v = qkv_ref[k_rows, 2 * width : 3 * width]
        allowed = block_mask(qb, kb, q_segments, segment_ref)
        place = jnp.minimum(qb - kb, 2)
        dk_add = jnp.zeros((BS, width), F32)
        dv_add = jnp.zeros((BS, width), F32)
        for h in range(heads):
            s = jnp.where(allowed, nt(q_heads[h], k) + bias[h, place], NEG)
            p = jnp.exp(s - totals[h])
            gp = nt(g_heads[h], v)
            ds = (p * (gp - deltas[h])).astype(BF16)
            dv_add += tn(p.astype(BF16), g_heads[h])
            dk_add += tn(ds, q_heads[h])
            dq = dq + own_head(nn(ds, k), lanes[h], heads)
            sums[h, place] += ds.astype(F32)
        dk[k_rows, :] += dk_add
        dv[k_rows, :] += dv_add
        return dq

    dq = lax.fori_loop(low, qb + 1, k_step, jnp.zeros((BS, width), F32))
    grad_qkv_ref[q_rows, 0:width] = (dq * scale).astype(BF16)


def backward_start(dk, dv, sums):
    dk[...] = jnp.zeros_like(dk)
    dv[...] = jnp.zeros_like(dv)
    sums[...] = jnp.zeros_like(sums)


def backward_end(heads, grad_qkv_ref, dk, dv):
    width = heads * HD
    grad_qkv_ref[:, width : 2 * width] = dk[...].astype(BF16)
    grad_qkv_ref[:, 2 * width : 3 * width] = dv[...].astype(BF16)


def diagonal_sums(heads, sums, diag_ref):
    row = lax.broadcasted_iota(jnp.int32, (BS, BS), 0)
    col = lax.broadcasted_iota(jnp.int32, (BS, BS), 1)
    upside_down = jnp.where(row + col == BS - 1, 1.0, 0.0).astype(F32)
    for h in range(heads):
        for t in range(2):
            flipped = jnp.dot(
                upside_down,
                sums[h, t],
                precision=lax.Precision.HIGHEST,
                preferred_element_type=F32,
            )
            wide = jnp.concatenate([flipped, jnp.zeros((BS, BS), F32)], axis=1)
            skewed = pltpu.roll(wide, 0, 1, stride=1, stride_axis=0)
            diag_ref[t, h : h + 1, :] = jnp.sum(skewed, axis=0, keepdims=True)
        rest = jnp.sum(sums[h, 2], axis=0, keepdims=True)
        diag_ref[2, h : h + 1, :] = jnp.concatenate([rest, jnp.zeros((1, BS), F32)], axis=1)


def attn_fwd_kernel(heads, blocks, lo_ref, qkv_ref, segment_ref, pattern_ref, out_ref, lse_ref, bias):
    build_bias(heads, pattern_ref, bias)

    def q_step(qb, _):
        forward_rows(heads, qb, lo_ref[qb], qkv_ref, segment_ref, bias, out_ref, lse_ref)
        return 0

    lax.fori_loop(0, blocks, q_step, 0)


def attn_bwd_kernel(
    heads,
    blocks,
    lo_ref,
    qkv_ref,
    out_ref,
    grad_ref,
    lse_ref,
    segment_ref,
    pattern_ref,
    grad_qkv_ref,
    diag_ref,
    bias,
    dk,
    dv,
    sums,
):
    build_bias(heads, pattern_ref, bias)
    backward_start(dk, dv, sums)

    def q_step(qb, _):
        backward_rows(
            heads,
            qb,
            lo_ref[qb],
            qkv_ref,
            out_ref,
            grad_ref,
            lse_ref,
            segment_ref,
            bias,
            grad_qkv_ref,
            dk,
            dv,
            sums,
        )
        return 0

    lax.fori_loop(0, blocks, q_step, 0)
    backward_end(heads, grad_qkv_ref, dk, dv)
    diagonal_sums(heads, sums, diag_ref)


def vspec():
    return pl.BlockSpec(memory_space=pltpu.VMEM)


def sspec():
    return pl.BlockSpec(memory_space=pltpu.SMEM)


def attention_forward(projected, lo, segments, patterns, heads):
    seq_len = projected.shape[0]
    blocks = seq_len // BS
    return pl.pallas_call(
        functools.partial(attn_fwd_kernel, heads, blocks),
        out_shape=(
            jax.ShapeDtypeStruct((seq_len, heads * HD), BF16),
            jax.ShapeDtypeStruct((seq_len, heads), F32),
        ),
        in_specs=[sspec(), vspec(), vspec(), vspec()],
        out_specs=(vspec(), vspec()),
        scratch_shapes=[pltpu.VMEM((heads, 3, BS, BS), F32)],
        compiler_params=pltpu.CompilerParams(vmem_limit_bytes=VMEM_LIMIT),
        name="attn_fwd",
    )(lo, projected, segments, patterns)


def attention_backward(projected, attended, grad, lse, lo, segments, patterns, heads):
    seq_len = projected.shape[0]
    blocks = seq_len // BS
    width = heads * HD
    return pl.pallas_call(
        functools.partial(attn_bwd_kernel, heads, blocks),
        out_shape=(
            jax.ShapeDtypeStruct((seq_len, 3 * width), BF16),
            jax.ShapeDtypeStruct((3, 8, 2 * BS), F32),
        ),
        in_specs=[sspec()] + [vspec()] * 6,
        out_specs=(vspec(), vspec()),
        scratch_shapes=backward_scratch(heads, seq_len),
        compiler_params=pltpu.CompilerParams(vmem_limit_bytes=VMEM_LIMIT),
        name="attn_bwd",
    )(lo, projected, attended, grad, lse, segments, patterns)


def backward_scratch(heads, seq_len):
    return [
        pltpu.VMEM((heads, 3, BS, BS), F32),
        pltpu.VMEM((seq_len, heads * HD), F32),
        pltpu.VMEM((seq_len, heads * HD), F32),
        pltpu.VMEM((heads, 3, BS, BS), F32),
    ]


MESH = pl.DeviceIdType.MESH
SMALL = 32


def remote(src, dst, send, recv, axis, peer):
    return pltpu.make_async_remote_copy(
        src_ref=src,
        dst_ref=dst,
        send_sem=send,
        recv_sem=recv,
        device_id={axis: peer},
        device_id_type=MESH,
    )


def greet(groups):
    barrier = pltpu.get_barrier_semaphore()
    total = 0
    for axis, n in groups:
        me = lax.axis_index(axis)
        for step in range(1, n):
            pl.semaphore_signal(
                barrier, inc=1, device_id={axis: lax.rem(me + step, n)}, device_id_type=MESH
            )
        total += n - 1
    pl.semaphore_wait(barrier, total)


class LineSum:
    def __init__(self, n, parts, send, recv, send_sem, recv_sem, total):
        self.n, self.parts = n, parts
        self.send, self.recv, self.send_sem, self.recv_sem = send, recv, send_sem, recv_sem
        self.total = total
        self.me = lax.axis_index("tensor")

    def flow(self, first, k):
        n, me = self.n, self.me
        near = me * 2 < n
        right = near if first else jnp.logical_not(near)
        block = jnp.where(right, n - 1 - k, k)
        comes = jnp.where(right, jnp.where(me > 0, me <= block, False), jnp.where(me < n - 1, me >= block, False))
        goes = jnp.where(right, me < block, me > block)
        peer = jnp.clip(jnp.where(right, me + 1, me - 1), 0, n - 1)
        out_slot = jnp.clip(jnp.where(right, k, n - 1 - me + k), 0, n - 2)
        in_slot = jnp.clip(jnp.where(right, k, n - me + k), 0, n)
        peer_slot = jnp.clip(jnp.where(right, k, n - peer + k), 0, n)
        return block, comes, goes, peer, out_slot, in_slot, peer_slot

    def copy(self, peer, out_slot, slot):
        return remote(
            self.send.at[out_slot],
            self.recv.at[slot],
            self.send_sem.at[out_slot],
            self.recv_sem.at[slot],
            "tensor",
            peer,
        )

    def start(self, partial=None):
        n, me = self.n, self.me

        def one(index, _):
            block = jnp.where(me * 2 < n, n - 1 - index, index)
            if partial is not None:
                value = partial(block)
                self.parts[block] = value.astype(BF16)

                @pl.when(block == me)
                def _():
                    self.total[...] = value

            @pl.when(jnp.logical_or(me == 0, me == n - 1) & (index < n - 1))
            def _():
                remote(
                    self.parts.at[block],
                    self.recv.at[jnp.where(me == 0, index, 2 + index)],
                    self.send_sem.at[index],
                    self.recv_sem.at[jnp.where(me == 0, index, 2 + index)],
                    "tensor",
                    jnp.where(me == 0, 1, n - 2),
                ).start()

            return 0

        lax.fori_loop(0, n, one, 0)
        if partial is None:
            self.total[...] = self.parts[me].astype(F32)

    def finish(self):
        for k in range(self.n - 1):
            self.step(k)

    def step(self, k):
        for first in (True, False):
            block, comes, goes, peer, out_slot, in_slot, peer_slot = self.flow(first, k)

            @pl.when(goes & comes)
            def _():
                self.copy(peer, out_slot, in_slot).wait_recv()
                self.send[out_slot] = (
                    self.parts[block].astype(F32) + self.recv[in_slot].astype(F32)
                ).astype(BF16)
                self.copy(peer, out_slot, peer_slot).start()

            @pl.when(comes & jnp.logical_not(goes))
            def _():
                self.copy(peer, 0, in_slot).wait_recv()
                self.total[...] += self.recv[in_slot].astype(F32)

    def drain(self):
        for k in range(self.n - 1):
            for first in (True, False):
                block, comes, goes, peer, out_slot, in_slot, peer_slot = self.flow(first, k)

                @pl.when(goes)
                def _():
                    self.copy(peer, out_slot, in_slot).wait_send()


def tail_kernel(
    n_dp,
    n_tensor,
    experts,
    table_rows,
    hidden_ref,
    grad_ref,
    weight_ref,
    attended_ref,
    branch_ref,
    small_ref,
    weight_own_ref,
    gain_own_ref,
    grad_hidden_ref,
    grad_qkv_ref,
    grad_out_ref,
    small_out_ref,
    parts,
    line_send,
    line_recv,
    qkv_send,
    qkv_recv,
    out_send,
    out_recv,
    small_recv,
    small_sum,
    gain_recv,
    line_send_sem,
    line_recv_sem,
    qkv_send_sem,
    qkv_recv_sem,
    out_send_sem,
    out_recv_sem,
    small_send_sem,
    small_recv_sem,
    gain_send_sem,
    gain_recv_sem,
):
    own_rows = grad_hidden_ref.shape[0]
    depth = weight_own_ref.shape[0]
    out_cols = grad_out_ref.shape[1]
    me = lax.axis_index("dp")
    me_t = lax.axis_index("tensor")
    greet([("dp", n_dp), ("tensor", n_tensor)])

    def partial(block):
        rows = pl.ds(pl.multiple_of(block * own_rows, own_rows), own_rows)
        return nt(grad_ref[rows, :], weight_ref[...])

    line = LineSum(
        n_tensor, parts, line_send, line_recv, line_send_sem, line_recv_sem, grad_hidden_ref
    )
    line.start(partial)
    copies = []
    for step in range(1, n_dp):
        peer = lax.rem(me + step, n_dp)
        copy = remote(
            small_ref.at[peer],
            small_recv.at[step - 1],
            small_send_sem.at[step - 1],
            small_recv_sem.at[step - 1],
            "dp",
            peer,
        )
        copy.start()
        copies.append(copy)
    for block in range(n_dp):
        cols = slice(block * depth, (block + 1) * depth)
        qkv_send[block] = tn(hidden_ref[:, cols], grad_ref[...]).astype(BF16)
    for step in range(1, n_dp):
        peer = lax.rem(me + step, n_dp)
        copy = remote(
            qkv_send.at[peer],
            qkv_recv.at[step - 1],
            qkv_send_sem.at[step - 1],
            qkv_recv_sem.at[step - 1],
            "dp",
            peer,
        )
        copy.start()
        copies.append(copy)
    for block in range(n_dp):
        cols = slice(block * out_cols, (block + 1) * out_cols)
        out_send[block] = tn(attended_ref[...], branch_ref[:, cols]).astype(BF16)
    for step in range(1, n_dp):
        peer = lax.rem(me + step, n_dp)
        copy = remote(
            out_send.at[peer],
            out_recv.at[step - 1],
            out_send_sem.at[step - 1],
            out_recv_sem.at[step - 1],
            "dp",
            peer,
        )
        copy.start()
        copies.append(copy)
    line.finish()
    for copy in copies:
        copy.wait()
    small_sum[...] = small_ref[me]
    grad_qkv_ref[...] = qkv_send[me].astype(F32)
    grad_out_ref[...] = out_send[me].astype(F32)
    for step in range(1, n_dp):
        small_sum[...] += small_recv[step - 1]
        grad_qkv_ref[...] += qkv_recv[step - 1].astype(F32)
        grad_out_ref[...] += out_recv[step - 1].astype(F32)
    column = jnp.sum(grad_qkv_ref[...] * weight_own_ref[...].astype(F32), axis=1, keepdims=True)
    eye = lax.broadcasted_iota(jnp.int32, (depth, depth), 0) == lax.broadcasted_iota(
        jnp.int32, (depth, depth), 1
    )
    row = jnp.sum(jnp.where(eye, column, 0.0), axis=0, keepdims=True)
    small_sum[experts + 1 : experts + 2, :] = row / gain_own_ref[...]
    gains = []
    for step in range(1, n_tensor):
        peer = lax.rem(me_t + step, n_tensor)
        copy = remote(
            small_sum,
            gain_recv.at[step - 1],
            gain_send_sem.at[step - 1],
            gain_recv_sem.at[step - 1],
            "tensor",
            peer,
        )
        copy.start()
        gains.append(copy)
    line.drain()
    for copy in gains:
        copy.wait()
    small_out_ref[...] = small_sum[...]
    shared = slice(0, experts + 2)
    for step in range(1, n_tensor):
        small_out_ref[shared, :] += gain_recv[step - 1, shared, :]


def tail(n_dp, n_tensor, experts, hidden, grad, weight, attended, branch, small, weight_own, gain_own):
    seq_len, width = hidden.shape
    own_rows = seq_len // n_tensor
    depth, cols = weight_own.shape
    heads_cols = attended.shape[1]
    out_cols = width // n_dp
    table_rows = NB // n_dp
    return pl.pallas_call(
        functools.partial(tail_kernel, n_dp, n_tensor, experts, table_rows),
        out_shape=(
            jax.ShapeDtypeStruct((own_rows, width), F32),
            jax.ShapeDtypeStruct((depth, cols), F32),
            jax.ShapeDtypeStruct((heads_cols, out_cols), F32),
            jax.ShapeDtypeStruct((SMALL, depth), F32),
        ),
        in_specs=[vspec()] * 8,
        out_specs=(vspec(),) * 4,
        scratch_shapes=[
            pltpu.VMEM((n_tensor, own_rows, width), BF16),
            pltpu.VMEM((n_tensor - 1, own_rows, width), BF16),
            pltpu.VMEM((n_tensor + 1, own_rows, width), BF16),
            pltpu.VMEM((n_dp, depth, cols), BF16),
            pltpu.VMEM((n_dp - 1, depth, cols), BF16),
            pltpu.VMEM((n_dp, heads_cols, out_cols), BF16),
            pltpu.VMEM((n_dp - 1, heads_cols, out_cols), BF16),
            pltpu.VMEM((n_dp - 1, SMALL, depth), F32),
            pltpu.VMEM((SMALL, depth), F32),
            pltpu.VMEM((n_tensor - 1, SMALL, depth), F32),
            pltpu.SemaphoreType.DMA((n_tensor - 1,)),
            pltpu.SemaphoreType.DMA((n_tensor + 1,)),
        ]
        + [pltpu.SemaphoreType.DMA((n_dp - 1,))] * 6
        + [pltpu.SemaphoreType.DMA((n_tensor - 1,))] * 2,
        compiler_params=pltpu.CompilerParams(
            vmem_limit_bytes=VMEM_LIMIT, collective_id=0, has_side_effects=True
        ),
        name="tail",
    )(hidden, grad, weight, attended, branch, small, weight_own, gain_own)


def diagonal(size):
    return lax.broadcasted_iota(jnp.int32, (size, size), 0) == lax.broadcasted_iota(
        jnp.int32, (size, size), 1
    )


def to_column(row):
    return jnp.sum(jnp.where(diagonal(row.shape[1]), row, 0.0), axis=1, keepdims=True)


def to_row(column):
    return jnp.sum(jnp.where(diagonal(column.shape[0]), column, 0.0), axis=0, keepdims=True)


def expert_kernel(
    n_dp,
    local,
    capacity,
    rows_ref,
    grad_ref,
    gates_ref,
    in_ref,
    out_ref,
    back_ref,
    gate_back_ref,
    value_ref,
    grad_in_ref,
    grad_out_ref,
    back_send,
    gate_send,
    zs,
    ups,
    gates_s,
    stage,
    value_stage,
    back_send_sem,
    back_recv_sem,
    gate_send_sem,
    gate_recv_sem,
    own_sem,
    stage_sem,
    value_sem,
):
    me = lax.axis_index("dp")
    pairs = n_dp // 2
    hidden = in_ref.shape[2]
    width = rows_ref.shape[2]
    two = 2 * capacity
    greet([("dp", n_dp)])

    def back_copy(expert, target, sender):
        part = slice(expert * capacity, (expert + 1) * capacity)
        return remote(
            back_send.at[target, part],
            back_ref.at[sender, part],
            back_send_sem.at[expert, target],
            back_recv_sem.at[expert, sender],
            "dp",
            target,
        )

    def own_copy(expert):
        part = slice(expert * capacity, (expert + 1) * capacity)
        return pltpu.make_async_copy(
            back_send.at[me, part], back_ref.at[me, part], own_sem.at[expert]
        )

    def stage_copy(slot, target):
        return pltpu.make_async_copy(stage.at[slot], target, stage_sem.at[slot])

    gate_send[...] = jnp.zeros_like(gate_send)
    staged = []

    def put(value, target):
        slot = len(staged) % 2
        if len(staged) >= 2:
            staged[-2].wait()
        stage[slot] = value
        copy = stage_copy(slot, target)
        copy.start()
        staged.append(copy)

    for expert in range(local):
        part = slice(expert * capacity, (expert + 1) * capacity)

        def group(index, _):
            pair = (me // 2) ^ (pairs - 1 - index)
            first = 2 * pair
            rows = rows_ref[pl.ds(first, 2), part, :].reshape(two, width)
            grads = grad_ref[pl.ds(first, 2), part, :].reshape(two, width)
            column = jnp.concatenate(
                [to_column(gates_ref[first + j, 0:1, part]) for j in range(2)], axis=0
            )
            gate = nt(rows, in_ref[expert, 0])
            up = nt(rows, in_ref[expert, 1])
            square = gate * gate
            bent = jnp.tanh(0.7978845608028654 * gate * (1.0 + 0.044715 * square))
            half = 0.5 * (1.0 + bent)
            gelu = gate * half
            slope = half + 0.5 * gate * (1.0 - bent * bent) * (
                0.7978845608028654 * (1.0 + 3 * 0.044715 * square)
            )
            z = gelu * up
            grad_z = nt(grads, out_ref[expert])
            gate_grad = jnp.sum(z * grad_z, axis=1, keepdims=True)
            grad_z = column * grad_z
            zs[pl.ds(first, 2)] = (column * z).astype(BF16).reshape(2, capacity, hidden)
            ups[0, pl.ds(first, 2)] = (grad_z * up * slope).astype(BF16).reshape(2, capacity, hidden)
            ups[1, pl.ds(first, 2)] = (grad_z * gelu).astype(BF16).reshape(2, capacity, hidden)
            for j in range(2):
                gate_send[first + j, 0:1, part] = to_row(
                    gate_grad[j * capacity : (j + 1) * capacity]
                )
            back = nn(ups[0, pl.ds(first, 2)].reshape(two, hidden), in_ref[expert, 0])
            back += nn(ups[1, pl.ds(first, 2)].reshape(two, hidden), in_ref[expert, 1])
            back_send[pl.ds(first, 2), part, :] = back.astype(BF16).reshape(2, capacity, width)
            for j in range(2):
                target = first + j

                @pl.when(target != me)
                def _():
                    back_copy(expert, target, me).start()

                @pl.when(target == me)
                def _():
                    own_copy(expert).start()

            return 0

        lax.fori_loop(0, pairs, group, 0)
        if expert == local - 1:
            gate_copies = []
            for step in range(1, n_dp):
                target = lax.rem(me + step, n_dp)
                copy = remote(
                    gate_send.at[target],
                    gate_back_ref.at[me],
                    gate_send_sem.at[step - 1],
                    gate_recv_sem.at[step - 1],
                    "dp",
                    target,
                )
                copy.start()
                gate_copies.append(copy)
            gate_back_ref[me] = gate_send[me]
        rows = rows_ref[:, part, :].reshape(n_dp * capacity, width)
        for half in range(2):
            put(tn(ups[half].reshape(n_dp * capacity, hidden), rows), grad_in_ref.at[expert, half])
        grads = grad_ref[:, part, :].reshape(n_dp * capacity, width)
        put(tn(zs[...].reshape(n_dp * capacity, hidden), grads), grad_out_ref.at[expert])
        if expert > 0:
            pltpu.make_async_copy(
                value_stage, value_ref.at[:, slice((expert - 1) * capacity, expert * capacity)], value_sem
            ).wait()

        def value(pair, _):
            out = nn(zs[pl.ds(2 * pair, 2)].reshape(two, hidden), out_ref[expert])
            value_stage[pl.ds(2 * pair, 2)] = out.astype(BF16).reshape(2, capacity, width)
            return 0

        lax.fori_loop(0, pairs, value, 0)
        pltpu.make_async_copy(value_stage, value_ref.at[:, part], value_sem).start()

    last = slice((local - 1) * capacity, local * capacity)
    pltpu.make_async_copy(value_stage, value_ref.at[:, last], value_sem).wait()
    for copy in staged[-2:]:
        copy.wait()
    for copy in gate_copies:
        copy.wait()
    for expert in range(local):
        own_copy(expert).wait()
        for step in range(1, n_dp):
            peer = lax.rem(me + step, n_dp)
            back_copy(expert, peer, me).wait_send()
            back_copy(expert, me, peer).wait_recv()


def any_spec():
    return pl.BlockSpec(memory_space=pl.ANY)


def run_experts(n_dp, capacity, rows, grads, gates, w_in, w_out):
    local, _, hidden, width = w_in.shape
    slots = local * capacity
    return pl.pallas_call(
        functools.partial(expert_kernel, n_dp, local, capacity),
        out_shape=(
            jax.ShapeDtypeStruct((n_dp, slots, width), BF16),
            jax.ShapeDtypeStruct((n_dp, 8, slots), F32),
            jax.ShapeDtypeStruct((n_dp, slots, width), BF16),
            jax.ShapeDtypeStruct(w_in.shape, F32),
            jax.ShapeDtypeStruct(w_out.shape, F32),
        ),
        in_specs=[vspec()] * 5,
        out_specs=(any_spec(), vspec(), any_spec(), any_spec(), any_spec()),
        scratch_shapes=[
            pltpu.VMEM((n_dp, slots, width), BF16),
            pltpu.VMEM((n_dp, 8, slots), F32),
            pltpu.VMEM((n_dp, capacity, hidden), BF16),
            pltpu.VMEM((2, n_dp, capacity, hidden), BF16),
            pltpu.VMEM((8, 128), F32),
            pltpu.VMEM((2, hidden, width), F32),
            pltpu.VMEM((n_dp, capacity, width), BF16),
            pltpu.SemaphoreType.DMA((local, n_dp)),
            pltpu.SemaphoreType.DMA((local, n_dp)),
            pltpu.SemaphoreType.DMA((n_dp - 1,)),
            pltpu.SemaphoreType.DMA((n_dp - 1,)),
            pltpu.SemaphoreType.DMA((local,)),
            pltpu.SemaphoreType.DMA((2,)),
            pltpu.SemaphoreType.DMA,
        ],
        compiler_params=pltpu.CompilerParams(
            vmem_limit_bytes=VMEM_LIMIT, collective_id=1, has_side_effects=True
        ),
        name="experts",
    )(rows, grads, gates, w_in, w_out)


def chosen_slots(columns, slots):
    lane = lax.broadcasted_iota(jnp.int32, (1, slots), 1)
    return columns[:, 0:1] == lane, columns[:, 1:2] == lane


def combine_kernel(
    n_dp,
    n_tensor,
    experts,
    rows_ref,
    gate_ref,
    slots_ref,
    routes_ref,
    residual_ref,
    hidden_ref,
    cotangent_ref,
    router_ref,
    gain_ref,
    weight_ref,
    value_ref,
    grad_residual_ref,
    branch_ref,
    grad_attended_ref,
    small_ref,
    merged_ref,
    parts,
    total,
    line_send,
    line_recv,
    gate_all,
    gate_send,
    gate_recv,
    value_back,
    line_send_sem,
    line_recv_sem,
    gate_send_sem,
    gate_recv_sem,
    value_send_sem,
    value_recv_sem,
    value_own_sem,
    gather_send_sem,
    gather_recv_sem,
):
    own_rows, width = residual_ref.shape
    slots = rows_ref.shape[0]
    per = slots // n_dp
    me = lax.axis_index("dp")
    me_t = lax.axis_index("tensor")
    greet([("dp", n_dp), ("tensor", n_tensor)])
    values = []
    for step in range(1, n_dp):
        peer = lax.rem(me + step, n_dp)
        copy = remote(
            value_ref.at[peer],
            value_back.at[me],
            value_send_sem.at[step - 1],
            value_recv_sem.at[step - 1],
            "dp",
            peer,
        )
        copy.start()
        values.append(copy)
    fetch = pltpu.make_async_copy(value_ref.at[me], value_back.at[me], value_own_sem)
    fetch.start()

    def partial(block):
        one, two = chosen_slots(
            slots_ref[pl.ds(pl.multiple_of(block * own_rows, own_rows), own_rows), :], slots
        )
        return nn(jnp.where(one | two, 1.0, 0.0).astype(BF16), rows_ref[...])

    line = LineSum(n_tensor, parts, line_send, line_recv, line_send_sem, line_recv_sem, total)
    line.start(partial)
    for peer in range(n_dp):
        gate_all[0:1, peer * per : (peer + 1) * per] = gate_ref[peer, 0:1, :]
    gate_send[...] = jnp.zeros_like(gate_send)
    gates = []
    for step in range(n_tensor):
        peer = lax.rem(me_t + step, n_tensor)
        picks = chosen_slots(
            slots_ref[pl.ds(pl.multiple_of(peer * own_rows, own_rows), own_rows), :], slots
        )
        for k in range(TOP):
            column = jnp.sum(
                jnp.where(picks[k], gate_all[0:1, :], 0.0), axis=1, keepdims=True
            )
            gate_send[step, k : k + 1, :] = to_row(column)
        if step:
            copy = remote(
                gate_send.at[step],
                gate_recv.at[step - 1],
                gate_send_sem.at[step - 1],
                gate_recv_sem.at[step - 1],
                "tensor",
                peer,
            )
            copy.start()
            gates.append(copy)
    hidden = hidden_ref[...]
    router = router_ref[...]
    logits = nt(router, hidden)
    exps = jnp.exp(logits - jnp.max(logits, axis=0, keepdims=True))
    probs = exps / jnp.sum(exps, axis=0, keepdims=True)
    ids = lax.broadcasted_iota(jnp.int32, (experts, own_rows), 0)
    own_lanes = pl.ds(pl.multiple_of(me_t * own_rows, own_rows), own_rows)
    first, second = ids == routes_ref[0:1, own_lanes], ids == routes_ref[1:2, own_lanes]
    prob_one = jnp.sum(jnp.where(first, probs, 0.0), axis=0, keepdims=True)
    prob_two = jnp.sum(jnp.where(second, probs, 0.0), axis=0, keepdims=True)
    both = prob_one + prob_two
    line.finish()
    for copy in gates:
        copy.wait()
    gate_sum = gate_send[0]
    for step in range(1, n_tensor):
        gate_sum = gate_sum + gate_recv[step - 1]
    grad_one, grad_two = gate_sum[0:1, :], gate_sum[1:2, :]
    mean_grad = (prob_one * grad_one + prob_two * grad_two) / both
    grad_probs = (
        jnp.where(first, grad_one - mean_grad, 0.0) + jnp.where(second, grad_two - mean_grad, 0.0)
    ) / both
    grad_logits = probs * (grad_probs - jnp.sum(grad_probs * probs, axis=0, keepdims=True))
    grad_hidden = total[...] + lax.dot_general(
        grad_logits,
        router.astype(F32),
        (((0,), (0,)), ((), ())),
        precision=lax.Precision.HIGHEST,
        preferred_element_type=F32,
    )
    residual = residual_ref[...]
    scale = lax.rsqrt(jnp.mean(residual * residual, axis=1, keepdims=True) + EPS)
    unit = residual * scale
    small_ref[...] = jnp.zeros_like(small_ref)
    small_ref[experts : experts + 1, :] = jnp.sum(grad_hidden * unit, axis=0, keepdims=True)
    grad_unit = grad_hidden * gain_ref[...]
    grad_residual = cotangent_ref[...].astype(F32) + scale * (
        grad_unit - unit * jnp.mean(grad_unit * unit, axis=1, keepdims=True)
    )
    grad_residual_ref[...] = grad_residual
    branch_ref[me_t] = grad_residual.astype(BF16)

    def on_block(block):
        grad_attended_ref[pl.ds(pl.multiple_of(block * own_rows, own_rows), own_rows), :] = nt(
            branch_ref[block], weight_ref[...]
        ).astype(BF16)

    lines = Streams(n_tensor, [branch_ref], gather_send_sem, gather_recv_sem)
    for turn in lines.turns():
        lines.turn(turn, lambda j, k: lines.each_new(j, k, on_block))
        if turn == n_tensor - 2:
            fetch.wait()
            for copy in values:
                copy.wait_recv()

            def merge(block, _):
                rows = pl.ds(pl.multiple_of(block * own_rows, own_rows), own_rows)
                one, two = chosen_slots(slots_ref[rows, :], slots)
                merged_ref[block] = nn(
                    jnp.where(one | two, 1.0, 0.0).astype(BF16), value_back[...].reshape(slots, width)
                ).astype(BF16)
                return 0

            lax.fori_loop(0, n_tensor, merge, 0)
    lines.drain()
    small_ref[0:experts, :] = jnp.dot(
        grad_logits,
        hidden.astype(F32),
        precision=lax.Precision.HIGHEST,
        preferred_element_type=F32,
    )
    line.drain()
    for copy in values:
        copy.wait_send()


def combine(
    n_dp,
    n_tensor,
    experts,
    rows,
    gates,
    slot_columns,
    routes_own,
    residual,
    hidden,
    cotangent,
    router_rows,
    gain,
    weight,
    value,
):
    own_rows, width = residual.shape
    slots = rows.shape[0]
    return pl.pallas_call(
        functools.partial(combine_kernel, n_dp, n_tensor, experts),
        out_shape=(
            jax.ShapeDtypeStruct((own_rows, width), F32),
            jax.ShapeDtypeStruct((n_tensor, own_rows, width), BF16),
            jax.ShapeDtypeStruct((n_tensor * own_rows, weight.shape[0]), BF16),
            jax.ShapeDtypeStruct((SMALL, width), F32),
            jax.ShapeDtypeStruct((n_tensor, own_rows, width), BF16),
        ),
        in_specs=[vspec()] * 10 + [any_spec()],
        out_specs=(vspec(),) * 5,
        scratch_shapes=[
            pltpu.VMEM((n_tensor, own_rows, width), BF16),
            pltpu.VMEM((own_rows, width), F32),
            pltpu.VMEM((n_tensor - 1, own_rows, width), BF16),
            pltpu.VMEM((n_tensor + 1, own_rows, width), BF16),
            pltpu.VMEM((8, slots), F32),
            pltpu.VMEM((n_tensor, 8, own_rows), F32),
            pltpu.VMEM((n_tensor - 1, 8, own_rows), F32),
            pltpu.VMEM(value.shape, BF16),
            pltpu.SemaphoreType.DMA((n_tensor - 1,)),
            pltpu.SemaphoreType.DMA((n_tensor + 1,)),
            pltpu.SemaphoreType.DMA((n_tensor - 1,)),
            pltpu.SemaphoreType.DMA((n_tensor - 1,)),
            pltpu.SemaphoreType.DMA((n_dp - 1,)),
            pltpu.SemaphoreType.DMA((n_dp - 1,)),
            pltpu.SemaphoreType.DMA,
            pltpu.SemaphoreType.DMA((1, 2, n_tensor - 1)),
            pltpu.SemaphoreType.DMA((1, 2, n_tensor - 1)),
        ],
        compiler_params=pltpu.CompilerParams(
            vmem_limit_bytes=VMEM_LIMIT, collective_id=2, has_side_effects=True
        ),
        name="combine",
    )(
        rows,
        gates,
        slot_columns,
        routes_own,
        residual,
        hidden,
        cotangent,
        router_rows,
        gain,
        weight,
        value,
    )


class Streams:
    def __init__(self, n, refs, send_sem, recv_sem):
        self.n, self.refs, self.send_sem, self.recv_sem = n, refs, send_sem, recv_sem
        self.me = lax.axis_index("tensor")

    def copy(self, j, block, slot, k, peer):
        ref = self.refs[j].at[block]
        return remote(
            ref, ref, self.send_sem.at[j, slot, k], self.recv_sem.at[j, slot, k], "tensor", peer
        )

    def outgoing(self, j, k, fn):
        for slot, sign in enumerate((1, -1)):
            block, peer = self.me - sign * k, self.me + sign

            @pl.when((block >= 0) & (block < self.n) & (peer >= 0) & (peer < self.n))
            def _():
                fn(self.copy(j, block, slot, k, peer))

    def incoming(self, j, k, fn):
        for slot, sign in enumerate((1, -1)):
            block = self.me - sign * (k + 1)

            @pl.when((block >= 0) & (block < self.n))
            def _():
                fn(self.copy(j, block, slot, k, jnp.clip(self.me - sign, 0, self.n - 1)), block)

    def turn(self, turn, used=None):
        moved = []
        for j in range(len(self.refs)):
            k = turn - j
            if k < 0 or k > self.n - 1:
                continue
            self.advance(j, k)
            moved.append((j, k))
        if used is not None:
            for j, k in moved:
                used(j, k)

    def turns(self):
        return range(self.n + len(self.refs) - 1)

    def advance(self, j, k):
        if k > 0:
            self.incoming(j, k - 1, lambda c, block: c.wait_recv())
        if k < self.n - 1:
            self.outgoing(j, k, lambda c: c.start())

    def each_new(self, j, k, fn):
        if k == 0:
            fn(self.me)
            return
        for sign in (1, -1):
            block = self.me - sign * k

            @pl.when((block >= 0) & (block < self.n))
            def _():
                fn(block)

    def drain(self):
        for j in range(len(self.refs)):
            for k in range(self.n - 1):
                self.outgoing(j, k, lambda c: c.wait_send())


class Spread:
    def __init__(self, n, ref, far_send, far_recv, near_send, near_recv):
        self.n, self.ref = n, ref
        self.far_send, self.far_recv = far_send, far_recv
        self.near_send, self.near_recv = near_send, near_recv
        self.me = lax.axis_index("dp")
        self.partner = self.me ^ 1

    def far(self, step, block, peer):
        ref = self.ref.at[block]
        return remote(ref, ref, self.far_send.at[step], self.far_recv.at[step], "dp", peer)

    def near(self, step, block):
        ref = self.ref.at[block]
        return remote(
            ref, ref, self.near_send.at[step], self.near_recv.at[step], "dp", self.partner
        )

    def start(self):
        for step in range(1, self.n // 2):
            self.far(step - 1, self.me, lax.rem(self.me + 2 * step, self.n)).start()
        self.near(0, self.me).start()

    def source(self, me, step):
        return lax.rem(me + self.n - 2 * step, self.n)

    def relay(self):
        for step in range(1, self.n // 2):
            block = self.source(self.me, step)
            self.far(step - 1, block, block).wait_recv()
            self.near(step, block).start()

    def finish(self):
        for step in range(self.n // 2):
            self.near(step, self.source(self.partner, step)).wait_recv()

    def drain(self):
        for step in range(1, self.n // 2):
            self.far(step - 1, self.me, lax.rem(self.me + 2 * step, self.n)).wait_send()
        for step in range(self.n // 2):
            self.near(step, self.source(self.me, step)).wait_send()


def one_hot(slot_rows, target, per):
    lane_slots = lax.broadcasted_iota(jnp.int32, (per, 1), 0) + target * per
    return jnp.where(
        (lane_slots == slot_rows[0:1, :]) | (lane_slots == slot_rows[1:2, :]), 1.0, 0.0
    ).astype(BF16)


def band(seq_len):
    return -(-(seq_len // 2 - 1) // BS)


def send_parameters(n_dp, n_tensor, weight_ref, extra_ref, out_ref, weights_ref, outs_ref, extras_ref, sems):
    me = lax.axis_index("dp")
    me_t = lax.axis_index("tensor")
    (extra_send, extra_recv, line_send, line_recv) = sems[:4]
    extras_ref[me] = extra_ref[...]
    small = []
    for step in range(1, n_dp):
        peer = lax.rem(me + step, n_dp)
        copy = remote(
            extra_ref, extras_ref.at[me], extra_send.at[step - 1], extra_recv.at[step - 1], "dp", peer
        )
        copy.start()
        small.append(copy)
    weights_ref[me] = weight_ref[...]
    weights = Spread(n_dp, weights_ref, *sems[4:8])
    weights.start()
    outs_ref[me, me_t] = out_ref[...]
    along = []
    for step in range(1, n_tensor):
        peer = lax.rem(me_t + step, n_tensor)
        copy = remote(
            out_ref,
            outs_ref.at[me, me_t],
            line_send.at[step - 1],
            line_recv.at[step - 1],
            "tensor",
            peer,
        )
        copy.start()
        along.append(copy)
    return small, weights, Spread(n_dp, outs_ref, *sems[8:12]), along


def unpack_parameters(n_dp, experts, extras_ref, selector_ref, router_ref, table, pattern_ref):
    depth = table.shape[1]
    rows_each = NB // n_dp
    for block in range(n_dp):
        router_ref[:, block * depth : (block + 1) * depth] = extras_ref[block, 0:experts, :]
        table[block * rows_each : (block + 1) * rows_each, :] = extras_ref[
            block, experts + 2 : experts + 2 + rows_each, :
        ].astype(F32)
    patterns = lax.dot_general(
        table[...],
        selector_ref[...],
        (((0,), (0,)), ((), ())),
        precision=lax.Precision.HIGHEST,
        preferred_element_type=F32,
    )
    for row in range(pattern_ref.shape[0]):
        pattern_ref[row : row + 1, :] = patterns[
            row // 2 : row // 2 + 1, (row % 2) * 2 * BS : (row % 2 + 1) * 2 * BS
        ]


def first_hidden(n_dp, experts, tokens_ref, extras_ref, gains_ref, small):
    depth = extras_ref.shape[2]
    x = tokens_ref[...].astype(F32)
    scaled = x * lax.rsqrt(jnp.mean(x * x, axis=1, keepdims=True) + EPS)
    for copy in small:
        copy.wait()
    for block in range(n_dp):
        gains_ref[0:2, block * depth : (block + 1) * depth] = extras_ref[
            block, experts : experts + 2, :
        ].astype(F32)
    return (scaled * gains_ref[0:1, :]).astype(BF16)


def parameter_sems(n_dp, n_tensor):
    dma = pltpu.SemaphoreType.DMA
    return (
        [dma((n_dp - 1,))] * 2 + [dma((n_tensor - 1,))] * 2 + [dma((n_dp // 2,))] * 8
    )


def front_kernel(
    n_dp,
    n_tensor,
    experts,
    tokens_ref,
    weight_ref,
    extra_ref,
    out_ref,
    selector_ref,
    hidden_ref,
    projected_ref,
    weights_ref,
    outs_ref,
    pattern_ref,
    router_ref,
    gains_ref,
    extras_ref,
    table,
    *sems,
):
    own_rows, width = tokens_ref.shape
    me_t = lax.axis_index("tensor")
    greet([("dp", n_dp), ("tensor", n_tensor)])
    small, weights, spread, along = send_parameters(
        n_dp, n_tensor, weight_ref, extra_ref, out_ref, weights_ref, outs_ref, extras_ref, sems
    )
    hidden_ref[me_t] = first_hidden(n_dp, experts, tokens_ref, extras_ref, gains_ref, small)
    lines = Streams(n_tensor, [hidden_ref], sems[12], sems[13])
    lines.turn(0)
    unpack_parameters(n_dp, experts, extras_ref, selector_ref, router_ref, table, pattern_ref)
    weights.relay()
    for copy in along:
        copy.wait_recv()
    spread.start()
    weights.finish()
    spread.relay()
    spread.finish()

    def project(block):
        rows = pl.ds(pl.multiple_of(block * own_rows, own_rows), own_rows)
        projected_ref[rows, :] = nn(
            hidden_ref[block], weights_ref[...].reshape(width, weights_ref.shape[2])
        ).astype(BF16)

    for turn in lines.turns():
        if turn:
            lines.turn(turn)

    def every(block, _):
        project(block)
        return 0

    lax.fori_loop(0, n_tensor, every, 0)
    lines.drain()
    weights.drain()
    spread.drain()
    for copy in along:
        copy.wait_send()


def front(n_dp, n_tensor, experts, tokens, weight, extra, out, selectors):
    own_rows, width = tokens.shape
    seq_len = own_rows * n_tensor
    depth, cols = weight.shape
    heads = cols // (3 * HD)
    dma = pltpu.SemaphoreType.DMA
    return pl.pallas_call(
        functools.partial(front_kernel, n_dp, n_tensor, experts),
        out_shape=(
            jax.ShapeDtypeStruct((n_tensor, own_rows, width), BF16),
            jax.ShapeDtypeStruct((seq_len, cols), BF16),
            jax.ShapeDtypeStruct((n_dp, depth, cols), BF16),
            jax.ShapeDtypeStruct((n_dp, n_tensor) + out.shape, BF16),
            jax.ShapeDtypeStruct((2 * heads, 2 * BS), F32),
            jax.ShapeDtypeStruct((experts, width), BF16),
            jax.ShapeDtypeStruct((2, width), F32),
        ),
        in_specs=[vspec()] * 5,
        out_specs=(vspec(),) * 7,
        scratch_shapes=[pltpu.VMEM((n_dp,) + extra.shape, BF16), pltpu.VMEM((NB, depth), F32)]
        + parameter_sems(n_dp, n_tensor)
        + [dma((1, 2, n_tensor - 1))] * 2,
        compiler_params=pltpu.CompilerParams(
            vmem_limit_bytes=VMEM_LIMIT, collective_id=3, has_side_effects=True
        ),
        name="front",
    )(tokens, weight, extra, out, selectors)


PARTS = 4


class Dispatch:
    def __init__(self, n_dp, picks, stage, rows_ref, send_sem, recv_sem, own_sem):
        self.n, self.picks, self.stage, self.rows = n_dp, picks, stage, rows_ref
        self.send_sem, self.recv_sem, self.own_sem = send_sem, recv_sem, own_sem
        self.me = lax.axis_index("dp")

    def cols(self, j):
        part = self.stage.shape[3]
        return slice(j * part, (j + 1) * part)

    def copy(self, j, target, sender):
        return remote(
            self.stage.at[j, target],
            self.rows.at[sender, :, self.cols(j)],
            self.send_sem.at[j, target],
            self.recv_sem.at[j, sender],
            "dp",
            target,
        )

    def own(self, j):
        return pltpu.make_async_copy(
            self.stage.at[j, self.me], self.rows.at[self.me, :, self.cols(j)], self.own_sem.at[j]
        )

    def start(self, j, values_ref):
        n_tensor, own_rows, part = values_ref.shape

        def one(index, _):
            mask = self.n - 1 - index
            target = self.me ^ mask
            self.stage[j, target] = nn(
                self.picks[target], values_ref[...].reshape(n_tensor * own_rows, part)
            ).astype(BF16)

            @pl.when(mask != 0)
            def _():
                self.copy(j, target, self.me).start()

            @pl.when(mask == 0)
            def _():
                self.own(j).start()

            return 0

        lax.fori_loop(0, self.n, one, 0)

    def finish(self):
        for j in range(self.stage.shape[0]):
            self.own(j).wait()
            for step in range(1, self.n):
                peer = lax.rem(self.me + step, self.n)
                self.copy(j, peer, self.me).wait_send()
                self.copy(j, self.me, peer).wait_recv()


def opening_kernel(
    n_dp,
    n_tensor,
    experts,
    capacity,
    tokens_ref,
    cotangent_ref,
    weight_ref,
    extra_ref,
    out_ref,
    routes_ref,
    segment_ref,
    selector_ref,
    hidden_ref,
    projected_ref,
    weights_ref,
    pattern_ref,
    router_ref,
    gains_ref,
    slots_ref,
    attended_ref,
    lse_ref,
    residual_ref,
    hidden_two_ref,
    weight_own_ref,
    rows_ref,
    grad_rows_ref,
    gates_ref,
    extras_ref,
    table,
    outs,
    out_matrix,
    grads,
    everyone,
    picks,
    grad_stage,
    row_stage,
    bias,
    slot_rows,
    attended_recv,
    logits,
    gate_stage,
    *sems,
):
    own_rows, width = tokens_ref.shape
    seq_len = own_rows * n_tensor
    heads = pattern_ref.shape[0] // 2
    head_cols = heads * HD
    out_cols = out_ref.shape[1]
    local = experts // n_dp
    per = local * capacity
    part = width // PARTS
    me = lax.axis_index("dp")
    me_t = lax.axis_index("tensor")
    (hop_send, hop_recv, late_send, late_recv) = sems[12:16]
    (grad_send, grad_recv, grad_own, row_send, row_recv, row_own) = sems[16:22]
    (gate_send, gate_recv, attended_send_sem, attended_recv_sem) = sems[22:26]
    greet([("dp", n_dp), ("tensor", n_tensor)])

    def rows_of(block):
        return pl.ds(pl.multiple_of(block * own_rows, own_rows), own_rows)

    for j in range(PARTS):
        grads[j, me_t] = cotangent_ref[:, j * part : (j + 1) * part]
    lines = Streams(
        n_tensor, [hidden_ref] + [grads.at[j] for j in range(PARTS)], hop_send, hop_recv
    )
    lines.advance(1, 0)
    small, weights, spread, along = send_parameters(
        n_dp, n_tensor, weight_ref, extra_ref, out_ref, weights_ref, outs, extras_ref, sems
    )
    hidden_ref[me_t] = first_hidden(n_dp, experts, tokens_ref, extras_ref, gains_ref, small)
    lines.advance(1, 1)
    unpack_parameters(n_dp, experts, extras_ref, selector_ref, router_ref, table, pattern_ref)
    lines.advance(1, 2)
    lines.advance(0, 0)

    ids = lax.broadcasted_iota(jnp.int32, (experts, seq_len), 0)
    hits = [ids == routes_ref[k : k + 1, :] for k in range(TOP)]
    before = lax.broadcasted_iota(jnp.int32, (seq_len, seq_len), 0) < lax.broadcasted_iota(
        jnp.int32, (seq_len, seq_len), 1
    )
    ranks = nn(
        jnp.where(hits[0] | hits[1], 1.0, 0.0).astype(BF16),
        jnp.where(before, 1.0, 0.0).astype(BF16),
    )
    places = ranks + (ids * capacity).astype(F32)
    for k in range(TOP):
        row = jnp.sum(jnp.where(hits[k], places, 0.0), axis=0, keepdims=True)
        slot_rows[k : k + 1, :] = row.astype(jnp.int32)
        for block in range(n_tensor):
            rows = slice(block * own_rows, (block + 1) * own_rows)
            slots_ref[rows, k : k + 1] = to_column(row[:, rows]).astype(jnp.int32)


    def pick(target, _):
        picks[target] = one_hot(slot_rows, target, per)
        return 0

    lax.fori_loop(0, n_dp, pick, 0)
    grad_moves = Dispatch(n_dp, picks, grad_stage, grad_rows_ref, grad_send, grad_recv, grad_own)
    lines.advance(1, 3)
    grad_moves.start(0, grads.at[0])
    weights.relay()
    for copy in along:
        copy.wait_recv()
    spread.start()
    build_bias(heads, pattern_ref, bias)

    def project(block):
        projected_ref[rows_of(block), :] = nn(
            hidden_ref[block], weights_ref[...].reshape(width, weights_ref.shape[2])
        ).astype(BF16)

    lines.advance(0, 1)
    weights.finish()
    project(me_t)
    lines.advance(0, 2)
    lines.advance(2, 0)
    lines.advance(3, 0)
    spread.relay()
    lines.each_new(0, 1, project)
    lines.advance(0, 3)
    lines.advance(2, 1)
    lines.advance(3, 1)
    lines.each_new(0, 2, project)
    lines.each_new(0, 3, project)

    def attended_copy(target, sender):
        return remote(
            attended_ref.at[rows_of(target)],
            attended_recv.at[sender],
            attended_send_sem.at[target],
            attended_recv_sem.at[sender],
            "tensor",
            target,
        )

    def attend(qb):
        forward_rows(
            heads,
            qb,
            max(0, qb - band(seq_len)),
            projected_ref,
            segment_ref,
            bias,
            attended_ref,
            lse_ref,
        )

        @pl.when(me_t == qb)
        def _():
            attended_recv[me_t] = attended_ref[rows_of(me_t), :]

        @pl.when(me_t != qb)
        def _():
            attended_copy(qb, me_t).start()

    lines.advance(2, 2)
    lines.advance(3, 2)
    attend(3)
    attend(0)
    lines.advance(2, 3)
    grad_moves.start(1, grads.at[1])
    lines.advance(3, 3)
    attend(2)
    attend(1)
    grad_moves.start(2, grads.at[2])
    spread.finish()
    for block in range(n_dp):
        out_matrix[:, block * out_cols : (block + 1) * out_cols] = outs[block].reshape(
            width, out_cols
        )
    weight_own_ref[...] = out_matrix[
        pl.ds(pl.multiple_of(me_t * head_cols, head_cols), head_cols), :
    ]
    for step in range(1, n_tensor):
        attended_copy(me_t, lax.rem(me_t + step, n_tensor)).wait_recv()
    residual = tokens_ref[...].astype(F32)
    for block in range(n_tensor):
        residual += nn(
            attended_recv[block], out_matrix[block * head_cols : (block + 1) * head_cols, :]
        )
    residual_ref[...] = residual
    hidden = (
        residual
        * lax.rsqrt(jnp.mean(residual * residual, axis=1, keepdims=True) + EPS)
        * gains_ref[1:2, :]
    ).astype(BF16)
    hidden_two_ref[...] = hidden
    for j in range(PARTS):
        everyone[j, me_t] = hidden[:, j * part : (j + 1) * part]
    late = Streams(n_tensor, [everyone.at[j] for j in range(PARTS)], late_send, late_recv)
    row_moves = Dispatch(n_dp, picks, row_stage, rows_ref, row_send, row_recv, row_own)

    def used(j, k):
        if k < n_tensor - 1:
            return
        row_moves.start(j, everyone.at[j])
        term = nt(
            router_ref[:, j * part : (j + 1) * part], everyone[j].reshape(seq_len, part)
        )
        if j == 0:
            logits[...] = term
        else:
            logits[...] += term

    for turn in late.turns():
        late.turn(turn, used)
        if turn >= n_tensor:
            lines.advance(4, turn - n_tensor)
    lines.advance(4, n_tensor - 1)
    grad_moves.start(3, grads.at[3])
    values = logits[...]
    exps = jnp.exp(values - jnp.max(values, axis=0, keepdims=True))
    probs = exps / jnp.sum(exps, axis=0, keepdims=True)
    named = (ids == routes_ref[0:1, :]) | (ids == routes_ref[1:2, :])
    shares = probs / jnp.sum(jnp.where(named, probs, 0.0), axis=0, keepdims=True)
    logits[...] = shares

    def gate_copy(target, sender):
        return remote(
            gate_stage.at[target],
            gates_ref.at[sender],
            gate_send.at[target],
            gate_recv.at[sender],
            "dp",
            target,
        )

    def gate(index, _):
        mask = n_dp - 1 - index
        target = me ^ mask
        for expert in range(local):
            row = jnp.sum(
                jnp.where(ids == target * local + expert, logits[...], 0.0), axis=0, keepdims=True
            )
            high = row.astype(BF16)
            rest = row - high.astype(F32)
            mid = rest.astype(BF16)
            low = (rest - mid.astype(F32)).astype(BF16)
            lanes = slice(expert * capacity, (expert + 1) * capacity)
            pieces = nt(
                jnp.concatenate([high, mid, low, jnp.zeros((5, seq_len), BF16)], axis=0),
                picks[target, lanes, :],
            )
            gate_stage[target, :, lanes] = jnp.broadcast_to(
                jnp.sum(pieces, axis=0, keepdims=True), (8, capacity)
            )

        @pl.when(mask != 0)
        def _():
            gate_copy(target, me).start()

        @pl.when(mask == 0)
        def _():
            gates_ref[target] = gate_stage[target]

        return 0

    lax.fori_loop(0, n_dp, gate, 0)
    lines.drain()
    late.drain()
    weights.drain()
    spread.drain()
    for copy in along:
        copy.wait_send()
    for step in range(1, n_tensor):
        attended_copy(lax.rem(me_t + step, n_tensor), me_t).wait_send()
    for step in range(1, n_dp):
        peer = lax.rem(me + step, n_dp)
        gate_copy(peer, me).wait_send()
        gate_copy(me, peer).wait_recv()
    grad_moves.finish()
    row_moves.finish()


def opening(
    n_dp,
    n_tensor,
    experts,
    capacity,
    tokens,
    cotangent,
    weight,
    extra,
    out,
    routes,
    segments,
    selectors,
):
    own_rows, width = tokens.shape
    seq_len = own_rows * n_tensor
    depth, cols = weight.shape
    per = experts // n_dp * capacity
    part = width // PARTS
    heads = cols // (3 * HD)
    dma = pltpu.SemaphoreType.DMA
    rows = jax.ShapeDtypeStruct((n_dp, per, width), BF16)
    return pl.pallas_call(
        functools.partial(opening_kernel, n_dp, n_tensor, experts, capacity),
        out_shape=(
            jax.ShapeDtypeStruct((n_tensor, own_rows, width), BF16),
            jax.ShapeDtypeStruct((seq_len, cols), BF16),
            jax.ShapeDtypeStruct((n_dp, depth, cols), BF16),
            jax.ShapeDtypeStruct((2 * heads, 2 * BS), F32),
            jax.ShapeDtypeStruct((experts, width), BF16),
            jax.ShapeDtypeStruct((2, width), F32),
            jax.ShapeDtypeStruct((seq_len, TOP), jnp.int32),
            jax.ShapeDtypeStruct((seq_len, heads * HD), BF16),
            jax.ShapeDtypeStruct((seq_len, heads), F32),
            jax.ShapeDtypeStruct((own_rows, width), F32),
            jax.ShapeDtypeStruct((own_rows, width), BF16),
            jax.ShapeDtypeStruct((heads * HD, width), BF16),
            rows,
            rows,
            jax.ShapeDtypeStruct((n_dp, 8, per), F32),
        ),
        in_specs=[vspec()] * 8,
        out_specs=(vspec(),) * 12 + (any_spec(), any_spec(), vspec()),
        scratch_shapes=[
            pltpu.VMEM((n_dp,) + extra.shape, BF16),
            pltpu.VMEM((NB, depth), F32),
            pltpu.VMEM((n_dp, n_tensor) + out.shape, BF16),
            pltpu.VMEM((width, width), BF16),
            pltpu.VMEM((PARTS, n_tensor, own_rows, part), BF16),
            pltpu.VMEM((PARTS, n_tensor, own_rows, part), BF16),
            pltpu.VMEM((n_dp, per, seq_len), BF16),
            pltpu.VMEM((PARTS, n_dp, per, part), BF16),
            pltpu.VMEM((PARTS, n_dp, per, part), BF16),
            pltpu.VMEM((heads, 3, BS, BS), F32),
            pltpu.VMEM((8, seq_len), jnp.int32),
            pltpu.VMEM((n_tensor, own_rows, heads * HD), BF16),
            pltpu.VMEM((experts, seq_len), F32),
            pltpu.VMEM((n_dp, 8, per), F32),
        ]
        + parameter_sems(n_dp, n_tensor)
        + [dma((PARTS + 1, 2, n_tensor - 1))] * 2
        + [dma((PARTS, 2, n_tensor - 1))] * 2
        + [dma((PARTS, n_dp)), dma((PARTS, n_dp)), dma((PARTS,))] * 2
        + [dma((n_dp,))] * 2
        + [dma((n_tensor,))] * 2,
        compiler_params=pltpu.CompilerParams(
            vmem_limit_bytes=VMEM_LIMIT, collective_id=4, has_side_effects=True
        ),
        name="opening",
    )(tokens, cotangent, weight, extra, out, routes, segments, selectors)


def last_kernel(
    n_dp,
    n_tensor,
    experts,
    heads,
    qkv_ref,
    attended_ref,
    grad_attended_ref,
    lse_ref,
    segment_ref,
    pattern_ref,
    skew_ref,
    hidden_ref,
    weight_ref,
    branch_ref,
    small_ref,
    weight_own_ref,
    gain_own_ref,
    merged_ref,
    residual_ref,
    grad_residual_ref,
    tokens_ref,
    gain_ref,
    layer_ref,
    grad_tokens_ref,
    grad_weight_ref,
    grad_out_ref,
    small_out_ref,
    bias,
    dk,
    dv,
    sums,
    grad_qkv,
    diag,
    parts,
    mixture,
    grad_hidden,
    mix_send,
    mix_recv,
    line_send,
    line_recv,
    qkv_send,
    qkv_recv,
    out_send,
    out_recv,
    small_send,
    small_recv,
    small_sum,
    gain_recv,
    mix_send_sem,
    mix_recv_sem,
    line_send_sem,
    line_recv_sem,
    qkv_send_sem,
    qkv_recv_sem,
    out_send_sem,
    out_recv_sem,
    small_send_sem,
    small_recv_sem,
    gain_send_sem,
    gain_recv_sem,
):
    own_rows, width = residual_ref.shape
    seq_len = own_rows * n_tensor
    depth = weight_own_ref.shape[0]
    out_cols = grad_out_ref.shape[1]
    me = lax.axis_index("dp")
    me_t = lax.axis_index("tensor")
    greet([("dp", n_dp), ("tensor", n_tensor)])

    def rows_of(block):
        return pl.ds(pl.multiple_of(block * own_rows, own_rows), own_rows)

    mix = LineSum(n_tensor, merged_ref, mix_send, mix_recv, mix_send_sem, mix_recv_sem, mixture)
    line = LineSum(n_tensor, parts, line_send, line_recv, line_send_sem, line_recv_sem, grad_hidden)
    copies = []

    def scatter(source, target, send_sem, recv_sem):
        for step in range(1, n_dp):
            peer = lax.rem(me + step, n_dp)
            copy = remote(
                source.at[peer],
                target.at[step - 1],
                send_sem.at[step - 1],
                recv_sem.at[step - 1],
                "dp",
                peer,
            )
            copy.start()
            copies.append(copy)

    mix.start()
    build_bias(heads, pattern_ref, bias)
    backward_start(dk, dv, sums)
    blocks = seq_len // BS
    for qb in range(blocks):
        backward_rows(
            heads,
            qb,
            max(0, qb - band(seq_len)),
            qkv_ref,
            attended_ref,
            grad_attended_ref,
            lse_ref,
            segment_ref,
            bias,
            grad_qkv,
            dk,
            dv,
            sums,
        )
        if qb == 0:
            for block in range(n_dp):
                cols = slice(block * out_cols, (block + 1) * out_cols)
                out_send[block] = tn(attended_ref[...], branch_ref[:, cols]).astype(BF16)
            scatter(out_send, out_recv, out_send_sem, out_recv_sem)
        if qb >= blocks - 2 and qb - (blocks - 2) < n_tensor - 1:
            mix.step(qb - (blocks - 2))
    backward_end(heads, grad_qkv, dk, dv)
    line.start(lambda block: nt(grad_qkv[rows_of(block), :], weight_ref[...]))
    for k in range(2, n_tensor - 1):
        mix.step(k)
    for block in range(n_dp):
        cols = slice(block * depth, (block + 1) * depth)
        qkv_send[block] = tn(hidden_ref[:, cols], grad_qkv[...]).astype(BF16)
    scatter(qkv_send, qkv_recv, qkv_send_sem, qkv_recv_sem)
    diag[...] = jnp.zeros_like(diag)
    diagonal_sums(heads, sums, diag)
    tables = lax.dot_general(
        skew_ref[...],
        jnp.concatenate([diag[0], diag[1]], axis=1),
        (((1,), (1,)), ((), ())),
        precision=lax.Precision.HIGHEST,
        preferred_element_type=F32,
    )
    far = jnp.sum(diag[2], axis=1, keepdims=True)
    head = lax.broadcasted_iota(jnp.int32, (8, 8), 0)
    lane = lax.broadcasted_iota(jnp.int32, (8, 8), 1)
    far_row = jnp.sum(jnp.where(head == lane, far, 0.0), axis=0, keepdims=True)
    bucket = lax.broadcasted_iota(jnp.int32, (NB, 8), 0)
    tables += jnp.where(bucket == NB - 1, far_row, 0.0)
    rows_each = NB // n_dp
    for block in range(n_dp):
        small_send[block] = small_ref[:, block * depth : (block + 1) * depth]
        small_send[block, experts + 2 : experts + 2 + rows_each, 0:8] = tables[
            block * rows_each : (block + 1) * rows_each, :
        ]
    scatter(small_send, small_recv, small_send_sem, small_recv_sem)
    layer_ref[...] = (residual_ref[...] + mixture[...]).astype(BF16)
    for k in range(n_tensor - 2):
        line.step(k)
    for copy in copies:
        copy.wait_recv()
    small_sum[...] = small_send[me]
    grad_weight_ref[...] = qkv_send[me].astype(F32)
    grad_out_ref[...] = out_send[me].astype(F32)
    for step in range(1, n_dp):
        small_sum[...] += small_recv[step - 1]
        grad_weight_ref[...] += qkv_recv[step - 1].astype(F32)
        grad_out_ref[...] += out_recv[step - 1].astype(F32)
    column = jnp.sum(grad_weight_ref[...] * weight_own_ref[...].astype(F32), axis=1, keepdims=True)
    small_sum[experts + 1 : experts + 2, :] = to_row(column) / gain_own_ref[...]
    gains = []
    for step in range(1, n_tensor):
        peer = lax.rem(me_t + step, n_tensor)
        copy = remote(
            small_sum,
            gain_recv.at[step - 1],
            gain_send_sem.at[step - 1],
            gain_recv_sem.at[step - 1],
            "tensor",
            peer,
        )
        copy.start()
        gains.append(copy)
    line.step(n_tensor - 2)
    x = tokens_ref[...].astype(F32)
    scale = lax.rsqrt(jnp.mean(x * x, axis=1, keepdims=True) + EPS)
    unit = x * scale
    grad_unit = grad_hidden[...] * gain_ref[...]
    grad_tokens_ref[...] = (
        grad_residual_ref[...]
        + scale * (grad_unit - unit * jnp.mean(grad_unit * unit, axis=1, keepdims=True))
    ).astype(BF16)
    mix.drain()
    line.drain()
    for copy in copies:
        copy.wait_send()
    for copy in gains:
        copy.wait()
    small_out_ref[...] = small_sum[...]
    shared = slice(0, experts + 2)
    for step in range(1, n_tensor):
        small_out_ref[shared, :] += gain_recv[step - 1, shared, :]


def last(
    n_dp,
    n_tensor,
    experts,
    heads,
    projected,
    attended,
    grad_attended,
    lse,
    segments,
    patterns,
    skew,
    hidden,
    weight,
    branch,
    small,
    weight_own,
    gain_own,
    merged,
    residual,
    grad_residual,
    tokens,
    gain,
):
    seq_len, width = hidden.shape
    own_rows = seq_len // n_tensor
    depth, cols = weight_own.shape
    out_cols = width // n_dp
    dma = pltpu.SemaphoreType.DMA
    line = [
        pltpu.VMEM((n_tensor - 1, own_rows, width), BF16),
        pltpu.VMEM((n_tensor + 1, own_rows, width), BF16),
    ]
    return pl.pallas_call(
        functools.partial(last_kernel, n_dp, n_tensor, experts, heads),
        out_shape=(
            jax.ShapeDtypeStruct((own_rows, width), BF16),
            jax.ShapeDtypeStruct((own_rows, width), BF16),
            jax.ShapeDtypeStruct((depth, cols), F32),
            jax.ShapeDtypeStruct((heads * HD, out_cols), F32),
            jax.ShapeDtypeStruct((SMALL, depth), F32),
        ),
        in_specs=[vspec()] * 18,
        out_specs=(vspec(),) * 5,
        scratch_shapes=backward_scratch(heads, seq_len)
        + [
            pltpu.VMEM((seq_len, cols), BF16),
            pltpu.VMEM((3, 8, 2 * BS), F32),
        ]
        + [pltpu.VMEM((n_tensor, own_rows, width), BF16)]
        + [pltpu.VMEM((own_rows, width), F32)] * 2
        + line * 2
        + [
            pltpu.VMEM((n_dp, depth, cols), BF16),
            pltpu.VMEM((n_dp - 1, depth, cols), BF16),
            pltpu.VMEM((n_dp, heads * HD, out_cols), BF16),
            pltpu.VMEM((n_dp - 1, heads * HD, out_cols), BF16),
            pltpu.VMEM((n_dp, SMALL, depth), F32),
            pltpu.VMEM((n_dp - 1, SMALL, depth), F32),
            pltpu.VMEM((SMALL, depth), F32),
            pltpu.VMEM((n_tensor - 1, SMALL, depth), F32),
        ]
        + [dma((n_tensor - 1,)), dma((n_tensor + 1,))] * 2
        + [dma((n_dp - 1,))] * 6
        + [dma((n_tensor - 1,))] * 2,
        compiler_params=pltpu.CompilerParams(
            vmem_limit_bytes=VMEM_LIMIT, collective_id=5, has_side_effects=True
        ),
        name="last",
    )(
        projected,
        attended,
        grad_attended,
        lse,
        segments,
        patterns,
        skew,
        hidden,
        weight,
        branch,
        small,
        weight_own,
        gain_own,
        merged,
        residual,
        grad_residual,
        tokens,
        gain,
    )


def deliver_kernel(
    grad_in_ref,
    grad_out_ref,
    layer_in_ref,
    tokens_in_ref,
    weight_in_ref,
    out_in_ref,
    small_ref,
    layer_ref,
    tokens_ref,
    weight_ref,
    out_ref,
    table_ref,
    gain_one_ref,
    gain_two_ref,
    router_ref,
    in_ref,
    down_ref,
    stage_in,
    stage_down,
    in_sem,
    down_sem,
    out_sem,
    last_sem,
):
    local, halves = grad_in_ref.shape[:2]
    pieces = [
        (grad_in_ref.at[e, g], stage_in.at[e, g], in_ref.at[e, g], in_sem.at[e, g], out_sem.at[e, g])
        for e in range(local)
        for g in range(halves)
    ] + [
        (grad_out_ref.at[e], stage_down.at[e], down_ref.at[e], down_sem.at[e], last_sem.at[e])
        for e in range(local)
    ]
    for source, stage, _, sem, _ in pieces:
        pltpu.make_async_copy(source, stage, sem).start()
    layer_ref[...] = layer_in_ref[...]
    tokens_ref[...] = tokens_in_ref[...]
    cols = weight_ref.shape[2]
    for part in range(3):
        weight_ref[part] = weight_in_ref[:, part * cols : (part + 1) * cols]
    out_ref[...] = out_in_ref[...]
    experts = router_ref.shape[0]
    router_ref[...] = small_ref[0:experts, :]
    gain_two_ref[...] = small_ref[experts : experts + 1, :]
    gain_one_ref[...] = small_ref[experts + 1 : experts + 2, :]
    table_ref[...] = small_ref[
        experts + 2 : experts + 2 + table_ref.shape[0], 0 : table_ref.shape[1]
    ]
    for source, stage, target, sem, done in pieces:
        pltpu.make_async_copy(source, stage, sem).wait()
        pltpu.make_async_copy(stage, target, done).start()
    for _, stage, target, _, done in pieces:
        pltpu.make_async_copy(stage, target, done).wait()


def deliver(experts, heads, table_rows, grad_in, grad_out, layer, tokens, weight, out, small):
    depth, cols = weight.shape
    local, halves = grad_in.shape[:2]
    dma = pltpu.SemaphoreType.DMA
    return pl.pallas_call(
        deliver_kernel,
        out_shape=(
            jax.ShapeDtypeStruct(layer.shape, BF16),
            jax.ShapeDtypeStruct(tokens.shape, BF16),
            jax.ShapeDtypeStruct((3, depth, cols // 3), F32),
            jax.ShapeDtypeStruct(out.shape, F32),
            jax.ShapeDtypeStruct((table_rows, heads), F32),
            jax.ShapeDtypeStruct((1, depth), F32),
            jax.ShapeDtypeStruct((1, depth), F32),
            jax.ShapeDtypeStruct((experts, depth), F32),
            jax.ShapeDtypeStruct(grad_in.shape, F32),
            jax.ShapeDtypeStruct(grad_out.shape, F32),
        ),
        in_specs=[any_spec()] * 2 + [vspec()] * 5,
        out_specs=(vspec(),) * 8 + (any_spec(),) * 2,
        scratch_shapes=[
            pltpu.VMEM(grad_in.shape, F32),
            pltpu.VMEM(grad_out.shape, F32),
            dma((local, halves)),
            dma((local,)),
            dma((local, halves)),
            dma((local,)),
        ],
        compiler_params=pltpu.CompilerParams(vmem_limit_bytes=VMEM_LIMIT),
        name="deliver",
    )(grad_in, grad_out, layer, tokens, weight, out, small)


def rms_scale(values):
    return lax.rsqrt(jnp.mean(values * values, axis=-1, keepdims=True) + EPS)


def norm_backward(grad_normed, values, scale_inv, gain):
    normed_unit = values * scale_inv
    grad_unit = grad_normed * gain
    grad_values = scale_inv * (
        grad_unit - normed_unit * jnp.mean(grad_unit * normed_unit, axis=-1, keepdims=True)
    )
    return (grad_values, jnp.sum(grad_normed * normed_unit, axis=0))


def gelu_tanh(values):
    return jax.nn.gelu(values, approximate=True)


def route_slots(route_ids, experts, capacity):
    flat_routes = route_ids.reshape(-1)
    onehot = (flat_routes[:, None] == jnp.arange(experts, dtype=jnp.int32)[None, :]).astype(
        jnp.int32
    )
    ranks = jnp.cumsum(onehot, axis=0) - 1
    rank_own = jnp.sum(ranks * onehot, axis=1)
    return (flat_routes * capacity + rank_own).reshape(-1, TOP)


def on_device(
    tokens,
    segments,
    routes,
    w_qkv,
    w_attn_out,
    bias_table,
    gain_attn,
    gain_moe,
    router,
    w_in,
    w_out,
    cotangent,
):
    own_rows, model_width = tokens.shape
    n_tensor = lax.axis_size("tensor")
    n_dp = lax.axis_size("dp")
    seq_len = own_rows * n_tensor
    own_start = lax.axis_index("tensor") * own_rows
    head_cols = w_qkv.shape[2]
    heads = head_cols // HD
    experts = router.shape[1]
    local_experts = w_in.shape[0]
    capacity = 5 * seq_len * TOP // (4 * experts)
    highest = lax.Precision.HIGHEST
    slots = experts * capacity

    depth = w_qkv.shape[0]
    bias_rows = NB // n_dp
    lanes = depth
    extra = jnp.concatenate(
        [
            jnp.transpose(router),
            gain_attn[None],
            gain_moe[None],
            jnp.pad(bias_table, ((0, SMALL - experts - 2 - bias_rows), (0, lanes - heads))),
        ],
        axis=0,
    )
    fast = n_dp == 8 and n_tensor == 4 and seq_len == 4 * BS and slots * model_width <= 4 * 1024 * 1024
    route_rows = jnp.pad(jnp.transpose(routes), ((0, 8 - TOP), (0, 0)))
    weight_shard = w_qkv.reshape(depth, 3 * head_cols)
    gain_shard = gain_attn[None].astype(F32)
    skew = jnp.asarray(skew_selectors().T)
    selectors = jnp.asarray(distance_selectors().T)

    def finish(layer_out, grad_tokens, reduced_qkv, reduced_attn_out, small_sum, grad_w_in, grad_w_out):
        (
            layer_out,
            grad_tokens,
            grad_w_qkv,
            grad_w_attn_out,
            grad_table,
            grad_gain_one,
            grad_gain_two,
            grad_router,
            grad_w_in,
            grad_w_out,
        ) = deliver(
            experts,
            heads,
            NB // n_dp,
            grad_w_in,
            grad_w_out,
            layer_out,
            grad_tokens,
            reduced_qkv,
            reduced_attn_out,
            small_sum,
        )
        return (
            layer_out,
            grad_tokens,
            jnp.transpose(grad_w_qkv, (1, 0, 2)),
            grad_w_attn_out,
            grad_table,
            grad_gain_one[0],
            grad_gain_two[0],
            jnp.transpose(grad_router),
            grad_w_in,
            grad_w_out,
        )

    if fast:
        (
            gathered,
            projected,
            weights_full,
            patterns,
            router_rows,
            gains,
            slot_columns,
            attended,
            lse,
            residual,
            hidden_two,
            weight_own,
            rows,
            grad_rows,
            row_gates,
        ) = opening(
            n_dp,
            n_tensor,
            experts,
            capacity,
            tokens,
            cotangent,
            weight_shard,
            extra,
            w_attn_out,
            route_rows,
            segments,
            selectors,
        )
        back, gate_back, value, grad_w_in, grad_w_out = run_experts(
            n_dp, capacity, rows, grad_rows, row_gates, w_in, w_out
        )
        grad_residual, grad_branch_all, grad_attended, small, merged = combine(
            n_dp,
            n_tensor,
            experts,
            back.reshape(slots, model_width),
            gate_back,
            slot_columns,
            route_rows,
            residual,
            hidden_two,
            cotangent,
            router_rows,
            gains[1:2],
            weight_own,
            value,
        )
        results = last(
            n_dp,
            n_tensor,
            experts,
            heads,
            projected,
            attended,
            grad_attended,
            lse,
            segments,
            patterns,
            skew,
            gathered.reshape(seq_len, model_width),
            weights_full.reshape(model_width, 3 * head_cols),
            grad_branch_all.reshape(seq_len, model_width),
            small,
            weight_shard,
            gain_shard,
            merged,
            residual,
            grad_residual,
            tokens,
            gains[0:1],
        )
        return finish(*results, grad_w_in, grad_w_out)
    gathered, projected, weights_full, outs_full, patterns, router_rows, gains = front(
        n_dp, n_tensor, experts, tokens, weight_shard, extra, w_attn_out, selectors
    )
    gathered_one = gathered.reshape(seq_len, model_width)
    qkv_matrix = weights_full.reshape(model_width, 3 * head_cols)
    outs_full = outs_full.reshape(n_dp, model_width, model_width // n_dp)
    tokens_float = tokens.astype(F32)
    scale_one = rms_scale(tokens_float)
    gain_one, gain_two = gains[0], gains[1]
    starts = segments[0, ::BS]
    ends = segments[0, BS - 1 :: BS]
    lowest = jnp.sum((ends[None, :] < starts[:, None]).astype(jnp.int32), axis=1)
    attended, lse = attention_forward(projected, lowest, segments, patterns, heads)
    router_full = jnp.transpose(router_rows)
    out_matrix = jnp.transpose(outs_full, (1, 0, 2)).reshape(model_width, model_width)
    attended_own = lax.all_to_all(
        attended.reshape(n_tensor, own_rows, head_cols), "tensor", 0, 0
    )
    attended_own = jnp.transpose(attended_own, (1, 0, 2)).reshape(own_rows, n_tensor * head_cols)
    branch = jnp.dot(attended_own, out_matrix, preferred_element_type=F32)
    residual = tokens_float + branch
    scale_two = rms_scale(residual)
    hidden_two = (residual * scale_two * gain_two).astype(BF16)
    gathered_two = lax.all_gather(hidden_two, "tensor", axis=0, tiled=True)

    expert_ids = jnp.arange(experts, dtype=jnp.int32)

    def gate_values(logit_values, route_rows):
        expert_probs = jax.nn.softmax(logit_values, axis=-1)
        picked = jnp.sum(
            jnp.where(
                route_rows[:, :, None] == expert_ids[None, None, :], expert_probs[:, None, :], 0.0
            ),
            axis=-1,
        )
        return picked / jnp.sum(picked, axis=1, keepdims=True)

    gates = gate_values(jnp.dot(gathered_two, router_full, preferred_element_type=F32), routes)
    slot_ids = route_slots(routes, experts, capacity)
    slot_flat = slot_ids.reshape(-1)
    token_ids = jnp.repeat(jnp.arange(seq_len, dtype=jnp.int32), TOP)
    sources = jnp.full((slots,), seq_len, jnp.int32).at[slot_flat].set(token_ids)
    slot_gates = jnp.zeros((slots,), F32).at[slot_flat].set(gates.reshape(-1))
    grad_gathered = lax.all_gather(cotangent, "tensor", axis=0, tiled=True)

    def exchange(rows):
        parts = rows.reshape(n_dp, local_experts, capacity, model_width)
        return [
            lax.all_to_all(parts[:, i], "dp", 0, 0).reshape(n_dp * capacity, model_width)
            for i in range(local_experts)
        ]

    def give_back(parts):
        back = [
            lax.all_to_all(part.reshape(n_dp, capacity, model_width), "dp", 0, 0) for part in parts
        ]
        return jnp.stack(back, axis=1).reshape(slots, model_width)

    zero_row = jnp.zeros((1, model_width), BF16)
    dispatched = exchange(jnp.concatenate([gathered_two, zero_row], axis=0)[sources])
    padded_grad = jnp.concatenate([grad_gathered, zero_row], axis=0)
    grad_expert = exchange((slot_gates[:, None] * padded_grad[sources]).astype(BF16))

    outs, backs, grads_in, grads_out = [], [], [], []
    for i in range(local_experts):
        rows, grad_rows = dispatched[i], grad_expert[i]
        gate_part = nt(rows, w_in[i, 0])
        up_part = nt(rows, w_in[i, 1])
        gelu_value, gelu_pull = jax.vjp(gelu_tanh, gate_part)
        activated = (gelu_value * up_part).astype(BF16)
        outs.append(nn(activated, w_out[i]).astype(BF16))
        grad_act = nt(grad_rows, w_out[i])
        grads_out.append(tn(activated, grad_rows))
        grad_gate = gelu_pull(grad_act * up_part)[0].astype(BF16)
        grad_up = (grad_act * gelu_value).astype(BF16)
        backs.append((nn(grad_gate, w_in[i, 0]) + nn(grad_up, w_in[i, 1])).astype(BF16))
        grads_in.append(jnp.stack([tn(grad_gate, rows), tn(grad_up, rows)]))
    grad_w_in = jnp.stack(grads_in)
    grad_w_out = jnp.stack(grads_out)
    expert_out = give_back(outs)
    grad_dispatched = give_back(backs)

    first, second = slot_ids[:, 0], slot_ids[:, 1]
    picked_first = expert_out[first].astype(F32)
    picked_second = expert_out[second].astype(F32)
    mixture = lax.psum_scatter(
        (gates[:, 0:1] * picked_first + gates[:, 1:2] * picked_second).astype(BF16),
        "tensor",
        scatter_dimension=0,
        tiled=True,
    ).astype(F32)
    layer_out = (residual + mixture).astype(BF16)
    grad_float = grad_gathered.astype(F32)
    grad_gate_part = jnp.stack(
        [
            jnp.sum(grad_float * picked_first, axis=1),
            jnp.sum(grad_float * picked_second, axis=1),
        ],
        axis=1,
    )
    grad_hidden_part = (
        grad_dispatched[first].astype(F32) + grad_dispatched[second].astype(F32)
    ).astype(BF16)
    grad_own = lax.psum_scatter(
        grad_hidden_part, "tensor", scatter_dimension=0, tiled=True
    ).astype(F32)
    grad_gate_own = lax.dynamic_slice_in_dim(
        lax.psum(grad_gate_part, "tensor"), own_start, own_rows, 0
    )
    own_routes = lax.dynamic_slice_in_dim(routes, own_start, own_rows, 0)
    own_logits = jnp.dot(hidden_two, router_full, preferred_element_type=F32)

    def own_gates(logit_values):
        return gate_values(logit_values, own_routes)

    _, gate_pull = jax.vjp(own_gates, own_logits)
    grad_logits = gate_pull(grad_gate_own)[0]
    router_float = router_full.astype(F32)
    grad_hidden_two = grad_own + jnp.dot(grad_logits, router_float.T, precision=highest)
    grad_router_part = jnp.dot(hidden_two.astype(F32).T, grad_logits, precision=highest)
    grad_from_norm, grad_gain_two = norm_backward(grad_hidden_two, residual, scale_two, gain_two)
    grad_residual = cotangent.astype(F32) + grad_from_norm

    grad_branch = grad_residual.astype(BF16)
    grad_attended_own = nt(grad_branch, out_matrix).astype(BF16)
    grad_attended = lax.all_to_all(
        jnp.transpose(grad_attended_own.reshape(own_rows, n_tensor, head_cols), (1, 0, 2)),
        "tensor",
        0,
        0,
    ).reshape(seq_len, head_cols)
    grad_branch_all = lax.all_gather(grad_branch, "tensor", axis=0, tiled=True)
    small = jnp.concatenate(
        [
            jnp.transpose(grad_router_part),
            grad_gain_two[None],
            jnp.zeros((SMALL - experts - 1, model_width), F32),
        ],
        axis=0,
    )
    grad_projected, diag = attention_backward(
        projected, attended, grad_attended, lse, lowest, segments, patterns, heads
    )
    near = jnp.concatenate([diag[0, :heads], diag[1, :heads]], axis=1)
    grad_table = lax.dot_general(skew, near, (((1,), (1,)), ((), ())), precision=highest)
    grad_table = grad_table.at[NB - 1].add(jnp.sum(diag[2, :heads], axis=1))
    small = jnp.transpose(small.reshape(SMALL, n_dp, depth), (1, 0, 2))
    small = lax.dynamic_update_slice(
        small, grad_table.reshape(n_dp, NB // n_dp, heads), (0, experts + 2, 0)
    )
    grad_hidden_one, reduced_qkv, reduced_attn_out, small_sum = tail(
        n_dp,
        n_tensor,
        experts,
        gathered_one,
        grad_projected,
        qkv_matrix,
        attended,
        grad_branch_all,
        small,
        weight_shard,
        gain_shard,
    )
    grad_from_first, _ = norm_backward(grad_hidden_one, tokens_float, scale_one, gain_one)
    grad_tokens = (grad_residual + grad_from_first).astype(BF16)
    return finish(
        layer_out, grad_tokens, reduced_qkv, reduced_attn_out, small_sum, grad_w_in, grad_w_out
    )


def solution(mesh):
    return jax.shard_map(
        on_device,
        mesh=mesh,
        in_specs=(
            P(("dp", "tensor"), None),
            P("dp", None),
            P("dp", None),
            P("dp", None, "tensor"),
            P("tensor", "dp"),
            P("dp", "tensor"),
            P("dp"),
            P("dp"),
            P("dp", None),
            P("dp", None, "tensor", None),
            P("dp", "tensor", None),
            P(("dp", "tensor"), None),
        ),
        out_specs=(
            P(("dp", "tensor"), None),
            P(("dp", "tensor"), None),
            P("dp", None, "tensor"),
            P("tensor", "dp"),
            P("dp", "tensor"),
            P("dp"),
            P("dp"),
            P("dp", None),
            P("dp", None, "tensor", None),
            P("dp", "tensor", None),
        ),
        check_vma=False,
    )
```

```python
import functools
import math

import jax
import jax.numpy as jnp
import numpy as np
from jax import lax
from jax.experimental import pallas as pl
from jax.experimental.pallas import tpu as pltpu
from jax.sharding import PartitionSpec as P

HD = 64
TOP = 2
NB = 32
NEAR = 128
BS = 256

EPS = 1e-06
NEG = -1e30
F32 = jnp.float32
BF16 = jnp.bfloat16
VMEM_LIMIT = 60 * 1024 * 1024


def distance_buckets():
    half_buckets = NB // 2
    thresholds = [bucket_level for bucket_level in range(1, half_buckets)]
    thresholds = thresholds + [
        int(
            math.ceil(
                half_buckets
                * (NEAR / half_buckets) ** ((bucket_level - half_buckets) / half_buckets)
            )
        )
        for bucket_level in range(half_buckets, NB)
    ]
    distance = np.arange(NEAR + 1)
    return (distance[:, None] >= np.array(thresholds)[None, :]).sum(axis=1)


def distance_selectors():
    buckets = distance_buckets()
    lanes = np.arange(2 * BS)
    signed = np.where(lanes < BS, lanes, lanes - 2 * BS)
    out = []
    for base in (0, BS):
        distance = np.clip(base - signed, 0, NEAR)
        out.append(buckets[distance][:, None] == np.arange(NB)[None, :])
    return np.concatenate(out, axis=0).astype(np.float32)


def skew_selectors():
    buckets = distance_buckets()
    lanes = np.arange(2 * BS)
    out = []
    for base in (0, BS):
        distance = np.clip(base + BS - 1 - lanes, 0, NEAR)
        out.append(buckets[distance][:, None] == np.arange(NB)[None, :])
    return np.concatenate(out, axis=0).astype(np.float32)


def nt(a, b):
    return lax.dot_general(a, b, (((1,), (1,)), ((), ())), preferred_element_type=F32)


def tn(a, b):
    return lax.dot_general(a, b, (((0,), (0,)), ((), ())), preferred_element_type=F32)


def nn(a, b):
    return lax.dot_general(a, b, (((1,), (0,)), ((), ())), preferred_element_type=F32)


def toeplitz(row):
    return pltpu.roll(jnp.broadcast_to(row, (BS, 2 * BS)), 0, 1, stride=1, stride_axis=0)[:, :BS]


def head_lanes(heads, width):
    lane = lax.broadcasted_iota(jnp.int32, (1, width), 1)
    return [(lane >= h * HD) & (lane < (h + 1) * HD) for h in range(heads)]


def own_head(value, lanes, heads):
    return value if heads == 1 else jnp.where(lanes, value, jnp.zeros((), value.dtype))


def build_bias(heads, pattern_ref, bias):
    for h in range(heads):
        for t in range(2):
            bias[h, t] = toeplitz(pattern_ref[2 * h + t : 2 * h + t + 1, :])
        bias[h, 2] = jnp.broadcast_to(pattern_ref[2 * h + 1 : 2 * h + 2, 0:1], (BS, BS))


def block_rows(block):
    if isinstance(block, int):
        return pl.ds(block * BS, BS)
    return pl.ds(pl.multiple_of(block * BS, BS), BS)


def segment_column(qb, segment_ref):
    return to_column(segment_ref[:, block_rows(qb)].astype(F32))


def block_mask(qb, kb, q_segments, segment_ref):
    k_segments = segment_ref[:, block_rows(kb)].astype(F32)
    row = lax.broadcasted_iota(jnp.int32, (BS, BS), 0) + (qb - kb) * BS
    col = lax.broadcasted_iota(jnp.int32, (BS, BS), 1)
    return (q_segments == k_segments) & (row >= col)


def forward_rows(heads, qb, low, qkv_ref, segment_ref, bias, out_ref, lse_ref):
    width = heads * HD
    lanes = head_lanes(heads, width)
    q_rows = block_rows(qb)
    q_all = (qkv_ref[q_rows, 0:width] * HD**-0.5).astype(BF16)
    q_heads = [own_head(q_all, lanes[h], heads) for h in range(heads)]
    q_segments = segment_column(qb, segment_ref)

    def k_step(kb, carry):
        k = qkv_ref[block_rows(kb), width : 2 * width]
        v = qkv_ref[block_rows(kb), 2 * width : 3 * width]
        allowed = block_mask(qb, kb, q_segments, segment_ref)
        place = jnp.minimum(qb - kb, 2)
        new = []
        for h in range(heads):
            top, total, acc = carry[3 * h : 3 * h + 3]
            s = jnp.where(allowed, nt(q_heads[h], k) + bias[h, place], NEG)
            top_new = jnp.maximum(top, jnp.max(s, axis=1, keepdims=True))
            alpha = jnp.exp(top - top_new)
            p = jnp.exp(s - top_new)
            total = alpha * total + jnp.sum(p, axis=1, keepdims=True)
            acc = alpha * acc + nn(p.astype(BF16), v)
            new += [top_new, total, acc]
        return tuple(new)

    init = []
    for h in range(heads):
        init += [jnp.full((BS, 1), NEG, F32), jnp.zeros((BS, 1), F32), jnp.zeros((BS, width), F32)]
    res = lax.fori_loop(low, qb + 1, k_step, tuple(init))
    out = jnp.zeros((BS, width), F32)
    for h in range(heads):
        top, total, acc = res[3 * h : 3 * h + 3]
        value = acc / total
        out = value if heads == 1 else jnp.where(lanes[h], value, out)
        lse_ref[q_rows, h : h + 1] = top + jnp.log(total)
    out_ref[q_rows, :] = out.astype(BF16)


def backward_rows(
    heads, qb, low, qkv_ref, out_ref, grad_ref, lse_ref, segment_ref, bias, grad_qkv_ref, dk, dv, sums
):
    width = heads * HD
    lanes = head_lanes(heads, width)
    scale = HD**-0.5
    q_rows = block_rows(qb)
    q_all = (qkv_ref[q_rows, 0:width] * scale).astype(BF16)
    g_all = grad_ref[q_rows, :]
    both = g_all.astype(F32) * out_ref[q_rows, :].astype(F32)
    q_heads = [own_head(q_all, lanes[h], heads) for h in range(heads)]
    g_heads = [own_head(g_all, lanes[h], heads) for h in range(heads)]
    deltas = [jnp.sum(own_head(both, lanes[h], heads), axis=1, keepdims=True) for h in range(heads)]
    totals = [lse_ref[q_rows, h : h + 1] for h in range(heads)]
    q_segments = segment_column(qb, segment_ref)

    def k_step(kb, dq):
        k_rows = block_rows(kb)
        k = qkv_ref[k_rows, width : 2 * width]
        v = qkv_ref[k_rows, 2 * width : 3 * width]
        allowed = block_mask(qb, kb, q_segments, segment_ref)
        place = jnp.minimum(qb - kb, 2)
        dk_add = jnp.zeros((BS, width), F32)
        dv_add = jnp.zeros((BS, width), F32)
        for h in range(heads):
            s = jnp.where(allowed, nt(q_heads[h], k) + bias[h, place], NEG)
            p = jnp.exp(s - totals[h])
            gp = nt(g_heads[h], v)
            ds = (p * (gp - deltas[h])).astype(BF16)
            dv_add += tn(p.astype(BF16), g_heads[h])
            dk_add += tn(ds, q_heads[h])
            dq = dq + own_head(nn(ds, k), lanes[h], heads)
            sums[h, place] += ds.astype(F32)
        dk[k_rows, :] += dk_add
        dv[k_rows, :] += dv_add
        return dq

    dq = lax.fori_loop(low, qb + 1, k_step, jnp.zeros((BS, width), F32))
    grad_qkv_ref[q_rows, 0:width] = (dq * scale).astype(BF16)


def backward_start(dk, dv, sums):
    dk[...] = jnp.zeros_like(dk)
    dv[...] = jnp.zeros_like(dv)
    sums[...] = jnp.zeros_like(sums)


def backward_end(heads, grad_qkv_ref, dk, dv):
    width = heads * HD
    grad_qkv_ref[:, width : 2 * width] = dk[...].astype(BF16)
    grad_qkv_ref[:, 2 * width : 3 * width] = dv[...].astype(BF16)


def diagonal_sums(heads, sums, diag_ref):
    row = lax.broadcasted_iota(jnp.int32, (BS, BS), 0)
    col = lax.broadcasted_iota(jnp.int32, (BS, BS), 1)
    upside_down = jnp.where(row + col == BS - 1, 1.0, 0.0).astype(F32)
    for h in range(heads):
        for t in range(2):
            flipped = jnp.dot(
                upside_down,
                sums[h, t],
                precision=lax.Precision.HIGHEST,
                preferred_element_type=F32,
            )
            wide = jnp.concatenate([flipped, jnp.zeros((BS, BS), F32)], axis=1)
            skewed = pltpu.roll(wide, 0, 1, stride=1, stride_axis=0)
            diag_ref[t, h : h + 1, :] = jnp.sum(skewed, axis=0, keepdims=True)
        rest = jnp.sum(sums[h, 2], axis=0, keepdims=True)
        diag_ref[2, h : h + 1, :] = jnp.concatenate([rest, jnp.zeros((1, BS), F32)], axis=1)


def attn_fwd_kernel(heads, blocks, lo_ref, qkv_ref, segment_ref, pattern_ref, out_ref, lse_ref, bias):
    build_bias(heads, pattern_ref, bias)

    def q_step(qb, _):
        forward_rows(heads, qb, lo_ref[qb], qkv_ref, segment_ref, bias, out_ref, lse_ref)
        return 0

    lax.fori_loop(0, blocks, q_step, 0)


def attn_bwd_kernel(
    heads,
    blocks,
    lo_ref,
    qkv_ref,
    out_ref,
    grad_ref,
    lse_ref,
    segment_ref,
    pattern_ref,
    grad_qkv_ref,
    diag_ref,
    bias,
    dk,
    dv,
    sums,
):
    build_bias(heads, pattern_ref, bias)
    backward_start(dk, dv, sums)

    def q_step(qb, _):
        backward_rows(
            heads,
            qb,
            lo_ref[qb],
            qkv_ref,
            out_ref,
            grad_ref,
            lse_ref,
            segment_ref,
            bias,
            grad_qkv_ref,
            dk,
            dv,
            sums,
        )
        return 0

    lax.fori_loop(0, blocks, q_step, 0)
    backward_end(heads, grad_qkv_ref, dk, dv)
    diagonal_sums(heads, sums, diag_ref)


def vspec():
    return pl.BlockSpec(memory_space=pltpu.VMEM)


def sspec():
    return pl.BlockSpec(memory_space=pltpu.SMEM)


def attention_forward(projected, lo, segments, patterns, heads):
    seq_len = projected.shape[0]
    blocks = seq_len // BS
    return pl.pallas_call(
        functools.partial(attn_fwd_kernel, heads, blocks),
        out_shape=(
            jax.ShapeDtypeStruct((seq_len, heads * HD), BF16),
            jax.ShapeDtypeStruct((seq_len, heads), F32),
        ),
        in_specs=[sspec(), vspec(), vspec(), vspec()],
        out_specs=(vspec(), vspec()),
        scratch_shapes=[pltpu.VMEM((heads, 3, BS, BS), F32)],
        compiler_params=pltpu.CompilerParams(vmem_limit_bytes=VMEM_LIMIT),
        name="attn_fwd",
    )(lo, projected, segments, patterns)


def attention_backward(projected, attended, grad, lse, lo, segments, patterns, heads):
    seq_len = projected.shape[0]
    blocks = seq_len // BS
    width = heads * HD
    return pl.pallas_call(
        functools.partial(attn_bwd_kernel, heads, blocks),
        out_shape=(
            jax.ShapeDtypeStruct((seq_len, 3 * width), BF16),
            jax.ShapeDtypeStruct((3, 8, 2 * BS), F32),
        ),
        in_specs=[sspec()] + [vspec()] * 6,
        out_specs=(vspec(), vspec()),
        scratch_shapes=backward_scratch(heads, seq_len),
        compiler_params=pltpu.CompilerParams(vmem_limit_bytes=VMEM_LIMIT),
        name="attn_bwd",
    )(lo, projected, attended, grad, lse, segments, patterns)


def backward_scratch(heads, seq_len):
    return [
        pltpu.VMEM((heads, 3, BS, BS), F32),
        pltpu.VMEM((seq_len, heads * HD), F32),
        pltpu.VMEM((seq_len, heads * HD), F32),
        pltpu.VMEM((heads, 3, BS, BS), F32),
    ]


MESH = pl.DeviceIdType.MESH
SMALL = 32


def remote(src, dst, send, recv, axis, peer):
    return pltpu.make_async_remote_copy(
        src_ref=src,
        dst_ref=dst,
        send_sem=send,
        recv_sem=recv,
        device_id={axis: peer},
        device_id_type=MESH,
    )


def staged(kernel, count, which):
    def run(*refs):
        inputs = list(refs[:count])
        buffers, sems = refs[-len(which) - 1 : -1], refs[-1]
        loads = []
        for place, (index, buffer) in enumerate(zip(which, buffers)):
            loads.append(pltpu.make_async_copy(inputs[index], buffer, sems.at[place]))
            loads[-1].start()
            inputs[index] = buffer
        kernel(loads, *inputs, *refs[count : -len(which) - 1])

    return run


def staged_specs(args, which):
    specs = [any_spec() if i in which else vspec() for i in range(len(args))]
    scratch = [pltpu.VMEM(args[i].shape, args[i].dtype) for i in which]
    return specs, scratch + [pltpu.SemaphoreType.DMA((len(which),))]


def greet(groups, loads=()):
    barrier = pltpu.get_barrier_semaphore()
    total = 0
    for axis, n in groups:
        me = lax.axis_index(axis)
        for step in range(1, n):
            pl.semaphore_signal(
                barrier, inc=1, device_id={axis: lax.rem(me + step, n)}, device_id_type=MESH
            )
        total += n - 1
    pl.semaphore_wait(barrier, total)
    for load in loads:
        load.wait()


class LineSum:
    def __init__(self, n, parts, send, recv, send_sem, recv_sem, total):
        self.n, self.parts = n, parts
        self.send, self.recv, self.send_sem, self.recv_sem = send, recv, send_sem, recv_sem
        self.total = total
        self.me = lax.axis_index("tensor")

    def flow(self, first, k):
        n, me = self.n, self.me
        near = me * 2 < n
        right = near if first else jnp.logical_not(near)
        block = jnp.where(right, n - 1 - k, k)
        comes = jnp.where(right, jnp.where(me > 0, me <= block, False), jnp.where(me < n - 1, me >= block, False))
        goes = jnp.where(right, me < block, me > block)
        peer = jnp.clip(jnp.where(right, me + 1, me - 1), 0, n - 1)
        out_slot = jnp.clip(jnp.where(right, k, n - 1 - me + k), 0, n - 2)
        in_slot = jnp.clip(jnp.where(right, k, n - me + k), 0, n)
        peer_slot = jnp.clip(jnp.where(right, k, n - peer + k), 0, n)
        return block, comes, goes, peer, out_slot, in_slot, peer_slot

    def copy(self, peer, out_slot, slot):
        return remote(
            self.send.at[out_slot],
            self.recv.at[slot],
            self.send_sem.at[out_slot],
            self.recv_sem.at[slot],
            "tensor",
            peer,
        )

    def start(self, partial=None):
        n, me = self.n, self.me

        def one(index, _):
            block = jnp.where(me * 2 < n, n - 1 - index, index)
            if partial is not None:
                value = partial(block)
                self.parts[block] = value.astype(BF16)

                @pl.when(block == me)
                def _():
                    self.total[...] = value

            @pl.when(jnp.logical_or(me == 0, me == n - 1) & (index < n - 1))
            def _():
                remote(
                    self.parts.at[block],
                    self.recv.at[jnp.where(me == 0, index, 2 + index)],
                    self.send_sem.at[index],
                    self.recv_sem.at[jnp.where(me == 0, index, 2 + index)],
                    "tensor",
                    jnp.where(me == 0, 1, n - 2),
                ).start()

            return 0

        lax.fori_loop(0, n, one, 0)
        if partial is None:
            self.total[...] = self.parts[me].astype(F32)

    def finish(self):
        for k in range(self.n - 1):
            self.step(k)

    def step(self, k):
        for first in (True, False):
            block, comes, goes, peer, out_slot, in_slot, peer_slot = self.flow(first, k)

            @pl.when(goes & comes)
            def _():
                self.copy(peer, out_slot, in_slot).wait_recv()
                self.send[out_slot] = (
                    self.parts[block].astype(F32) + self.recv[in_slot].astype(F32)
                ).astype(BF16)
                self.copy(peer, out_slot, peer_slot).start()

            @pl.when(comes & jnp.logical_not(goes))
            def _():
                self.copy(peer, 0, in_slot).wait_recv()
                self.total[...] += self.recv[in_slot].astype(F32)

    def drain(self):
        for k in range(self.n - 1):
            for first in (True, False):
                block, comes, goes, peer, out_slot, in_slot, peer_slot = self.flow(first, k)

                @pl.when(goes)
                def _():
                    self.copy(peer, out_slot, in_slot).wait_send()


def tail_kernel(
    n_dp,
    n_tensor,
    experts,
    table_rows,
    hidden_ref,
    grad_ref,
    weight_ref,
    attended_ref,
    branch_ref,
    small_ref,
    weight_own_ref,
    gain_own_ref,
    grad_hidden_ref,
    grad_qkv_ref,
    grad_out_ref,
    small_out_ref,
    parts,
    line_send,
    line_recv,
    qkv_send,
    qkv_recv,
    out_send,
    out_recv,
    small_recv,
    small_sum,
    gain_recv,
    line_send_sem,
    line_recv_sem,
    qkv_send_sem,
    qkv_recv_sem,
    out_send_sem,
    out_recv_sem,
    small_send_sem,
    small_recv_sem,
    gain_send_sem,
    gain_recv_sem,
):
    own_rows = grad_hidden_ref.shape[0]
    depth = weight_own_ref.shape[0]
    out_cols = grad_out_ref.shape[1]
    me = lax.axis_index("dp")
    me_t = lax.axis_index("tensor")
    greet([("dp", n_dp), ("tensor", n_tensor)])

    def partial(block):
        rows = pl.ds(pl.multiple_of(block * own_rows, own_rows), own_rows)
        return nt(grad_ref[rows, :], weight_ref[...])

    line = LineSum(
        n_tensor, parts, line_send, line_recv, line_send_sem, line_recv_sem, grad_hidden_ref
    )
    line.start(partial)
    copies = []
    for step in range(1, n_dp):
        peer = lax.rem(me + step, n_dp)
        copy = remote(
            small_ref.at[peer],
            small_recv.at[step - 1],
            small_send_sem.at[step - 1],
            small_recv_sem.at[step - 1],
            "dp",
            peer,
        )
        copy.start()
        copies.append(copy)
    for block in range(n_dp):
        cols = slice(block * depth, (block + 1) * depth)
        qkv_send[block] = tn(hidden_ref[:, cols], grad_ref[...]).astype(BF16)
    for step in range(1, n_dp):
        peer = lax.rem(me + step, n_dp)
        copy = remote(
            qkv_send.at[peer],
            qkv_recv.at[step - 1],
            qkv_send_sem.at[step - 1],
            qkv_recv_sem.at[step - 1],
            "dp",
            peer,
        )
        copy.start()
        copies.append(copy)
    for block in range(n_dp):
        cols = slice(block * out_cols, (block + 1) * out_cols)
        out_send[block] = tn(attended_ref[...], branch_ref[:, cols]).astype(BF16)
    for step in range(1, n_dp):
        peer = lax.rem(me + step, n_dp)
        copy = remote(
            out_send.at[peer],
            out_recv.at[step - 1],
            out_send_sem.at[step - 1],
            out_recv_sem.at[step - 1],
            "dp",
            peer,
        )
        copy.start()
        copies.append(copy)
    line.finish()
    for copy in copies:
        copy.wait()
    small_sum[...] = small_ref[me]
    grad_qkv_ref[...] = qkv_send[me].astype(F32)
    grad_out_ref[...] = out_send[me].astype(F32)
    for step in range(1, n_dp):
        small_sum[...] += small_recv[step - 1]
        grad_qkv_ref[...] += qkv_recv[step - 1].astype(F32)
        grad_out_ref[...] += out_recv[step - 1].astype(F32)
    column = jnp.sum(grad_qkv_ref[...] * weight_own_ref[...].astype(F32), axis=1, keepdims=True)
    eye = lax.broadcasted_iota(jnp.int32, (depth, depth), 0) == lax.broadcasted_iota(
        jnp.int32, (depth, depth), 1
    )
    row = jnp.sum(jnp.where(eye, column, 0.0), axis=0, keepdims=True)
    small_sum[experts + 1 : experts + 2, :] = row / gain_own_ref[...]
    gains = []
    for step in range(1, n_tensor):
        peer = lax.rem(me_t + step, n_tensor)
        copy = remote(
            small_sum,
            gain_recv.at[step - 1],
            gain_send_sem.at[step - 1],
            gain_recv_sem.at[step - 1],
            "tensor",
            peer,
        )
        copy.start()
        gains.append(copy)
    line.drain()
    for copy in gains:
        copy.wait()
    small_out_ref[...] = small_sum[...]
    shared = slice(0, experts + 2)
    for step in range(1, n_tensor):
        small_out_ref[shared, :] += gain_recv[step - 1, shared, :]


def tail(n_dp, n_tensor, experts, hidden, grad, weight, attended, branch, small, weight_own, gain_own):
    seq_len, width = hidden.shape
    own_rows = seq_len // n_tensor
    depth, cols = weight_own.shape
    heads_cols = attended.shape[1]
    out_cols = width // n_dp
    table_rows = NB // n_dp
    return pl.pallas_call(
        functools.partial(tail_kernel, n_dp, n_tensor, experts, table_rows),
        out_shape=(
            jax.ShapeDtypeStruct((own_rows, width), F32),
            jax.ShapeDtypeStruct((depth, cols), F32),
            jax.ShapeDtypeStruct((heads_cols, out_cols), F32),
            jax.ShapeDtypeStruct((SMALL, depth), F32),
        ),
        in_specs=[vspec()] * 8,
        out_specs=(vspec(),) * 4,
        scratch_shapes=[
            pltpu.VMEM((n_tensor, own_rows, width), BF16),
            pltpu.VMEM((n_tensor - 1, own_rows, width), BF16),
            pltpu.VMEM((n_tensor + 1, own_rows, width), BF16),
            pltpu.VMEM((n_dp, depth, cols), BF16),
            pltpu.VMEM((n_dp - 1, depth, cols), BF16),
            pltpu.VMEM((n_dp, heads_cols, out_cols), BF16),
            pltpu.VMEM((n_dp - 1, heads_cols, out_cols), BF16),
            pltpu.VMEM((n_dp - 1, SMALL, depth), F32),
            pltpu.VMEM((SMALL, depth), F32),
            pltpu.VMEM((n_tensor - 1, SMALL, depth), F32),
            pltpu.SemaphoreType.DMA((n_tensor - 1,)),
            pltpu.SemaphoreType.DMA((n_tensor + 1,)),
        ]
        + [pltpu.SemaphoreType.DMA((n_dp - 1,))] * 6
        + [pltpu.SemaphoreType.DMA((n_tensor - 1,))] * 2,
        compiler_params=pltpu.CompilerParams(
            vmem_limit_bytes=VMEM_LIMIT, collective_id=0, has_side_effects=True
        ),
        name="tail",
    )(hidden, grad, weight, attended, branch, small, weight_own, gain_own)


def diagonal(size):
    return lax.broadcasted_iota(jnp.int32, (size, size), 0) == lax.broadcasted_iota(
        jnp.int32, (size, size), 1
    )


def to_column(row):
    return jnp.sum(jnp.where(diagonal(row.shape[1]), row, 0.0), axis=1, keepdims=True)


def to_row(column):
    return jnp.sum(jnp.where(diagonal(column.shape[0]), column, 0.0), axis=0, keepdims=True)


def expert_kernel(
    n_dp,
    local,
    capacity,
    rows_hbm,
    grad_hbm,
    gates_ref,
    in_hbm,
    out_hbm,
    back_ref,
    gate_back_ref,
    value_ref,
    grad_in_ref,
    grad_out_ref,
    back_send,
    gate_send,
    zs,
    ups,
    gates_s,
    stage,
    value_stage,
    back_send_sem,
    back_recv_sem,
    gate_send_sem,
    gate_recv_sem,
    own_sem,
    stage_sem,
    value_sem,
    rows_ref,
    grad_ref,
    in_ref,
    out_ref,
    rows_sem,
    grad_sem,
    in_sem,
    out_sem,
):
    me = lax.axis_index("dp")
    pairs = n_dp // 2
    hidden = in_ref.shape[2]
    width = rows_ref.shape[2]
    two = 2 * capacity

    def pair_at(index):
        return (me // 2) ^ (pairs - 1 - index)

    def load_pair(index):
        where = pl.ds(2 * pair_at(index), 2)
        return (
            pltpu.make_async_copy(rows_hbm.at[where], rows_ref.at[where], rows_sem.at[index]),
            pltpu.make_async_copy(grad_hbm.at[where], grad_ref.at[where], grad_sem.at[index]),
        )

    def load_expert(expert):
        return (
            pltpu.make_async_copy(in_hbm.at[expert], in_ref.at[expert], in_sem.at[expert]),
            pltpu.make_async_copy(out_hbm.at[expert], out_ref.at[expert], out_sem.at[expert]),
        )

    for copy in load_expert(0) + load_pair(0):
        copy.start()
    for index in range(1, pairs):
        for copy in load_pair(index):
            copy.start()
    for expert in range(1, local):
        for copy in load_expert(expert):
            copy.start()
    greet([("dp", n_dp)])

    def back_copy(expert, target, sender):
        part = slice(expert * capacity, (expert + 1) * capacity)
        return remote(
            back_send.at[target, part],
            back_ref.at[sender, part],
            back_send_sem.at[expert, target],
            back_recv_sem.at[expert, sender],
            "dp",
            target,
        )

    def own_copy(expert):
        part = slice(expert * capacity, (expert + 1) * capacity)
        return pltpu.make_async_copy(
            back_send.at[me, part], back_ref.at[me, part], own_sem.at[expert]
        )

    def stage_copy(slot, target):
        return pltpu.make_async_copy(stage.at[slot], target, stage_sem.at[slot])

    gate_send[...] = jnp.zeros_like(gate_send)
    staged = []

    def put(value, target):
        slot = len(staged) % 2
        if len(staged) >= 2:
            staged[-2].wait()
        stage[slot] = value
        copy = stage_copy(slot, target)
        copy.start()
        staged.append(copy)

    for expert in range(local):
        part = slice(expert * capacity, (expert + 1) * capacity)

        for copy in load_expert(expert):
            copy.wait()

        def group(index, _):
            if expert == 0:
                for copy in load_pair(index):
                    copy.wait()
            first = 2 * pair_at(index)
            rows = rows_ref[pl.ds(first, 2), part, :].reshape(two, width)
            grads = grad_ref[pl.ds(first, 2), part, :].reshape(two, width)
            column = jnp.concatenate(
                [to_column(gates_ref[first + j, 0:1, part]) for j in range(2)], axis=0
            )
            gate = nt(rows, in_ref[expert, 0])
            up = nt(rows, in_ref[expert, 1])
            square = gate * gate
            bent = jnp.tanh(0.7978845608028654 * gate * (1.0 + 0.044715 * square))
            half = 0.5 * (1.0 + bent)
            gelu = gate * half
            slope = half + 0.5 * gate * (1.0 - bent * bent) * (
                0.7978845608028654 * (1.0 + 3 * 0.044715 * square)
            )
            z = gelu * up
            grad_z = nt(grads, out_ref[expert])
            gate_grad = jnp.sum(z * grad_z, axis=1, keepdims=True)
            grad_z = column * grad_z
            zs[pl.ds(first, 2)] = (column * z).astype(BF16).reshape(2, capacity, hidden)
            ups[0, pl.ds(first, 2)] = (grad_z * up * slope).astype(BF16).reshape(2, capacity, hidden)
            ups[1, pl.ds(first, 2)] = (grad_z * gelu).astype(BF16).reshape(2, capacity, hidden)
            for j in range(2):
                gate_send[first + j, 0:1, part] = to_row(
                    gate_grad[j * capacity : (j + 1) * capacity]
                )
            back = nn(ups[0, pl.ds(first, 2)].reshape(two, hidden), in_ref[expert, 0])
            back += nn(ups[1, pl.ds(first, 2)].reshape(two, hidden), in_ref[expert, 1])
            back_send[pl.ds(first, 2), part, :] = back.astype(BF16).reshape(2, capacity, width)
            for j in range(2):
                target = first + j

                @pl.when(target != me)
                def _():
                    back_copy(expert, target, me).start()

                @pl.when(target == me)
                def _():
                    own_copy(expert).start()

            return 0

        lax.fori_loop(0, pairs, group, 0)
        if expert == local - 1:
            gate_copies = []
            for step in range(1, n_dp):
                target = lax.rem(me + step, n_dp)
                copy = remote(
                    gate_send.at[target],
                    gate_back_ref.at[me],
                    gate_send_sem.at[step - 1],
                    gate_recv_sem.at[step - 1],
                    "dp",
                    target,
                )
                copy.start()
                gate_copies.append(copy)
            gate_back_ref[me] = gate_send[me]
        rows = rows_ref[:, part, :].reshape(n_dp * capacity, width)
        for half in range(2):
            put(tn(ups[half].reshape(n_dp * capacity, hidden), rows), grad_in_ref.at[expert, half])
        grads = grad_ref[:, part, :].reshape(n_dp * capacity, width)
        put(tn(zs[...].reshape(n_dp * capacity, hidden), grads), grad_out_ref.at[expert])
        if expert > 0:
            pltpu.make_async_copy(
                value_stage, value_ref.at[:, slice((expert - 1) * capacity, expert * capacity)], value_sem
            ).wait()

        def value(pair, _):
            out = nn(zs[pl.ds(2 * pair, 2)].reshape(two, hidden), out_ref[expert])
            value_stage[pl.ds(2 * pair, 2)] = out.astype(BF16).reshape(2, capacity, width)
            return 0

        lax.fori_loop(0, pairs, value, 0)
        pltpu.make_async_copy(value_stage, value_ref.at[:, part], value_sem).start()

    last = slice((local - 1) * capacity, local * capacity)
    pltpu.make_async_copy(value_stage, value_ref.at[:, last], value_sem).wait()
    for copy in staged[-2:]:
        copy.wait()
    for copy in gate_copies:
        copy.wait()
    for expert in range(local):
        own_copy(expert).wait()
        for step in range(1, n_dp):
            peer = lax.rem(me + step, n_dp)
            back_copy(expert, peer, me).wait_send()
            back_copy(expert, me, peer).wait_recv()


def any_spec():
    return pl.BlockSpec(memory_space=pl.ANY)


def run_experts(n_dp, capacity, rows, grads, gates, w_in, w_out):
    local, _, hidden, width = w_in.shape
    slots = local * capacity
    return pl.pallas_call(
        functools.partial(expert_kernel, n_dp, local, capacity),
        out_shape=(
            jax.ShapeDtypeStruct((n_dp, slots, width), BF16),
            jax.ShapeDtypeStruct((n_dp, 8, slots), F32),
            jax.ShapeDtypeStruct((n_dp, slots, width), BF16),
            jax.ShapeDtypeStruct(w_in.shape, F32),
            jax.ShapeDtypeStruct(w_out.shape, F32),
        ),
        in_specs=[any_spec(), any_spec(), vspec(), any_spec(), any_spec()],
        out_specs=(any_spec(), vspec(), any_spec(), any_spec(), any_spec()),
        scratch_shapes=[
            pltpu.VMEM((n_dp, slots, width), BF16),
            pltpu.VMEM((n_dp, 8, slots), F32),
            pltpu.VMEM((n_dp, capacity, hidden), BF16),
            pltpu.VMEM((2, n_dp, capacity, hidden), BF16),
            pltpu.VMEM((8, 128), F32),
            pltpu.VMEM((2, hidden, width), F32),
            pltpu.VMEM((n_dp, capacity, width), BF16),
            pltpu.SemaphoreType.DMA((local, n_dp)),
            pltpu.SemaphoreType.DMA((local, n_dp)),
            pltpu.SemaphoreType.DMA((n_dp - 1,)),
            pltpu.SemaphoreType.DMA((n_dp - 1,)),
            pltpu.SemaphoreType.DMA((local,)),
            pltpu.SemaphoreType.DMA((2,)),
            pltpu.SemaphoreType.DMA,
            pltpu.VMEM(rows.shape, BF16),
            pltpu.VMEM(grads.shape, BF16),
            pltpu.VMEM(w_in.shape, BF16),
            pltpu.VMEM(w_out.shape, BF16),
            pltpu.SemaphoreType.DMA((n_dp // 2,)),
            pltpu.SemaphoreType.DMA((n_dp // 2,)),
            pltpu.SemaphoreType.DMA((local,)),
            pltpu.SemaphoreType.DMA((local,)),
        ],
        compiler_params=pltpu.CompilerParams(
            vmem_limit_bytes=VMEM_LIMIT, collective_id=1, has_side_effects=True
        ),
        name="experts",
    )(rows, grads, gates, w_in, w_out)


def chosen_slots(columns, slots):
    lane = lax.broadcasted_iota(jnp.int32, (1, slots), 1)
    return columns[:, 0:1] == lane, columns[:, 1:2] == lane


def combine_kernel(
    n_dp,
    n_tensor,
    experts,
    loads,
    rows_ref,
    gate_ref,
    slots_ref,
    routes_ref,
    residual_ref,
    hidden_ref,
    cotangent_ref,
    router_ref,
    gain_ref,
    weight_ref,
    value_ref,
    grad_residual_ref,
    branch_ref,
    grad_attended_ref,
    small_ref,
    merged_ref,
    parts,
    total,
    line_send,
    line_recv,
    gate_all,
    gate_send,
    gate_recv,
    value_back,
    line_send_sem,
    line_recv_sem,
    gate_send_sem,
    gate_recv_sem,
    value_send_sem,
    value_recv_sem,
    value_own_sem,
    gather_send_sem,
    gather_recv_sem,
):
    own_rows, width = residual_ref.shape
    slots = rows_ref.shape[0]
    per = slots // n_dp
    me = lax.axis_index("dp")
    me_t = lax.axis_index("tensor")
    greet([("dp", n_dp), ("tensor", n_tensor)], loads)
    values = []
    for step in range(1, n_dp):
        peer = lax.rem(me + step, n_dp)
        copy = remote(
            value_ref.at[peer],
            value_back.at[me],
            value_send_sem.at[step - 1],
            value_recv_sem.at[step - 1],
            "dp",
            peer,
        )
        copy.start()
        values.append(copy)
    fetch = pltpu.make_async_copy(value_ref.at[me], value_back.at[me], value_own_sem)
    fetch.start()

    def partial(block):
        one, two = chosen_slots(
            slots_ref[pl.ds(pl.multiple_of(block * own_rows, own_rows), own_rows), :], slots
        )
        return nn(jnp.where(one | two, 1.0, 0.0).astype(BF16), rows_ref[...])

    line = LineSum(n_tensor, parts, line_send, line_recv, line_send_sem, line_recv_sem, total)
    line.start(partial)
    for peer in range(n_dp):
        gate_all[0:1, peer * per : (peer + 1) * per] = gate_ref[peer, 0:1, :]
    gate_send[...] = jnp.zeros_like(gate_send)
    gates = []
    for step in range(n_tensor):
        peer = lax.rem(me_t + step, n_tensor)
        picks = chosen_slots(
            slots_ref[pl.ds(pl.multiple_of(peer * own_rows, own_rows), own_rows), :], slots
        )
        for k in range(TOP):
            column = jnp.sum(
                jnp.where(picks[k], gate_all[0:1, :], 0.0), axis=1, keepdims=True
            )
            gate_send[step, k : k + 1, :] = to_row(column)
        if step:
            copy = remote(
                gate_send.at[step],
                gate_recv.at[step - 1],
                gate_send_sem.at[step - 1],
                gate_recv_sem.at[step - 1],
                "tensor",
                peer,
            )
            copy.start()
            gates.append(copy)
    hidden = hidden_ref[...]
    router = router_ref[...]
    logits = nt(router, hidden)
    exps = jnp.exp(logits - jnp.max(logits, axis=0, keepdims=True))
    probs = exps / jnp.sum(exps, axis=0, keepdims=True)
    ids = lax.broadcasted_iota(jnp.int32, (experts, own_rows), 0)
    own_lanes = pl.ds(pl.multiple_of(me_t * own_rows, own_rows), own_rows)
    first, second = ids == routes_ref[0:1, own_lanes], ids == routes_ref[1:2, own_lanes]
    prob_one = jnp.sum(jnp.where(first, probs, 0.0), axis=0, keepdims=True)
    prob_two = jnp.sum(jnp.where(second, probs, 0.0), axis=0, keepdims=True)
    both = prob_one + prob_two
    line.finish()
    for copy in gates:
        copy.wait()
    gate_sum = gate_send[0]
    for step in range(1, n_tensor):
        gate_sum = gate_sum + gate_recv[step - 1]
    grad_one, grad_two = gate_sum[0:1, :], gate_sum[1:2, :]
    mean_grad = (prob_one * grad_one + prob_two * grad_two) / both
    grad_probs = (
        jnp.where(first, grad_one - mean_grad, 0.0) + jnp.where(second, grad_two - mean_grad, 0.0)
    ) / both
    grad_logits = probs * (grad_probs - jnp.sum(grad_probs * probs, axis=0, keepdims=True))
    grad_hidden = total[...] + lax.dot_general(
        grad_logits,
        router.astype(F32),
        (((0,), (0,)), ((), ())),
        precision=lax.Precision.HIGHEST,
        preferred_element_type=F32,
    )
    residual = residual_ref[...]
    scale = lax.rsqrt(jnp.mean(residual * residual, axis=1, keepdims=True) + EPS)
    unit = residual * scale
    small_ref[...] = jnp.zeros_like(small_ref)
    small_ref[experts : experts + 1, :] = jnp.sum(grad_hidden * unit, axis=0, keepdims=True)
    grad_unit = grad_hidden * gain_ref[...]
    grad_residual = cotangent_ref[...].astype(F32) + scale * (
        grad_unit - unit * jnp.mean(grad_unit * unit, axis=1, keepdims=True)
    )
    grad_residual_ref[...] = grad_residual
    branch_ref[me_t] = grad_residual.astype(BF16)

    def on_block(block):
        grad_attended_ref[pl.ds(pl.multiple_of(block * own_rows, own_rows), own_rows), :] = nt(
            branch_ref[block], weight_ref[...]
        ).astype(BF16)

    lines = Streams(n_tensor, [branch_ref], gather_send_sem, gather_recv_sem)
    for turn in lines.turns():
        lines.turn(turn, lambda j, k: lines.each_new(j, k, on_block))
        if turn == n_tensor - 2:
            fetch.wait()
            for copy in values:
                copy.wait_recv()

            def merge(block, _):
                rows = pl.ds(pl.multiple_of(block * own_rows, own_rows), own_rows)
                one, two = chosen_slots(slots_ref[rows, :], slots)
                merged_ref[block] = nn(
                    jnp.where(one | two, 1.0, 0.0).astype(BF16), value_back[...].reshape(slots, width)
                ).astype(BF16)
                return 0

            lax.fori_loop(0, n_tensor, merge, 0)
    lines.drain()
    small_ref[0:experts, :] = jnp.dot(
        grad_logits,
        hidden.astype(F32),
        precision=lax.Precision.HIGHEST,
        preferred_element_type=F32,
    )
    line.drain()
    for copy in values:
        copy.wait_send()


def combine(
    n_dp,
    n_tensor,
    experts,
    rows,
    gates,
    slot_columns,
    routes_own,
    residual,
    hidden,
    cotangent,
    router_rows,
    gain,
    weight,
    value,
):
    own_rows, width = residual.shape
    slots = rows.shape[0]
    args = (
        rows,
        gates,
        slot_columns,
        routes_own,
        residual,
        hidden,
        cotangent,
        router_rows,
        gain,
        weight,
        value,
    )
    which = (0, 4, 5, 6, 9)
    specs, buffers = staged_specs(args[:10], which)
    return pl.pallas_call(
        staged(functools.partial(combine_kernel, n_dp, n_tensor, experts), len(args), which),
        out_shape=(
            jax.ShapeDtypeStruct((own_rows, width), F32),
            jax.ShapeDtypeStruct((n_tensor, own_rows, width), BF16),
            jax.ShapeDtypeStruct((n_tensor * own_rows, weight.shape[0]), BF16),
            jax.ShapeDtypeStruct((SMALL, width), F32),
            jax.ShapeDtypeStruct((n_tensor, own_rows, width), BF16),
        ),
        in_specs=specs + [any_spec()],
        out_specs=(vspec(),) * 5,
        scratch_shapes=[
            pltpu.VMEM((n_tensor, own_rows, width), BF16),
            pltpu.VMEM((own_rows, width), F32),
            pltpu.VMEM((n_tensor - 1, own_rows, width), BF16),
            pltpu.VMEM((n_tensor + 1, own_rows, width), BF16),
            pltpu.VMEM((8, slots), F32),
            pltpu.VMEM((n_tensor, 8, own_rows), F32),
            pltpu.VMEM((n_tensor - 1, 8, own_rows), F32),
            pltpu.VMEM(value.shape, BF16),
            pltpu.SemaphoreType.DMA((n_tensor - 1,)),
            pltpu.SemaphoreType.DMA((n_tensor + 1,)),
            pltpu.SemaphoreType.DMA((n_tensor - 1,)),
            pltpu.SemaphoreType.DMA((n_tensor - 1,)),
            pltpu.SemaphoreType.DMA((n_dp - 1,)),
            pltpu.SemaphoreType.DMA((n_dp - 1,)),
            pltpu.SemaphoreType.DMA,
            pltpu.SemaphoreType.DMA((1, 2, n_tensor - 1)),
            pltpu.SemaphoreType.DMA((1, 2, n_tensor - 1)),
        ]
        + buffers,
        compiler_params=pltpu.CompilerParams(
            vmem_limit_bytes=VMEM_LIMIT, collective_id=2, has_side_effects=True
        ),
        name="combine",
    )(*args)


class Streams:
    def __init__(self, n, refs, send_sem, recv_sem):
        self.n, self.refs, self.send_sem, self.recv_sem = n, refs, send_sem, recv_sem
        self.me = lax.axis_index("tensor")

    def copy(self, j, block, slot, k, peer):
        ref = self.refs[j].at[block]
        return remote(
            ref, ref, self.send_sem.at[j, slot, k], self.recv_sem.at[j, slot, k], "tensor", peer
        )

    def outgoing(self, j, k, fn):
        for slot, sign in enumerate((1, -1)):
            block, peer = self.me - sign * k, self.me + sign

            @pl.when((block >= 0) & (block < self.n) & (peer >= 0) & (peer < self.n))
            def _():
                fn(self.copy(j, block, slot, k, peer))

    def incoming(self, j, k, fn):
        for slot, sign in enumerate((1, -1)):
            block = self.me - sign * (k + 1)

            @pl.when((block >= 0) & (block < self.n))
            def _():
                fn(self.copy(j, block, slot, k, jnp.clip(self.me - sign, 0, self.n - 1)), block)

    def turn(self, turn, used=None):
        moved = []
        for j in range(len(self.refs)):
            k = turn - j
            if k < 0 or k > self.n - 1:
                continue
            self.advance(j, k)
            moved.append((j, k))
        if used is not None:
            for j, k in moved:
                used(j, k)

    def turns(self):
        return range(self.n + len(self.refs) - 1)

    def advance(self, j, k):
        if k > 0:
            self.incoming(j, k - 1, lambda c, block: c.wait_recv())
        if k < self.n - 1:
            self.outgoing(j, k, lambda c: c.start())

    def each_new(self, j, k, fn):
        if k == 0:
            fn(self.me)
            return
        for sign in (1, -1):
            block = self.me - sign * k

            @pl.when((block >= 0) & (block < self.n))
            def _():
                fn(block)

    def drain(self):
        for j in range(len(self.refs)):
            for k in range(self.n - 1):
                self.outgoing(j, k, lambda c: c.wait_send())


class Spread:
    def __init__(self, n, ref, far_send, far_recv, near_send, near_recv):
        self.n, self.ref = n, ref
        self.far_send, self.far_recv = far_send, far_recv
        self.near_send, self.near_recv = near_send, near_recv
        self.me = lax.axis_index("dp")
        self.partner = self.me ^ 1

    def far(self, step, block, peer):
        ref = self.ref.at[block]
        return remote(ref, ref, self.far_send.at[step], self.far_recv.at[step], "dp", peer)

    def near(self, step, block):
        ref = self.ref.at[block]
        return remote(
            ref, ref, self.near_send.at[step], self.near_recv.at[step], "dp", self.partner
        )

    def start(self):
        for step in range(1, self.n // 2):
            self.far(step - 1, self.me, lax.rem(self.me + 2 * step, self.n)).start()
        self.near(0, self.me).start()

    def source(self, me, step):
        return lax.rem(me + self.n - 2 * step, self.n)

    def relay(self):
        for step in range(1, self.n // 2):
            block = self.source(self.me, step)
            self.far(step - 1, block, block).wait_recv()
            self.near(step, block).start()

    def finish(self):
        for step in range(self.n // 2):
            self.near(step, self.source(self.partner, step)).wait_recv()

    def drain(self):
        for step in range(1, self.n // 2):
            self.far(step - 1, self.me, lax.rem(self.me + 2 * step, self.n)).wait_send()
        for step in range(self.n // 2):
            self.near(step, self.source(self.me, step)).wait_send()


def one_hot(slot_rows, target, per):
    lane_slots = lax.broadcasted_iota(jnp.int32, (per, 1), 0) + target * per
    return jnp.where(
        (lane_slots == slot_rows[0:1, :]) | (lane_slots == slot_rows[1:2, :]), 1.0, 0.0
    ).astype(BF16)


def band(seq_len):
    return -(-(seq_len // 2 - 1) // BS)


def send_parameters(n_dp, n_tensor, weight_ref, extra_ref, out_ref, weights_ref, outs_ref, extras_ref, sems):
    me = lax.axis_index("dp")
    me_t = lax.axis_index("tensor")
    (extra_send, extra_recv, line_send, line_recv) = sems[:4]
    extras_ref[me] = extra_ref[...]
    small = []
    for step in range(1, n_dp):
        peer = lax.rem(me + step, n_dp)
        copy = remote(
            extra_ref, extras_ref.at[me], extra_send.at[step - 1], extra_recv.at[step - 1], "dp", peer
        )
        copy.start()
        small.append(copy)
    weights_ref[me] = weight_ref[...]
    weights = Spread(n_dp, weights_ref, *sems[4:8])
    weights.start()
    outs_ref[me, me_t] = out_ref[...]
    along = []
    for step in range(1, n_tensor):
        peer = lax.rem(me_t + step, n_tensor)
        copy = remote(
            out_ref,
            outs_ref.at[me, me_t],
            line_send.at[step - 1],
            line_recv.at[step - 1],
            "tensor",
            peer,
        )
        copy.start()
        along.append(copy)
    return small, weights, Spread(n_dp, outs_ref, *sems[8:12]), along


def unpack_parameters(n_dp, experts, extras_ref, selector_ref, router_ref, table, pattern_ref):
    depth = table.shape[1]
    rows_each = NB // n_dp
    for block in range(n_dp):
        router_ref[:, block * depth : (block + 1) * depth] = extras_ref[block, 0:experts, :]
        table[block * rows_each : (block + 1) * rows_each, :] = extras_ref[
            block, experts + 2 : experts + 2 + rows_each, :
        ].astype(F32)
    patterns = lax.dot_general(
        table[...],
        selector_ref[...],
        (((0,), (0,)), ((), ())),
        precision=lax.Precision.HIGHEST,
        preferred_element_type=F32,
    )
    for row in range(pattern_ref.shape[0]):
        pattern_ref[row : row + 1, :] = patterns[
            row // 2 : row // 2 + 1, (row % 2) * 2 * BS : (row % 2 + 1) * 2 * BS
        ]


def first_hidden(n_dp, experts, tokens_ref, extras_ref, gains_ref, small):
    depth = extras_ref.shape[2]
    x = tokens_ref[...].astype(F32)
    scaled = x * lax.rsqrt(jnp.mean(x * x, axis=1, keepdims=True) + EPS)
    for copy in small:
        copy.wait()
    for block in range(n_dp):
        gains_ref[0:2, block * depth : (block + 1) * depth] = extras_ref[
            block, experts : experts + 2, :
        ].astype(F32)
    return (scaled * gains_ref[0:1, :]).astype(BF16)


def parameter_sems(n_dp, n_tensor):
    dma = pltpu.SemaphoreType.DMA
    return (
        [dma((n_dp - 1,))] * 2 + [dma((n_tensor - 1,))] * 2 + [dma((n_dp // 2,))] * 8
    )


def front_kernel(
    n_dp,
    n_tensor,
    experts,
    tokens_ref,
    weight_ref,
    extra_ref,
    out_ref,
    selector_ref,
    hidden_ref,
    projected_ref,
    weights_ref,
    outs_ref,
    pattern_ref,
    router_ref,
    gains_ref,
    extras_ref,
    table,
    *sems,
):
    own_rows, width = tokens_ref.shape
    me_t = lax.axis_index("tensor")
    greet([("dp", n_dp), ("tensor", n_tensor)])
    small, weights, spread, along = send_parameters(
        n_dp, n_tensor, weight_ref, extra_ref, out_ref, weights_ref, outs_ref, extras_ref, sems
    )
    hidden_ref[me_t] = first_hidden(n_dp, experts, tokens_ref, extras_ref, gains_ref, small)
    lines = Streams(n_tensor, [hidden_ref], sems[12], sems[13])
    lines.turn(0)
    unpack_parameters(n_dp, experts, extras_ref, selector_ref, router_ref, table, pattern_ref)
    weights.relay()
    for copy in along:
        copy.wait_recv()
    spread.start()
    weights.finish()
    spread.relay()
    spread.finish()

    def project(block):
        rows = pl.ds(pl.multiple_of(block * own_rows, own_rows), own_rows)
        projected_ref[rows, :] = nn(
            hidden_ref[block], weights_ref[...].reshape(width, weights_ref.shape[2])
        ).astype(BF16)

    for turn in lines.turns():
        if turn:
            lines.turn(turn)

    def every(block, _):
        project(block)
        return 0

    lax.fori_loop(0, n_tensor, every, 0)
    lines.drain()
    weights.drain()
    spread.drain()
    for copy in along:
        copy.wait_send()


def front(n_dp, n_tensor, experts, tokens, weight, extra, out, selectors):
    own_rows, width = tokens.shape
    seq_len = own_rows * n_tensor
    depth, cols = weight.shape
    heads = cols // (3 * HD)
    dma = pltpu.SemaphoreType.DMA
    return pl.pallas_call(
        functools.partial(front_kernel, n_dp, n_tensor, experts),
        out_shape=(
            jax.ShapeDtypeStruct((n_tensor, own_rows, width), BF16),
            jax.ShapeDtypeStruct((seq_len, cols), BF16),
            jax.ShapeDtypeStruct((n_dp, depth, cols), BF16),
            jax.ShapeDtypeStruct((n_dp, n_tensor) + out.shape, BF16),
            jax.ShapeDtypeStruct((2 * heads, 2 * BS), F32),
            jax.ShapeDtypeStruct((experts, width), BF16),
            jax.ShapeDtypeStruct((2, width), F32),
        ),
        in_specs=[vspec()] * 5,
        out_specs=(vspec(),) * 7,
        scratch_shapes=[pltpu.VMEM((n_dp,) + extra.shape, BF16), pltpu.VMEM((NB, depth), F32)]
        + parameter_sems(n_dp, n_tensor)
        + [dma((1, 2, n_tensor - 1))] * 2,
        compiler_params=pltpu.CompilerParams(
            vmem_limit_bytes=VMEM_LIMIT, collective_id=3, has_side_effects=True
        ),
        name="front",
    )(tokens, weight, extra, out, selectors)


PARTS = 4
ROW_PARTS = 8


class Dispatch:
    def __init__(self, n_dp, picks, stage, rows_ref, send_sem, recv_sem, own_sem):
        self.n, self.picks, self.stage, self.rows = n_dp, picks, stage, rows_ref
        self.send_sem, self.recv_sem, self.own_sem = send_sem, recv_sem, own_sem
        self.me = lax.axis_index("dp")

    def cols(self, j):
        part = self.stage.shape[3]
        return slice(j * part, (j + 1) * part)

    def copy(self, j, target, sender):
        return remote(
            self.stage.at[j, target],
            self.rows.at[sender, :, self.cols(j)],
            self.send_sem.at[j, target],
            self.recv_sem.at[j, sender],
            "dp",
            target,
        )

    def own(self, j):
        return pltpu.make_async_copy(
            self.stage.at[j, self.me], self.rows.at[self.me, :, self.cols(j)], self.own_sem.at[j]
        )

    def start(self, j, values_ref):
        n_tensor, own_rows, part = values_ref.shape

        def one(index, _):
            mask = self.n - 1 - index
            target = self.me ^ mask
            self.stage[j, target] = nn(
                self.picks[target], values_ref[...].reshape(n_tensor * own_rows, part)
            ).astype(BF16)

            @pl.when(mask != 0)
            def _():
                self.copy(j, target, self.me).start()

            @pl.when(mask == 0)
            def _():
                self.own(j).start()

            return 0

        lax.fori_loop(0, self.n, one, 0)

    def finish(self):
        for j in range(self.stage.shape[0]):
            self.own(j).wait()
            for step in range(1, self.n):
                peer = lax.rem(self.me + step, self.n)
                self.copy(j, peer, self.me).wait_send()
                self.copy(j, self.me, peer).wait_recv()


def opening_kernel(
    n_dp,
    n_tensor,
    experts,
    capacity,
    loads,
    tokens_ref,
    cotangent_ref,
    weight_ref,
    extra_ref,
    out_ref,
    routes_ref,
    segment_ref,
    selector_ref,
    hidden_ref,
    projected_ref,
    weights_ref,
    pattern_ref,
    router_ref,
    gains_ref,
    slots_ref,
    attended_ref,
    lse_ref,
    residual_ref,
    hidden_two_ref,
    weight_own_ref,
    rows_ref,
    grad_rows_ref,
    gates_ref,
    extras_ref,
    table,
    outs,
    out_matrix,
    grads,
    everyone,
    picks,
    grad_stage,
    row_stage,
    bias,
    slot_rows,
    attended_recv,
    logits,
    gate_stage,
    *sems,
):
    own_rows, width = tokens_ref.shape
    seq_len = own_rows * n_tensor
    heads = pattern_ref.shape[0] // 2
    head_cols = heads * HD
    out_cols = out_ref.shape[1]
    local = experts // n_dp
    per = local * capacity
    part = width // PARTS
    row_part = width // ROW_PARTS
    me = lax.axis_index("dp")
    me_t = lax.axis_index("tensor")
    (hop_send, hop_recv, late_send, late_recv) = sems[12:16]
    (grad_send, grad_recv, grad_own, row_send, row_recv, row_own) = sems[16:22]
    (gate_send, gate_recv, attended_send_sem, attended_recv_sem) = sems[22:26]
    greet([("dp", n_dp), ("tensor", n_tensor)], loads)

    def rows_of(block):
        return pl.ds(pl.multiple_of(block * own_rows, own_rows), own_rows)

    for j in range(PARTS):
        grads[j, me_t] = cotangent_ref[:, j * part : (j + 1) * part]
    lines = Streams(
        n_tensor, [hidden_ref] + [grads.at[j] for j in range(PARTS)], hop_send, hop_recv
    )
    lines.advance(1, 0)
    lines.advance(2, 0)
    small, weights, spread, along = send_parameters(
        n_dp, n_tensor, weight_ref, extra_ref, out_ref, weights_ref, outs, extras_ref, sems
    )
    hidden_ref[me_t] = first_hidden(n_dp, experts, tokens_ref, extras_ref, gains_ref, small)
    lines.advance(1, 1)
    lines.advance(2, 1)
    unpack_parameters(n_dp, experts, extras_ref, selector_ref, router_ref, table, pattern_ref)
    lines.advance(1, 2)
    lines.advance(2, 2)
    lines.advance(0, 0)

    ids = lax.broadcasted_iota(jnp.int32, (experts, seq_len), 0)
    hits = [ids == routes_ref[k : k + 1, :] for k in range(TOP)]
    before = lax.broadcasted_iota(jnp.int32, (seq_len, seq_len), 0) < lax.broadcasted_iota(
        jnp.int32, (seq_len, seq_len), 1
    )
    ranks = nn(
        jnp.where(hits[0] | hits[1], 1.0, 0.0).astype(BF16),
        jnp.where(before, 1.0, 0.0).astype(BF16),
    )
    places = ranks + (ids * capacity).astype(F32)
    for k in range(TOP):
        row = jnp.sum(jnp.where(hits[k], places, 0.0), axis=0, keepdims=True)
        slot_rows[k : k + 1, :] = row.astype(jnp.int32)
        for block in range(n_tensor):
            rows = slice(block * own_rows, (block + 1) * own_rows)
            slots_ref[rows, k : k + 1] = to_column(row[:, rows]).astype(jnp.int32)


    def pick(target, _):
        picks[target] = one_hot(slot_rows, target, per)
        return 0

    lax.fori_loop(0, n_dp, pick, 0)
    grad_moves = Dispatch(n_dp, picks, grad_stage, grad_rows_ref, grad_send, grad_recv, grad_own)
    lines.advance(1, 3)
    grad_moves.start(0, grads.at[0])
    lines.advance(2, 3)
    grad_moves.start(1, grads.at[1])
    weights.relay()
    for copy in along:
        copy.wait_recv()
    spread.start()
    build_bias(heads, pattern_ref, bias)

    def project(block):
        projected_ref[rows_of(block), :] = nn(
            hidden_ref[block], weights_ref[...].reshape(width, weights_ref.shape[2])
        ).astype(BF16)

    lines.advance(0, 1)
    weights.finish()
    project(me_t)
    lines.advance(0, 2)
    lines.advance(3, 0)
    lines.advance(4, 0)
    spread.relay()
    lines.each_new(0, 1, project)
    lines.advance(0, 3)
    lines.advance(3, 1)
    lines.advance(4, 1)
    lines.each_new(0, 2, project)
    lines.each_new(0, 3, project)

    def attended_copy(target, sender):
        return remote(
            attended_ref.at[rows_of(target)],
            attended_recv.at[sender],
            attended_send_sem.at[target],
            attended_recv_sem.at[sender],
            "tensor",
            target,
        )

    def attend(qb):
        forward_rows(
            heads,
            qb,
            max(0, qb - band(seq_len)),
            projected_ref,
            segment_ref,
            bias,
            attended_ref,
            lse_ref,
        )

        @pl.when(me_t == qb)
        def _():
            attended_recv[me_t] = attended_ref[rows_of(me_t), :]

        @pl.when(me_t != qb)
        def _():
            attended_copy(qb, me_t).start()

    lines.advance(3, 2)
    lines.advance(4, 2)
    attend(3)
    attend(0)
    lines.advance(3, 3)
    grad_moves.start(2, grads.at[2])
    lines.advance(4, 3)
    attend(2)
    attend(1)
    grad_moves.start(3, grads.at[3])
    spread.finish()
    for block in range(n_dp):
        out_matrix[:, block * out_cols : (block + 1) * out_cols] = outs[block].reshape(
            width, out_cols
        )
    weight_own_ref[...] = out_matrix[
        pl.ds(pl.multiple_of(me_t * head_cols, head_cols), head_cols), :
    ]
    for step in range(1, n_tensor):
        attended_copy(me_t, lax.rem(me_t + step, n_tensor)).wait_recv()
    residual = tokens_ref[...].astype(F32)
    for block in range(n_tensor):
        residual += nn(
            attended_recv[block], out_matrix[block * head_cols : (block + 1) * head_cols, :]
        )
    residual_ref[...] = residual
    hidden = (
        residual
        * lax.rsqrt(jnp.mean(residual * residual, axis=1, keepdims=True) + EPS)
        * gains_ref[1:2, :]
    ).astype(BF16)
    hidden_two_ref[...] = hidden
    for j in range(ROW_PARTS):
        everyone[j, me_t] = hidden[:, j * row_part : (j + 1) * row_part]
    late = Streams(n_tensor, [everyone.at[j] for j in range(ROW_PARTS)], late_send, late_recv)
    row_moves = Dispatch(n_dp, picks, row_stage, rows_ref, row_send, row_recv, row_own)

    def used(j, k):
        if k < n_tensor - 1:
            return
        row_moves.start(j, everyone.at[j])
        term = nt(
            router_ref[:, j * row_part : (j + 1) * row_part], everyone[j].reshape(seq_len, row_part)
        )
        if j == 0:
            logits[...] = term
        else:
            logits[...] += term

    for turn in late.turns():
        late.turn(turn, used)
    values = logits[...]
    exps = jnp.exp(values - jnp.max(values, axis=0, keepdims=True))
    probs = exps / jnp.sum(exps, axis=0, keepdims=True)
    named = (ids == routes_ref[0:1, :]) | (ids == routes_ref[1:2, :])
    shares = probs / jnp.sum(jnp.where(named, probs, 0.0), axis=0, keepdims=True)
    logits[...] = shares

    def gate_copy(target, sender):
        return remote(
            gate_stage.at[target],
            gates_ref.at[sender],
            gate_send.at[target],
            gate_recv.at[sender],
            "dp",
            target,
        )

    def gate(index, _):
        mask = n_dp - 1 - index
        target = me ^ mask
        for expert in range(local):
            row = jnp.sum(
                jnp.where(ids == target * local + expert, logits[...], 0.0), axis=0, keepdims=True
            )
            high = row.astype(BF16)
            rest = row - high.astype(F32)
            mid = rest.astype(BF16)
            low = (rest - mid.astype(F32)).astype(BF16)
            lanes = slice(expert * capacity, (expert + 1) * capacity)
            pieces = nt(
                jnp.concatenate([high, mid, low, jnp.zeros((5, seq_len), BF16)], axis=0),
                picks[target, lanes, :],
            )
            gate_stage[target, :, lanes] = jnp.broadcast_to(
                jnp.sum(pieces, axis=0, keepdims=True), (8, capacity)
            )

        @pl.when(mask != 0)
        def _():
            gate_copy(target, me).start()

        @pl.when(mask == 0)
        def _():
            gates_ref[target] = gate_stage[target]

        return 0

    lax.fori_loop(0, n_dp, gate, 0)
    lines.drain()
    late.drain()
    weights.drain()
    spread.drain()
    for copy in along:
        copy.wait_send()
    for step in range(1, n_tensor):
        attended_copy(lax.rem(me_t + step, n_tensor), me_t).wait_send()
    for step in range(1, n_dp):
        peer = lax.rem(me + step, n_dp)
        gate_copy(peer, me).wait_send()
        gate_copy(me, peer).wait_recv()
    grad_moves.finish()
    row_moves.finish()


def opening(
    n_dp,
    n_tensor,
    experts,
    capacity,
    tokens,
    cotangent,
    weight,
    extra,
    out,
    routes,
    segments,
    selectors,
):
    own_rows, width = tokens.shape
    seq_len = own_rows * n_tensor
    depth, cols = weight.shape
    per = experts // n_dp * capacity
    part = width // PARTS
    row_part = width // ROW_PARTS
    heads = cols // (3 * HD)
    dma = pltpu.SemaphoreType.DMA
    rows = jax.ShapeDtypeStruct((n_dp, per, width), BF16)
    args = (tokens, cotangent, weight, extra, out, routes, segments, selectors)
    which = (0, 1, 2, 4)
    specs, buffers = staged_specs(args, which)
    return pl.pallas_call(
        staged(
            functools.partial(opening_kernel, n_dp, n_tensor, experts, capacity), len(args), which
        ),
        out_shape=(
            jax.ShapeDtypeStruct((n_tensor, own_rows, width), BF16),
            jax.ShapeDtypeStruct((seq_len, cols), BF16),
            jax.ShapeDtypeStruct((n_dp, depth, cols), BF16),
            jax.ShapeDtypeStruct((2 * heads, 2 * BS), F32),
            jax.ShapeDtypeStruct((experts, width), BF16),
            jax.ShapeDtypeStruct((2, width), F32),
            jax.ShapeDtypeStruct((seq_len, TOP), jnp.int32),
            jax.ShapeDtypeStruct((seq_len, heads * HD), BF16),
            jax.ShapeDtypeStruct((seq_len, heads), F32),
            jax.ShapeDtypeStruct((own_rows, width), F32),
            jax.ShapeDtypeStruct((own_rows, width), BF16),
            jax.ShapeDtypeStruct((heads * HD, width), BF16),
            rows,
            rows,
            jax.ShapeDtypeStruct((n_dp, 8, per), F32),
        ),
        in_specs=specs,
        out_specs=(vspec(),) * 12 + (any_spec(), any_spec(), vspec()),
        scratch_shapes=[
            pltpu.VMEM((n_dp,) + extra.shape, BF16),
            pltpu.VMEM((NB, depth), F32),
            pltpu.VMEM((n_dp, n_tensor) + out.shape, BF16),
            pltpu.VMEM((width, width), BF16),
            pltpu.VMEM((PARTS, n_tensor, own_rows, part), BF16),
            pltpu.VMEM((ROW_PARTS, n_tensor, own_rows, row_part), BF16),
            pltpu.VMEM((n_dp, per, seq_len), BF16),
            pltpu.VMEM((PARTS, n_dp, per, part), BF16),
            pltpu.VMEM((ROW_PARTS, n_dp, per, row_part), BF16),
            pltpu.VMEM((heads, 3, BS, BS), F32),
            pltpu.VMEM((8, seq_len), jnp.int32),
            pltpu.VMEM((n_tensor, own_rows, heads * HD), BF16),
            pltpu.VMEM((experts, seq_len), F32),
            pltpu.VMEM((n_dp, 8, per), F32),
        ]
        + parameter_sems(n_dp, n_tensor)
        + [dma((PARTS + 1, 2, n_tensor - 1))] * 2
        + [dma((ROW_PARTS, 2, n_tensor - 1))] * 2
        + [dma((PARTS, n_dp)), dma((PARTS, n_dp)), dma((PARTS,))]
        + [dma((ROW_PARTS, n_dp)), dma((ROW_PARTS, n_dp)), dma((ROW_PARTS,))]
        + [dma((n_dp,))] * 2
        + [dma((n_tensor,))] * 2
        + buffers,
        compiler_params=pltpu.CompilerParams(
            vmem_limit_bytes=VMEM_LIMIT, collective_id=4, has_side_effects=True
        ),
        name="opening",
    )(*args)


def last_kernel(
    n_dp,
    n_tensor,
    experts,
    heads,
    loads,
    qkv_ref,
    attended_ref,
    grad_attended_ref,
    lse_ref,
    segment_ref,
    pattern_ref,
    skew_ref,
    hidden_ref,
    weight_ref,
    branch_ref,
    small_ref,
    weight_own_ref,
    gain_own_ref,
    merged_ref,
    residual_ref,
    grad_residual_ref,
    tokens_ref,
    gain_ref,
    layer_ref,
    grad_tokens_ref,
    grad_weight_ref,
    grad_out_ref,
    small_out_ref,
    bias,
    dk,
    dv,
    sums,
    grad_qkv,
    diag,
    parts,
    mixture,
    grad_hidden,
    mix_send,
    mix_recv,
    line_send,
    line_recv,
    qkv_send,
    qkv_recv,
    out_send,
    out_recv,
    small_send,
    small_recv,
    small_sum,
    gain_recv,
    mix_send_sem,
    mix_recv_sem,
    line_send_sem,
    line_recv_sem,
    qkv_send_sem,
    qkv_recv_sem,
    out_send_sem,
    out_recv_sem,
    small_send_sem,
    small_recv_sem,
    gain_send_sem,
    gain_recv_sem,
):
    own_rows, width = residual_ref.shape
    seq_len = own_rows * n_tensor
    depth = weight_own_ref.shape[0]
    out_cols = grad_out_ref.shape[1]
    me = lax.axis_index("dp")
    me_t = lax.axis_index("tensor")
    greet([("dp", n_dp), ("tensor", n_tensor)], loads)

    def rows_of(block):
        return pl.ds(pl.multiple_of(block * own_rows, own_rows), own_rows)

    mix = LineSum(n_tensor, merged_ref, mix_send, mix_recv, mix_send_sem, mix_recv_sem, mixture)
    line = LineSum(n_tensor, parts, line_send, line_recv, line_send_sem, line_recv_sem, grad_hidden)
    copies = []

    def scatter(source, target, send_sem, recv_sem):
        for step in range(1, n_dp):
            peer = lax.rem(me + step, n_dp)
            copy = remote(
                source.at[peer],
                target.at[step - 1],
                send_sem.at[step - 1],
                recv_sem.at[step - 1],
                "dp",
                peer,
            )
            copy.start()
            copies.append(copy)

    mix.start()
    build_bias(heads, pattern_ref, bias)
    backward_start(dk, dv, sums)
    blocks = seq_len // BS
    for qb in range(blocks):
        backward_rows(
            heads,
            qb,
            max(0, qb - band(seq_len)),
            qkv_ref,
            attended_ref,
            grad_attended_ref,
            lse_ref,
            segment_ref,
            bias,
            grad_qkv,
            dk,
            dv,
            sums,
        )
        if qb == 0:
            for block in range(n_dp):
                cols = slice(block * out_cols, (block + 1) * out_cols)
                out_send[block] = tn(attended_ref[...], branch_ref[:, cols]).astype(BF16)
            scatter(out_send, out_recv, out_send_sem, out_recv_sem)
        if qb >= blocks - 2 and qb - (blocks - 2) < n_tensor - 1:
            mix.step(qb - (blocks - 2))
    backward_end(heads, grad_qkv, dk, dv)
    line.start(lambda block: nt(grad_qkv[rows_of(block), :], weight_ref[...]))
    for k in range(2, n_tensor - 1):
        mix.step(k)
    for block in range(n_dp):
        cols = slice(block * depth, (block + 1) * depth)
        qkv_send[block] = tn(hidden_ref[:, cols], grad_qkv[...]).astype(BF16)
    scatter(qkv_send, qkv_recv, qkv_send_sem, qkv_recv_sem)
    diag[...] = jnp.zeros_like(diag)
    diagonal_sums(heads, sums, diag)
    tables = lax.dot_general(
        skew_ref[...],
        jnp.concatenate([diag[0], diag[1]], axis=1),
        (((1,), (1,)), ((), ())),
        precision=lax.Precision.HIGHEST,
        preferred_element_type=F32,
    )
    far = jnp.sum(diag[2], axis=1, keepdims=True)
    head = lax.broadcasted_iota(jnp.int32, (8, 8), 0)
    lane = lax.broadcasted_iota(jnp.int32, (8, 8), 1)
    far_row = jnp.sum(jnp.where(head == lane, far, 0.0), axis=0, keepdims=True)
    bucket = lax.broadcasted_iota(jnp.int32, (NB, 8), 0)
    tables += jnp.where(bucket == NB - 1, far_row, 0.0)
    rows_each = NB // n_dp
    for block in range(n_dp):
        small_send[block] = small_ref[:, block * depth : (block + 1) * depth]
        small_send[block, experts + 2 : experts + 2 + rows_each, 0:8] = tables[
            block * rows_each : (block + 1) * rows_each, :
        ]
    scatter(small_send, small_recv, small_send_sem, small_recv_sem)
    layer_ref[...] = (residual_ref[...] + mixture[...]).astype(BF16)
    for k in range(n_tensor - 2):
        line.step(k)
    for copy in copies:
        copy.wait_recv()
    small_sum[...] = small_send[me]
    grad_weight_ref[...] = qkv_send[me].astype(F32)
    grad_out_ref[...] = out_send[me].astype(F32)
    for step in range(1, n_dp):
        small_sum[...] += small_recv[step - 1]
        grad_weight_ref[...] += qkv_recv[step - 1].astype(F32)
        grad_out_ref[...] += out_recv[step - 1].astype(F32)
    column = jnp.sum(grad_weight_ref[...] * weight_own_ref[...].astype(F32), axis=1, keepdims=True)
    small_sum[experts + 1 : experts + 2, :] = to_row(column) / gain_own_ref[...]
    gains = []
    for step in range(1, n_tensor):
        peer = lax.rem(me_t + step, n_tensor)
        copy = remote(
            small_sum,
            gain_recv.at[step - 1],
            gain_send_sem.at[step - 1],
            gain_recv_sem.at[step - 1],
            "tensor",
            peer,
        )
        copy.start()
        gains.append(copy)
    line.step(n_tensor - 2)
    x = tokens_ref[...].astype(F32)
    scale = lax.rsqrt(jnp.mean(x * x, axis=1, keepdims=True) + EPS)
    unit = x * scale
    grad_unit = grad_hidden[...] * gain_ref[...]
    grad_tokens_ref[...] = (
        grad_residual_ref[...]
        + scale * (grad_unit - unit * jnp.mean(grad_unit * unit, axis=1, keepdims=True))
    ).astype(BF16)
    mix.drain()
    line.drain()
    for copy in copies:
        copy.wait_send()
    for copy in gains:
        copy.wait()
    small_out_ref[...] = small_sum[...]
    shared = slice(0, experts + 2)
    for step in range(1, n_tensor):
        small_out_ref[shared, :] += gain_recv[step - 1, shared, :]


def last(
    n_dp,
    n_tensor,
    experts,
    heads,
    projected,
    attended,
    grad_attended,
    lse,
    segments,
    patterns,
    skew,
    hidden,
    weight,
    branch,
    small,
    weight_own,
    gain_own,
    merged,
    residual,
    grad_residual,
    tokens,
    gain,
):
    seq_len, width = hidden.shape
    own_rows = seq_len // n_tensor
    depth, cols = weight_own.shape
    out_cols = width // n_dp
    dma = pltpu.SemaphoreType.DMA
    line = [
        pltpu.VMEM((n_tensor - 1, own_rows, width), BF16),
        pltpu.VMEM((n_tensor + 1, own_rows, width), BF16),
    ]
    args = (
        projected,
        attended,
        grad_attended,
        lse,
        segments,
        patterns,
        skew,
        hidden,
        weight,
        branch,
        small,
        weight_own,
        gain_own,
        merged,
        residual,
        grad_residual,
        tokens,
        gain,
    )
    which = (0, 1, 2, 7, 8, 9, 11, 13, 14, 15, 16)
    specs, buffers = staged_specs(args, which)
    return pl.pallas_call(
        staged(functools.partial(last_kernel, n_dp, n_tensor, experts, heads), len(args), which),
        out_shape=(
            jax.ShapeDtypeStruct((own_rows, width), BF16),
            jax.ShapeDtypeStruct((own_rows, width), BF16),
            jax.ShapeDtypeStruct((depth, cols), F32),
            jax.ShapeDtypeStruct((heads * HD, out_cols), F32),
            jax.ShapeDtypeStruct((SMALL, depth), F32),
        ),
        in_specs=specs,
        out_specs=(vspec(),) * 5,
        scratch_shapes=backward_scratch(heads, seq_len)
        + [
            pltpu.VMEM((seq_len, cols), BF16),
            pltpu.VMEM((3, 8, 2 * BS), F32),
        ]
        + [pltpu.VMEM((n_tensor, own_rows, width), BF16)]
        + [pltpu.VMEM((own_rows, width), F32)] * 2
        + line * 2
        + [
            pltpu.VMEM((n_dp, depth, cols), BF16),
            pltpu.VMEM((n_dp - 1, depth, cols), BF16),
            pltpu.VMEM((n_dp, heads * HD, out_cols), BF16),
            pltpu.VMEM((n_dp - 1, heads * HD, out_cols), BF16),
            pltpu.VMEM((n_dp, SMALL, depth), F32),
            pltpu.VMEM((n_dp - 1, SMALL, depth), F32),
            pltpu.VMEM((SMALL, depth), F32),
            pltpu.VMEM((n_tensor - 1, SMALL, depth), F32),
        ]
        + [dma((n_tensor - 1,)), dma((n_tensor + 1,))] * 2
        + [dma((n_dp - 1,))] * 6
        + [dma((n_tensor - 1,))] * 2
        + buffers,
        compiler_params=pltpu.CompilerParams(
            vmem_limit_bytes=VMEM_LIMIT, collective_id=5, has_side_effects=True
        ),
        name="last",
    )(*args)


def deliver_kernel(
    grad_in_ref,
    grad_out_ref,
    layer_in_ref,
    tokens_in_ref,
    weight_in_ref,
    out_in_ref,
    small_ref,
    layer_ref,
    tokens_ref,
    weight_ref,
    out_ref,
    table_ref,
    gain_one_ref,
    gain_two_ref,
    router_ref,
    in_ref,
    down_ref,
    stage_in,
    stage_down,
    in_sem,
    down_sem,
    out_sem,
    last_sem,
):
    local, halves = grad_in_ref.shape[:2]
    pieces = [
        (grad_in_ref.at[e, g], stage_in.at[e, g], in_ref.at[e, g], in_sem.at[e, g], out_sem.at[e, g])
        for e in range(local)
        for g in range(halves)
    ] + [
        (grad_out_ref.at[e], stage_down.at[e], down_ref.at[e], down_sem.at[e], last_sem.at[e])
        for e in range(local)
    ]
    for source, stage, _, sem, _ in pieces:
        pltpu.make_async_copy(source, stage, sem).start()
    layer_ref[...] = layer_in_ref[...]
    tokens_ref[...] = tokens_in_ref[...]
    cols = weight_ref.shape[2]
    for part in range(3):
        weight_ref[part] = weight_in_ref[:, part * cols : (part + 1) * cols]
    out_ref[...] = out_in_ref[...]
    experts = router_ref.shape[0]
    router_ref[...] = small_ref[0:experts, :]
    gain_two_ref[...] = small_ref[experts : experts + 1, :]
    gain_one_ref[...] = small_ref[experts + 1 : experts + 2, :]
    table_ref[...] = small_ref[
        experts + 2 : experts + 2 + table_ref.shape[0], 0 : table_ref.shape[1]
    ]
    for source, stage, target, sem, done in pieces:
        pltpu.make_async_copy(source, stage, sem).wait()
        pltpu.make_async_copy(stage, target, done).start()
    for _, stage, target, _, done in pieces:
        pltpu.make_async_copy(stage, target, done).wait()


def deliver(experts, heads, table_rows, grad_in, grad_out, layer, tokens, weight, out, small):
    depth, cols = weight.shape
    local, halves = grad_in.shape[:2]
    dma = pltpu.SemaphoreType.DMA
    return pl.pallas_call(
        deliver_kernel,
        out_shape=(
            jax.ShapeDtypeStruct(layer.shape, BF16),
            jax.ShapeDtypeStruct(tokens.shape, BF16),
            jax.ShapeDtypeStruct((3, depth, cols // 3), F32),
            jax.ShapeDtypeStruct(out.shape, F32),
            jax.ShapeDtypeStruct((table_rows, heads), F32),
            jax.ShapeDtypeStruct((1, depth), F32),
            jax.ShapeDtypeStruct((1, depth), F32),
            jax.ShapeDtypeStruct((experts, depth), F32),
            jax.ShapeDtypeStruct(grad_in.shape, F32),
            jax.ShapeDtypeStruct(grad_out.shape, F32),
        ),
        in_specs=[any_spec()] * 2 + [vspec()] * 5,
        out_specs=(vspec(),) * 8 + (any_spec(),) * 2,
        scratch_shapes=[
            pltpu.VMEM(grad_in.shape, F32),
            pltpu.VMEM(grad_out.shape, F32),
            dma((local, halves)),
            dma((local,)),
            dma((local, halves)),
            dma((local,)),
        ],
        compiler_params=pltpu.CompilerParams(vmem_limit_bytes=VMEM_LIMIT),
        name="deliver",
    )(grad_in, grad_out, layer, tokens, weight, out, small)


def rms_scale(values):
    return lax.rsqrt(jnp.mean(values * values, axis=-1, keepdims=True) + EPS)


def norm_backward(grad_normed, values, scale_inv, gain):
    normed_unit = values * scale_inv
    grad_unit = grad_normed * gain
    grad_values = scale_inv * (
        grad_unit - normed_unit * jnp.mean(grad_unit * normed_unit, axis=-1, keepdims=True)
    )
    return (grad_values, jnp.sum(grad_normed * normed_unit, axis=0))


def gelu_tanh(values):
    return jax.nn.gelu(values, approximate=True)


def route_slots(route_ids, experts, capacity):
    flat_routes = route_ids.reshape(-1)
    onehot = (flat_routes[:, None] == jnp.arange(experts, dtype=jnp.int32)[None, :]).astype(
        jnp.int32
    )
    ranks = jnp.cumsum(onehot, axis=0) - 1
    rank_own = jnp.sum(ranks * onehot, axis=1)
    return (flat_routes * capacity + rank_own).reshape(-1, TOP)


def on_device(
    tokens,
    segments,
    routes,
    w_qkv,
    w_attn_out,
    bias_table,
    gain_attn,
    gain_moe,
    router,
    w_in,
    w_out,
    cotangent,
):
    own_rows, model_width = tokens.shape
    n_tensor = lax.axis_size("tensor")
    n_dp = lax.axis_size("dp")
    seq_len = own_rows * n_tensor
    own_start = lax.axis_index("tensor") * own_rows
    head_cols = w_qkv.shape[2]
    heads = head_cols // HD
    experts = router.shape[1]
    local_experts = w_in.shape[0]
    capacity = 5 * seq_len * TOP // (4 * experts)
    highest = lax.Precision.HIGHEST
    slots = experts * capacity

    depth = w_qkv.shape[0]
    bias_rows = NB // n_dp
    lanes = depth
    extra = jnp.concatenate(
        [
            jnp.transpose(router),
            gain_attn[None],
            gain_moe[None],
            jnp.pad(bias_table, ((0, SMALL - experts - 2 - bias_rows), (0, lanes - heads))),
        ],
        axis=0,
    )
    fast = n_dp == 8 and n_tensor == 4 and seq_len == 4 * BS and slots * model_width <= 4 * 1024 * 1024
    route_rows = jnp.pad(jnp.transpose(routes), ((0, 8 - TOP), (0, 0)))
    weight_shard = w_qkv.reshape(depth, 3 * head_cols)
    gain_shard = gain_attn[None].astype(F32)
    skew = jnp.asarray(skew_selectors().T)
    selectors = jnp.asarray(distance_selectors().T)

    def finish(layer_out, grad_tokens, reduced_qkv, reduced_attn_out, small_sum, grad_w_in, grad_w_out):
        (
            layer_out,
            grad_tokens,
            grad_w_qkv,
            grad_w_attn_out,
            grad_table,
            grad_gain_one,
            grad_gain_two,
            grad_router,
            grad_w_in,
            grad_w_out,
        ) = deliver(
            experts,
            heads,
            NB // n_dp,
            grad_w_in,
            grad_w_out,
            layer_out,
            grad_tokens,
            reduced_qkv,
            reduced_attn_out,
            small_sum,
        )
        return (
            layer_out,
            grad_tokens,
            jnp.transpose(grad_w_qkv, (1, 0, 2)),
            grad_w_attn_out,
            grad_table,
            grad_gain_one[0],
            grad_gain_two[0],
            jnp.transpose(grad_router),
            grad_w_in,
            grad_w_out,
        )

    if fast:
        (
            gathered,
            projected,
            weights_full,
            patterns,
            router_rows,
            gains,
            slot_columns,
            attended,
            lse,
            residual,
            hidden_two,
            weight_own,
            rows,
            grad_rows,
            row_gates,
        ) = opening(
            n_dp,
            n_tensor,
            experts,
            capacity,
            tokens,
            cotangent,
            weight_shard,
            extra,
            w_attn_out,
            route_rows,
            segments,
            selectors,
        )
        back, gate_back, value, grad_w_in, grad_w_out = run_experts(
            n_dp, capacity, rows, grad_rows, row_gates, w_in, w_out
        )
        grad_residual, grad_branch_all, grad_attended, small, merged = combine(
            n_dp,
            n_tensor,
            experts,
            back.reshape(slots, model_width),
            gate_back,
            slot_columns,
            route_rows,
            residual,
            hidden_two,
            cotangent,
            router_rows,
            gains[1:2],
            weight_own,
            value,
        )
        results = last(
            n_dp,
            n_tensor,
            experts,
            heads,
            projected,
            attended,
            grad_attended,
            lse,
            segments,
            patterns,
            skew,
            gathered.reshape(seq_len, model_width),
            weights_full.reshape(model_width, 3 * head_cols),
            grad_branch_all.reshape(seq_len, model_width),
            small,
            weight_shard,
            gain_shard,
            merged,
            residual,
            grad_residual,
            tokens,
            gains[0:1],
        )
        return finish(*results, grad_w_in, grad_w_out)
    gathered, projected, weights_full, outs_full, patterns, router_rows, gains = front(
        n_dp, n_tensor, experts, tokens, weight_shard, extra, w_attn_out, selectors
    )
    gathered_one = gathered.reshape(seq_len, model_width)
    qkv_matrix = weights_full.reshape(model_width, 3 * head_cols)
    outs_full = outs_full.reshape(n_dp, model_width, model_width // n_dp)
    tokens_float = tokens.astype(F32)
    scale_one = rms_scale(tokens_float)
    gain_one, gain_two = gains[0], gains[1]
    starts = segments[0, ::BS]
    ends = segments[0, BS - 1 :: BS]
    lowest = jnp.sum((ends[None, :] < starts[:, None]).astype(jnp.int32), axis=1)
    attended, lse = attention_forward(projected, lowest, segments, patterns, heads)
    router_full = jnp.transpose(router_rows)
    out_matrix = jnp.transpose(outs_full, (1, 0, 2)).reshape(model_width, model_width)
    attended_own = lax.all_to_all(
        attended.reshape(n_tensor, own_rows, head_cols), "tensor", 0, 0
    )
    attended_own = jnp.transpose(attended_own, (1, 0, 2)).reshape(own_rows, n_tensor * head_cols)
    branch = jnp.dot(attended_own, out_matrix, preferred_element_type=F32)
    residual = tokens_float + branch
    scale_two = rms_scale(residual)
    hidden_two = (residual * scale_two * gain_two).astype(BF16)
    gathered_two = lax.all_gather(hidden_two, "tensor", axis=0, tiled=True)

    expert_ids = jnp.arange(experts, dtype=jnp.int32)

    def gate_values(logit_values, route_rows):
        expert_probs = jax.nn.softmax(logit_values, axis=-1)
        picked = jnp.sum(
            jnp.where(
                route_rows[:, :, None] == expert_ids[None, None, :], expert_probs[:, None, :], 0.0
            ),
            axis=-1,
        )
        return picked / jnp.sum(picked, axis=1, keepdims=True)

    gates = gate_values(jnp.dot(gathered_two, router_full, preferred_element_type=F32), routes)
    slot_ids = route_slots(routes, experts, capacity)
    slot_flat = slot_ids.reshape(-1)
    token_ids = jnp.repeat(jnp.arange(seq_len, dtype=jnp.int32), TOP)
    sources = jnp.full((slots,), seq_len, jnp.int32).at[slot_flat].set(token_ids)
    slot_gates = jnp.zeros((slots,), F32).at[slot_flat].set(gates.reshape(-1))
    grad_gathered = lax.all_gather(cotangent, "tensor", axis=0, tiled=True)

    def exchange(rows):
        parts = rows.reshape(n_dp, local_experts, capacity, model_width)
        return [
            lax.all_to_all(parts[:, i], "dp", 0, 0).reshape(n_dp * capacity, model_width)
            for i in range(local_experts)
        ]

    def give_back(parts):
        back = [
            lax.all_to_all(part.reshape(n_dp, capacity, model_width), "dp", 0, 0) for part in parts
        ]
        return jnp.stack(back, axis=1).reshape(slots, model_width)

    zero_row = jnp.zeros((1, model_width), BF16)
    dispatched = exchange(jnp.concatenate([gathered_two, zero_row], axis=0)[sources])
    padded_grad = jnp.concatenate([grad_gathered, zero_row], axis=0)
    grad_expert = exchange((slot_gates[:, None] * padded_grad[sources]).astype(BF16))

    outs, backs, grads_in, grads_out = [], [], [], []
    for i in range(local_experts):
        rows, grad_rows = dispatched[i], grad_expert[i]
        gate_part = nt(rows, w_in[i, 0])
        up_part = nt(rows, w_in[i, 1])
        gelu_value, gelu_pull = jax.vjp(gelu_tanh, gate_part)
        activated = (gelu_value * up_part).astype(BF16)
        outs.append(nn(activated, w_out[i]).astype(BF16))
        grad_act = nt(grad_rows, w_out[i])
        grads_out.append(tn(activated, grad_rows))
        grad_gate = gelu_pull(grad_act * up_part)[0].astype(BF16)
        grad_up = (grad_act * gelu_value).astype(BF16)
        backs.append((nn(grad_gate, w_in[i, 0]) + nn(grad_up, w_in[i, 1])).astype(BF16))
        grads_in.append(jnp.stack([tn(grad_gate, rows), tn(grad_up, rows)]))
    grad_w_in = jnp.stack(grads_in)
    grad_w_out = jnp.stack(grads_out)
    expert_out = give_back(outs)
    grad_dispatched = give_back(backs)

    first, second = slot_ids[:, 0], slot_ids[:, 1]
    picked_first = expert_out[first].astype(F32)
    picked_second = expert_out[second].astype(F32)
    mixture = lax.psum_scatter(
        (gates[:, 0:1] * picked_first + gates[:, 1:2] * picked_second).astype(BF16),
        "tensor",
        scatter_dimension=0,
        tiled=True,
    ).astype(F32)
    layer_out = (residual + mixture).astype(BF16)
    grad_float = grad_gathered.astype(F32)
    grad_gate_part = jnp.stack(
        [
            jnp.sum(grad_float * picked_first, axis=1),
            jnp.sum(grad_float * picked_second, axis=1),
        ],
        axis=1,
    )
    grad_hidden_part = (
        grad_dispatched[first].astype(F32) + grad_dispatched[second].astype(F32)
    ).astype(BF16)
    grad_own = lax.psum_scatter(
        grad_hidden_part, "tensor", scatter_dimension=0, tiled=True
    ).astype(F32)
    grad_gate_own = lax.dynamic_slice_in_dim(
        lax.psum(grad_gate_part, "tensor"), own_start, own_rows, 0
    )
    own_routes = lax.dynamic_slice_in_dim(routes, own_start, own_rows, 0)
    own_logits = jnp.dot(hidden_two, router_full, preferred_element_type=F32)

    def own_gates(logit_values):
        return gate_values(logit_values, own_routes)

    _, gate_pull = jax.vjp(own_gates, own_logits)
    grad_logits = gate_pull(grad_gate_own)[0]
    router_float = router_full.astype(F32)
    grad_hidden_two = grad_own + jnp.dot(grad_logits, router_float.T, precision=highest)
    grad_router_part = jnp.dot(hidden_two.astype(F32).T, grad_logits, precision=highest)
    grad_from_norm, grad_gain_two = norm_backward(grad_hidden_two, residual, scale_two, gain_two)
    grad_residual = cotangent.astype(F32) + grad_from_norm

    grad_branch = grad_residual.astype(BF16)
    grad_attended_own = nt(grad_branch, out_matrix).astype(BF16)
    grad_attended = lax.all_to_all(
        jnp.transpose(grad_attended_own.reshape(own_rows, n_tensor, head_cols), (1, 0, 2)),
        "tensor",
        0,
        0,
    ).reshape(seq_len, head_cols)
    grad_branch_all = lax.all_gather(grad_branch, "tensor", axis=0, tiled=True)
    small = jnp.concatenate(
        [
            jnp.transpose(grad_router_part),
            grad_gain_two[None],
            jnp.zeros((SMALL - experts - 1, model_width), F32),
        ],
        axis=0,
    )
    grad_projected, diag = attention_backward(
        projected, attended, grad_attended, lse, lowest, segments, patterns, heads
    )
    near = jnp.concatenate([diag[0, :heads], diag[1, :heads]], axis=1)
    grad_table = lax.dot_general(skew, near, (((1,), (1,)), ((), ())), precision=highest)
    grad_table = grad_table.at[NB - 1].add(jnp.sum(diag[2, :heads], axis=1))
    small = jnp.transpose(small.reshape(SMALL, n_dp, depth), (1, 0, 2))
    small = lax.dynamic_update_slice(
        small, grad_table.reshape(n_dp, NB // n_dp, heads), (0, experts + 2, 0)
    )
    grad_hidden_one, reduced_qkv, reduced_attn_out, small_sum = tail(
        n_dp,
        n_tensor,
        experts,
        gathered_one,
        grad_projected,
        qkv_matrix,
        attended,
        grad_branch_all,
        small,
        weight_shard,
        gain_shard,
    )
    grad_from_first, _ = norm_backward(grad_hidden_one, tokens_float, scale_one, gain_one)
    grad_tokens = (grad_residual + grad_from_first).astype(BF16)
    return finish(
        layer_out, grad_tokens, reduced_qkv, reduced_attn_out, small_sum, grad_w_in, grad_w_out
    )


def solution(mesh):
    return jax.shard_map(
        on_device,
        mesh=mesh,
        in_specs=(
            P(("dp", "tensor"), None),
            P("dp", None),
            P("dp", None),
            P("dp", None, "tensor"),
            P("tensor", "dp"),
            P("dp", "tensor"),
            P("dp"),
            P("dp"),
            P("dp", None),
            P("dp", None, "tensor", None),
            P("dp", "tensor", None),
            P(("dp", "tensor"), None),
        ),
        out_specs=(
            P(("dp", "tensor"), None),
            P(("dp", "tensor"), None),
            P("dp", None, "tensor"),
            P("tensor", "dp"),
            P("dp", "tensor"),
            P("dp"),
            P("dp"),
            P("dp", None),
            P("dp", None, "tensor", None),
            P("dp", "tensor", None),
        ),
        check_vma=False,
    )
```

```python
import functools
import math

import jax
import jax.numpy as jnp
import numpy as np
from jax import lax
from jax.experimental import pallas as pl
from jax.experimental.pallas import tpu as pltpu
from jax.sharding import PartitionSpec as P

HD = 64
TOP = 2
NB = 32
NEAR = 128
BS = 256

EPS = 1e-06
NEG = -1e30
F32 = jnp.float32
BF16 = jnp.bfloat16
VMEM_LIMIT = 60 * 1024 * 1024


def distance_buckets():
    half_buckets = NB // 2
    thresholds = [bucket_level for bucket_level in range(1, half_buckets)]
    thresholds = thresholds + [
        int(
            math.ceil(
                half_buckets
                * (NEAR / half_buckets) ** ((bucket_level - half_buckets) / half_buckets)
            )
        )
        for bucket_level in range(half_buckets, NB)
    ]
    distance = np.arange(NEAR + 1)
    return (distance[:, None] >= np.array(thresholds)[None, :]).sum(axis=1)


def distance_selectors():
    buckets = distance_buckets()
    lanes = np.arange(2 * BS)
    signed = np.where(lanes < BS, lanes, lanes - 2 * BS)
    out = []
    for base in (0, BS):
        distance = np.clip(base - signed, 0, NEAR)
        out.append(buckets[distance][:, None] == np.arange(NB)[None, :])
    return np.concatenate(out, axis=0).astype(np.float32)


def skew_selectors():
    buckets = distance_buckets()
    lanes = np.arange(2 * BS)
    out = []
    for base in (0, BS):
        distance = np.clip(base + BS - 1 - lanes, 0, NEAR)
        out.append(buckets[distance][:, None] == np.arange(NB)[None, :])
    return np.concatenate(out, axis=0).astype(np.float32)


def nt(a, b):
    return lax.dot_general(a, b, (((1,), (1,)), ((), ())), preferred_element_type=F32)


def tn(a, b):
    return lax.dot_general(a, b, (((0,), (0,)), ((), ())), preferred_element_type=F32)


def nn(a, b):
    return lax.dot_general(a, b, (((1,), (0,)), ((), ())), preferred_element_type=F32)


def toeplitz(row):
    return pltpu.roll(jnp.broadcast_to(row, (BS, 2 * BS)), 0, 1, stride=1, stride_axis=0)[:, :BS]


def head_lanes(heads, width):
    lane = lax.broadcasted_iota(jnp.int32, (1, width), 1)
    return [(lane >= h * HD) & (lane < (h + 1) * HD) for h in range(heads)]


def own_head(value, lanes, heads):
    return value if heads == 1 else jnp.where(lanes, value, jnp.zeros((), value.dtype))


def build_bias(heads, pattern_ref, bias):
    for h in range(heads):
        for t in range(2):
            bias[h, t] = toeplitz(pattern_ref[2 * h + t : 2 * h + t + 1, :])
        bias[h, 2] = jnp.broadcast_to(pattern_ref[2 * h + 1 : 2 * h + 2, 0:1], (BS, BS))


def block_rows(block):
    if isinstance(block, int):
        return pl.ds(block * BS, BS)
    return pl.ds(pl.multiple_of(block * BS, BS), BS)


def segment_column(qb, segment_ref):
    return to_column(segment_ref[:, block_rows(qb)].astype(F32))


def block_mask(qb, kb, q_segments, segment_ref):
    k_segments = segment_ref[:, block_rows(kb)].astype(F32)
    row = lax.broadcasted_iota(jnp.int32, (BS, BS), 0) + (qb - kb) * BS
    col = lax.broadcasted_iota(jnp.int32, (BS, BS), 1)
    return (q_segments == k_segments) & (row >= col)


def forward_rows(heads, qb, low, qkv_ref, segment_ref, bias, out_ref, lse_ref):
    width = heads * HD
    lanes = head_lanes(heads, width)
    q_rows = block_rows(qb)
    q_all = (qkv_ref[q_rows, 0:width] * HD**-0.5).astype(BF16)
    q_heads = [own_head(q_all, lanes[h], heads) for h in range(heads)]
    q_segments = segment_column(qb, segment_ref)

    def k_step(kb, carry):
        k = qkv_ref[block_rows(kb), width : 2 * width]
        v = qkv_ref[block_rows(kb), 2 * width : 3 * width]
        allowed = block_mask(qb, kb, q_segments, segment_ref)
        place = jnp.minimum(qb - kb, 2)
        new = []
        for h in range(heads):
            top, total, acc = carry[3 * h : 3 * h + 3]
            s = jnp.where(allowed, nt(q_heads[h], k) + bias[h, place], NEG)
            top_new = jnp.maximum(top, jnp.max(s, axis=1, keepdims=True))
            alpha = jnp.exp(top - top_new)
            p = jnp.exp(s - top_new)
            total = alpha * total + jnp.sum(p, axis=1, keepdims=True)
            acc = alpha * acc + nn(p.astype(BF16), v)
            new += [top_new, total, acc]
        return tuple(new)

    init = []
    for h in range(heads):
        init += [jnp.full((BS, 1), NEG, F32), jnp.zeros((BS, 1), F32), jnp.zeros((BS, width), F32)]
    res = lax.fori_loop(low, qb + 1, k_step, tuple(init))
    out = jnp.zeros((BS, width), F32)
    for h in range(heads):
        top, total, acc = res[3 * h : 3 * h + 3]
        value = acc / total
        out = value if heads == 1 else jnp.where(lanes[h], value, out)
        lse_ref[q_rows, h : h + 1] = top + jnp.log(total)
    out_ref[q_rows, :] = out.astype(BF16)


def backward_rows(
    heads, qb, low, qkv_ref, out_ref, grad_ref, lse_ref, segment_ref, bias, grad_qkv_ref, dk, dv, sums
):
    width = heads * HD
    lanes = head_lanes(heads, width)
    scale = HD**-0.5
    q_rows = block_rows(qb)
    q_all = (qkv_ref[q_rows, 0:width] * scale).astype(BF16)
    g_all = grad_ref[q_rows, :]
    both = g_all.astype(F32) * out_ref[q_rows, :].astype(F32)
    q_heads = [own_head(q_all, lanes[h], heads) for h in range(heads)]
    g_heads = [own_head(g_all, lanes[h], heads) for h in range(heads)]
    deltas = [jnp.sum(own_head(both, lanes[h], heads), axis=1, keepdims=True) for h in range(heads)]
    totals = [lse_ref[q_rows, h : h + 1] for h in range(heads)]
    q_segments = segment_column(qb, segment_ref)

    def k_step(kb, dq):
        k_rows = block_rows(kb)
        k = qkv_ref[k_rows, width : 2 * width]
        v = qkv_ref[k_rows, 2 * width : 3 * width]
        allowed = block_mask(qb, kb, q_segments, segment_ref)
        place = jnp.minimum(qb - kb, 2)
        dk_add = jnp.zeros((BS, width), F32)
        dv_add = jnp.zeros((BS, width), F32)
        for h in range(heads):
            s = jnp.where(allowed, nt(q_heads[h], k) + bias[h, place], NEG)
            p = jnp.exp(s - totals[h])
            gp = nt(g_heads[h], v)
            ds = (p * (gp - deltas[h])).astype(BF16)
            dv_add += tn(p.astype(BF16), g_heads[h])
            dk_add += tn(ds, q_heads[h])
            dq = dq + own_head(nn(ds, k), lanes[h], heads)
            sums[h, place] += ds.astype(F32)
        dk[k_rows, :] += dk_add
        dv[k_rows, :] += dv_add
        return dq

    dq = lax.fori_loop(low, qb + 1, k_step, jnp.zeros((BS, width), F32))
    grad_qkv_ref[q_rows, 0:width] = (dq * scale).astype(BF16)


def backward_start(dk, dv, sums):
    dk[...] = jnp.zeros_like(dk)
    dv[...] = jnp.zeros_like(dv)
    sums[...] = jnp.zeros_like(sums)


def backward_end(heads, grad_qkv_ref, dk, dv):
    width = heads * HD
    grad_qkv_ref[:, width : 2 * width] = dk[...].astype(BF16)
    grad_qkv_ref[:, 2 * width : 3 * width] = dv[...].astype(BF16)


def diagonal_sums(heads, sums, diag_ref):
    row = lax.broadcasted_iota(jnp.int32, (BS, BS), 0)
    col = lax.broadcasted_iota(jnp.int32, (BS, BS), 1)
    upside_down = jnp.where(row + col == BS - 1, 1.0, 0.0).astype(F32)
    for h in range(heads):
        for t in range(2):
            flipped = jnp.dot(
                upside_down,
                sums[h, t],
                precision=lax.Precision.HIGHEST,
                preferred_element_type=F32,
            )
            wide = jnp.concatenate([flipped, jnp.zeros((BS, BS), F32)], axis=1)
            skewed = pltpu.roll(wide, 0, 1, stride=1, stride_axis=0)
            diag_ref[t, h : h + 1, :] = jnp.sum(skewed, axis=0, keepdims=True)
        rest = jnp.sum(sums[h, 2], axis=0, keepdims=True)
        diag_ref[2, h : h + 1, :] = jnp.concatenate([rest, jnp.zeros((1, BS), F32)], axis=1)


def attn_fwd_kernel(heads, blocks, lo_ref, qkv_ref, segment_ref, pattern_ref, out_ref, lse_ref, bias):
    build_bias(heads, pattern_ref, bias)

    def q_step(qb, _):
        forward_rows(heads, qb, lo_ref[qb], qkv_ref, segment_ref, bias, out_ref, lse_ref)
        return 0

    lax.fori_loop(0, blocks, q_step, 0)


def attn_bwd_kernel(
    heads,
    blocks,
    lo_ref,
    qkv_ref,
    out_ref,
    grad_ref,
    lse_ref,
    segment_ref,
    pattern_ref,
    grad_qkv_ref,
    diag_ref,
    bias,
    dk,
    dv,
    sums,
):
    build_bias(heads, pattern_ref, bias)
    backward_start(dk, dv, sums)

    def q_step(qb, _):
        backward_rows(
            heads,
            qb,
            lo_ref[qb],
            qkv_ref,
            out_ref,
            grad_ref,
            lse_ref,
            segment_ref,
            bias,
            grad_qkv_ref,
            dk,
            dv,
            sums,
        )
        return 0

    lax.fori_loop(0, blocks, q_step, 0)
    backward_end(heads, grad_qkv_ref, dk, dv)
    diagonal_sums(heads, sums, diag_ref)


def vspec():
    return pl.BlockSpec(memory_space=pltpu.VMEM)


def sspec():
    return pl.BlockSpec(memory_space=pltpu.SMEM)


def attention_forward(projected, lo, segments, patterns, heads):
    seq_len = projected.shape[0]
    blocks = seq_len // BS
    return pl.pallas_call(
        functools.partial(attn_fwd_kernel, heads, blocks),
        out_shape=(
            jax.ShapeDtypeStruct((seq_len, heads * HD), BF16),
            jax.ShapeDtypeStruct((seq_len, heads), F32),
        ),
        in_specs=[sspec(), vspec(), vspec(), vspec()],
        out_specs=(vspec(), vspec()),
        scratch_shapes=[pltpu.VMEM((heads, 3, BS, BS), F32)],
        compiler_params=pltpu.CompilerParams(vmem_limit_bytes=VMEM_LIMIT),
        name="attn_fwd",
    )(lo, projected, segments, patterns)


def attention_backward(projected, attended, grad, lse, lo, segments, patterns, heads):
    seq_len = projected.shape[0]
    blocks = seq_len // BS
    width = heads * HD
    return pl.pallas_call(
        functools.partial(attn_bwd_kernel, heads, blocks),
        out_shape=(
            jax.ShapeDtypeStruct((seq_len, 3 * width), BF16),
            jax.ShapeDtypeStruct((3, 8, 2 * BS), F32),
        ),
        in_specs=[sspec()] + [vspec()] * 6,
        out_specs=(vspec(), vspec()),
        scratch_shapes=backward_scratch(heads, seq_len),
        compiler_params=pltpu.CompilerParams(vmem_limit_bytes=VMEM_LIMIT),
        name="attn_bwd",
    )(lo, projected, attended, grad, lse, segments, patterns)


def backward_scratch(heads, seq_len):
    return [
        pltpu.VMEM((heads, 3, BS, BS), F32),
        pltpu.VMEM((seq_len, heads * HD), F32),
        pltpu.VMEM((seq_len, heads * HD), F32),
        pltpu.VMEM((heads, 3, BS, BS), F32),
    ]


MESH = pl.DeviceIdType.MESH
SMALL = 32


def remote(src, dst, send, recv, axis, peer):
    return pltpu.make_async_remote_copy(
        src_ref=src,
        dst_ref=dst,
        send_sem=send,
        recv_sem=recv,
        device_id={axis: peer},
        device_id_type=MESH,
    )


class Staging:
    def __init__(self):
        self.loads, self.stores, self.flying = [], {}, []

    def wait(self):
        for load in self.loads:
            load.wait()

    def put(self, *indices):
        for index in indices:
            copy = self.stores.pop(index)
            copy.start()
            self.flying.append(copy)

    def close(self):
        self.put(*list(self.stores))
        for copy in self.flying:
            copy.wait()


def staged(kernel, count, which, outs=0, which_out=()):
    extra = len(which) + len(which_out) + 2

    def run(*refs):
        inputs, outputs = list(refs[:count]), list(refs[count : count + outs])
        tail = refs[-extra:]
        buffers, in_sems, out_sems = tail[:-2], tail[-2], tail[-1]
        staging = Staging()
        for place, index in enumerate(which):
            copy = pltpu.make_async_copy(inputs[index], buffers[place], in_sems.at[place])
            copy.start()
            staging.loads.append(copy)
            inputs[index] = buffers[place]
        for place, index in enumerate(which_out):
            buffer = buffers[len(which) + place]
            staging.stores[index] = pltpu.make_async_copy(
                buffer, outputs[index], out_sems.at[place]
            )
            outputs[index] = buffer
        kernel(staging, *inputs, *outputs, *refs[count + outs : -extra])
        staging.close()

    return run


def staged_specs(args, which, shapes=(), which_out=()):
    specs = [any_spec() if i in which else vspec() for i in range(len(args))]
    scratch = [pltpu.VMEM(args[i].shape, args[i].dtype) for i in which]
    scratch += [pltpu.VMEM(shapes[i].shape, shapes[i].dtype) for i in which_out]
    dma = pltpu.SemaphoreType.DMA
    return specs, scratch + [dma((len(which),)), dma((max(1, len(which_out)),))]


def greet(groups, staging=None):
    barrier = pltpu.get_barrier_semaphore()
    total = 0
    for axis, n in groups:
        me = lax.axis_index(axis)
        for step in range(1, n):
            pl.semaphore_signal(
                barrier, inc=1, device_id={axis: lax.rem(me + step, n)}, device_id_type=MESH
            )
        total += n - 1
    pl.semaphore_wait(barrier, total)
    if staging is not None:
        staging.wait()


class LineSum:
    def __init__(self, n, parts, send, recv, send_sem, recv_sem, total):
        self.n, self.parts = n, parts
        self.send, self.recv, self.send_sem, self.recv_sem = send, recv, send_sem, recv_sem
        self.total = total
        self.me = lax.axis_index("tensor")

    def flow(self, first, k):
        n, me = self.n, self.me
        near = me * 2 < n
        right = near if first else jnp.logical_not(near)
        block = jnp.where(right, n - 1 - k, k)
        comes = jnp.where(right, jnp.where(me > 0, me <= block, False), jnp.where(me < n - 1, me >= block, False))
        goes = jnp.where(right, me < block, me > block)
        peer = jnp.clip(jnp.where(right, me + 1, me - 1), 0, n - 1)
        out_slot = jnp.clip(jnp.where(right, k, n - 1 - me + k), 0, n - 2)
        in_slot = jnp.clip(jnp.where(right, k, n - me + k), 0, n)
        peer_slot = jnp.clip(jnp.where(right, k, n - peer + k), 0, n)
        return block, comes, goes, peer, out_slot, in_slot, peer_slot

    def copy(self, peer, out_slot, slot):
        return remote(
            self.send.at[out_slot],
            self.recv.at[slot],
            self.send_sem.at[out_slot],
            self.recv_sem.at[slot],
            "tensor",
            peer,
        )

    def start(self, partial=None):
        n, me = self.n, self.me

        def one(index, _):
            block = jnp.where(me * 2 < n, n - 1 - index, index)
            if partial is not None:
                value = partial(block)
                self.parts[block] = value.astype(BF16)

                @pl.when(block == me)
                def _():
                    self.total[...] = value

            @pl.when(jnp.logical_or(me == 0, me == n - 1) & (index < n - 1))
            def _():
                remote(
                    self.parts.at[block],
                    self.recv.at[jnp.where(me == 0, index, 2 + index)],
                    self.send_sem.at[index],
                    self.recv_sem.at[jnp.where(me == 0, index, 2 + index)],
                    "tensor",
                    jnp.where(me == 0, 1, n - 2),
                ).start()

            return 0

        lax.fori_loop(0, n, one, 0)
        if partial is None:
            self.total[...] = self.parts[me].astype(F32)

    def finish(self):
        for k in range(self.n - 1):
            self.step(k)

    def step(self, k):
        for first in (True, False):
            block, comes, goes, peer, out_slot, in_slot, peer_slot = self.flow(first, k)

            @pl.when(goes & comes)
            def _():
                self.copy(peer, out_slot, in_slot).wait_recv()
                self.send[out_slot] = (
                    self.parts[block].astype(F32) + self.recv[in_slot].astype(F32)
                ).astype(BF16)
                self.copy(peer, out_slot, peer_slot).start()

            @pl.when(comes & jnp.logical_not(goes))
            def _():
                self.copy(peer, 0, in_slot).wait_recv()
                self.total[...] += self.recv[in_slot].astype(F32)

    def drain(self):
        for k in range(self.n - 1):
            for first in (True, False):
                block, comes, goes, peer, out_slot, in_slot, peer_slot = self.flow(first, k)

                @pl.when(goes)
                def _():
                    self.copy(peer, out_slot, in_slot).wait_send()


def tail_kernel(
    n_dp,
    n_tensor,
    experts,
    table_rows,
    hidden_ref,
    grad_ref,
    weight_ref,
    attended_ref,
    branch_ref,
    small_ref,
    weight_own_ref,
    gain_own_ref,
    grad_hidden_ref,
    grad_qkv_ref,
    grad_out_ref,
    small_out_ref,
    parts,
    line_send,
    line_recv,
    qkv_send,
    qkv_recv,
    out_send,
    out_recv,
    small_recv,
    small_sum,
    gain_recv,
    line_send_sem,
    line_recv_sem,
    qkv_send_sem,
    qkv_recv_sem,
    out_send_sem,
    out_recv_sem,
    small_send_sem,
    small_recv_sem,
    gain_send_sem,
    gain_recv_sem,
):
    own_rows = grad_hidden_ref.shape[0]
    depth = weight_own_ref.shape[0]
    out_cols = grad_out_ref.shape[1]
    me = lax.axis_index("dp")
    me_t = lax.axis_index("tensor")
    greet([("dp", n_dp), ("tensor", n_tensor)])

    def partial(block):
        rows = pl.ds(pl.multiple_of(block * own_rows, own_rows), own_rows)
        return nt(grad_ref[rows, :], weight_ref[...])

    line = LineSum(
        n_tensor, parts, line_send, line_recv, line_send_sem, line_recv_sem, grad_hidden_ref
    )
    line.start(partial)
    copies = []
    for step in range(1, n_dp):
        peer = lax.rem(me + step, n_dp)
        copy = remote(
            small_ref.at[peer],
            small_recv.at[step - 1],
            small_send_sem.at[step - 1],
            small_recv_sem.at[step - 1],
            "dp",
            peer,
        )
        copy.start()
        copies.append(copy)
    for block in range(n_dp):
        cols = slice(block * depth, (block + 1) * depth)
        qkv_send[block] = tn(hidden_ref[:, cols], grad_ref[...]).astype(BF16)
    for step in range(1, n_dp):
        peer = lax.rem(me + step, n_dp)
        copy = remote(
            qkv_send.at[peer],
            qkv_recv.at[step - 1],
            qkv_send_sem.at[step - 1],
            qkv_recv_sem.at[step - 1],
            "dp",
            peer,
        )
        copy.start()
        copies.append(copy)
    for block in range(n_dp):
        cols = slice(block * out_cols, (block + 1) * out_cols)
        out_send[block] = tn(attended_ref[...], branch_ref[:, cols]).astype(BF16)
    for step in range(1, n_dp):
        peer = lax.rem(me + step, n_dp)
        copy = remote(
            out_send.at[peer],
            out_recv.at[step - 1],
            out_send_sem.at[step - 1],
            out_recv_sem.at[step - 1],
            "dp",
            peer,
        )
        copy.start()
        copies.append(copy)
    line.finish()
    for copy in copies:
        copy.wait()
    small_sum[...] = small_ref[me]
    grad_qkv_ref[...] = qkv_send[me].astype(F32)
    grad_out_ref[...] = out_send[me].astype(F32)
    for step in range(1, n_dp):
        small_sum[...] += small_recv[step - 1]
        grad_qkv_ref[...] += qkv_recv[step - 1].astype(F32)
        grad_out_ref[...] += out_recv[step - 1].astype(F32)
    column = jnp.sum(grad_qkv_ref[...] * weight_own_ref[...].astype(F32), axis=1, keepdims=True)
    eye = lax.broadcasted_iota(jnp.int32, (depth, depth), 0) == lax.broadcasted_iota(
        jnp.int32, (depth, depth), 1
    )
    row = jnp.sum(jnp.where(eye, column, 0.0), axis=0, keepdims=True)
    small_sum[experts + 1 : experts + 2, :] = row / gain_own_ref[...]
    gains = []
    for step in range(1, n_tensor):
        peer = lax.rem(me_t + step, n_tensor)
        copy = remote(
            small_sum,
            gain_recv.at[step - 1],
            gain_send_sem.at[step - 1],
            gain_recv_sem.at[step - 1],
            "tensor",
            peer,
        )
        copy.start()
        gains.append(copy)
    line.drain()
    for copy in gains:
        copy.wait()
    small_out_ref[...] = small_sum[...]
    shared = slice(0, experts + 2)
    for step in range(1, n_tensor):
        small_out_ref[shared, :] += gain_recv[step - 1, shared, :]


def tail(n_dp, n_tensor, experts, hidden, grad, weight, attended, branch, small, weight_own, gain_own):
    seq_len, width = hidden.shape
    own_rows = seq_len // n_tensor
    depth, cols = weight_own.shape
    heads_cols = attended.shape[1]
    out_cols = width // n_dp
    table_rows = NB // n_dp
    return pl.pallas_call(
        functools.partial(tail_kernel, n_dp, n_tensor, experts, table_rows),
        out_shape=(
            jax.ShapeDtypeStruct((own_rows, width), F32),
            jax.ShapeDtypeStruct((depth, cols), F32),
            jax.ShapeDtypeStruct((heads_cols, out_cols), F32),
            jax.ShapeDtypeStruct((SMALL, depth), F32),
        ),
        in_specs=[vspec()] * 8,
        out_specs=(vspec(),) * 4,
        scratch_shapes=[
            pltpu.VMEM((n_tensor, own_rows, width), BF16),
            pltpu.VMEM((n_tensor - 1, own_rows, width), BF16),
            pltpu.VMEM((n_tensor + 1, own_rows, width), BF16),
            pltpu.VMEM((n_dp, depth, cols), BF16),
            pltpu.VMEM((n_dp - 1, depth, cols), BF16),
            pltpu.VMEM((n_dp, heads_cols, out_cols), BF16),
            pltpu.VMEM((n_dp - 1, heads_cols, out_cols), BF16),
            pltpu.VMEM((n_dp - 1, SMALL, depth), F32),
            pltpu.VMEM((SMALL, depth), F32),
            pltpu.VMEM((n_tensor - 1, SMALL, depth), F32),
            pltpu.SemaphoreType.DMA((n_tensor - 1,)),
            pltpu.SemaphoreType.DMA((n_tensor + 1,)),
        ]
        + [pltpu.SemaphoreType.DMA((n_dp - 1,))] * 6
        + [pltpu.SemaphoreType.DMA((n_tensor - 1,))] * 2,
        compiler_params=pltpu.CompilerParams(
            vmem_limit_bytes=VMEM_LIMIT, collective_id=0, has_side_effects=True
        ),
        name="tail",
    )(hidden, grad, weight, attended, branch, small, weight_own, gain_own)


def diagonal(size):
    return lax.broadcasted_iota(jnp.int32, (size, size), 0) == lax.broadcasted_iota(
        jnp.int32, (size, size), 1
    )


def to_column(row):
    return jnp.sum(jnp.where(diagonal(row.shape[1]), row, 0.0), axis=1, keepdims=True)


def to_row(column):
    return jnp.sum(jnp.where(diagonal(column.shape[0]), column, 0.0), axis=0, keepdims=True)


def expert_kernel(
    n_dp,
    local,
    capacity,
    rows_hbm,
    grad_hbm,
    gates_ref,
    in_hbm,
    out_hbm,
    back_ref,
    gate_back_ref,
    value_ref,
    grad_in_ref,
    grad_out_ref,
    back_send,
    gate_send,
    zs,
    ups,
    gates_s,
    stage,
    value_stage,
    back_send_sem,
    back_recv_sem,
    gate_send_sem,
    gate_recv_sem,
    own_sem,
    stage_sem,
    value_sem,
    rows_ref,
    grad_ref,
    in_ref,
    out_ref,
    rows_sem,
    grad_sem,
    in_sem,
    out_sem,
):
    me = lax.axis_index("dp")
    pairs = n_dp // 2
    hidden = in_ref.shape[2]
    width = rows_ref.shape[2]
    two = 2 * capacity

    def pair_at(index):
        return (me // 2) ^ (pairs - 1 - index)

    def load_pair(index):
        where = pl.ds(2 * pair_at(index), 2)
        return (
            pltpu.make_async_copy(rows_hbm.at[where], rows_ref.at[where], rows_sem.at[index]),
            pltpu.make_async_copy(grad_hbm.at[where], grad_ref.at[where], grad_sem.at[index]),
        )

    def load_expert(expert):
        return (
            pltpu.make_async_copy(in_hbm.at[expert], in_ref.at[expert], in_sem.at[expert]),
            pltpu.make_async_copy(out_hbm.at[expert], out_ref.at[expert], out_sem.at[expert]),
        )

    for copy in load_expert(0) + load_pair(0):
        copy.start()
    for index in range(1, pairs):
        for copy in load_pair(index):
            copy.start()
    for expert in range(1, local):
        for copy in load_expert(expert):
            copy.start()
    greet([("dp", n_dp)])

    def back_copy(expert, target, sender):
        part = slice(expert * capacity, (expert + 1) * capacity)
        return remote(
            back_send.at[target, part],
            back_ref.at[sender, part],
            back_send_sem.at[expert, target],
            back_recv_sem.at[expert, sender],
            "dp",
            target,
        )

    def own_copy(expert):
        part = slice(expert * capacity, (expert + 1) * capacity)
        return pltpu.make_async_copy(
            back_send.at[me, part], back_ref.at[me, part], own_sem.at[expert]
        )

    def stage_copy(slot, target):
        return pltpu.make_async_copy(stage.at[slot], target, stage_sem.at[slot])

    gate_send[...] = jnp.zeros_like(gate_send)
    staged = []

    def put(value, target):
        slot = len(staged) % 2
        if len(staged) >= 2:
            staged[-2].wait()
        stage[slot] = value.astype(BF16)
        copy = stage_copy(slot, target)
        copy.start()
        staged.append(copy)

    for expert in range(local):
        part = slice(expert * capacity, (expert + 1) * capacity)

        for copy in load_expert(expert):
            copy.wait()

        def group(index, _):
            if expert == 0:
                for copy in load_pair(index):
                    copy.wait()
            first = 2 * pair_at(index)
            rows = rows_ref[pl.ds(first, 2), part, :].reshape(two, width)
            grads = grad_ref[pl.ds(first, 2), part, :].reshape(two, width)
            column = jnp.concatenate(
                [to_column(gates_ref[first + j, 0:1, part]) for j in range(2)], axis=0
            )
            gate = nt(rows, in_ref[expert, 0])
            up = nt(rows, in_ref[expert, 1])
            square = gate * gate
            bent = jnp.tanh(0.7978845608028654 * gate * (1.0 + 0.044715 * square))
            half = 0.5 * (1.0 + bent)
            gelu = gate * half
            slope = half + 0.5 * gate * (1.0 - bent * bent) * (
                0.7978845608028654 * (1.0 + 3 * 0.044715 * square)
            )
            z = gelu * up
            grad_z = nt(grads, out_ref[expert])
            gate_grad = jnp.sum(z * grad_z, axis=1, keepdims=True)
            grad_z = column * grad_z
            zs[pl.ds(first, 2)] = (column * z).astype(BF16).reshape(2, capacity, hidden)
            ups[0, pl.ds(first, 2)] = (grad_z * up * slope).astype(BF16).reshape(2, capacity, hidden)
            ups[1, pl.ds(first, 2)] = (grad_z * gelu).astype(BF16).reshape(2, capacity, hidden)
            for j in range(2):
                gate_send[first + j, 0:1, part] = to_row(
                    gate_grad[j * capacity : (j + 1) * capacity]
                )
            back = nn(ups[0, pl.ds(first, 2)].reshape(two, hidden), in_ref[expert, 0])
            back += nn(ups[1, pl.ds(first, 2)].reshape(two, hidden), in_ref[expert, 1])
            back_send[pl.ds(first, 2), part, :] = back.astype(BF16).reshape(2, capacity, width)
            for j in range(2):
                target = first + j

                @pl.when(target != me)
                def _():
                    back_copy(expert, target, me).start()

                @pl.when(target == me)
                def _():
                    own_copy(expert).start()

            return 0

        lax.fori_loop(0, pairs, group, 0)
        if expert == local - 1:
            gate_copies = []
            for step in range(1, n_dp):
                target = lax.rem(me + step, n_dp)
                copy = remote(
                    gate_send.at[target],
                    gate_back_ref.at[me],
                    gate_send_sem.at[step - 1],
                    gate_recv_sem.at[step - 1],
                    "dp",
                    target,
                )
                copy.start()
                gate_copies.append(copy)
            gate_back_ref[me] = gate_send[me]
        rows = rows_ref[:, part, :].reshape(n_dp * capacity, width)
        for half in range(2):
            put(tn(ups[half].reshape(n_dp * capacity, hidden), rows), grad_in_ref.at[expert, half])
        grads = grad_ref[:, part, :].reshape(n_dp * capacity, width)
        put(tn(zs[...].reshape(n_dp * capacity, hidden), grads), grad_out_ref.at[expert])
        if expert > 0:
            pltpu.make_async_copy(
                value_stage, value_ref.at[:, slice((expert - 1) * capacity, expert * capacity)], value_sem
            ).wait()

        def value(pair, _):
            out = nn(zs[pl.ds(2 * pair, 2)].reshape(two, hidden), out_ref[expert])
            value_stage[pl.ds(2 * pair, 2)] = out.astype(BF16).reshape(2, capacity, width)
            return 0

        lax.fori_loop(0, pairs, value, 0)
        pltpu.make_async_copy(value_stage, value_ref.at[:, part], value_sem).start()

    last = slice((local - 1) * capacity, local * capacity)
    pltpu.make_async_copy(value_stage, value_ref.at[:, last], value_sem).wait()
    for copy in staged[-2:]:
        copy.wait()
    for copy in gate_copies:
        copy.wait()
    for expert in range(local):
        own_copy(expert).wait()
        for step in range(1, n_dp):
            peer = lax.rem(me + step, n_dp)
            back_copy(expert, peer, me).wait_send()
            back_copy(expert, me, peer).wait_recv()


def any_spec():
    return pl.BlockSpec(memory_space=pl.ANY)


def run_experts(n_dp, capacity, rows, grads, gates, w_in, w_out):
    local, _, hidden, width = w_in.shape
    slots = local * capacity
    return pl.pallas_call(
        functools.partial(expert_kernel, n_dp, local, capacity),
        out_shape=(
            jax.ShapeDtypeStruct((n_dp, slots, width), BF16),
            jax.ShapeDtypeStruct((n_dp, 8, slots), F32),
            jax.ShapeDtypeStruct((n_dp, slots, width), BF16),
            jax.ShapeDtypeStruct(w_in.shape, BF16),
            jax.ShapeDtypeStruct(w_out.shape, BF16),
        ),
        in_specs=[any_spec(), any_spec(), vspec(), any_spec(), any_spec()],
        out_specs=(any_spec(), vspec(), any_spec(), any_spec(), any_spec()),
        scratch_shapes=[
            pltpu.VMEM((n_dp, slots, width), BF16),
            pltpu.VMEM((n_dp, 8, slots), F32),
            pltpu.VMEM((n_dp, capacity, hidden), BF16),
            pltpu.VMEM((2, n_dp, capacity, hidden), BF16),
            pltpu.VMEM((8, 128), F32),
            pltpu.VMEM((2, hidden, width), BF16),
            pltpu.VMEM((n_dp, capacity, width), BF16),
            pltpu.SemaphoreType.DMA((local, n_dp)),
            pltpu.SemaphoreType.DMA((local, n_dp)),
            pltpu.SemaphoreType.DMA((n_dp - 1,)),
            pltpu.SemaphoreType.DMA((n_dp - 1,)),
            pltpu.SemaphoreType.DMA((local,)),
            pltpu.SemaphoreType.DMA((2,)),
            pltpu.SemaphoreType.DMA,
            pltpu.VMEM(rows.shape, BF16),
            pltpu.VMEM(grads.shape, BF16),
            pltpu.VMEM(w_in.shape, BF16),
            pltpu.VMEM(w_out.shape, BF16),
            pltpu.SemaphoreType.DMA((n_dp // 2,)),
            pltpu.SemaphoreType.DMA((n_dp // 2,)),
            pltpu.SemaphoreType.DMA((local,)),
            pltpu.SemaphoreType.DMA((local,)),
        ],
        compiler_params=pltpu.CompilerParams(
            vmem_limit_bytes=VMEM_LIMIT, collective_id=1, has_side_effects=True
        ),
        name="experts",
    )(rows, grads, gates, w_in, w_out)


def chosen_slots(columns, slots):
    lane = lax.broadcasted_iota(jnp.int32, (1, slots), 1)
    return columns[:, 0:1] == lane, columns[:, 1:2] == lane


def combine_kernel(
    n_dp,
    n_tensor,
    experts,
    loads,
    rows_ref,
    gate_ref,
    slots_ref,
    routes_ref,
    residual_ref,
    hidden_ref,
    cotangent_ref,
    router_ref,
    gain_ref,
    weight_ref,
    value_ref,
    grad_residual_ref,
    branch_ref,
    grad_attended_ref,
    small_ref,
    merged_ref,
    parts,
    total,
    line_send,
    line_recv,
    gate_all,
    gate_send,
    gate_recv,
    value_back,
    line_send_sem,
    line_recv_sem,
    gate_send_sem,
    gate_recv_sem,
    value_send_sem,
    value_recv_sem,
    value_own_sem,
    gather_send_sem,
    gather_recv_sem,
):
    own_rows, width = residual_ref.shape
    slots = rows_ref.shape[0]
    per = slots // n_dp
    me = lax.axis_index("dp")
    me_t = lax.axis_index("tensor")
    greet([("dp", n_dp), ("tensor", n_tensor)], loads)
    values = []
    for step in range(1, n_dp):
        peer = lax.rem(me + step, n_dp)
        copy = remote(
            value_ref.at[peer],
            value_back.at[me],
            value_send_sem.at[step - 1],
            value_recv_sem.at[step - 1],
            "dp",
            peer,
        )
        copy.start()
        values.append(copy)
    fetch = pltpu.make_async_copy(value_ref.at[me], value_back.at[me], value_own_sem)
    fetch.start()

    def partial(block):
        one, two = chosen_slots(
            slots_ref[pl.ds(pl.multiple_of(block * own_rows, own_rows), own_rows), :], slots
        )
        return nn(jnp.where(one | two, 1.0, 0.0).astype(BF16), rows_ref[...])

    line = LineSum(n_tensor, parts, line_send, line_recv, line_send_sem, line_recv_sem, total)
    line.start(partial)
    for peer in range(n_dp):
        gate_all[0:1, peer * per : (peer + 1) * per] = gate_ref[peer, 0:1, :]
    gate_send[...] = jnp.zeros_like(gate_send)
    gates = []
    for step in range(n_tensor):
        peer = lax.rem(me_t + step, n_tensor)
        picks = chosen_slots(
            slots_ref[pl.ds(pl.multiple_of(peer * own_rows, own_rows), own_rows), :], slots
        )
        for k in range(TOP):
            column = jnp.sum(
                jnp.where(picks[k], gate_all[0:1, :], 0.0), axis=1, keepdims=True
            )
            gate_send[step, k : k + 1, :] = to_row(column)
        if step:
            copy = remote(
                gate_send.at[step],
                gate_recv.at[step - 1],
                gate_send_sem.at[step - 1],
                gate_recv_sem.at[step - 1],
                "tensor",
                peer,
            )
            copy.start()
            gates.append(copy)
    hidden = hidden_ref[...]
    router = router_ref[...]
    logits = nt(router, hidden)
    exps = jnp.exp(logits - jnp.max(logits, axis=0, keepdims=True))
    probs = exps / jnp.sum(exps, axis=0, keepdims=True)
    ids = lax.broadcasted_iota(jnp.int32, (experts, own_rows), 0)
    own_lanes = pl.ds(pl.multiple_of(me_t * own_rows, own_rows), own_rows)
    first, second = ids == routes_ref[0:1, own_lanes], ids == routes_ref[1:2, own_lanes]
    prob_one = jnp.sum(jnp.where(first, probs, 0.0), axis=0, keepdims=True)
    prob_two = jnp.sum(jnp.where(second, probs, 0.0), axis=0, keepdims=True)
    both = prob_one + prob_two
    line.finish()
    for copy in gates:
        copy.wait()
    gate_sum = gate_send[0]
    for step in range(1, n_tensor):
        gate_sum = gate_sum + gate_recv[step - 1]
    grad_one, grad_two = gate_sum[0:1, :], gate_sum[1:2, :]
    mean_grad = (prob_one * grad_one + prob_two * grad_two) / both
    grad_probs = (
        jnp.where(first, grad_one - mean_grad, 0.0) + jnp.where(second, grad_two - mean_grad, 0.0)
    ) / both
    grad_logits = probs * (grad_probs - jnp.sum(grad_probs * probs, axis=0, keepdims=True))
    grad_hidden = total[...] + lax.dot_general(
        grad_logits,
        router.astype(F32),
        (((0,), (0,)), ((), ())),
        precision=lax.Precision.HIGHEST,
        preferred_element_type=F32,
    )
    residual = residual_ref[...]
    scale = lax.rsqrt(jnp.mean(residual * residual, axis=1, keepdims=True) + EPS)
    unit = residual * scale
    small_ref[...] = jnp.zeros_like(small_ref)
    small_ref[experts : experts + 1, :] = jnp.sum(grad_hidden * unit, axis=0, keepdims=True)
    grad_unit = grad_hidden * gain_ref[...]
    grad_residual = cotangent_ref[...].astype(F32) + scale * (
        grad_unit - unit * jnp.mean(grad_unit * unit, axis=1, keepdims=True)
    )
    grad_residual_ref[...] = grad_residual
    loads.put(0)
    branch_ref[me_t] = grad_residual.astype(BF16)

    def on_block(block):
        grad_attended_ref[pl.ds(pl.multiple_of(block * own_rows, own_rows), own_rows), :] = nt(
            branch_ref[block], weight_ref[...]
        ).astype(BF16)

    lines = Streams(n_tensor, [branch_ref], gather_send_sem, gather_recv_sem)
    for turn in lines.turns():
        lines.turn(turn, lambda j, k: lines.each_new(j, k, on_block))
        if turn == n_tensor - 2:
            fetch.wait()
            for copy in values:
                copy.wait_recv()

            def merge(block, _):
                rows = pl.ds(pl.multiple_of(block * own_rows, own_rows), own_rows)
                one, two = chosen_slots(slots_ref[rows, :], slots)
                merged_ref[block] = nn(
                    jnp.where(one | two, 1.0, 0.0).astype(BF16), value_back[...].reshape(slots, width)
                ).astype(BF16)
                return 0

            lax.fori_loop(0, n_tensor, merge, 0)
            loads.put(4)
    loads.put(1, 2)
    lines.drain()
    small_ref[0:experts, :] = jnp.dot(
        grad_logits,
        hidden.astype(F32),
        precision=lax.Precision.HIGHEST,
        preferred_element_type=F32,
    )
    line.drain()
    for copy in values:
        copy.wait_send()


def combine(
    n_dp,
    n_tensor,
    experts,
    rows,
    gates,
    slot_columns,
    routes_own,
    residual,
    hidden,
    cotangent,
    router_rows,
    gain,
    weight,
    value,
):
    own_rows, width = residual.shape
    slots = rows.shape[0]
    args = (
        rows,
        gates,
        slot_columns,
        routes_own,
        residual,
        hidden,
        cotangent,
        router_rows,
        gain,
        weight,
        value,
    )
    which, which_out = (0, 4, 5, 6, 9), (0, 1, 2, 4)
    shapes = (
        jax.ShapeDtypeStruct((own_rows, width), F32),
        jax.ShapeDtypeStruct((n_tensor, own_rows, width), BF16),
        jax.ShapeDtypeStruct((n_tensor * own_rows, weight.shape[0]), BF16),
        jax.ShapeDtypeStruct((SMALL, width), F32),
        jax.ShapeDtypeStruct((n_tensor, own_rows, width), BF16),
    )
    specs, buffers = staged_specs(args[:10], which, shapes, which_out)
    return pl.pallas_call(
        staged(
            functools.partial(combine_kernel, n_dp, n_tensor, experts),
            len(args),
            which,
            len(shapes),
            which_out,
        ),
        out_shape=shapes,
        in_specs=specs + [any_spec()],
        out_specs=(any_spec(), any_spec(), any_spec(), vspec(), any_spec()),
        scratch_shapes=[
            pltpu.VMEM((n_tensor, own_rows, width), BF16),
            pltpu.VMEM((own_rows, width), F32),
            pltpu.VMEM((n_tensor - 1, own_rows, width), BF16),
            pltpu.VMEM((n_tensor + 1, own_rows, width), BF16),
            pltpu.VMEM((8, slots), F32),
            pltpu.VMEM((n_tensor, 8, own_rows), F32),
            pltpu.VMEM((n_tensor - 1, 8, own_rows), F32),
            pltpu.VMEM(value.shape, BF16),
            pltpu.SemaphoreType.DMA((n_tensor - 1,)),
            pltpu.SemaphoreType.DMA((n_tensor + 1,)),
            pltpu.SemaphoreType.DMA((n_tensor - 1,)),
            pltpu.SemaphoreType.DMA((n_tensor - 1,)),
            pltpu.SemaphoreType.DMA((n_dp - 1,)),
            pltpu.SemaphoreType.DMA((n_dp - 1,)),
            pltpu.SemaphoreType.DMA,
            pltpu.SemaphoreType.DMA((1, 2, n_tensor - 1)),
            pltpu.SemaphoreType.DMA((1, 2, n_tensor - 1)),
        ]
        + buffers,
        compiler_params=pltpu.CompilerParams(
            vmem_limit_bytes=VMEM_LIMIT, collective_id=2, has_side_effects=True
        ),
        name="combine",
    )(*args)


class Streams:
    def __init__(self, n, refs, send_sem, recv_sem):
        self.n, self.refs, self.send_sem, self.recv_sem = n, refs, send_sem, recv_sem
        self.me = lax.axis_index("tensor")

    def copy(self, j, block, slot, k, peer):
        ref = self.refs[j].at[block]
        return remote(
            ref, ref, self.send_sem.at[j, slot, k], self.recv_sem.at[j, slot, k], "tensor", peer
        )

    def outgoing(self, j, k, fn):
        for slot, sign in enumerate((1, -1)):
            block, peer = self.me - sign * k, self.me + sign

            @pl.when((block >= 0) & (block < self.n) & (peer >= 0) & (peer < self.n))
            def _():
                fn(self.copy(j, block, slot, k, peer))

    def incoming(self, j, k, fn):
        for slot, sign in enumerate((1, -1)):
            block = self.me - sign * (k + 1)

            @pl.when((block >= 0) & (block < self.n))
            def _():
                fn(self.copy(j, block, slot, k, jnp.clip(self.me - sign, 0, self.n - 1)), block)

    def turn(self, turn, used=None):
        moved = []
        for j in range(len(self.refs)):
            k = turn - j
            if k < 0 or k > self.n - 1:
                continue
            self.advance(j, k)
            moved.append((j, k))
        if used is not None:
            for j, k in moved:
                used(j, k)

    def turns(self):
        return range(self.n + len(self.refs) - 1)

    def advance(self, j, k):
        if k > 0:
            self.incoming(j, k - 1, lambda c, block: c.wait_recv())
        if k < self.n - 1:
            self.outgoing(j, k, lambda c: c.start())

    def each_new(self, j, k, fn):
        if k == 0:
            fn(self.me)
            return
        for sign in (1, -1):
            block = self.me - sign * k

            @pl.when((block >= 0) & (block < self.n))
            def _():
                fn(block)

    def drain(self):
        for j in range(len(self.refs)):
            for k in range(self.n - 1):
                self.outgoing(j, k, lambda c: c.wait_send())


class Spread:
    def __init__(self, n, ref, far_send, far_recv, near_send, near_recv):
        self.n, self.ref = n, ref
        self.far_send, self.far_recv = far_send, far_recv
        self.near_send, self.near_recv = near_send, near_recv
        self.me = lax.axis_index("dp")
        self.partner = self.me ^ 1

    def far(self, step, block, peer):
        ref = self.ref.at[block]
        return remote(ref, ref, self.far_send.at[step], self.far_recv.at[step], "dp", peer)

    def near(self, step, block):
        ref = self.ref.at[block]
        return remote(
            ref, ref, self.near_send.at[step], self.near_recv.at[step], "dp", self.partner
        )

    def start(self):
        for step in range(1, self.n // 2):
            self.far(step - 1, self.me, lax.rem(self.me + 2 * step, self.n)).start()
        self.near(0, self.me).start()

    def source(self, me, step):
        return lax.rem(me + self.n - 2 * step, self.n)

    def relay(self):
        for step in range(1, self.n // 2):
            block = self.source(self.me, step)
            self.far(step - 1, block, block).wait_recv()
            self.near(step, block).start()

    def finish(self):
        for step in range(self.n // 2):
            self.near(step, self.source(self.partner, step)).wait_recv()

    def drain(self):
        for step in range(1, self.n // 2):
            self.far(step - 1, self.me, lax.rem(self.me + 2 * step, self.n)).wait_send()
        for step in range(self.n // 2):
            self.near(step, self.source(self.me, step)).wait_send()


def one_hot(slot_rows, target, per):
    lane_slots = lax.broadcasted_iota(jnp.int32, (per, 1), 0) + target * per
    return jnp.where(
        (lane_slots == slot_rows[0:1, :]) | (lane_slots == slot_rows[1:2, :]), 1.0, 0.0
    ).astype(BF16)


def band(seq_len):
    return -(-(seq_len // 2 - 1) // BS)


def send_parameters(n_dp, n_tensor, weight_ref, extra_ref, out_ref, weights_ref, outs_ref, extras_ref, sems):
    me = lax.axis_index("dp")
    me_t = lax.axis_index("tensor")
    (extra_send, extra_recv, line_send, line_recv) = sems[:4]
    extras_ref[me] = extra_ref[...]
    small = []
    for step in range(1, n_dp):
        peer = lax.rem(me + step, n_dp)
        copy = remote(
            extra_ref, extras_ref.at[me], extra_send.at[step - 1], extra_recv.at[step - 1], "dp", peer
        )
        copy.start()
        small.append(copy)
    weights_ref[me] = weight_ref[...]
    weights = Spread(n_dp, weights_ref, *sems[4:8])
    weights.start()
    outs_ref[me, me_t] = out_ref[...]
    along = []
    for step in range(1, n_tensor):
        peer = lax.rem(me_t + step, n_tensor)
        copy = remote(
            out_ref,
            outs_ref.at[me, me_t],
            line_send.at[step - 1],
            line_recv.at[step - 1],
            "tensor",
            peer,
        )
        copy.start()
        along.append(copy)
    return small, weights, Spread(n_dp, outs_ref, *sems[8:12]), along


def unpack_parameters(n_dp, experts, extras_ref, selector_ref, router_ref, table, pattern_ref):
    depth = table.shape[1]
    rows_each = NB // n_dp
    for block in range(n_dp):
        router_ref[:, block * depth : (block + 1) * depth] = extras_ref[block, 0:experts, :]
        table[block * rows_each : (block + 1) * rows_each, :] = extras_ref[
            block, experts + 2 : experts + 2 + rows_each, :
        ].astype(F32)
    patterns = lax.dot_general(
        table[...],
        selector_ref[...],
        (((0,), (0,)), ((), ())),
        precision=lax.Precision.HIGHEST,
        preferred_element_type=F32,
    )
    for row in range(pattern_ref.shape[0]):
        pattern_ref[row : row + 1, :] = patterns[
            row // 2 : row // 2 + 1, (row % 2) * 2 * BS : (row % 2 + 1) * 2 * BS
        ]


def first_hidden(n_dp, experts, tokens_ref, extras_ref, gains_ref, small):
    depth = extras_ref.shape[2]
    x = tokens_ref[...].astype(F32)
    scaled = x * lax.rsqrt(jnp.mean(x * x, axis=1, keepdims=True) + EPS)
    for copy in small:
        copy.wait()
    for block in range(n_dp):
        gains_ref[0:2, block * depth : (block + 1) * depth] = extras_ref[
            block, experts : experts + 2, :
        ].astype(F32)
    return (scaled * gains_ref[0:1, :]).astype(BF16)


def parameter_sems(n_dp, n_tensor):
    dma = pltpu.SemaphoreType.DMA
    return (
        [dma((n_dp - 1,))] * 2 + [dma((n_tensor - 1,))] * 2 + [dma((n_dp // 2,))] * 8
    )


def front_kernel(
    n_dp,
    n_tensor,
    experts,
    tokens_ref,
    weight_ref,
    extra_ref,
    out_ref,
    selector_ref,
    hidden_ref,
    projected_ref,
    weights_ref,
    outs_ref,
    pattern_ref,
    router_ref,
    gains_ref,
    extras_ref,
    table,
    *sems,
):
    own_rows, width = tokens_ref.shape
    me_t = lax.axis_index("tensor")
    greet([("dp", n_dp), ("tensor", n_tensor)])
    small, weights, spread, along = send_parameters(
        n_dp, n_tensor, weight_ref, extra_ref, out_ref, weights_ref, outs_ref, extras_ref, sems
    )
    hidden_ref[me_t] = first_hidden(n_dp, experts, tokens_ref, extras_ref, gains_ref, small)
    lines = Streams(n_tensor, [hidden_ref], sems[12], sems[13])
    lines.turn(0)
    unpack_parameters(n_dp, experts, extras_ref, selector_ref, router_ref, table, pattern_ref)
    weights.relay()
    for copy in along:
        copy.wait_recv()
    spread.start()
    weights.finish()
    spread.relay()
    spread.finish()

    def project(block):
        rows = pl.ds(pl.multiple_of(block * own_rows, own_rows), own_rows)
        projected_ref[rows, :] = nn(
            hidden_ref[block], weights_ref[...].reshape(width, weights_ref.shape[2])
        ).astype(BF16)

    for turn in lines.turns():
        if turn:
            lines.turn(turn)

    def every(block, _):
        project(block)
        return 0

    lax.fori_loop(0, n_tensor, every, 0)
    lines.drain()
    weights.drain()
    spread.drain()
    for copy in along:
        copy.wait_send()


def front(n_dp, n_tensor, experts, tokens, weight, extra, out, selectors):
    own_rows, width = tokens.shape
    seq_len = own_rows * n_tensor
    depth, cols = weight.shape
    heads = cols // (3 * HD)
    dma = pltpu.SemaphoreType.DMA
    return pl.pallas_call(
        functools.partial(front_kernel, n_dp, n_tensor, experts),
        out_shape=(
            jax.ShapeDtypeStruct((n_tensor, own_rows, width), BF16),
            jax.ShapeDtypeStruct((seq_len, cols), BF16),
            jax.ShapeDtypeStruct((n_dp, depth, cols), BF16),
            jax.ShapeDtypeStruct((n_dp, n_tensor) + out.shape, BF16),
            jax.ShapeDtypeStruct((2 * heads, 2 * BS), F32),
            jax.ShapeDtypeStruct((experts, width), BF16),
            jax.ShapeDtypeStruct((2, width), F32),
        ),
        in_specs=[vspec()] * 5,
        out_specs=(vspec(),) * 7,
        scratch_shapes=[pltpu.VMEM((n_dp,) + extra.shape, BF16), pltpu.VMEM((NB, depth), F32)]
        + parameter_sems(n_dp, n_tensor)
        + [dma((1, 2, n_tensor - 1))] * 2,
        compiler_params=pltpu.CompilerParams(
            vmem_limit_bytes=VMEM_LIMIT, collective_id=3, has_side_effects=True
        ),
        name="front",
    )(tokens, weight, extra, out, selectors)


PARTS = 4
ROW_PARTS = 8


class Dispatch:
    def __init__(self, n_dp, picks, stage, rows_ref, send_sem, recv_sem, own_sem):
        self.n, self.picks, self.stage, self.rows = n_dp, picks, stage, rows_ref
        self.send_sem, self.recv_sem, self.own_sem = send_sem, recv_sem, own_sem
        self.me = lax.axis_index("dp")

    def cols(self, j):
        part = self.stage.shape[3]
        return slice(j * part, (j + 1) * part)

    def copy(self, j, target, sender):
        return remote(
            self.stage.at[j, target],
            self.rows.at[sender, :, self.cols(j)],
            self.send_sem.at[j, target],
            self.recv_sem.at[j, sender],
            "dp",
            target,
        )

    def own(self, j):
        return pltpu.make_async_copy(
            self.stage.at[j, self.me], self.rows.at[self.me, :, self.cols(j)], self.own_sem.at[j]
        )

    def start(self, j, values_ref):
        n_tensor, own_rows, part = values_ref.shape

        def one(index, _):
            mask = self.n - 1 - index
            target = self.me ^ mask
            self.stage[j, target] = nn(
                self.picks[target], values_ref[...].reshape(n_tensor * own_rows, part)
            ).astype(BF16)

            @pl.when(mask != 0)
            def _():
                self.copy(j, target, self.me).start()

            @pl.when(mask == 0)
            def _():
                self.own(j).start()

            return 0

        lax.fori_loop(0, self.n, one, 0)

    def finish(self):
        for j in range(self.stage.shape[0]):
            self.own(j).wait()
            for step in range(1, self.n):
                peer = lax.rem(self.me + step, self.n)
                self.copy(j, peer, self.me).wait_send()
                self.copy(j, self.me, peer).wait_recv()


def opening_kernel(
    n_dp,
    n_tensor,
    experts,
    capacity,
    loads,
    tokens_ref,
    cotangent_ref,
    weight_ref,
    extra_ref,
    out_ref,
    routes_ref,
    segment_ref,
    selector_ref,
    hidden_ref,
    projected_ref,
    weights_ref,
    pattern_ref,
    router_ref,
    gains_ref,
    slots_ref,
    attended_ref,
    lse_ref,
    residual_ref,
    hidden_two_ref,
    weight_own_ref,
    rows_ref,
    grad_rows_ref,
    gates_ref,
    extras_ref,
    table,
    outs,
    out_matrix,
    grads,
    everyone,
    picks,
    grad_stage,
    row_stage,
    bias,
    slot_rows,
    attended_recv,
    logits,
    gate_stage,
    *sems,
):
    own_rows, width = tokens_ref.shape
    seq_len = own_rows * n_tensor
    heads = pattern_ref.shape[0] // 2
    head_cols = heads * HD
    out_cols = out_ref.shape[1]
    local = experts // n_dp
    per = local * capacity
    part = width // PARTS
    row_part = width // ROW_PARTS
    me = lax.axis_index("dp")
    me_t = lax.axis_index("tensor")
    (hop_send, hop_recv, late_send, late_recv) = sems[12:16]
    (grad_send, grad_recv, grad_own, row_send, row_recv, row_own) = sems[16:22]
    (gate_send, gate_recv, attended_send_sem, attended_recv_sem) = sems[22:26]
    greet([("dp", n_dp), ("tensor", n_tensor)], loads)

    def rows_of(block):
        return pl.ds(pl.multiple_of(block * own_rows, own_rows), own_rows)

    for j in range(PARTS):
        grads[j, me_t] = cotangent_ref[:, j * part : (j + 1) * part]
    lines = Streams(
        n_tensor, [hidden_ref] + [grads.at[j] for j in range(PARTS)], hop_send, hop_recv
    )
    lines.advance(1, 0)
    lines.advance(2, 0)
    small, weights, spread, along = send_parameters(
        n_dp, n_tensor, weight_ref, extra_ref, out_ref, weights_ref, outs, extras_ref, sems
    )
    hidden_ref[me_t] = first_hidden(n_dp, experts, tokens_ref, extras_ref, gains_ref, small)
    lines.advance(1, 1)
    lines.advance(2, 1)
    unpack_parameters(n_dp, experts, extras_ref, selector_ref, router_ref, table, pattern_ref)
    lines.advance(1, 2)
    lines.advance(2, 2)
    lines.advance(0, 0)

    ids = lax.broadcasted_iota(jnp.int32, (experts, seq_len), 0)
    hits = [ids == routes_ref[k : k + 1, :] for k in range(TOP)]
    before = lax.broadcasted_iota(jnp.int32, (seq_len, seq_len), 0) < lax.broadcasted_iota(
        jnp.int32, (seq_len, seq_len), 1
    )
    ranks = nn(
        jnp.where(hits[0] | hits[1], 1.0, 0.0).astype(BF16),
        jnp.where(before, 1.0, 0.0).astype(BF16),
    )
    places = ranks + (ids * capacity).astype(F32)
    for k in range(TOP):
        row = jnp.sum(jnp.where(hits[k], places, 0.0), axis=0, keepdims=True)
        slot_rows[k : k + 1, :] = row.astype(jnp.int32)
        for block in range(n_tensor):
            rows = slice(block * own_rows, (block + 1) * own_rows)
            slots_ref[rows, k : k + 1] = to_column(row[:, rows]).astype(jnp.int32)


    def pick(target, _):
        picks[target] = one_hot(slot_rows, target, per)
        return 0

    lax.fori_loop(0, n_dp, pick, 0)
    grad_moves = Dispatch(n_dp, picks, grad_stage, grad_rows_ref, grad_send, grad_recv, grad_own)
    lines.advance(1, 3)
    grad_moves.start(0, grads.at[0])
    lines.advance(2, 3)
    grad_moves.start(1, grads.at[1])
    weights.relay()
    for copy in along:
        copy.wait_recv()
    spread.start()
    build_bias(heads, pattern_ref, bias)

    def project(block):
        projected_ref[rows_of(block), :] = nn(
            hidden_ref[block], weights_ref[...].reshape(width, weights_ref.shape[2])
        ).astype(BF16)

    lines.advance(0, 1)
    weights.finish()
    project(me_t)
    lines.advance(0, 2)
    lines.advance(3, 0)
    lines.advance(4, 0)
    spread.relay()
    lines.each_new(0, 1, project)
    lines.advance(0, 3)
    lines.advance(3, 1)
    lines.advance(4, 1)
    lines.each_new(0, 2, project)
    lines.each_new(0, 3, project)

    def attended_copy(target, sender):
        return remote(
            attended_ref.at[rows_of(target)],
            attended_recv.at[sender],
            attended_send_sem.at[target],
            attended_recv_sem.at[sender],
            "tensor",
            target,
        )

    def attend(qb):
        forward_rows(
            heads,
            qb,
            max(0, qb - band(seq_len)),
            projected_ref,
            segment_ref,
            bias,
            attended_ref,
            lse_ref,
        )

        @pl.when(me_t == qb)
        def _():
            attended_recv[me_t] = attended_ref[rows_of(me_t), :]

        @pl.when(me_t != qb)
        def _():
            attended_copy(qb, me_t).start()

    lines.advance(3, 2)
    lines.advance(4, 2)
    attend(3)
    attend(0)
    lines.advance(3, 3)
    grad_moves.start(2, grads.at[2])
    lines.advance(4, 3)
    attend(2)
    attend(1)
    grad_moves.start(3, grads.at[3])
    loads.put(0, 1, 2, 7)
    spread.finish()
    for block in range(n_dp):
        out_matrix[:, block * out_cols : (block + 1) * out_cols] = outs[block].reshape(
            width, out_cols
        )
    weight_own_ref[...] = out_matrix[
        pl.ds(pl.multiple_of(me_t * head_cols, head_cols), head_cols), :
    ]
    for step in range(1, n_tensor):
        attended_copy(me_t, lax.rem(me_t + step, n_tensor)).wait_recv()
    residual = tokens_ref[...].astype(F32)
    for block in range(n_tensor):
        residual += nn(
            attended_recv[block], out_matrix[block * head_cols : (block + 1) * head_cols, :]
        )
    residual_ref[...] = residual
    hidden = (
        residual
        * lax.rsqrt(jnp.mean(residual * residual, axis=1, keepdims=True) + EPS)
        * gains_ref[1:2, :]
    ).astype(BF16)
    hidden_two_ref[...] = hidden
    for j in range(ROW_PARTS):
        everyone[j, me_t] = hidden[:, j * row_part : (j + 1) * row_part]
    loads.put(9, 10, 11)
    late = Streams(n_tensor, [everyone.at[j] for j in range(ROW_PARTS)], late_send, late_recv)
    row_moves = Dispatch(n_dp, picks, row_stage, rows_ref, row_send, row_recv, row_own)

    def used(j, k):
        if k < n_tensor - 1:
            return
        row_moves.start(j, everyone.at[j])
        term = nt(
            router_ref[:, j * row_part : (j + 1) * row_part], everyone[j].reshape(seq_len, row_part)
        )
        if j == 0:
            logits[...] = term
        else:
            logits[...] += term

    for turn in late.turns():
        late.turn(turn, used)
    values = logits[...]
    exps = jnp.exp(values - jnp.max(values, axis=0, keepdims=True))
    probs = exps / jnp.sum(exps, axis=0, keepdims=True)
    named = (ids == routes_ref[0:1, :]) | (ids == routes_ref[1:2, :])
    shares = probs / jnp.sum(jnp.where(named, probs, 0.0), axis=0, keepdims=True)
    logits[...] = shares

    def gate_copy(target, sender):
        return remote(
            gate_stage.at[target],
            gates_ref.at[sender],
            gate_send.at[target],
            gate_recv.at[sender],
            "dp",
            target,
        )

    def gate(index, _):
        mask = n_dp - 1 - index
        target = me ^ mask
        for expert in range(local):
            row = jnp.sum(
                jnp.where(ids == target * local + expert, logits[...], 0.0), axis=0, keepdims=True
            )
            high = row.astype(BF16)
            rest = row - high.astype(F32)
            mid = rest.astype(BF16)
            low = (rest - mid.astype(F32)).astype(BF16)
            lanes = slice(expert * capacity, (expert + 1) * capacity)
            pieces = nt(
                jnp.concatenate([high, mid, low, jnp.zeros((5, seq_len), BF16)], axis=0),
                picks[target, lanes, :],
            )
            gate_stage[target, :, lanes] = jnp.broadcast_to(
                jnp.sum(pieces, axis=0, keepdims=True), (8, capacity)
            )

        @pl.when(mask != 0)
        def _():
            gate_copy(target, me).start()

        @pl.when(mask == 0)
        def _():
            gates_ref[target] = gate_stage[target]

        return 0

    lax.fori_loop(0, n_dp, gate, 0)
    lines.drain()
    late.drain()
    weights.drain()
    spread.drain()
    for copy in along:
        copy.wait_send()
    for step in range(1, n_tensor):
        attended_copy(lax.rem(me_t + step, n_tensor), me_t).wait_send()
    for step in range(1, n_dp):
        peer = lax.rem(me + step, n_dp)
        gate_copy(peer, me).wait_send()
        gate_copy(me, peer).wait_recv()
    grad_moves.finish()
    row_moves.finish()


def opening(
    n_dp,
    n_tensor,
    experts,
    capacity,
    tokens,
    cotangent,
    weight,
    extra,
    out,
    routes,
    segments,
    selectors,
):
    own_rows, width = tokens.shape
    seq_len = own_rows * n_tensor
    depth, cols = weight.shape
    per = experts // n_dp * capacity
    part = width // PARTS
    row_part = width // ROW_PARTS
    heads = cols // (3 * HD)
    dma = pltpu.SemaphoreType.DMA
    rows = jax.ShapeDtypeStruct((n_dp, per, width), BF16)
    args = (tokens, cotangent, weight, extra, out, routes, segments, selectors)
    which, which_out = (0, 1, 2, 4), (0, 1, 2, 7, 9, 10, 11)
    shapes = (
            jax.ShapeDtypeStruct((n_tensor, own_rows, width), BF16),
            jax.ShapeDtypeStruct((seq_len, cols), BF16),
            jax.ShapeDtypeStruct((n_dp, depth, cols), BF16),
            jax.ShapeDtypeStruct((2 * heads, 2 * BS), F32),
            jax.ShapeDtypeStruct((experts, width), BF16),
            jax.ShapeDtypeStruct((2, width), F32),
            jax.ShapeDtypeStruct((seq_len, TOP), jnp.int32),
            jax.ShapeDtypeStruct((seq_len, heads * HD), BF16),
            jax.ShapeDtypeStruct((seq_len, heads), F32),
            jax.ShapeDtypeStruct((own_rows, width), F32),
            jax.ShapeDtypeStruct((own_rows, width), BF16),
            jax.ShapeDtypeStruct((heads * HD, width), BF16),
            rows,
            rows,
            jax.ShapeDtypeStruct((n_dp, 8, per), F32),
    )
    specs, buffers = staged_specs(args, which, shapes, which_out)
    return pl.pallas_call(
        staged(
            functools.partial(opening_kernel, n_dp, n_tensor, experts, capacity),
            len(args),
            which,
            len(shapes),
            which_out,
        ),
        out_shape=shapes,
        in_specs=specs,
        out_specs=tuple(
            any_spec() if i in which_out or i in (12, 13) else vspec() for i in range(len(shapes))
        ),
        scratch_shapes=[
            pltpu.VMEM((n_dp,) + extra.shape, BF16),
            pltpu.VMEM((NB, depth), F32),
            pltpu.VMEM((n_dp, n_tensor) + out.shape, BF16),
            pltpu.VMEM((width, width), BF16),
            pltpu.VMEM((PARTS, n_tensor, own_rows, part), BF16),
            pltpu.VMEM((ROW_PARTS, n_tensor, own_rows, row_part), BF16),
            pltpu.VMEM((n_dp, per, seq_len), BF16),
            pltpu.VMEM((PARTS, n_dp, per, part), BF16),
            pltpu.VMEM((ROW_PARTS, n_dp, per, row_part), BF16),
            pltpu.VMEM((heads, 3, BS, BS), F32),
            pltpu.VMEM((8, seq_len), jnp.int32),
            pltpu.VMEM((n_tensor, own_rows, heads * HD), BF16),
            pltpu.VMEM((experts, seq_len), F32),
            pltpu.VMEM((n_dp, 8, per), F32),
        ]
        + parameter_sems(n_dp, n_tensor)
        + [dma((PARTS + 1, 2, n_tensor - 1))] * 2
        + [dma((ROW_PARTS, 2, n_tensor - 1))] * 2
        + [dma((PARTS, n_dp)), dma((PARTS, n_dp)), dma((PARTS,))]
        + [dma((ROW_PARTS, n_dp)), dma((ROW_PARTS, n_dp)), dma((ROW_PARTS,))]
        + [dma((n_dp,))] * 2
        + [dma((n_tensor,))] * 2
        + buffers,
        compiler_params=pltpu.CompilerParams(
            vmem_limit_bytes=VMEM_LIMIT, collective_id=4, has_side_effects=True
        ),
        name="opening",
    )(*args)


def last_kernel(
    n_dp,
    n_tensor,
    experts,
    heads,
    loads,
    qkv_ref,
    attended_ref,
    grad_attended_ref,
    lse_ref,
    segment_ref,
    pattern_ref,
    skew_ref,
    hidden_ref,
    weight_ref,
    branch_ref,
    small_ref,
    weight_own_ref,
    gain_own_ref,
    merged_ref,
    residual_ref,
    grad_residual_ref,
    tokens_ref,
    gain_ref,
    layer_ref,
    grad_tokens_ref,
    grad_weight_ref,
    grad_out_ref,
    small_out_ref,
    bias,
    dk,
    dv,
    sums,
    grad_qkv,
    diag,
    parts,
    mixture,
    grad_hidden,
    mix_send,
    mix_recv,
    line_send,
    line_recv,
    qkv_send,
    qkv_recv,
    out_send,
    out_recv,
    small_send,
    small_recv,
    small_sum,
    gain_recv,
    mix_send_sem,
    mix_recv_sem,
    line_send_sem,
    line_recv_sem,
    qkv_send_sem,
    qkv_recv_sem,
    out_send_sem,
    out_recv_sem,
    small_send_sem,
    small_recv_sem,
    gain_send_sem,
    gain_recv_sem,
):
    own_rows, width = residual_ref.shape
    seq_len = own_rows * n_tensor
    depth = weight_own_ref.shape[0]
    out_cols = grad_out_ref.shape[1]
    me = lax.axis_index("dp")
    me_t = lax.axis_index("tensor")
    greet([("dp", n_dp), ("tensor", n_tensor)], loads)

    def rows_of(block):
        return pl.ds(pl.multiple_of(block * own_rows, own_rows), own_rows)

    mix = LineSum(n_tensor, merged_ref, mix_send, mix_recv, mix_send_sem, mix_recv_sem, mixture)
    line = LineSum(n_tensor, parts, line_send, line_recv, line_send_sem, line_recv_sem, grad_hidden)
    copies = []

    def scatter(source, target, send_sem, recv_sem):
        for step in range(1, n_dp):
            peer = lax.rem(me + step, n_dp)
            copy = remote(
                source.at[peer],
                target.at[step - 1],
                send_sem.at[step - 1],
                recv_sem.at[step - 1],
                "dp",
                peer,
            )
            copy.start()
            copies.append(copy)

    mix.start()
    build_bias(heads, pattern_ref, bias)
    backward_start(dk, dv, sums)
    blocks = seq_len // BS
    for qb in range(blocks):
        backward_rows(
            heads,
            qb,
            max(0, qb - band(seq_len)),
            qkv_ref,
            attended_ref,
            grad_attended_ref,
            lse_ref,
            segment_ref,
            bias,
            grad_qkv,
            dk,
            dv,
            sums,
        )
        if qb == 0:
            for block in range(n_dp):
                cols = slice(block * out_cols, (block + 1) * out_cols)
                out_send[block] = tn(attended_ref[...], branch_ref[:, cols]).astype(BF16)
            scatter(out_send, out_recv, out_send_sem, out_recv_sem)
        if qb >= blocks - 2 and qb - (blocks - 2) < n_tensor - 1:
            mix.step(qb - (blocks - 2))
    backward_end(heads, grad_qkv, dk, dv)
    line.start(lambda block: nt(grad_qkv[rows_of(block), :], weight_ref[...]))
    for k in range(2, n_tensor - 1):
        mix.step(k)
    for block in range(n_dp):
        cols = slice(block * depth, (block + 1) * depth)
        qkv_send[block] = tn(hidden_ref[:, cols], grad_qkv[...]).astype(BF16)
    scatter(qkv_send, qkv_recv, qkv_send_sem, qkv_recv_sem)
    diag[...] = jnp.zeros_like(diag)
    diagonal_sums(heads, sums, diag)
    tables = lax.dot_general(
        skew_ref[...],
        jnp.concatenate([diag[0], diag[1]], axis=1),
        (((1,), (1,)), ((), ())),
        precision=lax.Precision.HIGHEST,
        preferred_element_type=F32,
    )
    far = jnp.sum(diag[2], axis=1, keepdims=True)
    head = lax.broadcasted_iota(jnp.int32, (8, 8), 0)
    lane = lax.broadcasted_iota(jnp.int32, (8, 8), 1)
    far_row = jnp.sum(jnp.where(head == lane, far, 0.0), axis=0, keepdims=True)
    bucket = lax.broadcasted_iota(jnp.int32, (NB, 8), 0)
    tables += jnp.where(bucket == NB - 1, far_row, 0.0)
    rows_each = NB // n_dp
    for block in range(n_dp):
        small_send[block] = small_ref[:, block * depth : (block + 1) * depth]
        small_send[block, experts + 2 : experts + 2 + rows_each, 0:8] = tables[
            block * rows_each : (block + 1) * rows_each, :
        ]
    scatter(small_send, small_recv, small_send_sem, small_recv_sem)
    layer_ref[...] = (residual_ref[...] + mixture[...]).astype(BF16)
    for k in range(n_tensor - 2):
        line.step(k)
    for copy in copies:
        copy.wait_recv()
    small_sum[...] = small_send[me]
    grad_weight_ref[...] = qkv_send[me].astype(F32)
    grad_out_ref[...] = out_send[me].astype(F32)
    for step in range(1, n_dp):
        small_sum[...] += small_recv[step - 1]
        grad_weight_ref[...] += qkv_recv[step - 1].astype(F32)
        grad_out_ref[...] += out_recv[step - 1].astype(F32)
    column = jnp.sum(grad_weight_ref[...] * weight_own_ref[...].astype(F32), axis=1, keepdims=True)
    small_sum[experts + 1 : experts + 2, :] = to_row(column) / gain_own_ref[...]
    gains = []
    for step in range(1, n_tensor):
        peer = lax.rem(me_t + step, n_tensor)
        copy = remote(
            small_sum,
            gain_recv.at[step - 1],
            gain_send_sem.at[step - 1],
            gain_recv_sem.at[step - 1],
            "tensor",
            peer,
        )
        copy.start()
        gains.append(copy)
    line.step(n_tensor - 2)
    x = tokens_ref[...].astype(F32)
    scale = lax.rsqrt(jnp.mean(x * x, axis=1, keepdims=True) + EPS)
    unit = x * scale
    grad_unit = grad_hidden[...] * gain_ref[...]
    grad_tokens_ref[...] = (
        grad_residual_ref[...]
        + scale * (grad_unit - unit * jnp.mean(grad_unit * unit, axis=1, keepdims=True))
    ).astype(BF16)
    mix.drain()
    line.drain()
    for copy in copies:
        copy.wait_send()
    for copy in gains:
        copy.wait()
    small_out_ref[...] = small_sum[...]
    shared = slice(0, experts + 2)
    for step in range(1, n_tensor):
        small_out_ref[shared, :] += gain_recv[step - 1, shared, :]


def last(
    n_dp,
    n_tensor,
    experts,
    heads,
    projected,
    attended,
    grad_attended,
    lse,
    segments,
    patterns,
    skew,
    hidden,
    weight,
    branch,
    small,
    weight_own,
    gain_own,
    merged,
    residual,
    grad_residual,
    tokens,
    gain,
):
    seq_len, width = hidden.shape
    own_rows = seq_len // n_tensor
    depth, cols = weight_own.shape
    out_cols = width // n_dp
    dma = pltpu.SemaphoreType.DMA
    line = [
        pltpu.VMEM((n_tensor - 1, own_rows, width), BF16),
        pltpu.VMEM((n_tensor + 1, own_rows, width), BF16),
    ]
    args = (
        projected,
        attended,
        grad_attended,
        lse,
        segments,
        patterns,
        skew,
        hidden,
        weight,
        branch,
        small,
        weight_own,
        gain_own,
        merged,
        residual,
        grad_residual,
        tokens,
        gain,
    )
    which = (0, 1, 2, 7, 8, 9, 11, 13, 14, 15, 16)
    specs, buffers = staged_specs(args, which)
    return pl.pallas_call(
        staged(functools.partial(last_kernel, n_dp, n_tensor, experts, heads), len(args), which),
        out_shape=(
            jax.ShapeDtypeStruct((own_rows, width), BF16),
            jax.ShapeDtypeStruct((own_rows, width), BF16),
            jax.ShapeDtypeStruct((depth, cols), F32),
            jax.ShapeDtypeStruct((heads * HD, out_cols), F32),
            jax.ShapeDtypeStruct((SMALL, depth), F32),
        ),
        in_specs=specs,
        out_specs=(vspec(),) * 5,
        scratch_shapes=backward_scratch(heads, seq_len)
        + [
            pltpu.VMEM((seq_len, cols), BF16),
            pltpu.VMEM((3, 8, 2 * BS), F32),
        ]
        + [pltpu.VMEM((n_tensor, own_rows, width), BF16)]
        + [pltpu.VMEM((own_rows, width), F32)] * 2
        + line * 2
        + [
            pltpu.VMEM((n_dp, depth, cols), BF16),
            pltpu.VMEM((n_dp - 1, depth, cols), BF16),
            pltpu.VMEM((n_dp, heads * HD, out_cols), BF16),
            pltpu.VMEM((n_dp - 1, heads * HD, out_cols), BF16),
            pltpu.VMEM((n_dp, SMALL, depth), F32),
            pltpu.VMEM((n_dp - 1, SMALL, depth), F32),
            pltpu.VMEM((SMALL, depth), F32),
            pltpu.VMEM((n_tensor - 1, SMALL, depth), F32),
        ]
        + [dma((n_tensor - 1,)), dma((n_tensor + 1,))] * 2
        + [dma((n_dp - 1,))] * 6
        + [dma((n_tensor - 1,))] * 2
        + buffers,
        compiler_params=pltpu.CompilerParams(
            vmem_limit_bytes=VMEM_LIMIT, collective_id=5, has_side_effects=True
        ),
        name="last",
    )(*args)


def deliver_kernel(
    grad_in_ref,
    grad_out_ref,
    layer_in_ref,
    tokens_in_ref,
    weight_in_ref,
    out_in_ref,
    small_ref,
    layer_ref,
    tokens_ref,
    weight_ref,
    out_ref,
    table_ref,
    gain_one_ref,
    gain_two_ref,
    router_ref,
    in_ref,
    down_ref,
    stage_in,
    stage_down,
    wide_in,
    wide_down,
    in_sem,
    down_sem,
    out_sem,
    last_sem,
):
    local, halves = grad_in_ref.shape[:2]
    pieces = [
        (
            grad_in_ref.at[e, g],
            stage_in.at[e, g],
            wide_in.at[e, g],
            in_ref.at[e, g],
            in_sem.at[e, g],
            out_sem.at[e, g],
        )
        for e in range(local)
        for g in range(halves)
    ] + [
        (
            grad_out_ref.at[e],
            stage_down.at[e],
            wide_down.at[e],
            down_ref.at[e],
            down_sem.at[e],
            last_sem.at[e],
        )
        for e in range(local)
    ]
    for source, stage, _, _, sem, _ in pieces:
        pltpu.make_async_copy(source, stage, sem).start()
    layer_ref[...] = layer_in_ref[...]
    tokens_ref[...] = tokens_in_ref[...]
    cols = weight_ref.shape[2]
    for part in range(3):
        weight_ref[part] = weight_in_ref[:, part * cols : (part + 1) * cols]
    out_ref[...] = out_in_ref[...]
    experts = router_ref.shape[0]
    router_ref[...] = small_ref[0:experts, :]
    gain_two_ref[...] = small_ref[experts : experts + 1, :]
    gain_one_ref[...] = small_ref[experts + 1 : experts + 2, :]
    table_ref[...] = small_ref[
        experts + 2 : experts + 2 + table_ref.shape[0], 0 : table_ref.shape[1]
    ]
    for source, stage, wide, target, sem, done in pieces:
        pltpu.make_async_copy(source, stage, sem).wait()
        wide[...] = stage[...].astype(F32)
        pltpu.make_async_copy(wide, target, done).start()
    for _, _, wide, target, _, done in pieces:
        pltpu.make_async_copy(wide, target, done).wait()


def deliver(experts, heads, table_rows, grad_in, grad_out, layer, tokens, weight, out, small):
    depth, cols = weight.shape
    local, halves = grad_in.shape[:2]
    dma = pltpu.SemaphoreType.DMA
    return pl.pallas_call(
        deliver_kernel,
        out_shape=(
            jax.ShapeDtypeStruct(layer.shape, BF16),
            jax.ShapeDtypeStruct(tokens.shape, BF16),
            jax.ShapeDtypeStruct((3, depth, cols // 3), F32),
            jax.ShapeDtypeStruct(out.shape, F32),
            jax.ShapeDtypeStruct((table_rows, heads), F32),
            jax.ShapeDtypeStruct((1, depth), F32),
            jax.ShapeDtypeStruct((1, depth), F32),
            jax.ShapeDtypeStruct((experts, depth), F32),
            jax.ShapeDtypeStruct(grad_in.shape, F32),
            jax.ShapeDtypeStruct(grad_out.shape, F32),
        ),
        in_specs=[any_spec()] * 2 + [vspec()] * 5,
        out_specs=(vspec(),) * 8 + (any_spec(),) * 2,
        scratch_shapes=[
            pltpu.VMEM(grad_in.shape, grad_in.dtype),
            pltpu.VMEM(grad_out.shape, grad_out.dtype),
            pltpu.VMEM(grad_in.shape, F32),
            pltpu.VMEM(grad_out.shape, F32),
            dma((local, halves)),
            dma((local,)),
            dma((local, halves)),
            dma((local,)),
        ],
        compiler_params=pltpu.CompilerParams(vmem_limit_bytes=VMEM_LIMIT),
        name="deliver",
    )(grad_in, grad_out, layer, tokens, weight, out, small)


def rms_scale(values):
    return lax.rsqrt(jnp.mean(values * values, axis=-1, keepdims=True) + EPS)


def norm_backward(grad_normed, values, scale_inv, gain):
    normed_unit = values * scale_inv
    grad_unit = grad_normed * gain
    grad_values = scale_inv * (
        grad_unit - normed_unit * jnp.mean(grad_unit * normed_unit, axis=-1, keepdims=True)
    )
    return (grad_values, jnp.sum(grad_normed * normed_unit, axis=0))


def gelu_tanh(values):
    return jax.nn.gelu(values, approximate=True)


def route_slots(route_ids, experts, capacity):
    flat_routes = route_ids.reshape(-1)
    onehot = (flat_routes[:, None] == jnp.arange(experts, dtype=jnp.int32)[None, :]).astype(
        jnp.int32
    )
    ranks = jnp.cumsum(onehot, axis=0) - 1
    rank_own = jnp.sum(ranks * onehot, axis=1)
    return (flat_routes * capacity + rank_own).reshape(-1, TOP)


def on_device(
    tokens,
    segments,
    routes,
    w_qkv,
    w_attn_out,
    bias_table,
    gain_attn,
    gain_moe,
    router,
    w_in,
    w_out,
    cotangent,
):
    own_rows, model_width = tokens.shape
    n_tensor = lax.axis_size("tensor")
    n_dp = lax.axis_size("dp")
    seq_len = own_rows * n_tensor
    own_start = lax.axis_index("tensor") * own_rows
    head_cols = w_qkv.shape[2]
    heads = head_cols // HD
    experts = router.shape[1]
    local_experts = w_in.shape[0]
    capacity = 5 * seq_len * TOP // (4 * experts)
    highest = lax.Precision.HIGHEST
    slots = experts * capacity

    depth = w_qkv.shape[0]
    bias_rows = NB // n_dp
    lanes = depth
    extra = jnp.concatenate(
        [
            jnp.transpose(router),
            gain_attn[None],
            gain_moe[None],
            jnp.pad(bias_table, ((0, SMALL - experts - 2 - bias_rows), (0, lanes - heads))),
        ],
        axis=0,
    )
    fast = n_dp == 8 and n_tensor == 4 and seq_len == 4 * BS and slots * model_width <= 4 * 1024 * 1024
    route_rows = jnp.pad(jnp.transpose(routes), ((0, 8 - TOP), (0, 0)))
    weight_shard = w_qkv.reshape(depth, 3 * head_cols)
    gain_shard = gain_attn[None].astype(F32)
    skew = jnp.asarray(skew_selectors().T)
    selectors = jnp.asarray(distance_selectors().T)

    def finish(layer_out, grad_tokens, reduced_qkv, reduced_attn_out, small_sum, grad_w_in, grad_w_out):
        (
            layer_out,
            grad_tokens,
            grad_w_qkv,
            grad_w_attn_out,
            grad_table,
            grad_gain_one,
            grad_gain_two,
            grad_router,
            grad_w_in,
            grad_w_out,
        ) = deliver(
            experts,
            heads,
            NB // n_dp,
            grad_w_in,
            grad_w_out,
            layer_out,
            grad_tokens,
            reduced_qkv,
            reduced_attn_out,
            small_sum,
        )
        return (
            layer_out,
            grad_tokens,
            jnp.transpose(grad_w_qkv, (1, 0, 2)),
            grad_w_attn_out,
            grad_table,
            grad_gain_one[0],
            grad_gain_two[0],
            jnp.transpose(grad_router),
            grad_w_in,
            grad_w_out,
        )

    if fast:
        (
            gathered,
            projected,
            weights_full,
            patterns,
            router_rows,
            gains,
            slot_columns,
            attended,
            lse,
            residual,
            hidden_two,
            weight_own,
            rows,
            grad_rows,
            row_gates,
        ) = opening(
            n_dp,
            n_tensor,
            experts,
            capacity,
            tokens,
            cotangent,
            weight_shard,
            extra,
            w_attn_out,
            route_rows,
            segments,
            selectors,
        )
        back, gate_back, value, grad_w_in, grad_w_out = run_experts(
            n_dp, capacity, rows, grad_rows, row_gates, w_in, w_out
        )
        grad_residual, grad_branch_all, grad_attended, small, merged = combine(
            n_dp,
            n_tensor,
            experts,
            back.reshape(slots, model_width),
            gate_back,
            slot_columns,
            route_rows,
            residual,
            hidden_two,
            cotangent,
            router_rows,
            gains[1:2],
            weight_own,
            value,
        )
        results = last(
            n_dp,
            n_tensor,
            experts,
            heads,
            projected,
            attended,
            grad_attended,
            lse,
            segments,
            patterns,
            skew,
            gathered.reshape(seq_len, model_width),
            weights_full.reshape(model_width, 3 * head_cols),
            grad_branch_all.reshape(seq_len, model_width),
            small,
            weight_shard,
            gain_shard,
            merged,
            residual,
            grad_residual,
            tokens,
            gains[0:1],
        )
        return finish(*results, grad_w_in, grad_w_out)
    gathered, projected, weights_full, outs_full, patterns, router_rows, gains = front(
        n_dp, n_tensor, experts, tokens, weight_shard, extra, w_attn_out, selectors
    )
    gathered_one = gathered.reshape(seq_len, model_width)
    qkv_matrix = weights_full.reshape(model_width, 3 * head_cols)
    outs_full = outs_full.reshape(n_dp, model_width, model_width // n_dp)
    tokens_float = tokens.astype(F32)
    scale_one = rms_scale(tokens_float)
    gain_one, gain_two = gains[0], gains[1]
    starts = segments[0, ::BS]
    ends = segments[0, BS - 1 :: BS]
    lowest = jnp.sum((ends[None, :] < starts[:, None]).astype(jnp.int32), axis=1)
    attended, lse = attention_forward(projected, lowest, segments, patterns, heads)
    router_full = jnp.transpose(router_rows)
    out_matrix = jnp.transpose(outs_full, (1, 0, 2)).reshape(model_width, model_width)
    attended_own = lax.all_to_all(
        attended.reshape(n_tensor, own_rows, head_cols), "tensor", 0, 0
    )
    attended_own = jnp.transpose(attended_own, (1, 0, 2)).reshape(own_rows, n_tensor * head_cols)
    branch = jnp.dot(attended_own, out_matrix, preferred_element_type=F32)
    residual = tokens_float + branch
    scale_two = rms_scale(residual)
    hidden_two = (residual * scale_two * gain_two).astype(BF16)
    gathered_two = lax.all_gather(hidden_two, "tensor", axis=0, tiled=True)

    expert_ids = jnp.arange(experts, dtype=jnp.int32)

    def gate_values(logit_values, route_rows):
        expert_probs = jax.nn.softmax(logit_values, axis=-1)
        picked = jnp.sum(
            jnp.where(
                route_rows[:, :, None] == expert_ids[None, None, :], expert_probs[:, None, :], 0.0
            ),
            axis=-1,
        )
        return picked / jnp.sum(picked, axis=1, keepdims=True)

    gates = gate_values(jnp.dot(gathered_two, router_full, preferred_element_type=F32), routes)
    slot_ids = route_slots(routes, experts, capacity)
    slot_flat = slot_ids.reshape(-1)
    token_ids = jnp.repeat(jnp.arange(seq_len, dtype=jnp.int32), TOP)
    sources = jnp.full((slots,), seq_len, jnp.int32).at[slot_flat].set(token_ids)
    slot_gates = jnp.zeros((slots,), F32).at[slot_flat].set(gates.reshape(-1))
    grad_gathered = lax.all_gather(cotangent, "tensor", axis=0, tiled=True)

    def exchange(rows):
        parts = rows.reshape(n_dp, local_experts, capacity, model_width)
        return [
            lax.all_to_all(parts[:, i], "dp", 0, 0).reshape(n_dp * capacity, model_width)
            for i in range(local_experts)
        ]

    def give_back(parts):
        back = [
            lax.all_to_all(part.reshape(n_dp, capacity, model_width), "dp", 0, 0) for part in parts
        ]
        return jnp.stack(back, axis=1).reshape(slots, model_width)

    zero_row = jnp.zeros((1, model_width), BF16)
    dispatched = exchange(jnp.concatenate([gathered_two, zero_row], axis=0)[sources])
    padded_grad = jnp.concatenate([grad_gathered, zero_row], axis=0)
    grad_expert = exchange((slot_gates[:, None] * padded_grad[sources]).astype(BF16))

    outs, backs, grads_in, grads_out = [], [], [], []
    for i in range(local_experts):
        rows, grad_rows = dispatched[i], grad_expert[i]
        gate_part = nt(rows, w_in[i, 0])
        up_part = nt(rows, w_in[i, 1])
        gelu_value, gelu_pull = jax.vjp(gelu_tanh, gate_part)
        activated = (gelu_value * up_part).astype(BF16)
        outs.append(nn(activated, w_out[i]).astype(BF16))
        grad_act = nt(grad_rows, w_out[i])
        grads_out.append(tn(activated, grad_rows))
        grad_gate = gelu_pull(grad_act * up_part)[0].astype(BF16)
        grad_up = (grad_act * gelu_value).astype(BF16)
        backs.append((nn(grad_gate, w_in[i, 0]) + nn(grad_up, w_in[i, 1])).astype(BF16))
        grads_in.append(jnp.stack([tn(grad_gate, rows), tn(grad_up, rows)]))
    grad_w_in = jnp.stack(grads_in)
    grad_w_out = jnp.stack(grads_out)
    expert_out = give_back(outs)
    grad_dispatched = give_back(backs)

    first, second = slot_ids[:, 0], slot_ids[:, 1]
    picked_first = expert_out[first].astype(F32)
    picked_second = expert_out[second].astype(F32)
    mixture = lax.psum_scatter(
        (gates[:, 0:1] * picked_first + gates[:, 1:2] * picked_second).astype(BF16),
        "tensor",
        scatter_dimension=0,
        tiled=True,
    ).astype(F32)
    layer_out = (residual + mixture).astype(BF16)
    grad_float = grad_gathered.astype(F32)
    grad_gate_part = jnp.stack(
        [
            jnp.sum(grad_float * picked_first, axis=1),
            jnp.sum(grad_float * picked_second, axis=1),
        ],
        axis=1,
    )
    grad_hidden_part = (
        grad_dispatched[first].astype(F32) + grad_dispatched[second].astype(F32)
    ).astype(BF16)
    grad_own = lax.psum_scatter(
        grad_hidden_part, "tensor", scatter_dimension=0, tiled=True
    ).astype(F32)
    grad_gate_own = lax.dynamic_slice_in_dim(
        lax.psum(grad_gate_part, "tensor"), own_start, own_rows, 0
    )
    own_routes = lax.dynamic_slice_in_dim(routes, own_start, own_rows, 0)
    own_logits = jnp.dot(hidden_two, router_full, preferred_element_type=F32)

    def own_gates(logit_values):
        return gate_values(logit_values, own_routes)

    _, gate_pull = jax.vjp(own_gates, own_logits)
    grad_logits = gate_pull(grad_gate_own)[0]
    router_float = router_full.astype(F32)
    grad_hidden_two = grad_own + jnp.dot(grad_logits, router_float.T, precision=highest)
    grad_router_part = jnp.dot(hidden_two.astype(F32).T, grad_logits, precision=highest)
    grad_from_norm, grad_gain_two = norm_backward(grad_hidden_two, residual, scale_two, gain_two)
    grad_residual = cotangent.astype(F32) + grad_from_norm

    grad_branch = grad_residual.astype(BF16)
    grad_attended_own = nt(grad_branch, out_matrix).astype(BF16)
    grad_attended = lax.all_to_all(
        jnp.transpose(grad_attended_own.reshape(own_rows, n_tensor, head_cols), (1, 0, 2)),
        "tensor",
        0,
        0,
    ).reshape(seq_len, head_cols)
    grad_branch_all = lax.all_gather(grad_branch, "tensor", axis=0, tiled=True)
    small = jnp.concatenate(
        [
            jnp.transpose(grad_router_part),
            grad_gain_two[None],
            jnp.zeros((SMALL - experts - 1, model_width), F32),
        ],
        axis=0,
    )
    grad_projected, diag = attention_backward(
        projected, attended, grad_attended, lse, lowest, segments, patterns, heads
    )
    near = jnp.concatenate([diag[0, :heads], diag[1, :heads]], axis=1)
    grad_table = lax.dot_general(skew, near, (((1,), (1,)), ((), ())), precision=highest)
    grad_table = grad_table.at[NB - 1].add(jnp.sum(diag[2, :heads], axis=1))
    small = jnp.transpose(small.reshape(SMALL, n_dp, depth), (1, 0, 2))
    small = lax.dynamic_update_slice(
        small, grad_table.reshape(n_dp, NB // n_dp, heads), (0, experts + 2, 0)
    )
    grad_hidden_one, reduced_qkv, reduced_attn_out, small_sum = tail(
        n_dp,
        n_tensor,
        experts,
        gathered_one,
        grad_projected,
        qkv_matrix,
        attended,
        grad_branch_all,
        small,
        weight_shard,
        gain_shard,
    )
    grad_from_first, _ = norm_backward(grad_hidden_one, tokens_float, scale_one, gain_one)
    grad_tokens = (grad_residual + grad_from_first).astype(BF16)
    return finish(
        layer_out, grad_tokens, reduced_qkv, reduced_attn_out, small_sum, grad_w_in, grad_w_out
    )


def solution(mesh):
    return jax.shard_map(
        on_device,
        mesh=mesh,
        in_specs=(
            P(("dp", "tensor"), None),
            P("dp", None),
            P("dp", None),
            P("dp", None, "tensor"),
            P("tensor", "dp"),
            P("dp", "tensor"),
            P("dp"),
            P("dp"),
            P("dp", None),
            P("dp", None, "tensor", None),
            P("dp", "tensor", None),
            P(("dp", "tensor"), None),
        ),
        out_specs=(
            P(("dp", "tensor"), None),
            P(("dp", "tensor"), None),
            P("dp", None, "tensor"),
            P("tensor", "dp"),
            P("dp", "tensor"),
            P("dp"),
            P("dp"),
            P("dp", None),
            P("dp", None, "tensor", None),
            P("dp", "tensor", None),
        ),
        check_vma=False,
    )
```

```python
import functools
import math

import jax
import jax.numpy as jnp
import numpy as np
from jax import lax
from jax.experimental import pallas as pl
from jax.experimental.pallas import tpu as pltpu
from jax.sharding import PartitionSpec as P

HD = 64
TOP = 2
NB = 32
NEAR = 128
BS = 256

EPS = 1e-06
NEG = -1e30
F32 = jnp.float32
BF16 = jnp.bfloat16
VMEM_LIMIT = 60 * 1024 * 1024


def distance_buckets():
    half_buckets = NB // 2
    thresholds = [bucket_level for bucket_level in range(1, half_buckets)]
    thresholds = thresholds + [
        int(
            math.ceil(
                half_buckets
                * (NEAR / half_buckets) ** ((bucket_level - half_buckets) / half_buckets)
            )
        )
        for bucket_level in range(half_buckets, NB)
    ]
    distance = np.arange(NEAR + 1)
    return (distance[:, None] >= np.array(thresholds)[None, :]).sum(axis=1)


def distance_selectors():
    buckets = distance_buckets()
    lanes = np.arange(2 * BS)
    signed = np.where(lanes < BS, lanes, lanes - 2 * BS)
    out = []
    for base in (0, BS):
        distance = np.clip(base - signed, 0, NEAR)
        out.append(buckets[distance][:, None] == np.arange(NB)[None, :])
    return np.concatenate(out, axis=0).astype(np.float32)


def skew_selectors():
    buckets = distance_buckets()
    lanes = np.arange(2 * BS)
    out = []
    for base in (0, BS):
        distance = np.clip(base + BS - 1 - lanes, 0, NEAR)
        out.append(buckets[distance][:, None] == np.arange(NB)[None, :])
    return np.concatenate(out, axis=0).astype(np.float32)


def nt(a, b):
    return lax.dot_general(a, b, (((1,), (1,)), ((), ())), preferred_element_type=F32)


def tn(a, b):
    return lax.dot_general(a, b, (((0,), (0,)), ((), ())), preferred_element_type=F32)


def nn(a, b):
    return lax.dot_general(a, b, (((1,), (0,)), ((), ())), preferred_element_type=F32)


def toeplitz(row):
    return pltpu.roll(jnp.broadcast_to(row, (BS, 2 * BS)), 0, 1, stride=1, stride_axis=0)[:, :BS]


def head_lanes(heads, width):
    lane = lax.broadcasted_iota(jnp.int32, (1, width), 1)
    return [(lane >= h * HD) & (lane < (h + 1) * HD) for h in range(heads)]


def own_head(value, lanes, heads):
    return value if heads == 1 else jnp.where(lanes, value, jnp.zeros((), value.dtype))


def build_bias(heads, pattern_ref, bias):
    for h in range(heads):
        for t in range(2):
            bias[h, t] = toeplitz(pattern_ref[2 * h + t : 2 * h + t + 1, :])
        bias[h, 2] = jnp.broadcast_to(pattern_ref[2 * h + 1 : 2 * h + 2, 0:1], (BS, BS))


def block_rows(block):
    if isinstance(block, int):
        return pl.ds(block * BS, BS)
    return pl.ds(pl.multiple_of(block * BS, BS), BS)


def segment_column(qb, segment_ref):
    return to_column(segment_ref[:, block_rows(qb)].astype(F32))


def block_mask(qb, kb, q_segments, segment_ref):
    k_segments = segment_ref[:, block_rows(kb)].astype(F32)
    row = lax.broadcasted_iota(jnp.int32, (BS, BS), 0) + (qb - kb) * BS
    col = lax.broadcasted_iota(jnp.int32, (BS, BS), 1)
    return (q_segments == k_segments) & (row >= col)


def forward_rows(heads, qb, low, qkv_ref, segment_ref, bias, out_ref, lse_ref):
    width = heads * HD
    lanes = head_lanes(heads, width)
    q_rows = block_rows(qb)
    q_all = (qkv_ref[q_rows, 0:width] * HD**-0.5).astype(BF16)
    q_heads = [own_head(q_all, lanes[h], heads) for h in range(heads)]
    q_segments = segment_column(qb, segment_ref)

    def k_step(kb, carry):
        k = qkv_ref[block_rows(kb), width : 2 * width]
        v = qkv_ref[block_rows(kb), 2 * width : 3 * width]
        allowed = block_mask(qb, kb, q_segments, segment_ref)
        place = jnp.minimum(qb - kb, 2)
        new = []
        for h in range(heads):
            top, total, acc = carry[3 * h : 3 * h + 3]
            s = jnp.where(allowed, nt(q_heads[h], k) + bias[h, place], NEG)
            top_new = jnp.maximum(top, jnp.max(s, axis=1, keepdims=True))
            alpha = jnp.exp(top - top_new)
            p = jnp.exp(s - top_new)
            total = alpha * total + jnp.sum(p, axis=1, keepdims=True)
            acc = alpha * acc + nn(p.astype(BF16), v)
            new += [top_new, total, acc]
        return tuple(new)

    init = []
    for h in range(heads):
        init += [jnp.full((BS, 1), NEG, F32), jnp.zeros((BS, 1), F32), jnp.zeros((BS, width), F32)]
    res = lax.fori_loop(low, qb + 1, k_step, tuple(init))
    out = jnp.zeros((BS, width), F32)
    for h in range(heads):
        top, total, acc = res[3 * h : 3 * h + 3]
        value = acc / total
        out = value if heads == 1 else jnp.where(lanes[h], value, out)
        lse_ref[q_rows, h : h + 1] = top + jnp.log(total)
    out_ref[q_rows, :] = out.astype(BF16)


def backward_rows(
    heads, qb, low, qkv_ref, out_ref, grad_ref, lse_ref, segment_ref, bias, grad_qkv_ref, dk, dv, sums
):
    width = heads * HD
    lanes = head_lanes(heads, width)
    scale = HD**-0.5
    q_rows = block_rows(qb)
    q_all = (qkv_ref[q_rows, 0:width] * scale).astype(BF16)
    g_all = grad_ref[q_rows, :]
    both = g_all.astype(F32) * out_ref[q_rows, :].astype(F32)
    q_heads = [own_head(q_all, lanes[h], heads) for h in range(heads)]
    g_heads = [own_head(g_all, lanes[h], heads) for h in range(heads)]
    deltas = [jnp.sum(own_head(both, lanes[h], heads), axis=1, keepdims=True) for h in range(heads)]
    totals = [lse_ref[q_rows, h : h + 1] for h in range(heads)]
    q_segments = segment_column(qb, segment_ref)

    def k_step(kb, dq):
        k_rows = block_rows(kb)
        k = qkv_ref[k_rows, width : 2 * width]
        v = qkv_ref[k_rows, 2 * width : 3 * width]
        allowed = block_mask(qb, kb, q_segments, segment_ref)
        place = jnp.minimum(qb - kb, 2)
        dk_add = jnp.zeros((BS, width), F32)
        dv_add = jnp.zeros((BS, width), F32)
        for h in range(heads):
            s = jnp.where(allowed, nt(q_heads[h], k) + bias[h, place], NEG)
            p = jnp.exp(s - totals[h])
            gp = nt(g_heads[h], v)
            ds = (p * (gp - deltas[h])).astype(BF16)
            dv_add += tn(p.astype(BF16), g_heads[h])
            dk_add += tn(ds, q_heads[h])
            dq = dq + own_head(nn(ds, k), lanes[h], heads)
            sums[h, place] += ds.astype(F32)
        dk[k_rows, :] += dk_add
        dv[k_rows, :] += dv_add
        return dq

    dq = lax.fori_loop(low, qb + 1, k_step, jnp.zeros((BS, width), F32))
    grad_qkv_ref[q_rows, 0:width] = (dq * scale).astype(BF16)


def backward_start(dk, dv, sums):
    dk[...] = jnp.zeros_like(dk)
    dv[...] = jnp.zeros_like(dv)
    sums[...] = jnp.zeros_like(sums)


def backward_end(heads, grad_qkv_ref, dk, dv):
    width = heads * HD
    grad_qkv_ref[:, width : 2 * width] = dk[...].astype(BF16)
    grad_qkv_ref[:, 2 * width : 3 * width] = dv[...].astype(BF16)


def diagonal_sums(heads, sums, diag_ref):
    row = lax.broadcasted_iota(jnp.int32, (BS, BS), 0)
    col = lax.broadcasted_iota(jnp.int32, (BS, BS), 1)
    upside_down = jnp.where(row + col == BS - 1, 1.0, 0.0).astype(F32)
    for h in range(heads):
        for t in range(2):
            flipped = jnp.dot(
                upside_down,
                sums[h, t],
                precision=lax.Precision.HIGHEST,
                preferred_element_type=F32,
            )
            wide = jnp.concatenate([flipped, jnp.zeros((BS, BS), F32)], axis=1)
            skewed = pltpu.roll(wide, 0, 1, stride=1, stride_axis=0)
            diag_ref[t, h : h + 1, :] = jnp.sum(skewed, axis=0, keepdims=True)
        rest = jnp.sum(sums[h, 2], axis=0, keepdims=True)
        diag_ref[2, h : h + 1, :] = jnp.concatenate([rest, jnp.zeros((1, BS), F32)], axis=1)


def attn_fwd_kernel(heads, blocks, lo_ref, qkv_ref, segment_ref, pattern_ref, out_ref, lse_ref, bias):
    build_bias(heads, pattern_ref, bias)

    def q_step(qb, _):
        forward_rows(heads, qb, lo_ref[qb], qkv_ref, segment_ref, bias, out_ref, lse_ref)
        return 0

    lax.fori_loop(0, blocks, q_step, 0)


def attn_bwd_kernel(
    heads,
    blocks,
    lo_ref,
    qkv_ref,
    out_ref,
    grad_ref,
    lse_ref,
    segment_ref,
    pattern_ref,
    grad_qkv_ref,
    diag_ref,
    bias,
    dk,
    dv,
    sums,
):
    build_bias(heads, pattern_ref, bias)
    backward_start(dk, dv, sums)

    def q_step(qb, _):
        backward_rows(
            heads,
            qb,
            lo_ref[qb],
            qkv_ref,
            out_ref,
            grad_ref,
            lse_ref,
            segment_ref,
            bias,
            grad_qkv_ref,
            dk,
            dv,
            sums,
        )
        return 0

    lax.fori_loop(0, blocks, q_step, 0)
    backward_end(heads, grad_qkv_ref, dk, dv)
    diagonal_sums(heads, sums, diag_ref)


def vspec():
    return pl.BlockSpec(memory_space=pltpu.VMEM)


def sspec():
    return pl.BlockSpec(memory_space=pltpu.SMEM)


def attention_forward(projected, lo, segments, patterns, heads):
    seq_len = projected.shape[0]
    blocks = seq_len // BS
    return pl.pallas_call(
        functools.partial(attn_fwd_kernel, heads, blocks),
        out_shape=(
            jax.ShapeDtypeStruct((seq_len, heads * HD), BF16),
            jax.ShapeDtypeStruct((seq_len, heads), F32),
        ),
        in_specs=[sspec(), vspec(), vspec(), vspec()],
        out_specs=(vspec(), vspec()),
        scratch_shapes=[pltpu.VMEM((heads, 3, BS, BS), F32)],
        compiler_params=pltpu.CompilerParams(vmem_limit_bytes=VMEM_LIMIT),
        name="attn_fwd",
    )(lo, projected, segments, patterns)


def attention_backward(projected, attended, grad, lse, lo, segments, patterns, heads):
    seq_len = projected.shape[0]
    blocks = seq_len // BS
    width = heads * HD
    return pl.pallas_call(
        functools.partial(attn_bwd_kernel, heads, blocks),
        out_shape=(
            jax.ShapeDtypeStruct((seq_len, 3 * width), BF16),
            jax.ShapeDtypeStruct((3, 8, 2 * BS), F32),
        ),
        in_specs=[sspec()] + [vspec()] * 6,
        out_specs=(vspec(), vspec()),
        scratch_shapes=backward_scratch(heads, seq_len),
        compiler_params=pltpu.CompilerParams(vmem_limit_bytes=VMEM_LIMIT),
        name="attn_bwd",
    )(lo, projected, attended, grad, lse, segments, patterns)


def backward_scratch(heads, seq_len):
    return [
        pltpu.VMEM((heads, 3, BS, BS), F32),
        pltpu.VMEM((seq_len, heads * HD), F32),
        pltpu.VMEM((seq_len, heads * HD), F32),
        pltpu.VMEM((heads, 3, BS, BS), F32),
    ]


MESH = pl.DeviceIdType.MESH
SMALL = 32


def remote(src, dst, send, recv, axis, peer):
    return pltpu.make_async_remote_copy(
        src_ref=src,
        dst_ref=dst,
        send_sem=send,
        recv_sem=recv,
        device_id={axis: peer},
        device_id_type=MESH,
    )


class Staging:
    def __init__(self):
        self.loads, self.stores, self.flying = [], {}, []

    def wait(self):
        for load in self.loads:
            load.wait()

    def put(self, *indices):
        for index in indices:
            copy = self.stores.pop(index)
            copy.start()
            self.flying.append(copy)

    def close(self):
        self.put(*list(self.stores))
        for copy in self.flying:
            copy.wait()


def staged(kernel, count, which, outs=0, which_out=()):
    extra = len(which) + len(which_out) + 2

    def run(*refs):
        inputs, outputs = list(refs[:count]), list(refs[count : count + outs])
        tail = refs[-extra:]
        buffers, in_sems, out_sems = tail[:-2], tail[-2], tail[-1]
        staging = Staging()
        for place, index in enumerate(which):
            copy = pltpu.make_async_copy(inputs[index], buffers[place], in_sems.at[place])
            copy.start()
            staging.loads.append(copy)
            inputs[index] = buffers[place]
        for place, index in enumerate(which_out):
            buffer = buffers[len(which) + place]
            staging.stores[index] = pltpu.make_async_copy(
                buffer, outputs[index], out_sems.at[place]
            )
            outputs[index] = buffer
        kernel(staging, *inputs, *outputs, *refs[count + outs : -extra])
        staging.close()

    return run


def staged_specs(args, which, shapes=(), which_out=()):
    specs = [any_spec() if i in which else vspec() for i in range(len(args))]
    scratch = [pltpu.VMEM(args[i].shape, args[i].dtype) for i in which]
    scratch += [pltpu.VMEM(shapes[i].shape, shapes[i].dtype) for i in which_out]
    dma = pltpu.SemaphoreType.DMA
    return specs, scratch + [dma((len(which),)), dma((max(1, len(which_out)),))]


def greet(groups, staging=None):
    barrier = pltpu.get_barrier_semaphore()
    total = 0
    for axis, n in groups:
        me = lax.axis_index(axis)
        for step in range(1, n):
            pl.semaphore_signal(
                barrier, inc=1, device_id={axis: lax.rem(me + step, n)}, device_id_type=MESH
            )
        total += n - 1
    pl.semaphore_wait(barrier, total)
    if staging is not None:
        staging.wait()


class LineSum:
    def __init__(self, n, parts, send, recv, send_sem, recv_sem, total):
        self.n, self.parts = n, parts
        self.send, self.recv, self.send_sem, self.recv_sem = send, recv, send_sem, recv_sem
        self.total = total
        self.me = lax.axis_index("tensor")

    def flow(self, first, k):
        n, me = self.n, self.me
        near = me * 2 < n
        right = near if first else jnp.logical_not(near)
        block = jnp.where(right, n - 1 - k, k)
        comes = jnp.where(right, jnp.where(me > 0, me <= block, False), jnp.where(me < n - 1, me >= block, False))
        goes = jnp.where(right, me < block, me > block)
        peer = jnp.clip(jnp.where(right, me + 1, me - 1), 0, n - 1)
        out_slot = jnp.clip(jnp.where(right, k, n - 1 - me + k), 0, n - 2)
        in_slot = jnp.clip(jnp.where(right, k, n - me + k), 0, n)
        peer_slot = jnp.clip(jnp.where(right, k, n - peer + k), 0, n)
        return block, comes, goes, peer, out_slot, in_slot, peer_slot

    def copy(self, peer, out_slot, slot):
        return remote(
            self.send.at[out_slot],
            self.recv.at[slot],
            self.send_sem.at[out_slot],
            self.recv_sem.at[slot],
            "tensor",
            peer,
        )

    def start(self, partial=None):
        n, me = self.n, self.me

        def one(index, _):
            block = jnp.where(me * 2 < n, n - 1 - index, index)
            if partial is not None:
                value = partial(block)
                self.parts[block] = value.astype(BF16)

                @pl.when(block == me)
                def _():
                    self.total[...] = value

            @pl.when(jnp.logical_or(me == 0, me == n - 1) & (index < n - 1))
            def _():
                remote(
                    self.parts.at[block],
                    self.recv.at[jnp.where(me == 0, index, 2 + index)],
                    self.send_sem.at[index],
                    self.recv_sem.at[jnp.where(me == 0, index, 2 + index)],
                    "tensor",
                    jnp.where(me == 0, 1, n - 2),
                ).start()

            return 0

        lax.fori_loop(0, n, one, 0)
        if partial is None:
            self.total[...] = self.parts[me].astype(F32)

    def finish(self):
        for k in range(self.n - 1):
            self.step(k)

    def step(self, k):
        for first in (True, False):
            block, comes, goes, peer, out_slot, in_slot, peer_slot = self.flow(first, k)

            @pl.when(goes & comes)
            def _():
                self.copy(peer, out_slot, in_slot).wait_recv()
                self.send[out_slot] = (
                    self.parts[block].astype(F32) + self.recv[in_slot].astype(F32)
                ).astype(BF16)
                self.copy(peer, out_slot, peer_slot).start()

            @pl.when(comes & jnp.logical_not(goes))
            def _():
                self.copy(peer, 0, in_slot).wait_recv()
                self.total[...] += self.recv[in_slot].astype(F32)

    def drain(self):
        for k in range(self.n - 1):
            for first in (True, False):
                block, comes, goes, peer, out_slot, in_slot, peer_slot = self.flow(first, k)

                @pl.when(goes)
                def _():
                    self.copy(peer, out_slot, in_slot).wait_send()


def tail_kernel(
    n_dp,
    n_tensor,
    experts,
    table_rows,
    hidden_ref,
    grad_ref,
    weight_ref,
    attended_ref,
    branch_ref,
    small_ref,
    weight_own_ref,
    gain_own_ref,
    grad_hidden_ref,
    grad_qkv_ref,
    grad_out_ref,
    small_out_ref,
    parts,
    line_send,
    line_recv,
    qkv_send,
    qkv_recv,
    out_send,
    out_recv,
    small_recv,
    small_sum,
    gain_recv,
    line_send_sem,
    line_recv_sem,
    qkv_send_sem,
    qkv_recv_sem,
    out_send_sem,
    out_recv_sem,
    small_send_sem,
    small_recv_sem,
    gain_send_sem,
    gain_recv_sem,
):
    own_rows = grad_hidden_ref.shape[0]
    depth = weight_own_ref.shape[0]
    out_cols = grad_out_ref.shape[1]
    me = lax.axis_index("dp")
    me_t = lax.axis_index("tensor")
    greet([("dp", n_dp), ("tensor", n_tensor)])

    def partial(block):
        rows = pl.ds(pl.multiple_of(block * own_rows, own_rows), own_rows)
        return nt(grad_ref[rows, :], weight_ref[...])

    line = LineSum(
        n_tensor, parts, line_send, line_recv, line_send_sem, line_recv_sem, grad_hidden_ref
    )
    line.start(partial)
    copies = []
    for step in range(1, n_dp):
        peer = lax.rem(me + step, n_dp)
        copy = remote(
            small_ref.at[peer],
            small_recv.at[step - 1],
            small_send_sem.at[step - 1],
            small_recv_sem.at[step - 1],
            "dp",
            peer,
        )
        copy.start()
        copies.append(copy)
    for block in range(n_dp):
        cols = slice(block * depth, (block + 1) * depth)
        qkv_send[block] = tn(hidden_ref[:, cols], grad_ref[...]).astype(BF16)
    for step in range(1, n_dp):
        peer = lax.rem(me + step, n_dp)
        copy = remote(
            qkv_send.at[peer],
            qkv_recv.at[step - 1],
            qkv_send_sem.at[step - 1],
            qkv_recv_sem.at[step - 1],
            "dp",
            peer,
        )
        copy.start()
        copies.append(copy)
    for block in range(n_dp):
        cols = slice(block * out_cols, (block + 1) * out_cols)
        out_send[block] = tn(attended_ref[...], branch_ref[:, cols]).astype(BF16)
    for step in range(1, n_dp):
        peer = lax.rem(me + step, n_dp)
        copy = remote(
            out_send.at[peer],
            out_recv.at[step - 1],
            out_send_sem.at[step - 1],
            out_recv_sem.at[step - 1],
            "dp",
            peer,
        )
        copy.start()
        copies.append(copy)
    line.finish()
    for copy in copies:
        copy.wait()
    small_sum[...] = small_ref[me]
    grad_qkv_ref[...] = qkv_send[me].astype(F32)
    grad_out_ref[...] = out_send[me].astype(F32)
    for step in range(1, n_dp):
        small_sum[...] += small_recv[step - 1]
        grad_qkv_ref[...] += qkv_recv[step - 1].astype(F32)
        grad_out_ref[...] += out_recv[step - 1].astype(F32)
    column = jnp.sum(grad_qkv_ref[...] * weight_own_ref[...].astype(F32), axis=1, keepdims=True)
    eye = lax.broadcasted_iota(jnp.int32, (depth, depth), 0) == lax.broadcasted_iota(
        jnp.int32, (depth, depth), 1
    )
    row = jnp.sum(jnp.where(eye, column, 0.0), axis=0, keepdims=True)
    small_sum[experts + 1 : experts + 2, :] = row / gain_own_ref[...]
    gains = []
    for step in range(1, n_tensor):
        peer = lax.rem(me_t + step, n_tensor)
        copy = remote(
            small_sum,
            gain_recv.at[step - 1],
            gain_send_sem.at[step - 1],
            gain_recv_sem.at[step - 1],
            "tensor",
            peer,
        )
        copy.start()
        gains.append(copy)
    line.drain()
    for copy in gains:
        copy.wait()
    small_out_ref[...] = small_sum[...]
    shared = slice(0, experts + 2)
    for step in range(1, n_tensor):
        small_out_ref[shared, :] += gain_recv[step - 1, shared, :]


def tail(n_dp, n_tensor, experts, hidden, grad, weight, attended, branch, small, weight_own, gain_own):
    seq_len, width = hidden.shape
    own_rows = seq_len // n_tensor
    depth, cols = weight_own.shape
    heads_cols = attended.shape[1]
    out_cols = width // n_dp
    table_rows = NB // n_dp
    return pl.pallas_call(
        functools.partial(tail_kernel, n_dp, n_tensor, experts, table_rows),
        out_shape=(
            jax.ShapeDtypeStruct((own_rows, width), F32),
            jax.ShapeDtypeStruct((depth, cols), F32),
            jax.ShapeDtypeStruct((heads_cols, out_cols), F32),
            jax.ShapeDtypeStruct((SMALL, depth), F32),
        ),
        in_specs=[vspec()] * 8,
        out_specs=(vspec(),) * 4,
        scratch_shapes=[
            pltpu.VMEM((n_tensor, own_rows, width), BF16),
            pltpu.VMEM((n_tensor - 1, own_rows, width), BF16),
            pltpu.VMEM((n_tensor + 1, own_rows, width), BF16),
            pltpu.VMEM((n_dp, depth, cols), BF16),
            pltpu.VMEM((n_dp - 1, depth, cols), BF16),
            pltpu.VMEM((n_dp, heads_cols, out_cols), BF16),
            pltpu.VMEM((n_dp - 1, heads_cols, out_cols), BF16),
            pltpu.VMEM((n_dp - 1, SMALL, depth), F32),
            pltpu.VMEM((SMALL, depth), F32),
            pltpu.VMEM((n_tensor - 1, SMALL, depth), F32),
            pltpu.SemaphoreType.DMA((n_tensor - 1,)),
            pltpu.SemaphoreType.DMA((n_tensor + 1,)),
        ]
        + [pltpu.SemaphoreType.DMA((n_dp - 1,))] * 6
        + [pltpu.SemaphoreType.DMA((n_tensor - 1,))] * 2,
        compiler_params=pltpu.CompilerParams(
            vmem_limit_bytes=VMEM_LIMIT, collective_id=0, has_side_effects=True
        ),
        name="tail",
    )(hidden, grad, weight, attended, branch, small, weight_own, gain_own)


def diagonal(size):
    return lax.broadcasted_iota(jnp.int32, (size, size), 0) == lax.broadcasted_iota(
        jnp.int32, (size, size), 1
    )


def to_column(row):
    return jnp.sum(jnp.where(diagonal(row.shape[1]), row, 0.0), axis=1, keepdims=True)


def to_row(column):
    return jnp.sum(jnp.where(diagonal(column.shape[0]), column, 0.0), axis=0, keepdims=True)


def expert_kernel(
    n_dp,
    local,
    capacity,
    rows_hbm,
    grad_hbm,
    gates_ref,
    in_hbm,
    out_hbm,
    back_ref,
    gate_back_ref,
    value_ref,
    grad_in_ref,
    grad_out_ref,
    back_send,
    gate_send,
    zs,
    ups,
    gates_s,
    stage,
    value_stage,
    back_send_sem,
    back_recv_sem,
    gate_send_sem,
    gate_recv_sem,
    own_sem,
    stage_sem,
    value_sem,
    rows_ref,
    grad_ref,
    in_ref,
    out_ref,
    rows_sem,
    grad_sem,
    in_sem,
    out_sem,
):
    me = lax.axis_index("dp")
    pairs = n_dp // 2
    hidden = in_ref.shape[2]
    width = rows_ref.shape[2]
    two = 2 * capacity

    def pair_at(index):
        return (me // 2) ^ (pairs - 1 - index)

    def load_pair(index):
        where = pl.ds(2 * pair_at(index), 2)
        return (
            pltpu.make_async_copy(rows_hbm.at[where], rows_ref.at[where], rows_sem.at[index]),
            pltpu.make_async_copy(grad_hbm.at[where], grad_ref.at[where], grad_sem.at[index]),
        )

    def load_expert(expert):
        return (
            pltpu.make_async_copy(in_hbm.at[expert], in_ref.at[expert], in_sem.at[expert]),
            pltpu.make_async_copy(out_hbm.at[expert], out_ref.at[expert], out_sem.at[expert]),
        )

    for copy in load_expert(0) + load_pair(0):
        copy.start()
    for index in range(1, pairs):
        for copy in load_pair(index):
            copy.start()
    for expert in range(1, local):
        for copy in load_expert(expert):
            copy.start()
    greet([("dp", n_dp)])

    def back_copy(expert, target, sender):
        part = slice(expert * capacity, (expert + 1) * capacity)
        return remote(
            back_send.at[target, part],
            back_ref.at[sender, part],
            back_send_sem.at[expert, target],
            back_recv_sem.at[expert, sender],
            "dp",
            target,
        )

    def own_copy(expert):
        part = slice(expert * capacity, (expert + 1) * capacity)
        return pltpu.make_async_copy(
            back_send.at[me, part], back_ref.at[me, part], own_sem.at[expert]
        )

    def stage_copy(slot, target):
        return pltpu.make_async_copy(stage.at[slot], target, stage_sem.at[slot])

    gate_send[...] = jnp.zeros_like(gate_send)
    staged = []

    def put(value, target):
        slot = len(staged) % 2
        if len(staged) >= 2:
            staged[-2].wait()
        stage[slot] = value.astype(BF16)
        copy = stage_copy(slot, target)
        copy.start()
        staged.append(copy)

    for expert in range(local):
        part = slice(expert * capacity, (expert + 1) * capacity)

        for copy in load_expert(expert):
            copy.wait()

        def group(index, _):
            if expert == 0:
                for copy in load_pair(index):
                    copy.wait()
            first = 2 * pair_at(index)
            rows = rows_ref[pl.ds(first, 2), part, :].reshape(two, width)
            grads = grad_ref[pl.ds(first, 2), part, :].reshape(two, width)
            column = jnp.concatenate(
                [to_column(gates_ref[first + j, 0:1, part]) for j in range(2)], axis=0
            )
            gate = nt(rows, in_ref[expert, 0])
            up = nt(rows, in_ref[expert, 1])
            square = gate * gate
            bent = jnp.tanh(0.7978845608028654 * gate * (1.0 + 0.044715 * square))
            half = 0.5 * (1.0 + bent)
            gelu = gate * half
            slope = half + 0.5 * gate * (1.0 - bent * bent) * (
                0.7978845608028654 * (1.0 + 3 * 0.044715 * square)
            )
            z = gelu * up
            grad_z = nt(grads, out_ref[expert])
            gate_grad = jnp.sum(z * grad_z, axis=1, keepdims=True)
            grad_z = column * grad_z
            zs[pl.ds(first, 2)] = (column * z).astype(BF16).reshape(2, capacity, hidden)
            ups[0, pl.ds(first, 2)] = (grad_z * up * slope).astype(BF16).reshape(2, capacity, hidden)
            ups[1, pl.ds(first, 2)] = (grad_z * gelu).astype(BF16).reshape(2, capacity, hidden)
            for j in range(2):
                gate_send[first + j, 0:1, part] = to_row(
                    gate_grad[j * capacity : (j + 1) * capacity]
                )
            back = nn(ups[0, pl.ds(first, 2)].reshape(two, hidden), in_ref[expert, 0])
            back += nn(ups[1, pl.ds(first, 2)].reshape(two, hidden), in_ref[expert, 1])
            back_send[pl.ds(first, 2), part, :] = back.astype(BF16).reshape(2, capacity, width)
            for j in range(2):
                target = first + j

                @pl.when(target != me)
                def _():
                    back_copy(expert, target, me).start()

                @pl.when(target == me)
                def _():
                    own_copy(expert).start()

            return 0

        lax.fori_loop(0, pairs, group, 0)
        if expert == local - 1:
            gate_copies = []
            for step in range(1, n_dp):
                target = lax.rem(me + step, n_dp)
                copy = remote(
                    gate_send.at[target],
                    gate_back_ref.at[me],
                    gate_send_sem.at[step - 1],
                    gate_recv_sem.at[step - 1],
                    "dp",
                    target,
                )
                copy.start()
                gate_copies.append(copy)
            gate_back_ref[me] = gate_send[me]
        rows = rows_ref[:, part, :].reshape(n_dp * capacity, width)
        for half in range(2):
            put(tn(ups[half].reshape(n_dp * capacity, hidden), rows), grad_in_ref.at[expert, half])
        grads = grad_ref[:, part, :].reshape(n_dp * capacity, width)
        put(tn(zs[...].reshape(n_dp * capacity, hidden), grads), grad_out_ref.at[expert])
        if expert > 0:
            pltpu.make_async_copy(
                value_stage, value_ref.at[:, slice((expert - 1) * capacity, expert * capacity)], value_sem
            ).wait()

        def value(pair, _):
            out = nn(zs[pl.ds(2 * pair, 2)].reshape(two, hidden), out_ref[expert])
            value_stage[pl.ds(2 * pair, 2)] = out.astype(BF16).reshape(2, capacity, width)
            return 0

        lax.fori_loop(0, pairs, value, 0)
        pltpu.make_async_copy(value_stage, value_ref.at[:, part], value_sem).start()

    last = slice((local - 1) * capacity, local * capacity)
    pltpu.make_async_copy(value_stage, value_ref.at[:, last], value_sem).wait()
    for copy in staged[-2:]:
        copy.wait()
    for copy in gate_copies:
        copy.wait()
    for expert in range(local):
        own_copy(expert).wait()
        for step in range(1, n_dp):
            peer = lax.rem(me + step, n_dp)
            back_copy(expert, peer, me).wait_send()
            back_copy(expert, me, peer).wait_recv()


def any_spec():
    return pl.BlockSpec(memory_space=pl.ANY)


def run_experts(n_dp, capacity, rows, grads, gates, w_in, w_out):
    local, _, hidden, width = w_in.shape
    slots = local * capacity
    return pl.pallas_call(
        functools.partial(expert_kernel, n_dp, local, capacity),
        out_shape=(
            jax.ShapeDtypeStruct((n_dp, slots, width), BF16),
            jax.ShapeDtypeStruct((n_dp, 8, slots), F32),
            jax.ShapeDtypeStruct((n_dp, slots, width), BF16),
            jax.ShapeDtypeStruct(w_in.shape, BF16),
            jax.ShapeDtypeStruct(w_out.shape, BF16),
        ),
        in_specs=[any_spec(), any_spec(), vspec(), any_spec(), any_spec()],
        out_specs=(any_spec(), vspec(), any_spec(), any_spec(), any_spec()),
        scratch_shapes=[
            pltpu.VMEM((n_dp, slots, width), BF16),
            pltpu.VMEM((n_dp, 8, slots), F32),
            pltpu.VMEM((n_dp, capacity, hidden), BF16),
            pltpu.VMEM((2, n_dp, capacity, hidden), BF16),
            pltpu.VMEM((8, 128), F32),
            pltpu.VMEM((2, hidden, width), BF16),
            pltpu.VMEM((n_dp, capacity, width), BF16),
            pltpu.SemaphoreType.DMA((local, n_dp)),
            pltpu.SemaphoreType.DMA((local, n_dp)),
            pltpu.SemaphoreType.DMA((n_dp - 1,)),
            pltpu.SemaphoreType.DMA((n_dp - 1,)),
            pltpu.SemaphoreType.DMA((local,)),
            pltpu.SemaphoreType.DMA((2,)),
            pltpu.SemaphoreType.DMA,
            pltpu.VMEM(rows.shape, BF16),
            pltpu.VMEM(grads.shape, BF16),
            pltpu.VMEM(w_in.shape, BF16),
            pltpu.VMEM(w_out.shape, BF16),
            pltpu.SemaphoreType.DMA((n_dp // 2,)),
            pltpu.SemaphoreType.DMA((n_dp // 2,)),
            pltpu.SemaphoreType.DMA((local,)),
            pltpu.SemaphoreType.DMA((local,)),
        ],
        compiler_params=pltpu.CompilerParams(
            vmem_limit_bytes=VMEM_LIMIT, collective_id=1, has_side_effects=True
        ),
        name="experts",
    )(rows, grads, gates, w_in, w_out)


def chosen_slots(columns, slots):
    lane = lax.broadcasted_iota(jnp.int32, (1, slots), 1)
    return columns[:, 0:1] == lane, columns[:, 1:2] == lane


def combine_kernel(
    n_dp,
    n_tensor,
    experts,
    loads,
    rows_ref,
    gate_ref,
    slots_ref,
    routes_ref,
    residual_ref,
    hidden_ref,
    cotangent_ref,
    router_ref,
    gain_ref,
    weight_ref,
    value_ref,
    grad_residual_ref,
    branch_ref,
    grad_attended_ref,
    small_ref,
    merged_ref,
    parts,
    total,
    line_send,
    line_recv,
    gate_all,
    gate_send,
    gate_recv,
    value_back,
    line_send_sem,
    line_recv_sem,
    gate_send_sem,
    gate_recv_sem,
    value_send_sem,
    value_recv_sem,
    value_own_sem,
    gather_send_sem,
    gather_recv_sem,
):
    own_rows, width = residual_ref.shape
    slots = rows_ref.shape[0]
    per = slots // n_dp
    me = lax.axis_index("dp")
    me_t = lax.axis_index("tensor")
    greet([("dp", n_dp), ("tensor", n_tensor)], loads)
    values = []
    for step in range(1, n_dp):
        peer = lax.rem(me + step, n_dp)
        copy = remote(
            value_ref.at[peer],
            value_back.at[me],
            value_send_sem.at[step - 1],
            value_recv_sem.at[step - 1],
            "dp",
            peer,
        )
        copy.start()
        values.append(copy)
    fetch = pltpu.make_async_copy(value_ref.at[me], value_back.at[me], value_own_sem)
    fetch.start()

    def partial(block):
        one, two = chosen_slots(
            slots_ref[pl.ds(pl.multiple_of(block * own_rows, own_rows), own_rows), :], slots
        )
        return nn(jnp.where(one | two, 1.0, 0.0).astype(BF16), rows_ref[...])

    line = LineSum(n_tensor, parts, line_send, line_recv, line_send_sem, line_recv_sem, total)
    line.start(partial)
    for peer in range(n_dp):
        gate_all[0:1, peer * per : (peer + 1) * per] = gate_ref[peer, 0:1, :]
    gate_send[...] = jnp.zeros_like(gate_send)
    gates = []
    for step in range(n_tensor):
        peer = lax.rem(me_t + step, n_tensor)
        picks = chosen_slots(
            slots_ref[pl.ds(pl.multiple_of(peer * own_rows, own_rows), own_rows), :], slots
        )
        for k in range(TOP):
            column = jnp.sum(
                jnp.where(picks[k], gate_all[0:1, :], 0.0), axis=1, keepdims=True
            )
            gate_send[step, k : k + 1, :] = to_row(column)
        if step:
            copy = remote(
                gate_send.at[step],
                gate_recv.at[step - 1],
                gate_send_sem.at[step - 1],
                gate_recv_sem.at[step - 1],
                "tensor",
                peer,
            )
            copy.start()
            gates.append(copy)
    hidden = hidden_ref[...]
    router = router_ref[...]
    logits = nt(router, hidden)
    exps = jnp.exp(logits - jnp.max(logits, axis=0, keepdims=True))
    probs = exps / jnp.sum(exps, axis=0, keepdims=True)
    ids = lax.broadcasted_iota(jnp.int32, (experts, own_rows), 0)
    own_lanes = pl.ds(pl.multiple_of(me_t * own_rows, own_rows), own_rows)
    first, second = ids == routes_ref[0:1, own_lanes], ids == routes_ref[1:2, own_lanes]
    prob_one = jnp.sum(jnp.where(first, probs, 0.0), axis=0, keepdims=True)
    prob_two = jnp.sum(jnp.where(second, probs, 0.0), axis=0, keepdims=True)
    both = prob_one + prob_two
    line.finish()
    for copy in gates:
        copy.wait()
    gate_sum = gate_send[0]
    for step in range(1, n_tensor):
        gate_sum = gate_sum + gate_recv[step - 1]
    grad_one, grad_two = gate_sum[0:1, :], gate_sum[1:2, :]
    mean_grad = (prob_one * grad_one + prob_two * grad_two) / both
    grad_probs = (
        jnp.where(first, grad_one - mean_grad, 0.0) + jnp.where(second, grad_two - mean_grad, 0.0)
    ) / both
    grad_logits = probs * (grad_probs - jnp.sum(grad_probs * probs, axis=0, keepdims=True))
    grad_hidden = total[...] + lax.dot_general(
        grad_logits,
        router.astype(F32),
        (((0,), (0,)), ((), ())),
        precision=lax.Precision.HIGHEST,
        preferred_element_type=F32,
    )
    residual = residual_ref[...]
    scale = lax.rsqrt(jnp.mean(residual * residual, axis=1, keepdims=True) + EPS)
    unit = residual * scale
    small_ref[...] = jnp.zeros_like(small_ref)
    small_ref[experts : experts + 1, :] = jnp.sum(grad_hidden * unit, axis=0, keepdims=True)
    grad_unit = grad_hidden * gain_ref[1:2, :]
    grad_residual = cotangent_ref[...].astype(F32) + scale * (
        grad_unit - unit * jnp.mean(grad_unit * unit, axis=1, keepdims=True)
    )
    grad_residual_ref[...] = grad_residual
    loads.put(0)
    branch_ref[me_t] = grad_residual.astype(BF16)

    def on_block(block):
        grad_attended_ref[pl.ds(pl.multiple_of(block * own_rows, own_rows), own_rows), :] = nt(
            branch_ref[block], weight_ref[...]
        ).astype(BF16)

    lines = Streams(n_tensor, [branch_ref], gather_send_sem, gather_recv_sem)
    for turn in lines.turns():
        lines.turn(turn, lambda j, k: lines.each_new(j, k, on_block))
        if turn == n_tensor - 2:
            fetch.wait()
            for copy in values:
                copy.wait_recv()

            def merge(block, _):
                rows = pl.ds(pl.multiple_of(block * own_rows, own_rows), own_rows)
                one, two = chosen_slots(slots_ref[rows, :], slots)
                merged_ref[block] = nn(
                    jnp.where(one | two, 1.0, 0.0).astype(BF16), value_back[...].reshape(slots, width)
                ).astype(BF16)
                return 0

            lax.fori_loop(0, n_tensor, merge, 0)
            loads.put(4)
    loads.put(1, 2)
    lines.drain()
    small_ref[0:experts, :] = jnp.dot(
        grad_logits,
        hidden.astype(F32),
        precision=lax.Precision.HIGHEST,
        preferred_element_type=F32,
    )
    line.drain()
    for copy in values:
        copy.wait_send()


def combine(
    n_dp,
    n_tensor,
    experts,
    rows,
    gates,
    slot_columns,
    routes_own,
    residual,
    hidden,
    cotangent,
    router_rows,
    gain,
    weight,
    value,
):
    own_rows, width = residual.shape
    slots = rows.shape[0]
    args = (
        rows,
        gates,
        slot_columns,
        routes_own,
        residual,
        hidden,
        cotangent,
        router_rows,
        gain,
        weight,
        value,
    )
    which, which_out = (0, 4, 5, 6, 9), (0, 1, 2, 4)
    shapes = (
        jax.ShapeDtypeStruct((own_rows, width), F32),
        jax.ShapeDtypeStruct((n_tensor, own_rows, width), BF16),
        jax.ShapeDtypeStruct((n_tensor * own_rows, weight.shape[0]), BF16),
        jax.ShapeDtypeStruct((SMALL, width), F32),
        jax.ShapeDtypeStruct((n_tensor, own_rows, width), BF16),
    )
    specs, buffers = staged_specs(args[:10], which, shapes, which_out)
    return pl.pallas_call(
        staged(
            functools.partial(combine_kernel, n_dp, n_tensor, experts),
            len(args),
            which,
            len(shapes),
            which_out,
        ),
        out_shape=shapes,
        in_specs=specs + [any_spec()],
        out_specs=(any_spec(), any_spec(), any_spec(), vspec(), any_spec()),
        scratch_shapes=[
            pltpu.VMEM((n_tensor, own_rows, width), BF16),
            pltpu.VMEM((own_rows, width), F32),
            pltpu.VMEM((n_tensor - 1, own_rows, width), BF16),
            pltpu.VMEM((n_tensor + 1, own_rows, width), BF16),
            pltpu.VMEM((8, slots), F32),
            pltpu.VMEM((n_tensor, 8, own_rows), F32),
            pltpu.VMEM((n_tensor - 1, 8, own_rows), F32),
            pltpu.VMEM(value.shape, BF16),
            pltpu.SemaphoreType.DMA((n_tensor - 1,)),
            pltpu.SemaphoreType.DMA((n_tensor + 1,)),
            pltpu.SemaphoreType.DMA((n_tensor - 1,)),
            pltpu.SemaphoreType.DMA((n_tensor - 1,)),
            pltpu.SemaphoreType.DMA((n_dp - 1,)),
            pltpu.SemaphoreType.DMA((n_dp - 1,)),
            pltpu.SemaphoreType.DMA,
            pltpu.SemaphoreType.DMA((1, 2, n_tensor - 1)),
            pltpu.SemaphoreType.DMA((1, 2, n_tensor - 1)),
        ]
        + buffers,
        compiler_params=pltpu.CompilerParams(
            vmem_limit_bytes=VMEM_LIMIT, collective_id=2, has_side_effects=True
        ),
        name="combine",
    )(*args)


class Streams:
    def __init__(self, n, refs, send_sem, recv_sem):
        self.n, self.refs, self.send_sem, self.recv_sem = n, refs, send_sem, recv_sem
        self.me = lax.axis_index("tensor")

    def copy(self, j, block, slot, k, peer):
        ref = self.refs[j].at[block]
        return remote(
            ref, ref, self.send_sem.at[j, slot, k], self.recv_sem.at[j, slot, k], "tensor", peer
        )

    def outgoing(self, j, k, fn):
        for slot, sign in enumerate((1, -1)):
            block, peer = self.me - sign * k, self.me + sign

            @pl.when((block >= 0) & (block < self.n) & (peer >= 0) & (peer < self.n))
            def _():
                fn(self.copy(j, block, slot, k, peer))

    def incoming(self, j, k, fn):
        for slot, sign in enumerate((1, -1)):
            block = self.me - sign * (k + 1)

            @pl.when((block >= 0) & (block < self.n))
            def _():
                fn(self.copy(j, block, slot, k, jnp.clip(self.me - sign, 0, self.n - 1)), block)

    def turn(self, turn, used=None):
        moved = []
        for j in range(len(self.refs)):
            k = turn - j
            if k < 0 or k > self.n - 1:
                continue
            self.advance(j, k)
            moved.append((j, k))
        if used is not None:
            for j, k in moved:
                used(j, k)

    def turns(self):
        return range(self.n + len(self.refs) - 1)

    def advance(self, j, k):
        if k > 0:
            self.incoming(j, k - 1, lambda c, block: c.wait_recv())
        if k < self.n - 1:
            self.outgoing(j, k, lambda c: c.start())

    def each_new(self, j, k, fn):
        if k == 0:
            fn(self.me)
            return
        for sign in (1, -1):
            block = self.me - sign * k

            @pl.when((block >= 0) & (block < self.n))
            def _():
                fn(block)

    def drain(self):
        for j in range(len(self.refs)):
            for k in range(self.n - 1):
                self.outgoing(j, k, lambda c: c.wait_send())


class Spread:
    def __init__(self, n, ref, far_send, far_recv, near_send, near_recv):
        self.n, self.ref = n, ref
        self.far_send, self.far_recv = far_send, far_recv
        self.near_send, self.near_recv = near_send, near_recv
        self.me = lax.axis_index("dp")
        self.partner = self.me ^ 1

    def far(self, step, block, peer):
        ref = self.ref.at[block]
        return remote(ref, ref, self.far_send.at[step], self.far_recv.at[step], "dp", peer)

    def near(self, step, block):
        ref = self.ref.at[block]
        return remote(
            ref, ref, self.near_send.at[step], self.near_recv.at[step], "dp", self.partner
        )

    def start(self):
        for step in range(1, self.n // 2):
            self.far(step - 1, self.me, lax.rem(self.me + 2 * step, self.n)).start()
        self.near(0, self.me).start()

    def source(self, me, step):
        return lax.rem(me + self.n - 2 * step, self.n)

    def relay(self):
        for step in range(1, self.n // 2):
            block = self.source(self.me, step)
            self.far(step - 1, block, block).wait_recv()
            self.near(step, block).start()

    def finish(self):
        for step in range(self.n // 2):
            self.near(step, self.source(self.partner, step)).wait_recv()

    def drain(self):
        for step in range(1, self.n // 2):
            self.far(step - 1, self.me, lax.rem(self.me + 2 * step, self.n)).wait_send()
        for step in range(self.n // 2):
            self.near(step, self.source(self.me, step)).wait_send()


def one_hot(slot_rows, target, per):
    lane_slots = lax.broadcasted_iota(jnp.int32, (per, 1), 0) + target * per
    return jnp.where(
        (lane_slots == slot_rows[0:1, :]) | (lane_slots == slot_rows[1:2, :]), 1.0, 0.0
    ).astype(BF16)


def band(seq_len):
    return -(-(seq_len // 2 - 1) // BS)


def send_parameters(n_dp, n_tensor, weight_ref, extra_ref, out_ref, weights_ref, outs_ref, extras_ref, sems):
    me = lax.axis_index("dp")
    me_t = lax.axis_index("tensor")
    (extra_send, extra_recv, line_send, line_recv) = sems[:4]
    extras_ref[me] = extra_ref[...]
    small = []
    for step in range(1, n_dp):
        peer = lax.rem(me + step, n_dp)
        copy = remote(
            extra_ref, extras_ref.at[me], extra_send.at[step - 1], extra_recv.at[step - 1], "dp", peer
        )
        copy.start()
        small.append(copy)
    cols = weight_ref.shape[2]
    for part in range(3):
        weights_ref[me, :, part * cols : (part + 1) * cols] = weight_ref[part]
    weights = Spread(n_dp, weights_ref, *sems[4:8])
    weights.start()
    outs_ref[me, me_t] = out_ref[...]
    along = []
    for step in range(1, n_tensor):
        peer = lax.rem(me_t + step, n_tensor)
        copy = remote(
            out_ref,
            outs_ref.at[me, me_t],
            line_send.at[step - 1],
            line_recv.at[step - 1],
            "tensor",
            peer,
        )
        copy.start()
        along.append(copy)
    return small, weights, Spread(n_dp, outs_ref, *sems[8:12]), along


def unpack_parameters(n_dp, experts, extras_ref, selector_ref, router_ref, table, pattern_ref):
    depth = table.shape[1]
    rows_each = NB // n_dp
    for block in range(n_dp):
        router_ref[:, block * depth : (block + 1) * depth] = extras_ref[block, 0:experts, :]
        table[block * rows_each : (block + 1) * rows_each, :] = extras_ref[
            block, experts + 2 : experts + 2 + rows_each, :
        ].astype(F32)
    patterns = lax.dot_general(
        table[...],
        selector_ref[...],
        (((0,), (0,)), ((), ())),
        precision=lax.Precision.HIGHEST,
        preferred_element_type=F32,
    )
    for row in range(pattern_ref.shape[0]):
        pattern_ref[row : row + 1, :] = patterns[
            row // 2 : row // 2 + 1, (row % 2) * 2 * BS : (row % 2 + 1) * 2 * BS
        ]


def first_hidden(n_dp, experts, tokens_ref, extras_ref, gains_ref, small):
    depth = extras_ref.shape[2]
    x = tokens_ref[...].astype(F32)
    scaled = x * lax.rsqrt(jnp.mean(x * x, axis=1, keepdims=True) + EPS)
    for copy in small:
        copy.wait()
    for block in range(n_dp):
        gains_ref[0:2, block * depth : (block + 1) * depth] = extras_ref[
            block, experts : experts + 2, :
        ].astype(F32)
    return (scaled * gains_ref[0:1, :]).astype(BF16)


def parameter_sems(n_dp, n_tensor):
    dma = pltpu.SemaphoreType.DMA
    return (
        [dma((n_dp - 1,))] * 2 + [dma((n_tensor - 1,))] * 2 + [dma((n_dp // 2,))] * 8
    )


def front_kernel(
    n_dp,
    n_tensor,
    experts,
    tokens_ref,
    weight_ref,
    extra_ref,
    out_ref,
    selector_ref,
    hidden_ref,
    projected_ref,
    weights_ref,
    outs_ref,
    pattern_ref,
    router_ref,
    gains_ref,
    extras_ref,
    table,
    *sems,
):
    own_rows, width = tokens_ref.shape
    me_t = lax.axis_index("tensor")
    greet([("dp", n_dp), ("tensor", n_tensor)])
    small, weights, spread, along = send_parameters(
        n_dp, n_tensor, weight_ref, extra_ref, out_ref, weights_ref, outs_ref, extras_ref, sems
    )
    hidden_ref[me_t] = first_hidden(n_dp, experts, tokens_ref, extras_ref, gains_ref, small)
    lines = Streams(n_tensor, [hidden_ref], sems[12], sems[13])
    lines.turn(0)
    unpack_parameters(n_dp, experts, extras_ref, selector_ref, router_ref, table, pattern_ref)
    weights.relay()
    for copy in along:
        copy.wait_recv()
    spread.start()
    weights.finish()
    spread.relay()
    spread.finish()

    def project(block):
        rows = pl.ds(pl.multiple_of(block * own_rows, own_rows), own_rows)
        projected_ref[rows, :] = nn(
            hidden_ref[block], weights_ref[...].reshape(width, weights_ref.shape[2])
        ).astype(BF16)

    for turn in lines.turns():
        if turn:
            lines.turn(turn)

    def every(block, _):
        project(block)
        return 0

    lax.fori_loop(0, n_tensor, every, 0)
    lines.drain()
    weights.drain()
    spread.drain()
    for copy in along:
        copy.wait_send()


def front(n_dp, n_tensor, experts, tokens, weight, extra, out, selectors):
    own_rows, width = tokens.shape
    seq_len = own_rows * n_tensor
    depth, cols = weight.shape[1], 3 * weight.shape[2]
    heads = cols // (3 * HD)
    dma = pltpu.SemaphoreType.DMA
    return pl.pallas_call(
        functools.partial(front_kernel, n_dp, n_tensor, experts),
        out_shape=(
            jax.ShapeDtypeStruct((n_tensor, own_rows, width), BF16),
            jax.ShapeDtypeStruct((seq_len, cols), BF16),
            jax.ShapeDtypeStruct((n_dp, depth, cols), BF16),
            jax.ShapeDtypeStruct((n_dp, n_tensor) + out.shape, BF16),
            jax.ShapeDtypeStruct((2 * heads, 2 * BS), F32),
            jax.ShapeDtypeStruct((experts, width), BF16),
            jax.ShapeDtypeStruct((2, width), F32),
        ),
        in_specs=[vspec()] * 5,
        out_specs=(vspec(),) * 7,
        scratch_shapes=[pltpu.VMEM((n_dp,) + extra.shape, BF16), pltpu.VMEM((NB, depth), F32)]
        + parameter_sems(n_dp, n_tensor)
        + [dma((1, 2, n_tensor - 1))] * 2,
        compiler_params=pltpu.CompilerParams(
            vmem_limit_bytes=VMEM_LIMIT, collective_id=3, has_side_effects=True
        ),
        name="front",
    )(tokens, weight, extra, out, selectors)


PARTS = 4
ROW_PARTS = 8


class Dispatch:
    def __init__(self, n_dp, picks, stage, rows_ref, send_sem, recv_sem, own_sem):
        self.n, self.picks, self.stage, self.rows = n_dp, picks, stage, rows_ref
        self.send_sem, self.recv_sem, self.own_sem = send_sem, recv_sem, own_sem
        self.me = lax.axis_index("dp")

    def cols(self, j):
        part = self.stage.shape[3]
        return slice(j * part, (j + 1) * part)

    def copy(self, j, target, sender):
        return remote(
            self.stage.at[j, target],
            self.rows.at[sender, :, self.cols(j)],
            self.send_sem.at[j, target],
            self.recv_sem.at[j, sender],
            "dp",
            target,
        )

    def own(self, j):
        return pltpu.make_async_copy(
            self.stage.at[j, self.me], self.rows.at[self.me, :, self.cols(j)], self.own_sem.at[j]
        )

    def start(self, j, values_ref):
        n_tensor, own_rows, part = values_ref.shape

        def one(index, _):
            mask = self.n - 1 - index
            target = self.me ^ mask
            self.stage[j, target] = nn(
                self.picks[target], values_ref[...].reshape(n_tensor * own_rows, part)
            ).astype(BF16)

            @pl.when(mask != 0)
            def _():
                self.copy(j, target, self.me).start()

            @pl.when(mask == 0)
            def _():
                self.own(j).start()

            return 0

        lax.fori_loop(0, self.n, one, 0)

    def finish(self):
        for j in range(self.stage.shape[0]):
            self.own(j).wait()
            for step in range(1, self.n):
                peer = lax.rem(self.me + step, self.n)
                self.copy(j, peer, self.me).wait_send()
                self.copy(j, self.me, peer).wait_recv()


def opening_kernel(
    n_dp,
    n_tensor,
    experts,
    capacity,
    loads,
    tokens_ref,
    cotangent_ref,
    weight_ref,
    extra_ref,
    out_ref,
    routes_ref,
    segment_ref,
    selector_ref,
    hidden_ref,
    projected_ref,
    weights_ref,
    pattern_ref,
    router_ref,
    gains_ref,
    slots_ref,
    attended_ref,
    lse_ref,
    residual_ref,
    hidden_two_ref,
    weight_own_ref,
    rows_ref,
    grad_rows_ref,
    gates_ref,
    extras_ref,
    table,
    outs,
    out_matrix,
    grads,
    everyone,
    picks,
    grad_stage,
    row_stage,
    bias,
    slot_rows,
    attended_recv,
    logits,
    gate_stage,
    *sems,
):
    own_rows, width = tokens_ref.shape
    seq_len = own_rows * n_tensor
    heads = pattern_ref.shape[0] // 2
    head_cols = heads * HD
    out_cols = out_ref.shape[1]
    local = experts // n_dp
    per = local * capacity
    part = width // PARTS
    row_part = width // ROW_PARTS
    me = lax.axis_index("dp")
    me_t = lax.axis_index("tensor")
    (hop_send, hop_recv, late_send, late_recv) = sems[12:16]
    (grad_send, grad_recv, grad_own, row_send, row_recv, row_own) = sems[16:22]
    (gate_send, gate_recv, attended_send_sem, attended_recv_sem) = sems[22:26]
    greet([("dp", n_dp), ("tensor", n_tensor)], loads)

    def rows_of(block):
        return pl.ds(pl.multiple_of(block * own_rows, own_rows), own_rows)

    for j in range(PARTS):
        grads[j, me_t] = cotangent_ref[:, j * part : (j + 1) * part]
    lines = Streams(
        n_tensor, [hidden_ref] + [grads.at[j] for j in range(PARTS)], hop_send, hop_recv
    )
    lines.advance(1, 0)
    lines.advance(2, 0)
    small, weights, spread, along = send_parameters(
        n_dp, n_tensor, weight_ref, extra_ref, out_ref, weights_ref, outs, extras_ref, sems
    )
    hidden_ref[me_t] = first_hidden(n_dp, experts, tokens_ref, extras_ref, gains_ref, small)
    lines.advance(1, 1)
    lines.advance(2, 1)
    unpack_parameters(n_dp, experts, extras_ref, selector_ref, router_ref, table, pattern_ref)
    lines.advance(1, 2)
    lines.advance(2, 2)
    lines.advance(0, 0)

    ids = lax.broadcasted_iota(jnp.int32, (experts, seq_len), 0)
    hits = [ids == routes_ref[k : k + 1, :] for k in range(TOP)]
    before = lax.broadcasted_iota(jnp.int32, (seq_len, seq_len), 0) < lax.broadcasted_iota(
        jnp.int32, (seq_len, seq_len), 1
    )
    ranks = nn(
        jnp.where(hits[0] | hits[1], 1.0, 0.0).astype(BF16),
        jnp.where(before, 1.0, 0.0).astype(BF16),
    )
    places = ranks + (ids * capacity).astype(F32)
    for k in range(TOP):
        row = jnp.sum(jnp.where(hits[k], places, 0.0), axis=0, keepdims=True)
        slot_rows[k : k + 1, :] = row.astype(jnp.int32)
        for block in range(n_tensor):
            rows = slice(block * own_rows, (block + 1) * own_rows)
            slots_ref[rows, k : k + 1] = to_column(row[:, rows]).astype(jnp.int32)


    def pick(target, _):
        picks[target] = one_hot(slot_rows, target, per)
        return 0

    lax.fori_loop(0, n_dp, pick, 0)
    grad_moves = Dispatch(n_dp, picks, grad_stage, grad_rows_ref, grad_send, grad_recv, grad_own)
    lines.advance(1, 3)
    grad_moves.start(0, grads.at[0])
    lines.advance(2, 3)
    grad_moves.start(1, grads.at[1])
    weights.relay()
    for copy in along:
        copy.wait_recv()
    spread.start()
    build_bias(heads, pattern_ref, bias)

    def project(block):
        projected_ref[rows_of(block), :] = nn(
            hidden_ref[block], weights_ref[...].reshape(width, weights_ref.shape[2])
        ).astype(BF16)

    lines.advance(0, 1)
    weights.finish()
    project(me_t)
    lines.advance(0, 2)
    lines.advance(3, 0)
    lines.advance(4, 0)
    spread.relay()
    lines.each_new(0, 1, project)
    lines.advance(0, 3)
    lines.advance(3, 1)
    lines.advance(4, 1)
    lines.each_new(0, 2, project)
    lines.each_new(0, 3, project)

    def attended_copy(target, sender):
        return remote(
            attended_ref.at[rows_of(target)],
            attended_recv.at[sender],
            attended_send_sem.at[target],
            attended_recv_sem.at[sender],
            "tensor",
            target,
        )

    def attend(qb):
        forward_rows(
            heads,
            qb,
            max(0, qb - band(seq_len)),
            projected_ref,
            segment_ref,
            bias,
            attended_ref,
            lse_ref,
        )

        @pl.when(me_t == qb)
        def _():
            attended_recv[me_t] = attended_ref[rows_of(me_t), :]

        @pl.when(me_t != qb)
        def _():
            attended_copy(qb, me_t).start()

    lines.advance(3, 2)
    lines.advance(4, 2)
    attend(3)
    attend(0)
    lines.advance(3, 3)
    grad_moves.start(2, grads.at[2])
    lines.advance(4, 3)
    attend(2)
    attend(1)
    grad_moves.start(3, grads.at[3])
    loads.put(0, 1, 2, 7)
    spread.finish()
    for block in range(n_dp):
        out_matrix[:, block * out_cols : (block + 1) * out_cols] = outs[block].reshape(
            width, out_cols
        )
    weight_own_ref[...] = out_matrix[
        pl.ds(pl.multiple_of(me_t * head_cols, head_cols), head_cols), :
    ]
    for step in range(1, n_tensor):
        attended_copy(me_t, lax.rem(me_t + step, n_tensor)).wait_recv()
    residual = tokens_ref[...].astype(F32)
    for block in range(n_tensor):
        residual += nn(
            attended_recv[block], out_matrix[block * head_cols : (block + 1) * head_cols, :]
        )
    residual_ref[...] = residual
    hidden = (
        residual
        * lax.rsqrt(jnp.mean(residual * residual, axis=1, keepdims=True) + EPS)
        * gains_ref[1:2, :]
    ).astype(BF16)
    hidden_two_ref[...] = hidden
    for j in range(ROW_PARTS):
        everyone[j, me_t] = hidden[:, j * row_part : (j + 1) * row_part]
    loads.put(9, 10, 11)
    late = Streams(n_tensor, [everyone.at[j] for j in range(ROW_PARTS)], late_send, late_recv)
    row_moves = Dispatch(n_dp, picks, row_stage, rows_ref, row_send, row_recv, row_own)

    def used(j, k):
        if k < n_tensor - 1:
            return
        row_moves.start(j, everyone.at[j])
        term = nt(
            router_ref[:, j * row_part : (j + 1) * row_part], everyone[j].reshape(seq_len, row_part)
        )
        if j == 0:
            logits[...] = term
        else:
            logits[...] += term

    for turn in late.turns():
        late.turn(turn, used)
    values = logits[...]
    exps = jnp.exp(values - jnp.max(values, axis=0, keepdims=True))
    probs = exps / jnp.sum(exps, axis=0, keepdims=True)
    named = (ids == routes_ref[0:1, :]) | (ids == routes_ref[1:2, :])
    shares = probs / jnp.sum(jnp.where(named, probs, 0.0), axis=0, keepdims=True)
    logits[...] = shares

    def gate_copy(target, sender):
        return remote(
            gate_stage.at[target],
            gates_ref.at[sender],
            gate_send.at[target],
            gate_recv.at[sender],
            "dp",
            target,
        )

    def gate(index, _):
        mask = n_dp - 1 - index
        target = me ^ mask
        for expert in range(local):
            row = jnp.sum(
                jnp.where(ids == target * local + expert, logits[...], 0.0), axis=0, keepdims=True
            )
            high = row.astype(BF16)
            rest = row - high.astype(F32)
            mid = rest.astype(BF16)
            low = (rest - mid.astype(F32)).astype(BF16)
            lanes = slice(expert * capacity, (expert + 1) * capacity)
            pieces = nt(
                jnp.concatenate([high, mid, low, jnp.zeros((5, seq_len), BF16)], axis=0),
                picks[target, lanes, :],
            )
            gate_stage[target, :, lanes] = jnp.broadcast_to(
                jnp.sum(pieces, axis=0, keepdims=True), (8, capacity)
            )

        @pl.when(mask != 0)
        def _():
            gate_copy(target, me).start()

        @pl.when(mask == 0)
        def _():
            gates_ref[target] = gate_stage[target]

        return 0

    lax.fori_loop(0, n_dp, gate, 0)
    lines.drain()
    late.drain()
    weights.drain()
    spread.drain()
    for copy in along:
        copy.wait_send()
    for step in range(1, n_tensor):
        attended_copy(lax.rem(me_t + step, n_tensor), me_t).wait_send()
    for step in range(1, n_dp):
        peer = lax.rem(me + step, n_dp)
        gate_copy(peer, me).wait_send()
        gate_copy(me, peer).wait_recv()
    grad_moves.finish()
    row_moves.finish()


def opening(
    n_dp,
    n_tensor,
    experts,
    capacity,
    tokens,
    cotangent,
    weight,
    extra,
    out,
    routes,
    segments,
    selectors,
):
    own_rows, width = tokens.shape
    seq_len = own_rows * n_tensor
    depth, cols = weight.shape[1], 3 * weight.shape[2]
    per = experts // n_dp * capacity
    part = width // PARTS
    row_part = width // ROW_PARTS
    heads = cols // (3 * HD)
    dma = pltpu.SemaphoreType.DMA
    rows = jax.ShapeDtypeStruct((n_dp, per, width), BF16)
    args = (tokens, cotangent, weight, extra, out, routes, segments, selectors)
    which, which_out = (0, 1, 2, 4), (0, 1, 2, 7, 9, 10, 11)
    shapes = (
            jax.ShapeDtypeStruct((n_tensor, own_rows, width), BF16),
            jax.ShapeDtypeStruct((seq_len, cols), BF16),
            jax.ShapeDtypeStruct((n_dp, depth, cols), BF16),
            jax.ShapeDtypeStruct((2 * heads, 2 * BS), F32),
            jax.ShapeDtypeStruct((experts, width), BF16),
            jax.ShapeDtypeStruct((2, width), F32),
            jax.ShapeDtypeStruct((seq_len, TOP), jnp.int32),
            jax.ShapeDtypeStruct((seq_len, heads * HD), BF16),
            jax.ShapeDtypeStruct((seq_len, heads), F32),
            jax.ShapeDtypeStruct((own_rows, width), F32),
            jax.ShapeDtypeStruct((own_rows, width), BF16),
            jax.ShapeDtypeStruct((heads * HD, width), BF16),
            rows,
            rows,
            jax.ShapeDtypeStruct((n_dp, 8, per), F32),
    )
    specs, buffers = staged_specs(args, which, shapes, which_out)
    return pl.pallas_call(
        staged(
            functools.partial(opening_kernel, n_dp, n_tensor, experts, capacity),
            len(args),
            which,
            len(shapes),
            which_out,
        ),
        out_shape=shapes,
        in_specs=specs,
        out_specs=tuple(
            any_spec() if i in which_out or i in (12, 13) else vspec() for i in range(len(shapes))
        ),
        scratch_shapes=[
            pltpu.VMEM((n_dp,) + extra.shape, BF16),
            pltpu.VMEM((NB, depth), F32),
            pltpu.VMEM((n_dp, n_tensor) + out.shape, BF16),
            pltpu.VMEM((width, width), BF16),
            pltpu.VMEM((PARTS, n_tensor, own_rows, part), BF16),
            pltpu.VMEM((ROW_PARTS, n_tensor, own_rows, row_part), BF16),
            pltpu.VMEM((n_dp, per, seq_len), BF16),
            pltpu.VMEM((PARTS, n_dp, per, part), BF16),
            pltpu.VMEM((ROW_PARTS, n_dp, per, row_part), BF16),
            pltpu.VMEM((heads, 3, BS, BS), F32),
            pltpu.VMEM((8, seq_len), jnp.int32),
            pltpu.VMEM((n_tensor, own_rows, heads * HD), BF16),
            pltpu.VMEM((experts, seq_len), F32),
            pltpu.VMEM((n_dp, 8, per), F32),
        ]
        + parameter_sems(n_dp, n_tensor)
        + [dma((PARTS + 1, 2, n_tensor - 1))] * 2
        + [dma((ROW_PARTS, 2, n_tensor - 1))] * 2
        + [dma((PARTS, n_dp)), dma((PARTS, n_dp)), dma((PARTS,))]
        + [dma((ROW_PARTS, n_dp)), dma((ROW_PARTS, n_dp)), dma((ROW_PARTS,))]
        + [dma((n_dp,))] * 2
        + [dma((n_tensor,))] * 2
        + buffers,
        compiler_params=pltpu.CompilerParams(
            vmem_limit_bytes=VMEM_LIMIT, collective_id=4, has_side_effects=True
        ),
        name="opening",
    )(*args)


def last_kernel(
    n_dp,
    n_tensor,
    experts,
    heads,
    loads,
    qkv_ref,
    attended_ref,
    grad_attended_ref,
    lse_ref,
    segment_ref,
    pattern_ref,
    skew_ref,
    hidden_ref,
    weight_ref,
    branch_ref,
    small_ref,
    weight_own_ref,
    gain_own_ref,
    merged_ref,
    residual_ref,
    grad_residual_ref,
    tokens_ref,
    gain_ref,
    layer_ref,
    grad_tokens_ref,
    grad_weight_ref,
    grad_out_ref,
    small_out_ref,
    bias,
    dk,
    dv,
    sums,
    grad_qkv,
    diag,
    parts,
    mixture,
    grad_hidden,
    mix_send,
    mix_recv,
    line_send,
    line_recv,
    qkv_send,
    qkv_recv,
    out_send,
    out_recv,
    small_send,
    small_recv,
    small_sum,
    gain_recv,
    mix_send_sem,
    mix_recv_sem,
    line_send_sem,
    line_recv_sem,
    qkv_send_sem,
    qkv_recv_sem,
    out_send_sem,
    out_recv_sem,
    small_send_sem,
    small_recv_sem,
    gain_send_sem,
    gain_recv_sem,
):
    own_rows, width = residual_ref.shape
    seq_len = own_rows * n_tensor
    depth = weight_own_ref.shape[1]
    out_cols = grad_out_ref.shape[1]
    me = lax.axis_index("dp")
    me_t = lax.axis_index("tensor")
    greet([("dp", n_dp), ("tensor", n_tensor)], loads)

    def rows_of(block):
        return pl.ds(pl.multiple_of(block * own_rows, own_rows), own_rows)

    mix = LineSum(n_tensor, merged_ref, mix_send, mix_recv, mix_send_sem, mix_recv_sem, mixture)
    line = LineSum(n_tensor, parts, line_send, line_recv, line_send_sem, line_recv_sem, grad_hidden)
    copies = []

    def scatter(source, target, send_sem, recv_sem):
        for step in range(1, n_dp):
            peer = lax.rem(me + step, n_dp)
            copy = remote(
                source.at[peer],
                target.at[step - 1],
                send_sem.at[step - 1],
                recv_sem.at[step - 1],
                "dp",
                peer,
            )
            copy.start()
            copies.append(copy)

    mix.start()
    build_bias(heads, pattern_ref, bias)
    backward_start(dk, dv, sums)
    blocks = seq_len // BS
    for qb in range(blocks):
        backward_rows(
            heads,
            qb,
            max(0, qb - band(seq_len)),
            qkv_ref,
            attended_ref,
            grad_attended_ref,
            lse_ref,
            segment_ref,
            bias,
            grad_qkv,
            dk,
            dv,
            sums,
        )
        if qb == 0:
            for block in range(n_dp):
                cols = slice(block * out_cols, (block + 1) * out_cols)
                out_send[block] = tn(attended_ref[...], branch_ref[:, cols]).astype(BF16)
            scatter(out_send, out_recv, out_send_sem, out_recv_sem)
        if qb >= blocks - 2 and qb - (blocks - 2) < n_tensor - 1:
            mix.step(qb - (blocks - 2))
    backward_end(heads, grad_qkv, dk, dv)
    line.start(lambda block: nt(grad_qkv[rows_of(block), :], weight_ref[...]))
    for k in range(2, n_tensor - 1):
        mix.step(k)
    for block in range(n_dp):
        cols = slice(block * depth, (block + 1) * depth)
        qkv_send[block] = tn(hidden_ref[:, cols], grad_qkv[...]).astype(BF16)
    scatter(qkv_send, qkv_recv, qkv_send_sem, qkv_recv_sem)
    diag[...] = jnp.zeros_like(diag)
    diagonal_sums(heads, sums, diag)
    tables = lax.dot_general(
        skew_ref[...],
        jnp.concatenate([diag[0], diag[1]], axis=1),
        (((1,), (1,)), ((), ())),
        precision=lax.Precision.HIGHEST,
        preferred_element_type=F32,
    )
    far = jnp.sum(diag[2], axis=1, keepdims=True)
    head = lax.broadcasted_iota(jnp.int32, (8, 8), 0)
    lane = lax.broadcasted_iota(jnp.int32, (8, 8), 1)
    far_row = jnp.sum(jnp.where(head == lane, far, 0.0), axis=0, keepdims=True)
    bucket = lax.broadcasted_iota(jnp.int32, (NB, 8), 0)
    tables += jnp.where(bucket == NB - 1, far_row, 0.0)
    rows_each = NB // n_dp
    for block in range(n_dp):
        small_send[block] = small_ref[:, block * depth : (block + 1) * depth]
        small_send[block, experts + 2 : experts + 2 + rows_each, 0:8] = tables[
            block * rows_each : (block + 1) * rows_each, :
        ]
    scatter(small_send, small_recv, small_send_sem, small_recv_sem)
    layer_ref[...] = (residual_ref[...] + mixture[...]).astype(BF16)
    for k in range(n_tensor - 2):
        line.step(k)
    for copy in copies:
        copy.wait_recv()
    small_sum[...] = small_send[me]
    grad_weight_ref[...] = qkv_send[me].astype(F32)
    grad_out_ref[...] = out_send[me].astype(F32)
    for step in range(1, n_dp):
        small_sum[...] += small_recv[step - 1]
        grad_weight_ref[...] += qkv_recv[step - 1].astype(F32)
        grad_out_ref[...] += out_recv[step - 1].astype(F32)
    column = jnp.zeros((depth, 1), F32)
    part = weight_own_ref.shape[2]
    for k in range(3):
        column += jnp.sum(
            grad_weight_ref[:, k * part : (k + 1) * part] * weight_own_ref[k].astype(F32),
            axis=1,
            keepdims=True,
        )
    small_sum[experts + 1 : experts + 2, :] = to_row(column) / gain_own_ref[...].astype(F32)
    gains = []
    for step in range(1, n_tensor):
        peer = lax.rem(me_t + step, n_tensor)
        copy = remote(
            small_sum,
            gain_recv.at[step - 1],
            gain_send_sem.at[step - 1],
            gain_recv_sem.at[step - 1],
            "tensor",
            peer,
        )
        copy.start()
        gains.append(copy)
    line.step(n_tensor - 2)
    x = tokens_ref[...].astype(F32)
    scale = lax.rsqrt(jnp.mean(x * x, axis=1, keepdims=True) + EPS)
    unit = x * scale
    grad_unit = grad_hidden[...] * gain_ref[0:1, :]
    grad_tokens_ref[...] = (
        grad_residual_ref[...]
        + scale * (grad_unit - unit * jnp.mean(grad_unit * unit, axis=1, keepdims=True))
    ).astype(BF16)
    mix.drain()
    line.drain()
    for copy in copies:
        copy.wait_send()
    for copy in gains:
        copy.wait()
    small_out_ref[...] = small_sum[...]
    shared = slice(0, experts + 2)
    for step in range(1, n_tensor):
        small_out_ref[shared, :] += gain_recv[step - 1, shared, :]


def last(
    n_dp,
    n_tensor,
    experts,
    heads,
    projected,
    attended,
    grad_attended,
    lse,
    segments,
    patterns,
    skew,
    hidden,
    weight,
    branch,
    small,
    weight_own,
    gain_own,
    merged,
    residual,
    grad_residual,
    tokens,
    gain,
):
    seq_len, width = hidden.shape
    own_rows = seq_len // n_tensor
    depth, cols = weight_own.shape[1], 3 * weight_own.shape[2]
    out_cols = width // n_dp
    dma = pltpu.SemaphoreType.DMA
    line = [
        pltpu.VMEM((n_tensor - 1, own_rows, width), BF16),
        pltpu.VMEM((n_tensor + 1, own_rows, width), BF16),
    ]
    args = (
        projected,
        attended,
        grad_attended,
        lse,
        segments,
        patterns,
        skew,
        hidden,
        weight,
        branch,
        small,
        weight_own,
        gain_own,
        merged,
        residual,
        grad_residual,
        tokens,
        gain,
    )
    which = (0, 1, 2, 7, 8, 9, 11, 13, 14, 15, 16)
    specs, buffers = staged_specs(args, which)
    return pl.pallas_call(
        staged(functools.partial(last_kernel, n_dp, n_tensor, experts, heads), len(args), which),
        out_shape=(
            jax.ShapeDtypeStruct((own_rows, width), BF16),
            jax.ShapeDtypeStruct((own_rows, width), BF16),
            jax.ShapeDtypeStruct((depth, cols), F32),
            jax.ShapeDtypeStruct((heads * HD, out_cols), F32),
            jax.ShapeDtypeStruct((SMALL, depth), F32),
        ),
        in_specs=specs,
        out_specs=(vspec(),) * 5,
        scratch_shapes=backward_scratch(heads, seq_len)
        + [
            pltpu.VMEM((seq_len, cols), BF16),
            pltpu.VMEM((3, 8, 2 * BS), F32),
        ]
        + [pltpu.VMEM((n_tensor, own_rows, width), BF16)]
        + [pltpu.VMEM((own_rows, width), F32)] * 2
        + line * 2
        + [
            pltpu.VMEM((n_dp, depth, cols), BF16),
            pltpu.VMEM((n_dp - 1, depth, cols), BF16),
            pltpu.VMEM((n_dp, heads * HD, out_cols), BF16),
            pltpu.VMEM((n_dp - 1, heads * HD, out_cols), BF16),
            pltpu.VMEM((n_dp, SMALL, depth), F32),
            pltpu.VMEM((n_dp - 1, SMALL, depth), F32),
            pltpu.VMEM((SMALL, depth), F32),
            pltpu.VMEM((n_tensor - 1, SMALL, depth), F32),
        ]
        + [dma((n_tensor - 1,)), dma((n_tensor + 1,))] * 2
        + [dma((n_dp - 1,))] * 6
        + [dma((n_tensor - 1,))] * 2
        + buffers,
        compiler_params=pltpu.CompilerParams(
            vmem_limit_bytes=VMEM_LIMIT, collective_id=5, has_side_effects=True
        ),
        name="last",
    )(*args)


def deliver_kernel(
    grad_in_ref,
    grad_out_ref,
    layer_in_ref,
    tokens_in_ref,
    weight_in_ref,
    out_in_ref,
    small_ref,
    layer_ref,
    tokens_ref,
    weight_ref,
    out_ref,
    table_ref,
    gain_one_ref,
    gain_two_ref,
    router_ref,
    in_ref,
    down_ref,
    stage_in,
    stage_down,
    wide_in,
    wide_down,
    in_sem,
    down_sem,
    out_sem,
    last_sem,
):
    local, halves = grad_in_ref.shape[:2]
    pieces = [
        (
            grad_in_ref.at[e, g],
            stage_in.at[e, g],
            wide_in.at[e, g],
            in_ref.at[e, g],
            in_sem.at[e, g],
            out_sem.at[e, g],
        )
        for e in range(local)
        for g in range(halves)
    ] + [
        (
            grad_out_ref.at[e],
            stage_down.at[e],
            wide_down.at[e],
            down_ref.at[e],
            down_sem.at[e],
            last_sem.at[e],
        )
        for e in range(local)
    ]
    for source, stage, _, _, sem, _ in pieces:
        pltpu.make_async_copy(source, stage, sem).start()
    layer_ref[...] = layer_in_ref[...]
    tokens_ref[...] = tokens_in_ref[...]
    cols = weight_ref.shape[2]
    for part in range(3):
        weight_ref[part] = weight_in_ref[:, part * cols : (part + 1) * cols]
    out_ref[...] = out_in_ref[...]
    experts = router_ref.shape[0]
    router_ref[...] = small_ref[0:experts, :]
    gain_two_ref[...] = small_ref[experts : experts + 1, :]
    gain_one_ref[...] = small_ref[experts + 1 : experts + 2, :]
    table_ref[...] = small_ref[
        experts + 2 : experts + 2 + table_ref.shape[0], 0 : table_ref.shape[1]
    ]
    for source, stage, wide, target, sem, done in pieces:
        pltpu.make_async_copy(source, stage, sem).wait()
        wide[...] = stage[...].astype(F32)
        pltpu.make_async_copy(wide, target, done).start()
    for _, _, wide, target, _, done in pieces:
        pltpu.make_async_copy(wide, target, done).wait()


def deliver(experts, heads, table_rows, grad_in, grad_out, layer, tokens, weight, out, small):
    depth, cols = weight.shape
    local, halves = grad_in.shape[:2]
    dma = pltpu.SemaphoreType.DMA
    return pl.pallas_call(
        deliver_kernel,
        out_shape=(
            jax.ShapeDtypeStruct(layer.shape, BF16),
            jax.ShapeDtypeStruct(tokens.shape, BF16),
            jax.ShapeDtypeStruct((3, depth, cols // 3), F32),
            jax.ShapeDtypeStruct(out.shape, F32),
            jax.ShapeDtypeStruct((table_rows, heads), F32),
            jax.ShapeDtypeStruct((1, depth), F32),
            jax.ShapeDtypeStruct((1, depth), F32),
            jax.ShapeDtypeStruct((experts, depth), F32),
            jax.ShapeDtypeStruct(grad_in.shape, F32),
            jax.ShapeDtypeStruct(grad_out.shape, F32),
        ),
        in_specs=[any_spec()] * 2 + [vspec()] * 5,
        out_specs=(vspec(),) * 8 + (any_spec(),) * 2,
        scratch_shapes=[
            pltpu.VMEM(grad_in.shape, grad_in.dtype),
            pltpu.VMEM(grad_out.shape, grad_out.dtype),
            pltpu.VMEM(grad_in.shape, F32),
            pltpu.VMEM(grad_out.shape, F32),
            dma((local, halves)),
            dma((local,)),
            dma((local, halves)),
            dma((local,)),
        ],
        compiler_params=pltpu.CompilerParams(vmem_limit_bytes=VMEM_LIMIT),
        name="deliver",
    )(grad_in, grad_out, layer, tokens, weight, out, small)


def rms_scale(values):
    return lax.rsqrt(jnp.mean(values * values, axis=-1, keepdims=True) + EPS)


def norm_backward(grad_normed, values, scale_inv, gain):
    normed_unit = values * scale_inv
    grad_unit = grad_normed * gain
    grad_values = scale_inv * (
        grad_unit - normed_unit * jnp.mean(grad_unit * normed_unit, axis=-1, keepdims=True)
    )
    return (grad_values, jnp.sum(grad_normed * normed_unit, axis=0))


def gelu_tanh(values):
    return jax.nn.gelu(values, approximate=True)


def route_slots(route_ids, experts, capacity):
    flat_routes = route_ids.reshape(-1)
    onehot = (flat_routes[:, None] == jnp.arange(experts, dtype=jnp.int32)[None, :]).astype(
        jnp.int32
    )
    ranks = jnp.cumsum(onehot, axis=0) - 1
    rank_own = jnp.sum(ranks * onehot, axis=1)
    return (flat_routes * capacity + rank_own).reshape(-1, TOP)


def on_device(
    tokens,
    segments,
    routes,
    w_qkv,
    w_attn_out,
    bias_table,
    gain_attn,
    gain_moe,
    router,
    w_in,
    w_out,
    cotangent,
):
    own_rows, model_width = tokens.shape
    n_tensor = lax.axis_size("tensor")
    n_dp = lax.axis_size("dp")
    seq_len = own_rows * n_tensor
    own_start = lax.axis_index("tensor") * own_rows
    head_cols = w_qkv.shape[2]
    heads = head_cols // HD
    experts = router.shape[1]
    local_experts = w_in.shape[0]
    capacity = 5 * seq_len * TOP // (4 * experts)
    highest = lax.Precision.HIGHEST
    slots = experts * capacity

    depth = w_qkv.shape[0]
    bias_rows = NB // n_dp
    lanes = depth
    extra = jnp.concatenate(
        [
            jnp.transpose(router),
            gain_attn[None],
            gain_moe[None],
            jnp.pad(bias_table, ((0, SMALL - experts - 2 - bias_rows), (0, lanes - heads))),
        ],
        axis=0,
    )
    fast = n_dp == 8 and n_tensor == 4 and seq_len == 4 * BS and slots * model_width <= 4 * 1024 * 1024
    route_rows = jnp.transpose(routes)
    weight_parts = jnp.transpose(w_qkv, (1, 0, 2))
    skew = jnp.asarray(skew_selectors().T)
    selectors = jnp.asarray(distance_selectors().T)

    def finish(layer_out, grad_tokens, reduced_qkv, reduced_attn_out, small_sum, grad_w_in, grad_w_out):
        (
            layer_out,
            grad_tokens,
            grad_w_qkv,
            grad_w_attn_out,
            grad_table,
            grad_gain_one,
            grad_gain_two,
            grad_router,
            grad_w_in,
            grad_w_out,
        ) = deliver(
            experts,
            heads,
            NB // n_dp,
            grad_w_in,
            grad_w_out,
            layer_out,
            grad_tokens,
            reduced_qkv,
            reduced_attn_out,
            small_sum,
        )
        return (
            layer_out,
            grad_tokens,
            jnp.transpose(grad_w_qkv, (1, 0, 2)),
            grad_w_attn_out,
            grad_table,
            grad_gain_one[0],
            grad_gain_two[0],
            jnp.transpose(grad_router),
            grad_w_in,
            grad_w_out,
        )

    if fast:
        (
            gathered,
            projected,
            weights_full,
            patterns,
            router_rows,
            gains,
            slot_columns,
            attended,
            lse,
            residual,
            hidden_two,
            weight_own,
            rows,
            grad_rows,
            row_gates,
        ) = opening(
            n_dp,
            n_tensor,
            experts,
            capacity,
            tokens,
            cotangent,
            weight_parts,
            extra,
            w_attn_out,
            route_rows,
            segments,
            selectors,
        )
        back, gate_back, value, grad_w_in, grad_w_out = run_experts(
            n_dp, capacity, rows, grad_rows, row_gates, w_in, w_out
        )
        grad_residual, grad_branch_all, grad_attended, small, merged = combine(
            n_dp,
            n_tensor,
            experts,
            back.reshape(slots, model_width),
            gate_back,
            slot_columns,
            route_rows,
            residual,
            hidden_two,
            cotangent,
            router_rows,
            gains,
            weight_own,
            value,
        )
        results = last(
            n_dp,
            n_tensor,
            experts,
            heads,
            projected,
            attended,
            grad_attended,
            lse,
            segments,
            patterns,
            skew,
            gathered.reshape(seq_len, model_width),
            weights_full.reshape(model_width, 3 * head_cols),
            grad_branch_all.reshape(seq_len, model_width),
            small,
            weight_parts,
            gain_attn[None],
            merged,
            residual,
            grad_residual,
            tokens,
            gains,
        )
        return finish(*results, grad_w_in, grad_w_out)
    gathered, projected, weights_full, outs_full, patterns, router_rows, gains = front(
        n_dp, n_tensor, experts, tokens, weight_parts, extra, w_attn_out, selectors
    )
    gathered_one = gathered.reshape(seq_len, model_width)
    qkv_matrix = weights_full.reshape(model_width, 3 * head_cols)
    outs_full = outs_full.reshape(n_dp, model_width, model_width // n_dp)
    tokens_float = tokens.astype(F32)
    scale_one = rms_scale(tokens_float)
    gain_one, gain_two = gains[0], gains[1]
    starts = segments[0, ::BS]
    ends = segments[0, BS - 1 :: BS]
    lowest = jnp.sum((ends[None, :] < starts[:, None]).astype(jnp.int32), axis=1)
    attended, lse = attention_forward(projected, lowest, segments, patterns, heads)
    router_full = jnp.transpose(router_rows)
    out_matrix = jnp.transpose(outs_full, (1, 0, 2)).reshape(model_width, model_width)
    attended_own = lax.all_to_all(
        attended.reshape(n_tensor, own_rows, head_cols), "tensor", 0, 0
    )
    attended_own = jnp.transpose(attended_own, (1, 0, 2)).reshape(own_rows, n_tensor * head_cols)
    branch = jnp.dot(attended_own, out_matrix, preferred_element_type=F32)
    residual = tokens_float + branch
    scale_two = rms_scale(residual)
    hidden_two = (residual * scale_two * gain_two).astype(BF16)
    gathered_two = lax.all_gather(hidden_two, "tensor", axis=0, tiled=True)

    expert_ids = jnp.arange(experts, dtype=jnp.int32)

    def gate_values(logit_values, route_rows):
        expert_probs = jax.nn.softmax(logit_values, axis=-1)
        picked = jnp.sum(
            jnp.where(
                route_rows[:, :, None] == expert_ids[None, None, :], expert_probs[:, None, :], 0.0
            ),
            axis=-1,
        )
        return picked / jnp.sum(picked, axis=1, keepdims=True)

    gates = gate_values(jnp.dot(gathered_two, router_full, preferred_element_type=F32), routes)
    slot_ids = route_slots(routes, experts, capacity)
    slot_flat = slot_ids.reshape(-1)
    token_ids = jnp.repeat(jnp.arange(seq_len, dtype=jnp.int32), TOP)
    sources = jnp.full((slots,), seq_len, jnp.int32).at[slot_flat].set(token_ids)
    slot_gates = jnp.zeros((slots,), F32).at[slot_flat].set(gates.reshape(-1))
    grad_gathered = lax.all_gather(cotangent, "tensor", axis=0, tiled=True)

    def exchange(rows):
        parts = rows.reshape(n_dp, local_experts, capacity, model_width)
        return [
            lax.all_to_all(parts[:, i], "dp", 0, 0).reshape(n_dp * capacity, model_width)
            for i in range(local_experts)
        ]

    def give_back(parts):
        back = [
            lax.all_to_all(part.reshape(n_dp, capacity, model_width), "dp", 0, 0) for part in parts
        ]
        return jnp.stack(back, axis=1).reshape(slots, model_width)

    zero_row = jnp.zeros((1, model_width), BF16)
    dispatched = exchange(jnp.concatenate([gathered_two, zero_row], axis=0)[sources])
    padded_grad = jnp.concatenate([grad_gathered, zero_row], axis=0)
    grad_expert = exchange((slot_gates[:, None] * padded_grad[sources]).astype(BF16))

    outs, backs, grads_in, grads_out = [], [], [], []
    for i in range(local_experts):
        rows, grad_rows = dispatched[i], grad_expert[i]
        gate_part = nt(rows, w_in[i, 0])
        up_part = nt(rows, w_in[i, 1])
        gelu_value, gelu_pull = jax.vjp(gelu_tanh, gate_part)
        activated = (gelu_value * up_part).astype(BF16)
        outs.append(nn(activated, w_out[i]).astype(BF16))
        grad_act = nt(grad_rows, w_out[i])
        grads_out.append(tn(activated, grad_rows))
        grad_gate = gelu_pull(grad_act * up_part)[0].astype(BF16)
        grad_up = (grad_act * gelu_value).astype(BF16)
        backs.append((nn(grad_gate, w_in[i, 0]) + nn(grad_up, w_in[i, 1])).astype(BF16))
        grads_in.append(jnp.stack([tn(grad_gate, rows), tn(grad_up, rows)]))
    grad_w_in = jnp.stack(grads_in)
    grad_w_out = jnp.stack(grads_out)
    expert_out = give_back(outs)
    grad_dispatched = give_back(backs)

    first, second = slot_ids[:, 0], slot_ids[:, 1]
    picked_first = expert_out[first].astype(F32)
    picked_second = expert_out[second].astype(F32)
    mixture = lax.psum_scatter(
        (gates[:, 0:1] * picked_first + gates[:, 1:2] * picked_second).astype(BF16),
        "tensor",
        scatter_dimension=0,
        tiled=True,
    ).astype(F32)
    layer_out = (residual + mixture).astype(BF16)
    grad_float = grad_gathered.astype(F32)
    grad_gate_part = jnp.stack(
        [
            jnp.sum(grad_float * picked_first, axis=1),
            jnp.sum(grad_float * picked_second, axis=1),
        ],
        axis=1,
    )
    grad_hidden_part = (
        grad_dispatched[first].astype(F32) + grad_dispatched[second].astype(F32)
    ).astype(BF16)
    grad_own = lax.psum_scatter(
        grad_hidden_part, "tensor", scatter_dimension=0, tiled=True
    ).astype(F32)
    grad_gate_own = lax.dynamic_slice_in_dim(
        lax.psum(grad_gate_part, "tensor"), own_start, own_rows, 0
    )
    own_routes = lax.dynamic_slice_in_dim(routes, own_start, own_rows, 0)
    own_logits = jnp.dot(hidden_two, router_full, preferred_element_type=F32)

    def own_gates(logit_values):
        return gate_values(logit_values, own_routes)

    _, gate_pull = jax.vjp(own_gates, own_logits)
    grad_logits = gate_pull(grad_gate_own)[0]
    router_float = router_full.astype(F32)
    grad_hidden_two = grad_own + jnp.dot(grad_logits, router_float.T, precision=highest)
    grad_router_part = jnp.dot(hidden_two.astype(F32).T, grad_logits, precision=highest)
    grad_from_norm, grad_gain_two = norm_backward(grad_hidden_two, residual, scale_two, gain_two)
    grad_residual = cotangent.astype(F32) + grad_from_norm

    grad_branch = grad_residual.astype(BF16)
    grad_attended_own = nt(grad_branch, out_matrix).astype(BF16)
    grad_attended = lax.all_to_all(
        jnp.transpose(grad_attended_own.reshape(own_rows, n_tensor, head_cols), (1, 0, 2)),
        "tensor",
        0,
        0,
    ).reshape(seq_len, head_cols)
    grad_branch_all = lax.all_gather(grad_branch, "tensor", axis=0, tiled=True)
    small = jnp.concatenate(
        [
            jnp.transpose(grad_router_part),
            grad_gain_two[None],
            jnp.zeros((SMALL - experts - 1, model_width), F32),
        ],
        axis=0,
    )
    grad_projected, diag = attention_backward(
        projected, attended, grad_attended, lse, lowest, segments, patterns, heads
    )
    near = jnp.concatenate([diag[0, :heads], diag[1, :heads]], axis=1)
    grad_table = lax.dot_general(skew, near, (((1,), (1,)), ((), ())), precision=highest)
    grad_table = grad_table.at[NB - 1].add(jnp.sum(diag[2, :heads], axis=1))
    small = jnp.transpose(small.reshape(SMALL, n_dp, depth), (1, 0, 2))
    small = lax.dynamic_update_slice(
        small, grad_table.reshape(n_dp, NB // n_dp, heads), (0, experts + 2, 0)
    )
    grad_hidden_one, reduced_qkv, reduced_attn_out, small_sum = tail(
        n_dp,
        n_tensor,
        experts,
        gathered_one,
        grad_projected,
        qkv_matrix,
        attended,
        grad_branch_all,
        small,
        w_qkv.reshape(depth, 3 * head_cols),
        gain_attn[None].astype(F32),
    )
    grad_from_first, _ = norm_backward(grad_hidden_one, tokens_float, scale_one, gain_one)
    grad_tokens = (grad_residual + grad_from_first).astype(BF16)
    return finish(
        layer_out, grad_tokens, reduced_qkv, reduced_attn_out, small_sum, grad_w_in, grad_w_out
    )


def solution(mesh):
    return jax.shard_map(
        on_device,
        mesh=mesh,
        in_specs=(
            P(("dp", "tensor"), None),
            P("dp", None),
            P("dp", None),
            P("dp", None, "tensor"),
            P("tensor", "dp"),
            P("dp", "tensor"),
            P("dp"),
            P("dp"),
            P("dp", None),
            P("dp", None, "tensor", None),
            P("dp", "tensor", None),
            P(("dp", "tensor"), None),
        ),
        out_specs=(
            P(("dp", "tensor"), None),
            P(("dp", "tensor"), None),
            P("dp", None, "tensor"),
            P("tensor", "dp"),
            P("dp", "tensor"),
            P("dp"),
            P("dp"),
            P("dp", None),
            P("dp", None, "tensor", None),
            P("dp", "tensor", None),
        ),
        check_vma=False,
    )
```

```python
import functools
import math

import jax
import jax.numpy as jnp
import numpy as np
from jax import lax
from jax.experimental import pallas as pl
from jax.experimental.pallas import tpu as pltpu
from jax.sharding import PartitionSpec as P

HD = 64
TOP = 2
NB = 32
NEAR = 128
BS = 256

EPS = 1e-06
NEG = -1e30
F32 = jnp.float32
BF16 = jnp.bfloat16
VMEM_LIMIT = 60 * 1024 * 1024


def distance_buckets():
    half_buckets = NB // 2
    thresholds = [bucket_level for bucket_level in range(1, half_buckets)]
    thresholds = thresholds + [
        int(
            math.ceil(
                half_buckets
                * (NEAR / half_buckets) ** ((bucket_level - half_buckets) / half_buckets)
            )
        )
        for bucket_level in range(half_buckets, NB)
    ]
    distance = np.arange(NEAR + 1)
    return (distance[:, None] >= np.array(thresholds)[None, :]).sum(axis=1)


def distance_selectors():
    buckets = distance_buckets()
    lanes = np.arange(2 * BS)
    signed = np.where(lanes < BS, lanes, lanes - 2 * BS)
    out = []
    for base in (0, BS):
        distance = np.clip(base - signed, 0, NEAR)
        out.append(buckets[distance][:, None] == np.arange(NB)[None, :])
    return np.concatenate(out, axis=0).astype(np.float32)


def skew_selectors():
    buckets = distance_buckets()
    lanes = np.arange(2 * BS)
    out = []
    for base in (0, BS):
        distance = np.clip(base + BS - 1 - lanes, 0, NEAR)
        out.append(buckets[distance][:, None] == np.arange(NB)[None, :])
    return np.concatenate(out, axis=0).astype(np.float32)


def nt(a, b):
    return lax.dot_general(a, b, (((1,), (1,)), ((), ())), preferred_element_type=F32)


def tn(a, b):
    return lax.dot_general(a, b, (((0,), (0,)), ((), ())), preferred_element_type=F32)


def nn(a, b):
    return lax.dot_general(a, b, (((1,), (0,)), ((), ())), preferred_element_type=F32)


def toeplitz(row):
    return pltpu.roll(jnp.broadcast_to(row, (BS, 2 * BS)), 0, 1, stride=1, stride_axis=0)[:, :BS]


def head_lanes(heads, width):
    lane = lax.broadcasted_iota(jnp.int32, (1, width), 1)
    return [(lane >= h * HD) & (lane < (h + 1) * HD) for h in range(heads)]


def own_head(value, lanes, heads):
    return value if heads == 1 else jnp.where(lanes, value, jnp.zeros((), value.dtype))


def build_bias(heads, pattern_ref, bias):
    for h in range(heads):
        for t in range(2):
            bias[h, t] = toeplitz(pattern_ref[2 * h + t : 2 * h + t + 1, :])
        bias[h, 2] = jnp.broadcast_to(pattern_ref[2 * h + 1 : 2 * h + 2, 0:1], (BS, BS))


def block_rows(block):
    if isinstance(block, int):
        return pl.ds(block * BS, BS)
    return pl.ds(pl.multiple_of(block * BS, BS), BS)


def segment_column(qb, segment_ref):
    return to_column(segment_ref[:, block_rows(qb)].astype(F32))


def block_mask(qb, kb, q_segments, segment_ref):
    k_segments = segment_ref[:, block_rows(kb)].astype(F32)
    row = lax.broadcasted_iota(jnp.int32, (BS, BS), 0) + (qb - kb) * BS
    col = lax.broadcasted_iota(jnp.int32, (BS, BS), 1)
    return (q_segments == k_segments) & (row >= col)


def forward_rows(heads, qb, low, qkv_ref, segment_ref, bias, out_ref, lse_ref):
    width = heads * HD
    lanes = head_lanes(heads, width)
    q_rows = block_rows(qb)
    q_all = (qkv_ref[q_rows, 0:width] * HD**-0.5).astype(BF16)
    q_heads = [own_head(q_all, lanes[h], heads) for h in range(heads)]
    q_segments = segment_column(qb, segment_ref)

    def k_step(kb, carry):
        k = qkv_ref[block_rows(kb), width : 2 * width]
        v = qkv_ref[block_rows(kb), 2 * width : 3 * width]
        allowed = block_mask(qb, kb, q_segments, segment_ref)
        place = jnp.minimum(qb - kb, 2)
        new = []
        for h in range(heads):
            top, total, acc = carry[3 * h : 3 * h + 3]
            s = jnp.where(allowed, nt(q_heads[h], k) + bias[h, place], NEG)
            top_new = jnp.maximum(top, jnp.max(s, axis=1, keepdims=True))
            alpha = jnp.exp(top - top_new)
            p = jnp.exp(s - top_new)
            total = alpha * total + jnp.sum(p, axis=1, keepdims=True)
            acc = alpha * acc + nn(p.astype(BF16), v)
            new += [top_new, total, acc]
        return tuple(new)

    init = []
    for h in range(heads):
        init += [jnp.full((BS, 1), NEG, F32), jnp.zeros((BS, 1), F32), jnp.zeros((BS, width), F32)]
    res = lax.fori_loop(low, qb + 1, k_step, tuple(init))
    out = jnp.zeros((BS, width), F32)
    for h in range(heads):
        top, total, acc = res[3 * h : 3 * h + 3]
        value = acc / total
        out = value if heads == 1 else jnp.where(lanes[h], value, out)
        lse_ref[q_rows, h : h + 1] = top + jnp.log(total)
    out_ref[q_rows, :] = out.astype(BF16)


def backward_rows(
    heads, qb, low, qkv_ref, out_ref, grad_ref, lse_ref, segment_ref, bias, grad_qkv_ref, dk, dv, sums
):
    width = heads * HD
    lanes = head_lanes(heads, width)
    scale = HD**-0.5
    q_rows = block_rows(qb)
    q_all = (qkv_ref[q_rows, 0:width] * scale).astype(BF16)
    g_all = grad_ref[q_rows, :]
    both = g_all.astype(F32) * out_ref[q_rows, :].astype(F32)
    q_heads = [own_head(q_all, lanes[h], heads) for h in range(heads)]
    g_heads = [own_head(g_all, lanes[h], heads) for h in range(heads)]
    deltas = [jnp.sum(own_head(both, lanes[h], heads), axis=1, keepdims=True) for h in range(heads)]
    totals = [lse_ref[q_rows, h : h + 1] for h in range(heads)]
    q_segments = segment_column(qb, segment_ref)

    def k_step(kb, dq):
        k_rows = block_rows(kb)
        k = qkv_ref[k_rows, width : 2 * width]
        v = qkv_ref[k_rows, 2 * width : 3 * width]
        allowed = block_mask(qb, kb, q_segments, segment_ref)
        place = jnp.minimum(qb - kb, 2)
        dk_add = jnp.zeros((BS, width), F32)
        dv_add = jnp.zeros((BS, width), F32)
        for h in range(heads):
            s = jnp.where(allowed, nt(q_heads[h], k) + bias[h, place], NEG)
            p = jnp.exp(s - totals[h])
            gp = nt(g_heads[h], v)
            ds = (p * (gp - deltas[h])).astype(BF16)
            dv_add += tn(p.astype(BF16), g_heads[h])
            dk_add += tn(ds, q_heads[h])
            dq = dq + own_head(nn(ds, k), lanes[h], heads)
            sums[h, place] += ds.astype(F32)
        dk[k_rows, :] += dk_add
        dv[k_rows, :] += dv_add
        return dq

    dq = lax.fori_loop(low, qb + 1, k_step, jnp.zeros((BS, width), F32))
    grad_qkv_ref[q_rows, 0:width] = (dq * scale).astype(BF16)


def backward_start(dk, dv, sums):
    dk[...] = jnp.zeros_like(dk)
    dv[...] = jnp.zeros_like(dv)
    sums[...] = jnp.zeros_like(sums)


def backward_end(heads, grad_qkv_ref, dk, dv):
    width = heads * HD
    grad_qkv_ref[:, width : 2 * width] = dk[...].astype(BF16)
    grad_qkv_ref[:, 2 * width : 3 * width] = dv[...].astype(BF16)


def diagonal_sums(heads, sums, diag_ref):
    row = lax.broadcasted_iota(jnp.int32, (BS, BS), 0)
    col = lax.broadcasted_iota(jnp.int32, (BS, BS), 1)
    upside_down = jnp.where(row + col == BS - 1, 1.0, 0.0).astype(F32)
    for h in range(heads):
        for t in range(2):
            flipped = jnp.dot(
                upside_down,
                sums[h, t],
                precision=lax.Precision.HIGHEST,
                preferred_element_type=F32,
            )
            wide = jnp.concatenate([flipped, jnp.zeros((BS, BS), F32)], axis=1)
            skewed = pltpu.roll(wide, 0, 1, stride=1, stride_axis=0)
            diag_ref[t, h : h + 1, :] = jnp.sum(skewed, axis=0, keepdims=True)
        rest = jnp.sum(sums[h, 2], axis=0, keepdims=True)
        diag_ref[2, h : h + 1, :] = jnp.concatenate([rest, jnp.zeros((1, BS), F32)], axis=1)


def attn_fwd_kernel(heads, blocks, lo_ref, qkv_ref, segment_ref, pattern_ref, out_ref, lse_ref, bias):
    build_bias(heads, pattern_ref, bias)

    def q_step(qb, _):
        forward_rows(heads, qb, lo_ref[qb], qkv_ref, segment_ref, bias, out_ref, lse_ref)
        return 0

    lax.fori_loop(0, blocks, q_step, 0)


def attn_bwd_kernel(
    heads,
    blocks,
    lo_ref,
    qkv_ref,
    out_ref,
    grad_ref,
    lse_ref,
    segment_ref,
    pattern_ref,
    grad_qkv_ref,
    diag_ref,
    bias,
    dk,
    dv,
    sums,
):
    build_bias(heads, pattern_ref, bias)
    backward_start(dk, dv, sums)

    def q_step(qb, _):
        backward_rows(
            heads,
            qb,
            lo_ref[qb],
            qkv_ref,
            out_ref,
            grad_ref,
            lse_ref,
            segment_ref,
            bias,
            grad_qkv_ref,
            dk,
            dv,
            sums,
        )
        return 0

    lax.fori_loop(0, blocks, q_step, 0)
    backward_end(heads, grad_qkv_ref, dk, dv)
    diagonal_sums(heads, sums, diag_ref)


def vspec():
    return pl.BlockSpec(memory_space=pltpu.VMEM)


def sspec():
    return pl.BlockSpec(memory_space=pltpu.SMEM)


def attention_forward(projected, lo, segments, patterns, heads):
    seq_len = projected.shape[0]
    blocks = seq_len // BS
    return pl.pallas_call(
        functools.partial(attn_fwd_kernel, heads, blocks),
        out_shape=(
            jax.ShapeDtypeStruct((seq_len, heads * HD), BF16),
            jax.ShapeDtypeStruct((seq_len, heads), F32),
        ),
        in_specs=[sspec(), vspec(), vspec(), vspec()],
        out_specs=(vspec(), vspec()),
        scratch_shapes=[pltpu.VMEM((heads, 3, BS, BS), F32)],
        compiler_params=pltpu.CompilerParams(vmem_limit_bytes=VMEM_LIMIT),
        name="attn_fwd",
    )(lo, projected, segments, patterns)


def attention_backward(projected, attended, grad, lse, lo, segments, patterns, heads):
    seq_len = projected.shape[0]
    blocks = seq_len // BS
    width = heads * HD
    return pl.pallas_call(
        functools.partial(attn_bwd_kernel, heads, blocks),
        out_shape=(
            jax.ShapeDtypeStruct((seq_len, 3 * width), BF16),
            jax.ShapeDtypeStruct((3, 8, 2 * BS), F32),
        ),
        in_specs=[sspec()] + [vspec()] * 6,
        out_specs=(vspec(), vspec()),
        scratch_shapes=backward_scratch(heads, seq_len),
        compiler_params=pltpu.CompilerParams(vmem_limit_bytes=VMEM_LIMIT),
        name="attn_bwd",
    )(lo, projected, attended, grad, lse, segments, patterns)


def backward_scratch(heads, seq_len):
    return [
        pltpu.VMEM((heads, 3, BS, BS), F32),
        pltpu.VMEM((seq_len, heads * HD), F32),
        pltpu.VMEM((seq_len, heads * HD), F32),
        pltpu.VMEM((heads, 3, BS, BS), F32),
    ]


MESH = pl.DeviceIdType.MESH
SMALL = 32


def remote(src, dst, send, recv, axis, peer):
    return pltpu.make_async_remote_copy(
        src_ref=src,
        dst_ref=dst,
        send_sem=send,
        recv_sem=recv,
        device_id={axis: peer},
        device_id_type=MESH,
    )


class Staging:
    def __init__(self):
        self.loads, self.stores, self.flying = [], {}, []

    def wait(self):
        for load in self.loads:
            load.wait()

    def put(self, *indices):
        for index in indices:
            copy = self.stores.pop(index)
            copy.start()
            self.flying.append(copy)

    def close(self):
        self.put(*list(self.stores))
        for copy in self.flying:
            copy.wait()


def staged(kernel, count, which, outs=0, which_out=()):
    extra = len(which) + len(which_out) + 2

    def run(*refs):
        inputs, outputs = list(refs[:count]), list(refs[count : count + outs])
        tail = refs[-extra:]
        buffers, in_sems, out_sems = tail[:-2], tail[-2], tail[-1]
        staging = Staging()
        for place, index in enumerate(which):
            copy = pltpu.make_async_copy(inputs[index], buffers[place], in_sems.at[place])
            copy.start()
            staging.loads.append(copy)
            inputs[index] = buffers[place]
        for place, index in enumerate(which_out):
            buffer = buffers[len(which) + place]
            staging.stores[index] = pltpu.make_async_copy(
                buffer, outputs[index], out_sems.at[place]
            )
            outputs[index] = buffer
        kernel(staging, *inputs, *outputs, *refs[count + outs : -extra])
        staging.close()

    return run


def staged_specs(args, which, shapes=(), which_out=()):
    specs = [any_spec() if i in which else vspec() for i in range(len(args))]
    scratch = [pltpu.VMEM(args[i].shape, args[i].dtype) for i in which]
    scratch += [pltpu.VMEM(shapes[i].shape, shapes[i].dtype) for i in which_out]
    dma = pltpu.SemaphoreType.DMA
    return specs, scratch + [dma((len(which),)), dma((max(1, len(which_out)),))]


def greet(groups, staging=None):
    barrier = pltpu.get_barrier_semaphore()
    total = 0
    for axis, n in groups:
        me = lax.axis_index(axis)
        for step in range(1, n):
            pl.semaphore_signal(
                barrier, inc=1, device_id={axis: lax.rem(me + step, n)}, device_id_type=MESH
            )
        total += n - 1
    pl.semaphore_wait(barrier, total)
    if staging is not None:
        staging.wait()


class LineSum:
    def __init__(self, n, parts, send, recv, send_sem, recv_sem, total):
        self.n, self.parts = n, parts
        self.send, self.recv, self.send_sem, self.recv_sem = send, recv, send_sem, recv_sem
        self.total = total
        self.me = lax.axis_index("tensor")

    def flow(self, first, k):
        n, me = self.n, self.me
        near = me * 2 < n
        right = near if first else jnp.logical_not(near)
        block = jnp.where(right, n - 1 - k, k)
        comes = jnp.where(right, jnp.where(me > 0, me <= block, False), jnp.where(me < n - 1, me >= block, False))
        goes = jnp.where(right, me < block, me > block)
        peer = jnp.clip(jnp.where(right, me + 1, me - 1), 0, n - 1)
        out_slot = jnp.clip(jnp.where(right, k, n - 1 - me + k), 0, n - 2)
        in_slot = jnp.clip(jnp.where(right, k, n - me + k), 0, n)
        peer_slot = jnp.clip(jnp.where(right, k, n - peer + k), 0, n)
        return block, comes, goes, peer, out_slot, in_slot, peer_slot

    def copy(self, peer, out_slot, slot):
        return remote(
            self.send.at[out_slot],
            self.recv.at[slot],
            self.send_sem.at[out_slot],
            self.recv_sem.at[slot],
            "tensor",
            peer,
        )

    def start(self, partial=None):
        n, me = self.n, self.me

        def one(index, _):
            block = jnp.where(me * 2 < n, n - 1 - index, index)
            if partial is not None:
                value = partial(block)
                self.parts[block] = value.astype(BF16)

                @pl.when(block == me)
                def _():
                    self.total[...] = value

            @pl.when(jnp.logical_or(me == 0, me == n - 1) & (index < n - 1))
            def _():
                remote(
                    self.parts.at[block],
                    self.recv.at[jnp.where(me == 0, index, 2 + index)],
                    self.send_sem.at[index],
                    self.recv_sem.at[jnp.where(me == 0, index, 2 + index)],
                    "tensor",
                    jnp.where(me == 0, 1, n - 2),
                ).start()

            return 0

        lax.fori_loop(0, n, one, 0)
        if partial is None:
            self.total[...] = self.parts[me].astype(F32)

    def finish(self):
        for k in range(self.n - 1):
            self.step(k)

    def step(self, k, flows=(True, False)):
        for first in flows:
            block, comes, goes, peer, out_slot, in_slot, peer_slot = self.flow(first, k)

            @pl.when(goes & comes)
            def _():
                self.copy(peer, out_slot, in_slot).wait_recv()
                self.send[out_slot] = (
                    self.parts[block].astype(F32) + self.recv[in_slot].astype(F32)
                ).astype(BF16)
                self.copy(peer, out_slot, peer_slot).start()

            @pl.when(comes & jnp.logical_not(goes))
            def _():
                self.copy(peer, 0, in_slot).wait_recv()
                self.total[...] += self.recv[in_slot].astype(F32)

    def drain(self):
        for k in range(self.n - 1):
            for first in (True, False):
                block, comes, goes, peer, out_slot, in_slot, peer_slot = self.flow(first, k)

                @pl.when(goes)
                def _():
                    self.copy(peer, out_slot, in_slot).wait_send()


def tail_kernel(
    n_dp,
    n_tensor,
    experts,
    table_rows,
    hidden_ref,
    grad_ref,
    weight_ref,
    attended_ref,
    branch_ref,
    small_ref,
    weight_own_ref,
    gain_own_ref,
    grad_hidden_ref,
    grad_qkv_ref,
    grad_out_ref,
    small_out_ref,
    parts,
    line_send,
    line_recv,
    qkv_send,
    qkv_recv,
    out_send,
    out_recv,
    small_recv,
    small_sum,
    gain_recv,
    line_send_sem,
    line_recv_sem,
    qkv_send_sem,
    qkv_recv_sem,
    out_send_sem,
    out_recv_sem,
    small_send_sem,
    small_recv_sem,
    gain_send_sem,
    gain_recv_sem,
):
    own_rows = grad_hidden_ref.shape[0]
    depth = weight_own_ref.shape[0]
    out_cols = grad_out_ref.shape[1]
    me = lax.axis_index("dp")
    me_t = lax.axis_index("tensor")
    greet([("dp", n_dp), ("tensor", n_tensor)])

    def partial(block):
        rows = pl.ds(pl.multiple_of(block * own_rows, own_rows), own_rows)
        return nt(grad_ref[rows, :], weight_ref[...])

    line = LineSum(
        n_tensor, parts, line_send, line_recv, line_send_sem, line_recv_sem, grad_hidden_ref
    )
    line.start(partial)
    copies = []
    for step in range(1, n_dp):
        peer = lax.rem(me + step, n_dp)
        copy = remote(
            small_ref.at[peer],
            small_recv.at[step - 1],
            small_send_sem.at[step - 1],
            small_recv_sem.at[step - 1],
            "dp",
            peer,
        )
        copy.start()
        copies.append(copy)
    for block in range(n_dp):
        cols = slice(block * depth, (block + 1) * depth)
        qkv_send[block] = tn(hidden_ref[:, cols], grad_ref[...]).astype(BF16)
    for step in range(1, n_dp):
        peer = lax.rem(me + step, n_dp)
        copy = remote(
            qkv_send.at[peer],
            qkv_recv.at[step - 1],
            qkv_send_sem.at[step - 1],
            qkv_recv_sem.at[step - 1],
            "dp",
            peer,
        )
        copy.start()
        copies.append(copy)
    for block in range(n_dp):
        cols = slice(block * out_cols, (block + 1) * out_cols)
        out_send[block] = tn(attended_ref[...], branch_ref[:, cols]).astype(BF16)
    for step in range(1, n_dp):
        peer = lax.rem(me + step, n_dp)
        copy = remote(
            out_send.at[peer],
            out_recv.at[step - 1],
            out_send_sem.at[step - 1],
            out_recv_sem.at[step - 1],
            "dp",
            peer,
        )
        copy.start()
        copies.append(copy)
    line.finish()
    for copy in copies:
        copy.wait()
    small_sum[...] = small_ref[me]
    grad_qkv_ref[...] = qkv_send[me].astype(F32)
    grad_out_ref[...] = out_send[me].astype(F32)
    for step in range(1, n_dp):
        small_sum[...] += small_recv[step - 1]
        grad_qkv_ref[...] += qkv_recv[step - 1].astype(F32)
        grad_out_ref[...] += out_recv[step - 1].astype(F32)
    column = jnp.sum(grad_qkv_ref[...] * weight_own_ref[...].astype(F32), axis=1, keepdims=True)
    eye = lax.broadcasted_iota(jnp.int32, (depth, depth), 0) == lax.broadcasted_iota(
        jnp.int32, (depth, depth), 1
    )
    row = jnp.sum(jnp.where(eye, column, 0.0), axis=0, keepdims=True)
    small_sum[experts + 1 : experts + 2, :] = row / gain_own_ref[...]
    gains = []
    for step in range(1, n_tensor):
        peer = lax.rem(me_t + step, n_tensor)
        copy = remote(
            small_sum,
            gain_recv.at[step - 1],
            gain_send_sem.at[step - 1],
            gain_recv_sem.at[step - 1],
            "tensor",
            peer,
        )
        copy.start()
        gains.append(copy)
    line.drain()
    for copy in gains:
        copy.wait()
    small_out_ref[...] = small_sum[...]
    shared = slice(0, experts + 2)
    for step in range(1, n_tensor):
        small_out_ref[shared, :] += gain_recv[step - 1, shared, :]


def tail(n_dp, n_tensor, experts, hidden, grad, weight, attended, branch, small, weight_own, gain_own):
    seq_len, width = hidden.shape
    own_rows = seq_len // n_tensor
    depth, cols = weight_own.shape
    heads_cols = attended.shape[1]
    out_cols = width // n_dp
    table_rows = NB // n_dp
    return pl.pallas_call(
        functools.partial(tail_kernel, n_dp, n_tensor, experts, table_rows),
        out_shape=(
            jax.ShapeDtypeStruct((own_rows, width), F32),
            jax.ShapeDtypeStruct((depth, cols), F32),
            jax.ShapeDtypeStruct((heads_cols, out_cols), F32),
            jax.ShapeDtypeStruct((SMALL, depth), F32),
        ),
        in_specs=[vspec()] * 8,
        out_specs=(vspec(),) * 4,
        scratch_shapes=[
            pltpu.VMEM((n_tensor, own_rows, width), BF16),
            pltpu.VMEM((n_tensor - 1, own_rows, width), BF16),
            pltpu.VMEM((n_tensor + 1, own_rows, width), BF16),
            pltpu.VMEM((n_dp, depth, cols), BF16),
            pltpu.VMEM((n_dp - 1, depth, cols), BF16),
            pltpu.VMEM((n_dp, heads_cols, out_cols), BF16),
            pltpu.VMEM((n_dp - 1, heads_cols, out_cols), BF16),
            pltpu.VMEM((n_dp - 1, SMALL, depth), F32),
            pltpu.VMEM((SMALL, depth), F32),
            pltpu.VMEM((n_tensor - 1, SMALL, depth), F32),
            pltpu.SemaphoreType.DMA((n_tensor - 1,)),
            pltpu.SemaphoreType.DMA((n_tensor + 1,)),
        ]
        + [pltpu.SemaphoreType.DMA((n_dp - 1,))] * 6
        + [pltpu.SemaphoreType.DMA((n_tensor - 1,))] * 2,
        compiler_params=pltpu.CompilerParams(
            vmem_limit_bytes=VMEM_LIMIT, collective_id=0, has_side_effects=True
        ),
        name="tail",
    )(hidden, grad, weight, attended, branch, small, weight_own, gain_own)


def diagonal(size):
    return lax.broadcasted_iota(jnp.int32, (size, size), 0) == lax.broadcasted_iota(
        jnp.int32, (size, size), 1
    )


def to_column(row):
    return jnp.sum(jnp.where(diagonal(row.shape[1]), row, 0.0), axis=1, keepdims=True)


def to_row(column):
    return jnp.sum(jnp.where(diagonal(column.shape[0]), column, 0.0), axis=0, keepdims=True)


def expert_kernel(
    n_dp,
    local,
    capacity,
    rows_hbm,
    grad_hbm,
    gates_ref,
    in_hbm,
    out_hbm,
    back_ref,
    gate_back_ref,
    value_ref,
    grad_in_ref,
    grad_out_ref,
    back_send,
    gate_send,
    zs,
    ups,
    gates_s,
    stage,
    value_stage,
    back_send_sem,
    back_recv_sem,
    gate_send_sem,
    gate_recv_sem,
    own_sem,
    stage_sem,
    value_sem,
    rows_ref,
    grad_ref,
    in_ref,
    out_ref,
    rows_sem,
    grad_sem,
    in_sem,
    out_sem,
):
    me = lax.axis_index("dp")
    pairs = n_dp // 2
    hidden = in_ref.shape[2]
    width = rows_ref.shape[2]
    two = 2 * capacity

    def pair_at(index):
        return (me // 2) ^ (pairs - 1 - index)

    def load_pair(index):
        where = pl.ds(2 * pair_at(index), 2)
        return (
            pltpu.make_async_copy(rows_hbm.at[where], rows_ref.at[where], rows_sem.at[index]),
            pltpu.make_async_copy(grad_hbm.at[where], grad_ref.at[where], grad_sem.at[index]),
        )

    def load_expert(expert):
        return (
            pltpu.make_async_copy(in_hbm.at[expert], in_ref.at[expert], in_sem.at[expert]),
            pltpu.make_async_copy(out_hbm.at[expert], out_ref.at[expert], out_sem.at[expert]),
        )

    for copy in load_expert(0) + load_pair(0):
        copy.start()
    for index in range(1, pairs):
        for copy in load_pair(index):
            copy.start()
    for expert in range(1, local):
        for copy in load_expert(expert):
            copy.start()
    greet([("dp", n_dp)])

    def back_copy(expert, target, sender):
        part = slice(expert * capacity, (expert + 1) * capacity)
        return remote(
            back_send.at[target, part],
            back_ref.at[sender, part],
            back_send_sem.at[expert, target],
            back_recv_sem.at[expert, sender],
            "dp",
            target,
        )

    def own_copy(expert):
        part = slice(expert * capacity, (expert + 1) * capacity)
        return pltpu.make_async_copy(
            back_send.at[me, part], back_ref.at[me, part], own_sem.at[expert]
        )

    def stage_copy(slot, target):
        return pltpu.make_async_copy(stage.at[slot], target, stage_sem.at[slot])

    gate_send[...] = jnp.zeros_like(gate_send)
    staged = []

    def put(value, target):
        slot = len(staged) % 2
        if len(staged) >= 2:
            staged[-2].wait()
        stage[slot] = value.astype(BF16)
        copy = stage_copy(slot, target)
        copy.start()
        staged.append(copy)

    for expert in range(local):
        part = slice(expert * capacity, (expert + 1) * capacity)

        for copy in load_expert(expert):
            copy.wait()

        def group(index, _):
            if expert == 0:
                for copy in load_pair(index):
                    copy.wait()
            first = 2 * pair_at(index)
            rows = rows_ref[pl.ds(first, 2), part, :].reshape(two, width)
            grads = grad_ref[pl.ds(first, 2), part, :].reshape(two, width)
            column = jnp.concatenate(
                [to_column(gates_ref[first + j, 0:1, part]) for j in range(2)], axis=0
            )
            gate = nt(rows, in_ref[expert, 0])
            up = nt(rows, in_ref[expert, 1])
            square = gate * gate
            bent = jnp.tanh(0.7978845608028654 * gate * (1.0 + 0.044715 * square))
            half = 0.5 * (1.0 + bent)
            gelu = gate * half
            slope = half + 0.5 * gate * (1.0 - bent * bent) * (
                0.7978845608028654 * (1.0 + 3 * 0.044715 * square)
            )
            z = gelu * up
            grad_z = nt(grads, out_ref[expert])
            gate_grad = jnp.sum(z * grad_z, axis=1, keepdims=True)
            grad_z = column * grad_z
            zs[pl.ds(first, 2)] = (column * z).astype(BF16).reshape(2, capacity, hidden)
            ups[0, pl.ds(first, 2)] = (grad_z * up * slope).astype(BF16).reshape(2, capacity, hidden)
            ups[1, pl.ds(first, 2)] = (grad_z * gelu).astype(BF16).reshape(2, capacity, hidden)
            for j in range(2):
                gate_send[first + j, 0:1, part] = to_row(
                    gate_grad[j * capacity : (j + 1) * capacity]
                )
            back = nn(ups[0, pl.ds(first, 2)].reshape(two, hidden), in_ref[expert, 0])
            back += nn(ups[1, pl.ds(first, 2)].reshape(two, hidden), in_ref[expert, 1])
            back_send[pl.ds(first, 2), part, :] = back.astype(BF16).reshape(2, capacity, width)
            for j in range(2):
                target = first + j

                @pl.when(target != me)
                def _():
                    back_copy(expert, target, me).start()

                @pl.when(target == me)
                def _():
                    own_copy(expert).start()

            return 0

        lax.fori_loop(0, pairs, group, 0)
        if expert == local - 1:
            gate_copies = []
            for step in range(1, n_dp):
                target = lax.rem(me + step, n_dp)
                copy = remote(
                    gate_send.at[target],
                    gate_back_ref.at[me],
                    gate_send_sem.at[step - 1],
                    gate_recv_sem.at[step - 1],
                    "dp",
                    target,
                )
                copy.start()
                gate_copies.append(copy)
            gate_back_ref[me] = gate_send[me]
        rows = rows_ref[:, part, :].reshape(n_dp * capacity, width)
        for half in range(2):
            put(tn(ups[half].reshape(n_dp * capacity, hidden), rows), grad_in_ref.at[expert, half])
        grads = grad_ref[:, part, :].reshape(n_dp * capacity, width)
        put(tn(zs[...].reshape(n_dp * capacity, hidden), grads), grad_out_ref.at[expert])
        if expert > 0:
            pltpu.make_async_copy(
                value_stage, value_ref.at[:, slice((expert - 1) * capacity, expert * capacity)], value_sem
            ).wait()

        def value(pair, _):
            out = nn(zs[pl.ds(2 * pair, 2)].reshape(two, hidden), out_ref[expert])
            value_stage[pl.ds(2 * pair, 2)] = out.astype(BF16).reshape(2, capacity, width)
            return 0

        lax.fori_loop(0, pairs, value, 0)
        pltpu.make_async_copy(value_stage, value_ref.at[:, part], value_sem).start()

    last = slice((local - 1) * capacity, local * capacity)
    pltpu.make_async_copy(value_stage, value_ref.at[:, last], value_sem).wait()
    for copy in staged[-2:]:
        copy.wait()
    for copy in gate_copies:
        copy.wait()
    for expert in range(local):
        own_copy(expert).wait()
        for step in range(1, n_dp):
            peer = lax.rem(me + step, n_dp)
            back_copy(expert, peer, me).wait_send()
            back_copy(expert, me, peer).wait_recv()


def any_spec():
    return pl.BlockSpec(memory_space=pl.ANY)


def run_experts(n_dp, capacity, rows, grads, gates, w_in, w_out):
    local, _, hidden, width = w_in.shape
    slots = local * capacity
    return pl.pallas_call(
        functools.partial(expert_kernel, n_dp, local, capacity),
        out_shape=(
            jax.ShapeDtypeStruct((n_dp, slots, width), BF16),
            jax.ShapeDtypeStruct((n_dp, 8, slots), F32),
            jax.ShapeDtypeStruct((n_dp, slots, width), BF16),
            jax.ShapeDtypeStruct(w_in.shape, BF16),
            jax.ShapeDtypeStruct(w_out.shape, BF16),
        ),
        in_specs=[any_spec(), any_spec(), vspec(), any_spec(), any_spec()],
        out_specs=(any_spec(), vspec(), any_spec(), any_spec(), any_spec()),
        scratch_shapes=[
            pltpu.VMEM((n_dp, slots, width), BF16),
            pltpu.VMEM((n_dp, 8, slots), F32),
            pltpu.VMEM((n_dp, capacity, hidden), BF16),
            pltpu.VMEM((2, n_dp, capacity, hidden), BF16),
            pltpu.VMEM((8, 128), F32),
            pltpu.VMEM((2, hidden, width), BF16),
            pltpu.VMEM((n_dp, capacity, width), BF16),
            pltpu.SemaphoreType.DMA((local, n_dp)),
            pltpu.SemaphoreType.DMA((local, n_dp)),
            pltpu.SemaphoreType.DMA((n_dp - 1,)),
            pltpu.SemaphoreType.DMA((n_dp - 1,)),
            pltpu.SemaphoreType.DMA((local,)),
            pltpu.SemaphoreType.DMA((2,)),
            pltpu.SemaphoreType.DMA,
            pltpu.VMEM(rows.shape, BF16),
            pltpu.VMEM(grads.shape, BF16),
            pltpu.VMEM(w_in.shape, BF16),
            pltpu.VMEM(w_out.shape, BF16),
            pltpu.SemaphoreType.DMA((n_dp // 2,)),
            pltpu.SemaphoreType.DMA((n_dp // 2,)),
            pltpu.SemaphoreType.DMA((local,)),
            pltpu.SemaphoreType.DMA((local,)),
        ],
        compiler_params=pltpu.CompilerParams(
            vmem_limit_bytes=VMEM_LIMIT, collective_id=1, has_side_effects=True
        ),
        name="experts",
    )(rows, grads, gates, w_in, w_out)


def chosen_slots(columns, slots):
    lane = lax.broadcasted_iota(jnp.int32, (1, slots), 1)
    return columns[:, 0:1] == lane, columns[:, 1:2] == lane


def combine_kernel(
    n_dp,
    n_tensor,
    experts,
    loads,
    rows_ref,
    gate_ref,
    slots_ref,
    routes_ref,
    residual_ref,
    hidden_ref,
    cotangent_ref,
    router_ref,
    gain_ref,
    weight_ref,
    value_ref,
    grad_residual_ref,
    branch_ref,
    grad_attended_ref,
    small_ref,
    merged_ref,
    parts,
    total,
    line_send,
    line_recv,
    gate_all,
    gate_send,
    gate_recv,
    value_back,
    line_send_sem,
    line_recv_sem,
    gate_send_sem,
    gate_recv_sem,
    value_send_sem,
    value_recv_sem,
    value_own_sem,
    gather_send_sem,
    gather_recv_sem,
):
    own_rows, width = residual_ref.shape
    slots = rows_ref.shape[0]
    per = slots // n_dp
    me = lax.axis_index("dp")
    me_t = lax.axis_index("tensor")
    greet([("dp", n_dp), ("tensor", n_tensor)], loads)
    values = []
    for step in range(1, n_dp):
        peer = lax.rem(me + step, n_dp)
        copy = remote(
            value_ref.at[peer],
            value_back.at[me],
            value_send_sem.at[step - 1],
            value_recv_sem.at[step - 1],
            "dp",
            peer,
        )
        copy.start()
        values.append(copy)
    fetch = pltpu.make_async_copy(value_ref.at[me], value_back.at[me], value_own_sem)
    fetch.start()

    def partial(block):
        one, two = chosen_slots(
            slots_ref[pl.ds(pl.multiple_of(block * own_rows, own_rows), own_rows), :], slots
        )
        return nn(jnp.where(one | two, 1.0, 0.0).astype(BF16), rows_ref[...])

    line = LineSum(n_tensor, parts, line_send, line_recv, line_send_sem, line_recv_sem, total)
    line.start(partial)
    for peer in range(n_dp):
        gate_all[0:1, peer * per : (peer + 1) * per] = gate_ref[peer, 0:1, :]
    gate_send[...] = jnp.zeros_like(gate_send)
    gates = []
    for step in range(n_tensor):
        peer = lax.rem(me_t + step, n_tensor)
        picks = chosen_slots(
            slots_ref[pl.ds(pl.multiple_of(peer * own_rows, own_rows), own_rows), :], slots
        )
        for k in range(TOP):
            column = jnp.sum(
                jnp.where(picks[k], gate_all[0:1, :], 0.0), axis=1, keepdims=True
            )
            gate_send[step, k : k + 1, :] = to_row(column)
        if step:
            copy = remote(
                gate_send.at[step],
                gate_recv.at[step - 1],
                gate_send_sem.at[step - 1],
                gate_recv_sem.at[step - 1],
                "tensor",
                peer,
            )
            copy.start()
            gates.append(copy)
    hidden = hidden_ref[...]
    router = router_ref[...]
    logits = nt(router, hidden)
    exps = jnp.exp(logits - jnp.max(logits, axis=0, keepdims=True))
    probs = exps / jnp.sum(exps, axis=0, keepdims=True)
    ids = lax.broadcasted_iota(jnp.int32, (experts, own_rows), 0)
    own_lanes = pl.ds(pl.multiple_of(me_t * own_rows, own_rows), own_rows)
    first, second = ids == routes_ref[0:1, own_lanes], ids == routes_ref[1:2, own_lanes]
    prob_one = jnp.sum(jnp.where(first, probs, 0.0), axis=0, keepdims=True)
    prob_two = jnp.sum(jnp.where(second, probs, 0.0), axis=0, keepdims=True)
    both = prob_one + prob_two
    line.finish()
    for copy in gates:
        copy.wait()
    gate_sum = gate_send[0]
    for step in range(1, n_tensor):
        gate_sum = gate_sum + gate_recv[step - 1]
    grad_one, grad_two = gate_sum[0:1, :], gate_sum[1:2, :]
    mean_grad = (prob_one * grad_one + prob_two * grad_two) / both
    grad_probs = (
        jnp.where(first, grad_one - mean_grad, 0.0) + jnp.where(second, grad_two - mean_grad, 0.0)
    ) / both
    grad_logits = probs * (grad_probs - jnp.sum(grad_probs * probs, axis=0, keepdims=True))
    grad_hidden = total[...] + lax.dot_general(
        grad_logits,
        router.astype(F32),
        (((0,), (0,)), ((), ())),
        precision=lax.Precision.HIGHEST,
        preferred_element_type=F32,
    )
    residual = residual_ref[...]
    scale = lax.rsqrt(jnp.mean(residual * residual, axis=1, keepdims=True) + EPS)
    unit = residual * scale
    small_ref[...] = jnp.zeros_like(small_ref)
    small_ref[experts : experts + 1, :] = jnp.sum(grad_hidden * unit, axis=0, keepdims=True)
    grad_unit = grad_hidden * gain_ref[1:2, :]
    grad_residual = cotangent_ref[...].astype(F32) + scale * (
        grad_unit - unit * jnp.mean(grad_unit * unit, axis=1, keepdims=True)
    )
    grad_residual_ref[...] = grad_residual
    loads.put(0)
    branch_ref[me_t] = grad_residual.astype(BF16)

    def on_block(block):
        grad_attended_ref[pl.ds(pl.multiple_of(block * own_rows, own_rows), own_rows), :] = nt(
            branch_ref[block], weight_ref[...]
        ).astype(BF16)

    lines = Streams(n_tensor, [branch_ref], gather_send_sem, gather_recv_sem)
    for turn in lines.turns():
        lines.turn(turn, lambda j, k: lines.each_new(j, k, on_block))
        if turn == n_tensor - 2:
            fetch.wait()
            for copy in values:
                copy.wait_recv()

            def merge(block, _):
                rows = pl.ds(pl.multiple_of(block * own_rows, own_rows), own_rows)
                one, two = chosen_slots(slots_ref[rows, :], slots)
                merged_ref[block] = nn(
                    jnp.where(one | two, 1.0, 0.0).astype(BF16), value_back[...].reshape(slots, width)
                ).astype(BF16)
                return 0

            lax.fori_loop(0, n_tensor, merge, 0)
            loads.put(4)
    loads.put(1, 2)
    lines.drain()
    small_ref[0:experts, :] = jnp.dot(
        grad_logits,
        hidden.astype(F32),
        precision=lax.Precision.HIGHEST,
        preferred_element_type=F32,
    )
    line.drain()
    for copy in values:
        copy.wait_send()


def combine(
    n_dp,
    n_tensor,
    experts,
    rows,
    gates,
    slot_columns,
    routes_own,
    residual,
    hidden,
    cotangent,
    router_rows,
    gain,
    weight,
    value,
):
    own_rows, width = residual.shape
    slots = rows.shape[0]
    args = (
        rows,
        gates,
        slot_columns,
        routes_own,
        residual,
        hidden,
        cotangent,
        router_rows,
        gain,
        weight,
        value,
    )
    which, which_out = (0, 4, 5, 6, 9), (0, 1, 2, 4)
    shapes = (
        jax.ShapeDtypeStruct((own_rows, width), F32),
        jax.ShapeDtypeStruct((n_tensor, own_rows, width), BF16),
        jax.ShapeDtypeStruct((n_tensor * own_rows, weight.shape[0]), BF16),
        jax.ShapeDtypeStruct((SMALL, width), F32),
        jax.ShapeDtypeStruct((n_tensor, own_rows, width), BF16),
    )
    specs, buffers = staged_specs(args[:10], which, shapes, which_out)
    return pl.pallas_call(
        staged(
            functools.partial(combine_kernel, n_dp, n_tensor, experts),
            len(args),
            which,
            len(shapes),
            which_out,
        ),
        out_shape=shapes,
        in_specs=specs + [any_spec()],
        out_specs=(any_spec(), any_spec(), any_spec(), vspec(), any_spec()),
        scratch_shapes=[
            pltpu.VMEM((n_tensor, own_rows, width), BF16),
            pltpu.VMEM((own_rows, width), F32),
            pltpu.VMEM((n_tensor - 1, own_rows, width), BF16),
            pltpu.VMEM((n_tensor + 1, own_rows, width), BF16),
            pltpu.VMEM((8, slots), F32),
            pltpu.VMEM((n_tensor, 8, own_rows), F32),
            pltpu.VMEM((n_tensor - 1, 8, own_rows), F32),
            pltpu.VMEM(value.shape, BF16),
            pltpu.SemaphoreType.DMA((n_tensor - 1,)),
            pltpu.SemaphoreType.DMA((n_tensor + 1,)),
            pltpu.SemaphoreType.DMA((n_tensor - 1,)),
            pltpu.SemaphoreType.DMA((n_tensor - 1,)),
            pltpu.SemaphoreType.DMA((n_dp - 1,)),
            pltpu.SemaphoreType.DMA((n_dp - 1,)),
            pltpu.SemaphoreType.DMA,
            pltpu.SemaphoreType.DMA((1, 2, n_tensor - 1)),
            pltpu.SemaphoreType.DMA((1, 2, n_tensor - 1)),
        ]
        + buffers,
        compiler_params=pltpu.CompilerParams(
            vmem_limit_bytes=VMEM_LIMIT, collective_id=2, has_side_effects=True
        ),
        name="combine",
    )(*args)


class Streams:
    def __init__(self, n, refs, send_sem, recv_sem):
        self.n, self.refs, self.send_sem, self.recv_sem = n, refs, send_sem, recv_sem
        self.me = lax.axis_index("tensor")

    def copy(self, j, block, slot, k, peer):
        ref = self.refs[j].at[block]
        return remote(
            ref, ref, self.send_sem.at[j, slot, k], self.recv_sem.at[j, slot, k], "tensor", peer
        )

    def outgoing(self, j, k, fn):
        for slot, sign in enumerate((1, -1)):
            block, peer = self.me - sign * k, self.me + sign

            @pl.when((block >= 0) & (block < self.n) & (peer >= 0) & (peer < self.n))
            def _():
                fn(self.copy(j, block, slot, k, peer))

    def incoming(self, j, k, fn):
        for slot, sign in enumerate((1, -1)):
            block = self.me - sign * (k + 1)

            @pl.when((block >= 0) & (block < self.n))
            def _():
                fn(self.copy(j, block, slot, k, jnp.clip(self.me - sign, 0, self.n - 1)), block)

    def turn(self, turn, used=None):
        moved = []
        for j in range(len(self.refs)):
            k = turn - j
            if k < 0 or k > self.n - 1:
                continue
            self.advance(j, k)
            moved.append((j, k))
        if used is not None:
            for j, k in moved:
                used(j, k)

    def turns(self):
        return range(self.n + len(self.refs) - 1)

    def advance(self, j, k):
        if k > 0:
            self.incoming(j, k - 1, lambda c, block: c.wait_recv())
        if k < self.n - 1:
            self.outgoing(j, k, lambda c: c.start())

    def each_new(self, j, k, fn):
        if k == 0:
            fn(self.me)
            return
        for sign in (1, -1):
            block = self.me - sign * k

            @pl.when((block >= 0) & (block < self.n))
            def _():
                fn(block)

    def drain(self):
        for j in range(len(self.refs)):
            for k in range(self.n - 1):
                self.outgoing(j, k, lambda c: c.wait_send())


class Spread:
    def __init__(self, n, ref, far_send, far_recv, near_send, near_recv):
        self.n, self.ref = n, ref
        self.far_send, self.far_recv = far_send, far_recv
        self.near_send, self.near_recv = near_send, near_recv
        self.me = lax.axis_index("dp")
        self.partner = self.me ^ 1

    def far(self, step, block, peer):
        ref = self.ref.at[block]
        return remote(ref, ref, self.far_send.at[step], self.far_recv.at[step], "dp", peer)

    def near(self, step, block):
        ref = self.ref.at[block]
        return remote(
            ref, ref, self.near_send.at[step], self.near_recv.at[step], "dp", self.partner
        )

    def start(self):
        for step in range(1, self.n // 2):
            self.far(step - 1, self.me, lax.rem(self.me + 2 * step, self.n)).start()
        self.near(0, self.me).start()

    def source(self, me, step):
        return lax.rem(me + self.n - 2 * step, self.n)

    def relay(self):
        for step in range(1, self.n // 2):
            block = self.source(self.me, step)
            self.far(step - 1, block, block).wait_recv()
            self.near(step, block).start()

    def finish(self):
        for step in range(self.n // 2):
            self.near(step, self.source(self.partner, step)).wait_recv()

    def drain(self):
        for step in range(1, self.n // 2):
            self.far(step - 1, self.me, lax.rem(self.me + 2 * step, self.n)).wait_send()
        for step in range(self.n // 2):
            self.near(step, self.source(self.me, step)).wait_send()


def one_hot(slot_rows, target, per):
    lane_slots = lax.broadcasted_iota(jnp.int32, (per, 1), 0) + target * per
    return jnp.where(
        (lane_slots == slot_rows[0:1, :]) | (lane_slots == slot_rows[1:2, :]), 1.0, 0.0
    ).astype(BF16)


def band(seq_len):
    return -(-(seq_len // 2 - 1) // BS)


def send_parameters(n_dp, n_tensor, weight_ref, extra_ref, out_ref, weights_ref, outs_ref, extras_ref, sems):
    me = lax.axis_index("dp")
    me_t = lax.axis_index("tensor")
    (extra_send, extra_recv, line_send, line_recv) = sems[:4]
    extras_ref[me] = extra_ref[...]
    small = []
    for step in range(1, n_dp):
        peer = lax.rem(me + step, n_dp)
        copy = remote(
            extra_ref, extras_ref.at[me], extra_send.at[step - 1], extra_recv.at[step - 1], "dp", peer
        )
        copy.start()
        small.append(copy)
    cols = weight_ref.shape[2]
    for part in range(3):
        weights_ref[me, :, part * cols : (part + 1) * cols] = weight_ref[part]
    weights = Spread(n_dp, weights_ref, *sems[4:8])
    weights.start()
    outs_ref[me, me_t] = out_ref[...]
    along = []
    for step in range(1, n_tensor):
        peer = lax.rem(me_t + step, n_tensor)
        copy = remote(
            out_ref,
            outs_ref.at[me, me_t],
            line_send.at[step - 1],
            line_recv.at[step - 1],
            "tensor",
            peer,
        )
        copy.start()
        along.append(copy)
    return small, weights, Spread(n_dp, outs_ref, *sems[8:12]), along


def unpack_parameters(n_dp, experts, extras_ref, selector_ref, router_ref, table, pattern_ref):
    depth = table.shape[1]
    rows_each = NB // n_dp
    for block in range(n_dp):
        router_ref[:, block * depth : (block + 1) * depth] = extras_ref[block, 0:experts, :]
        table[block * rows_each : (block + 1) * rows_each, :] = extras_ref[
            block, experts + 2 : experts + 2 + rows_each, :
        ].astype(F32)
    patterns = lax.dot_general(
        table[...],
        selector_ref[...],
        (((0,), (0,)), ((), ())),
        precision=lax.Precision.HIGHEST,
        preferred_element_type=F32,
    )
    for row in range(pattern_ref.shape[0]):
        pattern_ref[row : row + 1, :] = patterns[
            row // 2 : row // 2 + 1, (row % 2) * 2 * BS : (row % 2 + 1) * 2 * BS
        ]


def first_hidden(n_dp, experts, tokens_ref, extras_ref, gains_ref, small):
    depth = extras_ref.shape[2]
    x = tokens_ref[...].astype(F32)
    scaled = x * lax.rsqrt(jnp.mean(x * x, axis=1, keepdims=True) + EPS)
    for copy in small:
        copy.wait()
    for block in range(n_dp):
        gains_ref[0:2, block * depth : (block + 1) * depth] = extras_ref[
            block, experts : experts + 2, :
        ].astype(F32)
    return (scaled * gains_ref[0:1, :]).astype(BF16)


def parameter_sems(n_dp, n_tensor):
    dma = pltpu.SemaphoreType.DMA
    return (
        [dma((n_dp - 1,))] * 2 + [dma((n_tensor - 1,))] * 2 + [dma((n_dp // 2,))] * 8
    )


def front_kernel(
    n_dp,
    n_tensor,
    experts,
    tokens_ref,
    weight_ref,
    extra_ref,
    out_ref,
    selector_ref,
    hidden_ref,
    projected_ref,
    weights_ref,
    outs_ref,
    pattern_ref,
    router_ref,
    gains_ref,
    extras_ref,
    table,
    *sems,
):
    own_rows, width = tokens_ref.shape
    me_t = lax.axis_index("tensor")
    greet([("dp", n_dp), ("tensor", n_tensor)])
    small, weights, spread, along = send_parameters(
        n_dp, n_tensor, weight_ref, extra_ref, out_ref, weights_ref, outs_ref, extras_ref, sems
    )
    hidden_ref[me_t] = first_hidden(n_dp, experts, tokens_ref, extras_ref, gains_ref, small)
    lines = Streams(n_tensor, [hidden_ref], sems[12], sems[13])
    lines.turn(0)
    unpack_parameters(n_dp, experts, extras_ref, selector_ref, router_ref, table, pattern_ref)
    weights.relay()
    for copy in along:
        copy.wait_recv()
    spread.start()
    weights.finish()
    spread.relay()
    spread.finish()

    def project(block):
        rows = pl.ds(pl.multiple_of(block * own_rows, own_rows), own_rows)
        projected_ref[rows, :] = nn(
            hidden_ref[block], weights_ref[...].reshape(width, weights_ref.shape[2])
        ).astype(BF16)

    for turn in lines.turns():
        if turn:
            lines.turn(turn)

    def every(block, _):
        project(block)
        return 0

    lax.fori_loop(0, n_tensor, every, 0)
    lines.drain()
    weights.drain()
    spread.drain()
    for copy in along:
        copy.wait_send()


def front(n_dp, n_tensor, experts, tokens, weight, extra, out, selectors):
    own_rows, width = tokens.shape
    seq_len = own_rows * n_tensor
    depth, cols = weight.shape[1], 3 * weight.shape[2]
    heads = cols // (3 * HD)
    dma = pltpu.SemaphoreType.DMA
    return pl.pallas_call(
        functools.partial(front_kernel, n_dp, n_tensor, experts),
        out_shape=(
            jax.ShapeDtypeStruct((n_tensor, own_rows, width), BF16),
            jax.ShapeDtypeStruct((seq_len, cols), BF16),
            jax.ShapeDtypeStruct((n_dp, depth, cols), BF16),
            jax.ShapeDtypeStruct((n_dp, n_tensor) + out.shape, BF16),
            jax.ShapeDtypeStruct((2 * heads, 2 * BS), F32),
            jax.ShapeDtypeStruct((experts, width), BF16),
            jax.ShapeDtypeStruct((2, width), F32),
        ),
        in_specs=[vspec()] * 5,
        out_specs=(vspec(),) * 7,
        scratch_shapes=[pltpu.VMEM((n_dp,) + extra.shape, BF16), pltpu.VMEM((NB, depth), F32)]
        + parameter_sems(n_dp, n_tensor)
        + [dma((1, 2, n_tensor - 1))] * 2,
        compiler_params=pltpu.CompilerParams(
            vmem_limit_bytes=VMEM_LIMIT, collective_id=3, has_side_effects=True
        ),
        name="front",
    )(tokens, weight, extra, out, selectors)


PARTS = 4
ROW_PARTS = 8


class Dispatch:
    def __init__(self, n_dp, picks, stage, rows_ref, send_sem, recv_sem, own_sem):
        self.n, self.picks, self.stage, self.rows = n_dp, picks, stage, rows_ref
        self.send_sem, self.recv_sem, self.own_sem = send_sem, recv_sem, own_sem
        self.me = lax.axis_index("dp")

    def cols(self, j):
        part = self.stage.shape[3]
        return slice(j * part, (j + 1) * part)

    def copy(self, j, target, sender):
        return remote(
            self.stage.at[j, target],
            self.rows.at[sender, :, self.cols(j)],
            self.send_sem.at[j, target],
            self.recv_sem.at[j, sender],
            "dp",
            target,
        )

    def own(self, j):
        return pltpu.make_async_copy(
            self.stage.at[j, self.me], self.rows.at[self.me, :, self.cols(j)], self.own_sem.at[j]
        )

    def start(self, j, values_ref):
        n_tensor, own_rows, part = values_ref.shape

        def one(index, _):
            mask = self.n - 1 - index
            target = self.me ^ mask
            self.stage[j, target] = nn(
                self.picks[target], values_ref[...].reshape(n_tensor * own_rows, part)
            ).astype(BF16)

            @pl.when(mask != 0)
            def _():
                self.copy(j, target, self.me).start()

            @pl.when(mask == 0)
            def _():
                self.own(j).start()

            return 0

        lax.fori_loop(0, self.n, one, 0)

    def finish(self):
        for j in range(self.stage.shape[0]):
            self.own(j).wait()
            for step in range(1, self.n):
                peer = lax.rem(self.me + step, self.n)
                self.copy(j, peer, self.me).wait_send()
                self.copy(j, self.me, peer).wait_recv()


def opening_kernel(
    n_dp,
    n_tensor,
    experts,
    capacity,
    loads,
    tokens_ref,
    cotangent_ref,
    weight_ref,
    extra_ref,
    out_ref,
    routes_ref,
    segment_ref,
    selector_ref,
    hidden_ref,
    projected_ref,
    weights_ref,
    pattern_ref,
    router_ref,
    gains_ref,
    slots_ref,
    attended_ref,
    lse_ref,
    residual_ref,
    hidden_two_ref,
    weight_own_ref,
    rows_ref,
    grad_rows_ref,
    gates_ref,
    extras_ref,
    table,
    outs,
    out_matrix,
    grads,
    everyone,
    picks,
    grad_stage,
    row_stage,
    bias,
    slot_rows,
    attended_recv,
    logits,
    gate_stage,
    *sems,
):
    own_rows, width = tokens_ref.shape
    seq_len = own_rows * n_tensor
    heads = pattern_ref.shape[0] // 2
    head_cols = heads * HD
    out_cols = out_ref.shape[1]
    local = experts // n_dp
    per = local * capacity
    part = width // PARTS
    row_part = width // ROW_PARTS
    me = lax.axis_index("dp")
    me_t = lax.axis_index("tensor")
    (hop_send, hop_recv, late_send, late_recv) = sems[12:16]
    (grad_send, grad_recv, grad_own, row_send, row_recv, row_own) = sems[16:22]
    (gate_send, gate_recv, attended_send_sem, attended_recv_sem) = sems[22:26]
    greet([("dp", n_dp), ("tensor", n_tensor)], loads)

    def rows_of(block):
        return pl.ds(pl.multiple_of(block * own_rows, own_rows), own_rows)

    for j in range(PARTS):
        grads[j, me_t] = cotangent_ref[:, j * part : (j + 1) * part]
    lines = Streams(
        n_tensor, [hidden_ref] + [grads.at[j] for j in range(PARTS)], hop_send, hop_recv
    )
    lines.advance(1, 0)
    lines.advance(2, 0)
    small, weights, spread, along = send_parameters(
        n_dp, n_tensor, weight_ref, extra_ref, out_ref, weights_ref, outs, extras_ref, sems
    )
    hidden_ref[me_t] = first_hidden(n_dp, experts, tokens_ref, extras_ref, gains_ref, small)
    lines.advance(1, 1)
    lines.advance(2, 1)
    unpack_parameters(n_dp, experts, extras_ref, selector_ref, router_ref, table, pattern_ref)
    lines.advance(1, 2)
    lines.advance(2, 2)
    lines.advance(0, 0)

    ids = lax.broadcasted_iota(jnp.int32, (experts, seq_len), 0)
    hits = [ids == routes_ref[k : k + 1, :] for k in range(TOP)]
    before = lax.broadcasted_iota(jnp.int32, (seq_len, seq_len), 0) < lax.broadcasted_iota(
        jnp.int32, (seq_len, seq_len), 1
    )
    ranks = nn(
        jnp.where(hits[0] | hits[1], 1.0, 0.0).astype(BF16),
        jnp.where(before, 1.0, 0.0).astype(BF16),
    )
    places = ranks + (ids * capacity).astype(F32)
    for k in range(TOP):
        row = jnp.sum(jnp.where(hits[k], places, 0.0), axis=0, keepdims=True)
        slot_rows[k : k + 1, :] = row.astype(jnp.int32)
        for block in range(n_tensor):
            rows = slice(block * own_rows, (block + 1) * own_rows)
            slots_ref[rows, k : k + 1] = to_column(row[:, rows]).astype(jnp.int32)


    def pick(target, _):
        picks[target] = one_hot(slot_rows, target, per)
        return 0

    lax.fori_loop(0, n_dp, pick, 0)
    grad_moves = Dispatch(n_dp, picks, grad_stage, grad_rows_ref, grad_send, grad_recv, grad_own)
    lines.advance(1, 3)
    grad_moves.start(0, grads.at[0])
    lines.advance(2, 3)
    grad_moves.start(1, grads.at[1])
    weights.relay()
    for copy in along:
        copy.wait_recv()
    spread.start()
    build_bias(heads, pattern_ref, bias)

    def project(block):
        projected_ref[rows_of(block), :] = nn(
            hidden_ref[block], weights_ref[...].reshape(width, weights_ref.shape[2])
        ).astype(BF16)

    lines.advance(0, 1)
    weights.finish()
    project(me_t)
    lines.advance(0, 2)
    lines.advance(3, 0)
    lines.advance(4, 0)
    spread.relay()
    lines.each_new(0, 1, project)
    lines.advance(0, 3)
    lines.advance(3, 1)
    lines.advance(4, 1)
    lines.each_new(0, 2, project)
    lines.each_new(0, 3, project)

    def attended_copy(target, sender):
        return remote(
            attended_ref.at[rows_of(target)],
            attended_recv.at[sender],
            attended_send_sem.at[target],
            attended_recv_sem.at[sender],
            "tensor",
            target,
        )

    def attend(qb):
        forward_rows(
            heads,
            qb,
            max(0, qb - band(seq_len)),
            projected_ref,
            segment_ref,
            bias,
            attended_ref,
            lse_ref,
        )

        @pl.when(me_t == qb)
        def _():
            attended_recv[me_t] = attended_ref[rows_of(me_t), :]

        @pl.when(me_t != qb)
        def _():
            attended_copy(qb, me_t).start()

    lines.advance(3, 2)
    lines.advance(4, 2)
    attend(3)
    attend(0)
    lines.advance(3, 3)
    grad_moves.start(2, grads.at[2])
    lines.advance(4, 3)
    attend(2)
    attend(1)
    grad_moves.start(3, grads.at[3])
    loads.put(0, 1, 2, 7)
    spread.finish()
    for block in range(n_dp):
        out_matrix[:, block * out_cols : (block + 1) * out_cols] = outs[block].reshape(
            width, out_cols
        )
    weight_own_ref[...] = out_matrix[
        pl.ds(pl.multiple_of(me_t * head_cols, head_cols), head_cols), :
    ]
    for step in range(1, n_tensor):
        attended_copy(me_t, lax.rem(me_t + step, n_tensor)).wait_recv()
    residual = tokens_ref[...].astype(F32)
    for block in range(n_tensor):
        residual += nn(
            attended_recv[block], out_matrix[block * head_cols : (block + 1) * head_cols, :]
        )
    residual_ref[...] = residual
    hidden = (
        residual
        * lax.rsqrt(jnp.mean(residual * residual, axis=1, keepdims=True) + EPS)
        * gains_ref[1:2, :]
    ).astype(BF16)
    hidden_two_ref[...] = hidden
    for j in range(ROW_PARTS):
        everyone[j, me_t] = hidden[:, j * row_part : (j + 1) * row_part]
    loads.put(9, 10, 11)
    late = Streams(n_tensor, [everyone.at[j] for j in range(ROW_PARTS)], late_send, late_recv)
    row_moves = Dispatch(n_dp, picks, row_stage, rows_ref, row_send, row_recv, row_own)

    def used(j, k):
        if k < n_tensor - 1:
            return
        row_moves.start(j, everyone.at[j])
        term = nt(
            router_ref[:, j * row_part : (j + 1) * row_part], everyone[j].reshape(seq_len, row_part)
        )
        if j == 0:
            logits[...] = term
        else:
            logits[...] += term

    for turn in late.turns():
        late.turn(turn, used)
    values = logits[...]
    exps = jnp.exp(values - jnp.max(values, axis=0, keepdims=True))
    probs = exps / jnp.sum(exps, axis=0, keepdims=True)
    named = (ids == routes_ref[0:1, :]) | (ids == routes_ref[1:2, :])
    shares = probs / jnp.sum(jnp.where(named, probs, 0.0), axis=0, keepdims=True)
    logits[...] = shares

    def gate_copy(target, sender):
        return remote(
            gate_stage.at[target],
            gates_ref.at[sender],
            gate_send.at[target],
            gate_recv.at[sender],
            "dp",
            target,
        )

    def gate(index, _):
        mask = n_dp - 1 - index
        target = me ^ mask
        for expert in range(local):
            row = jnp.sum(
                jnp.where(ids == target * local + expert, logits[...], 0.0), axis=0, keepdims=True
            )
            high = row.astype(BF16)
            rest = row - high.astype(F32)
            mid = rest.astype(BF16)
            low = (rest - mid.astype(F32)).astype(BF16)
            lanes = slice(expert * capacity, (expert + 1) * capacity)
            pieces = nt(
                jnp.concatenate([high, mid, low, jnp.zeros((5, seq_len), BF16)], axis=0),
                picks[target, lanes, :],
            )
            gate_stage[target, :, lanes] = jnp.broadcast_to(
                jnp.sum(pieces, axis=0, keepdims=True), (8, capacity)
            )

        @pl.when(mask != 0)
        def _():
            gate_copy(target, me).start()

        @pl.when(mask == 0)
        def _():
            gates_ref[target] = gate_stage[target]

        return 0

    lax.fori_loop(0, n_dp, gate, 0)
    lines.drain()
    late.drain()
    weights.drain()
    spread.drain()
    for copy in along:
        copy.wait_send()
    for step in range(1, n_tensor):
        attended_copy(lax.rem(me_t + step, n_tensor), me_t).wait_send()
    for step in range(1, n_dp):
        peer = lax.rem(me + step, n_dp)
        gate_copy(peer, me).wait_send()
        gate_copy(me, peer).wait_recv()
    grad_moves.finish()
    row_moves.finish()


def opening(
    n_dp,
    n_tensor,
    experts,
    capacity,
    tokens,
    cotangent,
    weight,
    extra,
    out,
    routes,
    segments,
    selectors,
):
    own_rows, width = tokens.shape
    seq_len = own_rows * n_tensor
    depth, cols = weight.shape[1], 3 * weight.shape[2]
    per = experts // n_dp * capacity
    part = width // PARTS
    row_part = width // ROW_PARTS
    heads = cols // (3 * HD)
    dma = pltpu.SemaphoreType.DMA
    rows = jax.ShapeDtypeStruct((n_dp, per, width), BF16)
    args = (tokens, cotangent, weight, extra, out, routes, segments, selectors)
    which, which_out = (0, 1, 2, 4), (0, 1, 2, 7, 9, 10, 11)
    shapes = (
            jax.ShapeDtypeStruct((n_tensor, own_rows, width), BF16),
            jax.ShapeDtypeStruct((seq_len, cols), BF16),
            jax.ShapeDtypeStruct((n_dp, depth, cols), BF16),
            jax.ShapeDtypeStruct((2 * heads, 2 * BS), F32),
            jax.ShapeDtypeStruct((experts, width), BF16),
            jax.ShapeDtypeStruct((2, width), F32),
            jax.ShapeDtypeStruct((seq_len, TOP), jnp.int32),
            jax.ShapeDtypeStruct((seq_len, heads * HD), BF16),
            jax.ShapeDtypeStruct((seq_len, heads), F32),
            jax.ShapeDtypeStruct((own_rows, width), F32),
            jax.ShapeDtypeStruct((own_rows, width), BF16),
            jax.ShapeDtypeStruct((heads * HD, width), BF16),
            rows,
            rows,
            jax.ShapeDtypeStruct((n_dp, 8, per), F32),
    )
    specs, buffers = staged_specs(args, which, shapes, which_out)
    return pl.pallas_call(
        staged(
            functools.partial(opening_kernel, n_dp, n_tensor, experts, capacity),
            len(args),
            which,
            len(shapes),
            which_out,
        ),
        out_shape=shapes,
        in_specs=specs,
        out_specs=tuple(
            any_spec() if i in which_out or i in (12, 13) else vspec() for i in range(len(shapes))
        ),
        scratch_shapes=[
            pltpu.VMEM((n_dp,) + extra.shape, BF16),
            pltpu.VMEM((NB, depth), F32),
            pltpu.VMEM((n_dp, n_tensor) + out.shape, BF16),
            pltpu.VMEM((width, width), BF16),
            pltpu.VMEM((PARTS, n_tensor, own_rows, part), BF16),
            pltpu.VMEM((ROW_PARTS, n_tensor, own_rows, row_part), BF16),
            pltpu.VMEM((n_dp, per, seq_len), BF16),
            pltpu.VMEM((PARTS, n_dp, per, part), BF16),
            pltpu.VMEM((ROW_PARTS, n_dp, per, row_part), BF16),
            pltpu.VMEM((heads, 3, BS, BS), F32),
            pltpu.VMEM((8, seq_len), jnp.int32),
            pltpu.VMEM((n_tensor, own_rows, heads * HD), BF16),
            pltpu.VMEM((experts, seq_len), F32),
            pltpu.VMEM((n_dp, 8, per), F32),
        ]
        + parameter_sems(n_dp, n_tensor)
        + [dma((PARTS + 1, 2, n_tensor - 1))] * 2
        + [dma((ROW_PARTS, 2, n_tensor - 1))] * 2
        + [dma((PARTS, n_dp)), dma((PARTS, n_dp)), dma((PARTS,))]
        + [dma((ROW_PARTS, n_dp)), dma((ROW_PARTS, n_dp)), dma((ROW_PARTS,))]
        + [dma((n_dp,))] * 2
        + [dma((n_tensor,))] * 2
        + buffers,
        compiler_params=pltpu.CompilerParams(
            vmem_limit_bytes=VMEM_LIMIT, collective_id=4, has_side_effects=True
        ),
        name="opening",
    )(*args)


def last_kernel(
    n_dp,
    n_tensor,
    experts,
    heads,
    loads,
    qkv_ref,
    attended_ref,
    grad_attended_ref,
    lse_ref,
    segment_ref,
    pattern_ref,
    skew_ref,
    hidden_ref,
    weight_ref,
    branch_ref,
    small_ref,
    weight_own_ref,
    gain_own_ref,
    merged_ref,
    residual_ref,
    grad_residual_ref,
    tokens_ref,
    gain_ref,
    layer_ref,
    grad_tokens_ref,
    grad_weight_ref,
    grad_out_ref,
    small_out_ref,
    bias,
    dk,
    dv,
    sums,
    grad_qkv,
    diag,
    parts,
    mixture,
    grad_hidden,
    mix_send,
    mix_recv,
    line_send,
    line_recv,
    qkv_send,
    qkv_recv,
    out_send,
    out_recv,
    small_send,
    small_recv,
    small_sum,
    gain_recv,
    mix_send_sem,
    mix_recv_sem,
    line_send_sem,
    line_recv_sem,
    qkv_send_sem,
    qkv_recv_sem,
    out_send_sem,
    out_recv_sem,
    small_send_sem,
    small_recv_sem,
    gain_send_sem,
    gain_recv_sem,
):
    own_rows, width = residual_ref.shape
    seq_len = own_rows * n_tensor
    depth = weight_own_ref.shape[1]
    out_cols = grad_out_ref.shape[1]
    me = lax.axis_index("dp")
    me_t = lax.axis_index("tensor")
    greet([("dp", n_dp), ("tensor", n_tensor)], loads)

    def rows_of(block):
        return pl.ds(pl.multiple_of(block * own_rows, own_rows), own_rows)

    mix = LineSum(n_tensor, merged_ref, mix_send, mix_recv, mix_send_sem, mix_recv_sem, mixture)
    line = LineSum(n_tensor, parts, line_send, line_recv, line_send_sem, line_recv_sem, grad_hidden)
    copies = []

    def scatter(source, target, send_sem, recv_sem):
        for step in range(1, n_dp):
            peer = lax.rem(me + step, n_dp)
            copy = remote(
                source.at[peer],
                target.at[step - 1],
                send_sem.at[step - 1],
                recv_sem.at[step - 1],
                "dp",
                peer,
            )
            copy.start()
            copies.append(copy)

    mix.start()
    build_bias(heads, pattern_ref, bias)
    backward_start(dk, dv, sums)
    blocks = seq_len // BS
    for qb in range(blocks):
        backward_rows(
            heads,
            qb,
            max(0, qb - band(seq_len)),
            qkv_ref,
            attended_ref,
            grad_attended_ref,
            lse_ref,
            segment_ref,
            bias,
            grad_qkv,
            dk,
            dv,
            sums,
        )
        if qb == 0:
            for block in range(n_dp):
                cols = slice(block * out_cols, (block + 1) * out_cols)
                out_send[block] = tn(attended_ref[...], branch_ref[:, cols]).astype(BF16)
            scatter(out_send, out_recv, out_send_sem, out_recv_sem)
        if qb == blocks - 2:
            mix.step(0, (True,))
    mix.step(0, (False,))
    mix.step(1, (True,))
    backward_end(heads, grad_qkv, dk, dv)
    line.start(lambda block: nt(grad_qkv[rows_of(block), :], weight_ref[...]))
    for block in range(n_dp):
        cols = slice(block * depth, (block + 1) * depth)
        qkv_send[block] = tn(hidden_ref[:, cols], grad_qkv[...]).astype(BF16)
    scatter(qkv_send, qkv_recv, qkv_send_sem, qkv_recv_sem)
    line.step(0, (True,))
    diag[...] = jnp.zeros_like(diag)
    diagonal_sums(heads, sums, diag)
    tables = lax.dot_general(
        skew_ref[...],
        jnp.concatenate([diag[0], diag[1]], axis=1),
        (((1,), (1,)), ((), ())),
        precision=lax.Precision.HIGHEST,
        preferred_element_type=F32,
    )
    far = jnp.sum(diag[2], axis=1, keepdims=True)
    head = lax.broadcasted_iota(jnp.int32, (8, 8), 0)
    lane = lax.broadcasted_iota(jnp.int32, (8, 8), 1)
    far_row = jnp.sum(jnp.where(head == lane, far, 0.0), axis=0, keepdims=True)
    bucket = lax.broadcasted_iota(jnp.int32, (NB, 8), 0)
    tables += jnp.where(bucket == NB - 1, far_row, 0.0)
    rows_each = NB // n_dp
    for block in range(n_dp):
        small_send[block] = small_ref[:, block * depth : (block + 1) * depth]
        small_send[block, experts + 2 : experts + 2 + rows_each, 0:8] = tables[
            block * rows_each : (block + 1) * rows_each, :
        ]
    scatter(small_send, small_recv, small_send_sem, small_recv_sem)
    mix.step(1, (False,))
    for k in range(2, n_tensor - 1):
        mix.step(k)
    layer_ref[...] = (residual_ref[...] + mixture[...]).astype(BF16)
    line.step(0, (False,))
    for k in range(1, n_tensor - 2):
        line.step(k)
    for copy in copies:
        copy.wait_recv()
    small_sum[...] = small_send[me]
    grad_weight_ref[...] = qkv_send[me].astype(F32)
    grad_out_ref[...] = out_send[me].astype(F32)
    for step in range(1, n_dp):
        small_sum[...] += small_recv[step - 1]
        grad_weight_ref[...] += qkv_recv[step - 1].astype(F32)
        grad_out_ref[...] += out_recv[step - 1].astype(F32)
    column = jnp.zeros((depth, 1), F32)
    part = weight_own_ref.shape[2]
    for k in range(3):
        column += jnp.sum(
            grad_weight_ref[:, k * part : (k + 1) * part] * weight_own_ref[k].astype(F32),
            axis=1,
            keepdims=True,
        )
    small_sum[experts + 1 : experts + 2, :] = to_row(column) / gain_own_ref[...].astype(F32)
    gains = []
    for step in range(1, n_tensor):
        peer = lax.rem(me_t + step, n_tensor)
        copy = remote(
            small_sum,
            gain_recv.at[step - 1],
            gain_send_sem.at[step - 1],
            gain_recv_sem.at[step - 1],
            "tensor",
            peer,
        )
        copy.start()
        gains.append(copy)
    line.step(n_tensor - 2)
    x = tokens_ref[...].astype(F32)
    scale = lax.rsqrt(jnp.mean(x * x, axis=1, keepdims=True) + EPS)
    unit = x * scale
    grad_unit = grad_hidden[...] * gain_ref[0:1, :]
    grad_tokens_ref[...] = (
        grad_residual_ref[...]
        + scale * (grad_unit - unit * jnp.mean(grad_unit * unit, axis=1, keepdims=True))
    ).astype(BF16)
    mix.drain()
    line.drain()
    for copy in copies:
        copy.wait_send()
    for copy in gains:
        copy.wait()
    small_out_ref[...] = small_sum[...]
    shared = slice(0, experts + 2)
    for step in range(1, n_tensor):
        small_out_ref[shared, :] += gain_recv[step - 1, shared, :]


def last(
    n_dp,
    n_tensor,
    experts,
    heads,
    projected,
    attended,
    grad_attended,
    lse,
    segments,
    patterns,
    skew,
    hidden,
    weight,
    branch,
    small,
    weight_own,
    gain_own,
    merged,
    residual,
    grad_residual,
    tokens,
    gain,
):
    seq_len, width = hidden.shape
    own_rows = seq_len // n_tensor
    depth, cols = weight_own.shape[1], 3 * weight_own.shape[2]
    out_cols = width // n_dp
    dma = pltpu.SemaphoreType.DMA
    line = [
        pltpu.VMEM((n_tensor - 1, own_rows, width), BF16),
        pltpu.VMEM((n_tensor + 1, own_rows, width), BF16),
    ]
    args = (
        projected,
        attended,
        grad_attended,
        lse,
        segments,
        patterns,
        skew,
        hidden,
        weight,
        branch,
        small,
        weight_own,
        gain_own,
        merged,
        residual,
        grad_residual,
        tokens,
        gain,
    )
    which = (0, 1, 2, 7, 8, 9, 11, 13, 14, 15, 16)
    specs, buffers = staged_specs(args, which)
    return pl.pallas_call(
        staged(functools.partial(last_kernel, n_dp, n_tensor, experts, heads), len(args), which),
        out_shape=(
            jax.ShapeDtypeStruct((own_rows, width), BF16),
            jax.ShapeDtypeStruct((own_rows, width), BF16),
            jax.ShapeDtypeStruct((depth, cols), F32),
            jax.ShapeDtypeStruct((heads * HD, out_cols), F32),
            jax.ShapeDtypeStruct((SMALL, depth), F32),
        ),
        in_specs=specs,
        out_specs=(vspec(),) * 5,
        scratch_shapes=backward_scratch(heads, seq_len)
        + [
            pltpu.VMEM((seq_len, cols), BF16),
            pltpu.VMEM((3, 8, 2 * BS), F32),
        ]
        + [pltpu.VMEM((n_tensor, own_rows, width), BF16)]
        + [pltpu.VMEM((own_rows, width), F32)] * 2
        + line * 2
        + [
            pltpu.VMEM((n_dp, depth, cols), BF16),
            pltpu.VMEM((n_dp - 1, depth, cols), BF16),
            pltpu.VMEM((n_dp, heads * HD, out_cols), BF16),
            pltpu.VMEM((n_dp - 1, heads * HD, out_cols), BF16),
            pltpu.VMEM((n_dp, SMALL, depth), F32),
            pltpu.VMEM((n_dp - 1, SMALL, depth), F32),
            pltpu.VMEM((SMALL, depth), F32),
            pltpu.VMEM((n_tensor - 1, SMALL, depth), F32),
        ]
        + [dma((n_tensor - 1,)), dma((n_tensor + 1,))] * 2
        + [dma((n_dp - 1,))] * 6
        + [dma((n_tensor - 1,))] * 2
        + buffers,
        compiler_params=pltpu.CompilerParams(
            vmem_limit_bytes=VMEM_LIMIT, collective_id=5, has_side_effects=True
        ),
        name="last",
    )(*args)


def deliver_kernel(
    grad_in_ref,
    grad_out_ref,
    layer_in_ref,
    tokens_in_ref,
    weight_in_ref,
    out_in_ref,
    small_ref,
    layer_ref,
    tokens_ref,
    weight_ref,
    out_ref,
    table_ref,
    gain_one_ref,
    gain_two_ref,
    router_ref,
    in_ref,
    down_ref,
    stage_in,
    stage_down,
    wide_in,
    wide_down,
    in_sem,
    down_sem,
    out_sem,
    last_sem,
):
    local, halves = grad_in_ref.shape[:2]
    pieces = [
        (
            grad_in_ref.at[e, g],
            stage_in.at[e, g],
            wide_in.at[e, g],
            in_ref.at[e, g],
            in_sem.at[e, g],
            out_sem.at[e, g],
        )
        for e in range(local)
        for g in range(halves)
    ] + [
        (
            grad_out_ref.at[e],
            stage_down.at[e],
            wide_down.at[e],
            down_ref.at[e],
            down_sem.at[e],
            last_sem.at[e],
        )
        for e in range(local)
    ]
    for source, stage, _, _, sem, _ in pieces:
        pltpu.make_async_copy(source, stage, sem).start()
    layer_ref[...] = layer_in_ref[...]
    tokens_ref[...] = tokens_in_ref[...]
    cols = weight_ref.shape[2]
    for part in range(3):
        weight_ref[part] = weight_in_ref[:, part * cols : (part + 1) * cols]
    out_ref[...] = out_in_ref[...]
    experts = router_ref.shape[0]
    router_ref[...] = small_ref[0:experts, :]
    gain_two_ref[...] = small_ref[experts : experts + 1, :]
    gain_one_ref[...] = small_ref[experts + 1 : experts + 2, :]
    table_ref[...] = small_ref[
        experts + 2 : experts + 2 + table_ref.shape[0], 0 : table_ref.shape[1]
    ]
    for source, stage, wide, target, sem, done in pieces:
        pltpu.make_async_copy(source, stage, sem).wait()
        wide[...] = stage[...].astype(F32)
        pltpu.make_async_copy(wide, target, done).start()
    for _, _, wide, target, _, done in pieces:
        pltpu.make_async_copy(wide, target, done).wait()


def deliver(experts, heads, table_rows, grad_in, grad_out, layer, tokens, weight, out, small):
    depth, cols = weight.shape
    local, halves = grad_in.shape[:2]
    dma = pltpu.SemaphoreType.DMA
    return pl.pallas_call(
        deliver_kernel,
        out_shape=(
            jax.ShapeDtypeStruct(layer.shape, BF16),
            jax.ShapeDtypeStruct(tokens.shape, BF16),
            jax.ShapeDtypeStruct((3, depth, cols // 3), F32),
            jax.ShapeDtypeStruct(out.shape, F32),
            jax.ShapeDtypeStruct((table_rows, heads), F32),
            jax.ShapeDtypeStruct((1, depth), F32),
            jax.ShapeDtypeStruct((1, depth), F32),
            jax.ShapeDtypeStruct((experts, depth), F32),
            jax.ShapeDtypeStruct(grad_in.shape, F32),
            jax.ShapeDtypeStruct(grad_out.shape, F32),
        ),
        in_specs=[any_spec()] * 2 + [vspec()] * 5,
        out_specs=(vspec(),) * 8 + (any_spec(),) * 2,
        scratch_shapes=[
            pltpu.VMEM(grad_in.shape, grad_in.dtype),
            pltpu.VMEM(grad_out.shape, grad_out.dtype),
            pltpu.VMEM(grad_in.shape, F32),
            pltpu.VMEM(grad_out.shape, F32),
            dma((local, halves)),
            dma((local,)),
            dma((local, halves)),
            dma((local,)),
        ],
        compiler_params=pltpu.CompilerParams(vmem_limit_bytes=VMEM_LIMIT),
        name="deliver",
    )(grad_in, grad_out, layer, tokens, weight, out, small)


def rms_scale(values):
    return lax.rsqrt(jnp.mean(values * values, axis=-1, keepdims=True) + EPS)


def norm_backward(grad_normed, values, scale_inv, gain):
    normed_unit = values * scale_inv
    grad_unit = grad_normed * gain
    grad_values = scale_inv * (
        grad_unit - normed_unit * jnp.mean(grad_unit * normed_unit, axis=-1, keepdims=True)
    )
    return (grad_values, jnp.sum(grad_normed * normed_unit, axis=0))


def gelu_tanh(values):
    return jax.nn.gelu(values, approximate=True)


def route_slots(route_ids, experts, capacity):
    flat_routes = route_ids.reshape(-1)
    onehot = (flat_routes[:, None] == jnp.arange(experts, dtype=jnp.int32)[None, :]).astype(
        jnp.int32
    )
    ranks = jnp.cumsum(onehot, axis=0) - 1
    rank_own = jnp.sum(ranks * onehot, axis=1)
    return (flat_routes * capacity + rank_own).reshape(-1, TOP)


def on_device(
    tokens,
    segments,
    routes,
    w_qkv,
    w_attn_out,
    bias_table,
    gain_attn,
    gain_moe,
    router,
    w_in,
    w_out,
    cotangent,
):
    own_rows, model_width = tokens.shape
    n_tensor = lax.axis_size("tensor")
    n_dp = lax.axis_size("dp")
    seq_len = own_rows * n_tensor
    own_start = lax.axis_index("tensor") * own_rows
    head_cols = w_qkv.shape[2]
    heads = head_cols // HD
    experts = router.shape[1]
    local_experts = w_in.shape[0]
    capacity = 5 * seq_len * TOP // (4 * experts)
    highest = lax.Precision.HIGHEST
    slots = experts * capacity

    depth = w_qkv.shape[0]
    bias_rows = NB // n_dp
    lanes = depth
    extra = jnp.concatenate(
        [
            jnp.transpose(router),
            gain_attn[None],
            gain_moe[None],
            jnp.pad(bias_table, ((0, SMALL - experts - 2 - bias_rows), (0, lanes - heads))),
        ],
        axis=0,
    )
    fast = n_dp == 8 and n_tensor == 4 and seq_len == 4 * BS and slots * model_width <= 4 * 1024 * 1024
    route_rows = jnp.transpose(routes)
    weight_parts = jnp.transpose(w_qkv, (1, 0, 2))
    skew = jnp.asarray(skew_selectors().T)
    selectors = jnp.asarray(distance_selectors().T)

    def finish(layer_out, grad_tokens, reduced_qkv, reduced_attn_out, small_sum, grad_w_in, grad_w_out):
        (
            layer_out,
            grad_tokens,
            grad_w_qkv,
            grad_w_attn_out,
            grad_table,
            grad_gain_one,
            grad_gain_two,
            grad_router,
            grad_w_in,
            grad_w_out,
        ) = deliver(
            experts,
            heads,
            NB // n_dp,
            grad_w_in,
            grad_w_out,
            layer_out,
            grad_tokens,
            reduced_qkv,
            reduced_attn_out,
            small_sum,
        )
        return (
            layer_out,
            grad_tokens,
            jnp.transpose(grad_w_qkv, (1, 0, 2)),
            grad_w_attn_out,
            grad_table,
            grad_gain_one[0],
            grad_gain_two[0],
            jnp.transpose(grad_router),
            grad_w_in,
            grad_w_out,
        )

    if fast:
        (
            gathered,
            projected,
            weights_full,
            patterns,
            router_rows,
            gains,
            slot_columns,
            attended,
            lse,
            residual,
            hidden_two,
            weight_own,
            rows,
            grad_rows,
            row_gates,
        ) = opening(
            n_dp,
            n_tensor,
            experts,
            capacity,
            tokens,
            cotangent,
            weight_parts,
            extra,
            w_attn_out,
            route_rows,
            segments,
            selectors,
        )
        back, gate_back, value, grad_w_in, grad_w_out = run_experts(
            n_dp, capacity, rows, grad_rows, row_gates, w_in, w_out
        )
        grad_residual, grad_branch_all, grad_attended, small, merged = combine(
            n_dp,
            n_tensor,
            experts,
            back.reshape(slots, model_width),
            gate_back,
            slot_columns,
            route_rows,
            residual,
            hidden_two,
            cotangent,
            router_rows,
            gains,
            weight_own,
            value,
        )
        results = last(
            n_dp,
            n_tensor,
            experts,
            heads,
            projected,
            attended,
            grad_attended,
            lse,
            segments,
            patterns,
            skew,
            gathered.reshape(seq_len, model_width),
            weights_full.reshape(model_width, 3 * head_cols),
            grad_branch_all.reshape(seq_len, model_width),
            small,
            weight_parts,
            gain_attn[None],
            merged,
            residual,
            grad_residual,
            tokens,
            gains,
        )
        return finish(*results, grad_w_in, grad_w_out)
    gathered, projected, weights_full, outs_full, patterns, router_rows, gains = front(
        n_dp, n_tensor, experts, tokens, weight_parts, extra, w_attn_out, selectors
    )
    gathered_one = gathered.reshape(seq_len, model_width)
    qkv_matrix = weights_full.reshape(model_width, 3 * head_cols)
    outs_full = outs_full.reshape(n_dp, model_width, model_width // n_dp)
    tokens_float = tokens.astype(F32)
    scale_one = rms_scale(tokens_float)
    gain_one, gain_two = gains[0], gains[1]
    starts = segments[0, ::BS]
    ends = segments[0, BS - 1 :: BS]
    lowest = jnp.sum((ends[None, :] < starts[:, None]).astype(jnp.int32), axis=1)
    attended, lse = attention_forward(projected, lowest, segments, patterns, heads)
    router_full = jnp.transpose(router_rows)
    out_matrix = jnp.transpose(outs_full, (1, 0, 2)).reshape(model_width, model_width)
    attended_own = lax.all_to_all(
        attended.reshape(n_tensor, own_rows, head_cols), "tensor", 0, 0
    )
    attended_own = jnp.transpose(attended_own, (1, 0, 2)).reshape(own_rows, n_tensor * head_cols)
    branch = jnp.dot(attended_own, out_matrix, preferred_element_type=F32)
    residual = tokens_float + branch
    scale_two = rms_scale(residual)
    hidden_two = (residual * scale_two * gain_two).astype(BF16)
    gathered_two = lax.all_gather(hidden_two, "tensor", axis=0, tiled=True)

    expert_ids = jnp.arange(experts, dtype=jnp.int32)

    def gate_values(logit_values, route_rows):
        expert_probs = jax.nn.softmax(logit_values, axis=-1)
        picked = jnp.sum(
            jnp.where(
                route_rows[:, :, None] == expert_ids[None, None, :], expert_probs[:, None, :], 0.0
            ),
            axis=-1,
        )
        return picked / jnp.sum(picked, axis=1, keepdims=True)

    gates = gate_values(jnp.dot(gathered_two, router_full, preferred_element_type=F32), routes)
    slot_ids = route_slots(routes, experts, capacity)
    slot_flat = slot_ids.reshape(-1)
    token_ids = jnp.repeat(jnp.arange(seq_len, dtype=jnp.int32), TOP)
    sources = jnp.full((slots,), seq_len, jnp.int32).at[slot_flat].set(token_ids)
    slot_gates = jnp.zeros((slots,), F32).at[slot_flat].set(gates.reshape(-1))
    grad_gathered = lax.all_gather(cotangent, "tensor", axis=0, tiled=True)

    def exchange(rows):
        parts = rows.reshape(n_dp, local_experts, capacity, model_width)
        return [
            lax.all_to_all(parts[:, i], "dp", 0, 0).reshape(n_dp * capacity, model_width)
            for i in range(local_experts)
        ]

    def give_back(parts):
        back = [
            lax.all_to_all(part.reshape(n_dp, capacity, model_width), "dp", 0, 0) for part in parts
        ]
        return jnp.stack(back, axis=1).reshape(slots, model_width)

    zero_row = jnp.zeros((1, model_width), BF16)
    dispatched = exchange(jnp.concatenate([gathered_two, zero_row], axis=0)[sources])
    padded_grad = jnp.concatenate([grad_gathered, zero_row], axis=0)
    grad_expert = exchange((slot_gates[:, None] * padded_grad[sources]).astype(BF16))

    outs, backs, grads_in, grads_out = [], [], [], []
    for i in range(local_experts):
        rows, grad_rows = dispatched[i], grad_expert[i]
        gate_part = nt(rows, w_in[i, 0])
        up_part = nt(rows, w_in[i, 1])
        gelu_value, gelu_pull = jax.vjp(gelu_tanh, gate_part)
        activated = (gelu_value * up_part).astype(BF16)
        outs.append(nn(activated, w_out[i]).astype(BF16))
        grad_act = nt(grad_rows, w_out[i])
        grads_out.append(tn(activated, grad_rows))
        grad_gate = gelu_pull(grad_act * up_part)[0].astype(BF16)
        grad_up = (grad_act * gelu_value).astype(BF16)
        backs.append((nn(grad_gate, w_in[i, 0]) + nn(grad_up, w_in[i, 1])).astype(BF16))
        grads_in.append(jnp.stack([tn(grad_gate, rows), tn(grad_up, rows)]))
    grad_w_in = jnp.stack(grads_in)
    grad_w_out = jnp.stack(grads_out)
    expert_out = give_back(outs)
    grad_dispatched = give_back(backs)

    first, second = slot_ids[:, 0], slot_ids[:, 1]
    picked_first = expert_out[first].astype(F32)
    picked_second = expert_out[second].astype(F32)
    mixture = lax.psum_scatter(
        (gates[:, 0:1] * picked_first + gates[:, 1:2] * picked_second).astype(BF16),
        "tensor",
        scatter_dimension=0,
        tiled=True,
    ).astype(F32)
    layer_out = (residual + mixture).astype(BF16)
    grad_float = grad_gathered.astype(F32)
    grad_gate_part = jnp.stack(
        [
            jnp.sum(grad_float * picked_first, axis=1),
            jnp.sum(grad_float * picked_second, axis=1),
        ],
        axis=1,
    )
    grad_hidden_part = (
        grad_dispatched[first].astype(F32) + grad_dispatched[second].astype(F32)
    ).astype(BF16)
    grad_own = lax.psum_scatter(
        grad_hidden_part, "tensor", scatter_dimension=0, tiled=True
    ).astype(F32)
    grad_gate_own = lax.dynamic_slice_in_dim(
        lax.psum(grad_gate_part, "tensor"), own_start, own_rows, 0
    )
    own_routes = lax.dynamic_slice_in_dim(routes, own_start, own_rows, 0)
    own_logits = jnp.dot(hidden_two, router_full, preferred_element_type=F32)

    def own_gates(logit_values):
        return gate_values(logit_values, own_routes)

    _, gate_pull = jax.vjp(own_gates, own_logits)
    grad_logits = gate_pull(grad_gate_own)[0]
    router_float = router_full.astype(F32)
    grad_hidden_two = grad_own + jnp.dot(grad_logits, router_float.T, precision=highest)
    grad_router_part = jnp.dot(hidden_two.astype(F32).T, grad_logits, precision=highest)
    grad_from_norm, grad_gain_two = norm_backward(grad_hidden_two, residual, scale_two, gain_two)
    grad_residual = cotangent.astype(F32) + grad_from_norm

    grad_branch = grad_residual.astype(BF16)
    grad_attended_own = nt(grad_branch, out_matrix).astype(BF16)
    grad_attended = lax.all_to_all(
        jnp.transpose(grad_attended_own.reshape(own_rows, n_tensor, head_cols), (1, 0, 2)),
        "tensor",
        0,
        0,
    ).reshape(seq_len, head_cols)
    grad_branch_all = lax.all_gather(grad_branch, "tensor", axis=0, tiled=True)
    small = jnp.concatenate(
        [
            jnp.transpose(grad_router_part),
            grad_gain_two[None],
            jnp.zeros((SMALL - experts - 1, model_width), F32),
        ],
        axis=0,
    )
    grad_projected, diag = attention_backward(
        projected, attended, grad_attended, lse, lowest, segments, patterns, heads
    )
    near = jnp.concatenate([diag[0, :heads], diag[1, :heads]], axis=1)
    grad_table = lax.dot_general(skew, near, (((1,), (1,)), ((), ())), precision=highest)
    grad_table = grad_table.at[NB - 1].add(jnp.sum(diag[2, :heads], axis=1))
    small = jnp.transpose(small.reshape(SMALL, n_dp, depth), (1, 0, 2))
    small = lax.dynamic_update_slice(
        small, grad_table.reshape(n_dp, NB // n_dp, heads), (0, experts + 2, 0)
    )
    grad_hidden_one, reduced_qkv, reduced_attn_out, small_sum = tail(
        n_dp,
        n_tensor,
        experts,
        gathered_one,
        grad_projected,
        qkv_matrix,
        attended,
        grad_branch_all,
        small,
        w_qkv.reshape(depth, 3 * head_cols),
        gain_attn[None].astype(F32),
    )
    grad_from_first, _ = norm_backward(grad_hidden_one, tokens_float, scale_one, gain_one)
    grad_tokens = (grad_residual + grad_from_first).astype(BF16)
    return finish(
        layer_out, grad_tokens, reduced_qkv, reduced_attn_out, small_sum, grad_w_in, grad_w_out
    )


def solution(mesh):
    return jax.shard_map(
        on_device,
        mesh=mesh,
        in_specs=(
            P(("dp", "tensor"), None),
            P("dp", None),
            P("dp", None),
            P("dp", None, "tensor"),
            P("tensor", "dp"),
            P("dp", "tensor"),
            P("dp"),
            P("dp"),
            P("dp", None),
            P("dp", None, "tensor", None),
            P("dp", "tensor", None),
            P(("dp", "tensor"), None),
        ),
        out_specs=(
            P(("dp", "tensor"), None),
            P(("dp", "tensor"), None),
            P("dp", None, "tensor"),
            P("tensor", "dp"),
            P("dp", "tensor"),
            P("dp"),
            P("dp"),
            P("dp", None),
            P("dp", None, "tensor", None),
            P("dp", "tensor", None),
        ),
        check_vma=False,
    )
```
